32 devices in a mesh: seq: 8 (over z, x), shard: 4 (over y, core).
Axes of the slice: x: 2, y: 2, z: 4, core: 2. Of those that a mesh axis runs over, the one named last changes fastest.
Arguments:
- tokens: bfloat16 [2, 4, 512, 2048], P(None, 'shard', 'seq'), may hold values from -6 to 6
- first_gain: float32 [2048], replicated, may hold values from 0.5 to 1.5
- branch_weight: bfloat16 [2048, 2736], P('shard'), may hold values from -0.125 to 0.125
- input_weight: bfloat16 [2048, 2736], P('shard'), may hold values from -0.125 to 0.125
- conv_weight: bfloat16 [4, 2736], P(None, 'seq'), may hold values from -3 to 3
- conv_bias: float32 [2736], P('seq'), may hold values from -3 to 3
- rate_weight: bfloat16 [16, 171, 171], P('seq'), may hold values from -0.4375 to 0.4375
- rate_bias: float32 [2736], P('seq'), may hold values from -4 to 4
- entry_weight: bfloat16 [16, 171, 171], P('seq'), may hold values from -0.4375 to 0.4375
- entry_bias: float32 [2736], P('seq'), may hold values from -4 to 4
- decay_param: float32 [2736], P('seq'), may hold values from 4.3 to 9
- output_weight: bfloat16 [2736, 2048], P(None, 'shard'), may hold values from -0.109375 to 0.109375
- second_gain: float32 [2048], replicated, may hold values from 0.5 to 1.5
- hidden_gate: bfloat16 [2048, 6144], P(None, 'shard'), may hold values from -0.125 to 0.125
- hidden_up: bfloat16 [2048, 6144], P(None, 'shard'), may hold values from -0.125 to 0.125
- hidden_down: bfloat16 [6144, 2048], P('shard'), may hold values from -0.078125 to 0.078125
- cotangent: bfloat16 [2, 4, 512, 2048], P(None, 'shard', 'seq'), may hold values from -6 to 6
Outputs:
- result: bfloat16 [2, 4, 512, 2048], P(None, 'shard', 'seq')
- tokens_grad: float32 [2, 4, 512, 2048], P(None, 'shard', 'seq')
- first_gain_grad: float32 [2048], P(('seq', 'shard'))
- branch_weight_grad: float32 [2048, 2736], P(('seq', 'shard'))
- input_weight_grad: float32 [2048, 2736], P(('seq', 'shard'))
- conv_weight_grad: float32 [4, 2736], P(None, 'seq')
- conv_bias_grad: float32 [2736], P('seq')
- rate_weight_grad: float32 [16, 171, 171], P('seq')
- rate_bias_grad: float32 [2736], P('seq')
- entry_weight_grad: float32 [16, 171, 171], P('seq')
- entry_bias_grad: float32 [2736], P('seq')
- decay_grad: float32 [2736], P('seq')
- output_weight_grad: float32 [2736, 2048], P(None, ('seq', 'shard'))
- second_gain_grad: float32 [2048], P(('seq', 'shard'))
- hidden_gate_grad: float32 [2048, 6144], P(('seq', 'shard'))
- hidden_up_grad: float32 [2048, 6144], P(('seq', 'shard'))
- hidden_down_grad: float32 [6144, 2048], P(None, ('seq', 'shard'))
The draws below stay inside these ranges and needn't reach their ends.
All inputs are finite; a program needn't handle non-finite values.
Results may differ from the reference program's by a relative error of at most 0.012.
Values may be sent and summed in bfloat16 or wider, within the bound.
A program may use at most 576 MiB of HBM per device.

```python
import jax
import jax.numpy as jnp
from jax import lax

D = 2048
BLOCKS = 16
BLOCK_W = 171
FF = 6144
CONV = 4
QUARTERS = 2
LRU = 2736
QLEN = 512
SEQS = 4


def block_scale(key, dims, shards, low, top_value):
    def one(axis_at, shards_of):
        draws = jax.random.uniform(jax.random.fold_in(jax.random.fold_in(key, 6), axis_at), (shards_of,), jnp.float32, low / len(shards), top_value / len(shards))
        return jnp.repeat(jnp.exp(draws), dims[axis_at] // shards_of).reshape((-1,) + (1,) * (len(dims) - axis_at - 1))

    loudness = one(*shards[0])
    for cut in shards[1:]:
        loudness = loudness * one(*cut)
    return loudness


def bell_draw(stream_key, dims, spread, reach, cuts=(), dtype=jnp.bfloat16):
    values = jax.random.normal(stream_key, dims, jnp.float32) * spread
    if len(cuts) > 0:
        values = block_scale(stream_key, dims, cuts, -0.22, 0.18) * values
    return jnp.clip(values, min=-reach, max=reach).astype(dtype)


def setup_inputs(seed: int = 0) -> dict:
    key_list = jax.random.split(jax.random.key(seed), 18)
    tokens = bell_draw(key_list[0], (QUARTERS, SEQS, QLEN, D), 1.0, 6.0, ((1, 4), (2, 8)))
    first_gain = jnp.clip(1.0 + 0.1 * jax.random.normal(key_list[1], (D,), jnp.float32), 0.5, 1.5)
    branch_weight = bell_draw(key_list[2], (D, LRU), D ** -0.5, 0.125, ((0, 4),))
    input_weight = bell_draw(key_list[3], (D, LRU), D ** -0.5, 0.125, ((0, 4),))
    conv_weight = bell_draw(key_list[4], (CONV, LRU), CONV ** -0.5, 3.0, ((1, 8),))
    conv_bias = bell_draw(key_list[5], (LRU,), 0.5, 3.0, ((0, 8),), jnp.float32)
    rate_weight = bell_draw(key_list[6], (BLOCKS, BLOCK_W, BLOCK_W), BLOCK_W ** -0.5, 0.4375, ((0, 8),))
    rate_bias = bell_draw(key_list[7], (LRU,), 1.0, 4.0, ((0, 8),), jnp.float32)
    entry_weight = bell_draw(key_list[8], (BLOCKS, BLOCK_W, BLOCK_W), BLOCK_W ** -0.5, 0.4375, ((0, 8),))
    entry_bias = bell_draw(key_list[9], (LRU,), 1.0, 4.0, ((0, 8),), jnp.float32)
    decay_param = jnp.clip(4.3 + 4.7 * jax.random.uniform(key_list[10], (LRU,), jnp.float32) ** block_scale(key_list[10], (LRU,), ((0, 8),), -0.2, 0.2), 4.3, 9.0)
    output_weight = bell_draw(key_list[11], (LRU, D), LRU ** -0.5, 0.109375, ((1, 4),))
    second_gain = jnp.clip(1.0 + 0.1 * jax.random.normal(key_list[12], (D,), jnp.float32), 0.5, 1.5)
    hidden_gate = bell_draw(key_list[13], (D, FF), D ** -0.5, 0.125, ((1, 4),))
    hidden_up = bell_draw(key_list[14], (D, FF), D ** -0.5, 0.125, ((1, 4),))
    hidden_down = bell_draw(key_list[15], (FF, D), FF ** -0.5, 0.078125, ((0, 4),))
    cotangent = bell_draw(key_list[16], (QUARTERS, SEQS, QLEN, D), 1.0, 6.0, ((1, 4), (2, 8)))
    return dict(tokens=tokens, first_gain=first_gain, branch_weight=branch_weight, input_weight=input_weight, conv_weight=conv_weight, conv_bias=conv_bias, rate_weight=rate_weight, rate_bias=rate_bias, entry_weight=entry_weight, entry_bias=entry_bias, decay_param=decay_param, output_weight=output_weight, second_gain=second_gain, hidden_gate=hidden_gate, hidden_up=hidden_up, hidden_down=hidden_down, cotangent=cotangent)


EPSILON = 1e-06
DECAY_SCALE = 8.0
MULT_FLOOR = 0.01
HIGHEST_PRECISION = lax.Precision.HIGHEST

@jax.custom_vjp
def low(v):
    return lax.optimization_barrier(v.astype(jnp.bfloat16)).astype(jnp.float32)

@jax.custom_vjp
def low_back(v):
    return v

def low_keep(v):
    return (low(v), None)

def low_pass(kept, grad):
    return (grad,)

def back_keep(v):
    return (v, None)

def back_low(kept, grad):
    return (low(grad),)
low.defvjp(low_keep, low_pass)
low_back.defvjp(back_keep, back_low)

def norm_scale(values, gain_vec):
    inv_root = lax.rsqrt(lax.optimization_barrier(jnp.mean(values * values, axis=-1, keepdims=True)) + EPSILON)
    return values * inv_root * gain_vec

def gelu_tanh(values):
    return jax.nn.gelu(values, approximate=True)

def causal_conv(series, weight, shift_bias):
    tap_count = weight.shape[0]
    length = series.shape[0]
    padded = jnp.pad(series, ((tap_count - 1, 0), (0, 0)))
    running = jnp.zeros_like(series) + shift_bias
    for offset in range(tap_count):
        running = running + weight[offset] * padded[tap_count - 1 - offset:tap_count - 1 - offset + length]
    return running

def combine_pairs(earlier, later_pair):
    return (earlier[0] * later_pair[0], later_pair[0] * earlier[1] + later_pair[1])

def recurrence(rate_pre, entry_pre, mixed_vals, decay_raw):
    log_decay = -DECAY_SCALE * jax.nn.sigmoid(rate_pre) * jax.nn.softplus(-decay_raw)
    decay_step = jnp.exp(log_decay)
    multiplier = jnp.sqrt(jnp.maximum(1.0 - decay_step * decay_step, MULT_FLOOR))
    pushed = multiplier * jax.nn.sigmoid(entry_pre) * mixed_vals
    decay_total, states = lax.associative_scan(combine_pairs, (decay_step, pushed), axis=0)
    return states

def matmul(left_op, right_op):
    return jnp.dot(left_op, right_op, precision=HIGHEST_PRECISION)

def block(params, series):
    first_gain, branch_weight, input_weight, conv_weight, conv_bias, rate_weight, rate_bias, entry_weight, entry_bias, decay_param, output_weight, second_gain, hidden_gate, hidden_up, hidden_down = params
    first_low = low(norm_scale(series, first_gain))
    branch_pre = low_back(matmul(first_low, branch_weight))
    input_low = low(low_back(matmul(first_low, input_weight)))
    mixed_vals = low(causal_conv(input_low, conv_weight, conv_bias))
    grouped = mixed_vals.reshape(mixed_vals.shape[0], BLOCKS, BLOCK_W)
    rate_pre = low_back(jnp.einsum('lkb,kbc->lkc', grouped, rate_weight, precision=HIGHEST_PRECISION).reshape(mixed_vals.shape) + rate_bias)
    entry_pre = low_back(jnp.einsum('lkb,kbc->lkc', grouped, entry_weight, precision=HIGHEST_PRECISION).reshape(mixed_vals.shape) + entry_bias)
    states = recurrence(rate_pre, entry_pre, mixed_vals, decay_param)
    state_low = low(low_back(states))
    gated_low = low(state_low * gelu_tanh(branch_pre))
    middle = series + low_back(matmul(gated_low, output_weight))
    second_low = low(norm_scale(middle, second_gain))
    gate_pre = low_back(matmul(second_low, hidden_gate))
    up_pre = low_back(matmul(second_low, hidden_up))
    hidden_low = low(gelu_tanh(gate_pre) * up_pre)
    return middle + matmul(hidden_low, hidden_down)

def reference(tokens, first_gain, branch_weight, input_weight, conv_weight, conv_bias, rate_weight, rate_bias, entry_weight, entry_bias, decay_param, output_weight, second_gain, hidden_gate, hidden_up, hidden_down, cotangent):
    params = tuple((argument.astype(jnp.float32) for argument in (first_gain, branch_weight, input_weight, conv_weight, conv_bias, rate_weight, rate_bias, entry_weight, entry_bias, decay_param, output_weight, second_gain, hidden_gate, hidden_up, hidden_down)))
    positions = QUARTERS * QLEN
    series_all = jnp.transpose(tokens.astype(jnp.float32), (1, 0, 2, 3)).reshape(SEQS, positions, D)
    upstream_all = jnp.transpose(cotangent.astype(jnp.float32), (1, 0, 2, 3)).reshape(SEQS, positions, D)

    def one_sequence(totals, sequence_pair):
        series, upstream = sequence_pair
        output, pullback = jax.vjp(block, params, series)
        param_grads, series_grad = pullback(upstream)
        totals = jax.tree.map(jnp.add, totals, param_grads)
        return (totals, (output, series_grad))
    initial = jax.tree.map(jnp.zeros_like, params)
    totals, (outputs, series_grads) = lax.scan(one_sequence, initial, (series_all, upstream_all))

    def back_layout(values):
        return jnp.transpose(values.reshape(SEQS, QUARTERS, QLEN, D), (1, 0, 2, 3))
    return (back_layout(outputs).astype(jnp.bfloat16), back_layout(series_grads), totals[0], totals[1], totals[2], totals[3], totals[4], totals[5], totals[6], totals[7], totals[8], totals[9], totals[10], totals[11], totals[12], totals[13], totals[14])
```

```python
import functools

import jax
import jax.numpy as jnp
from jax import lax
from jax.experimental import pallas as pl
from jax.experimental.pallas import tpu as pltpu
from jax.sharding import PartitionSpec as P

EPSILON = 1e-06
DECAY_SCALE = 8.0
MULT_FLOOR = 0.01
LANES = 128
SEGMENTS = 8
GELU_C = 0.7978845608028654
GELU_A = 0.044715
F32 = jnp.float32
BF16 = jnp.bfloat16


def dot(left, right, dims=((1,), (0,))):
    return lax.dot_general(left, right, (dims, ((), ())), preferred_element_type=F32)


def gelu_and_slope(x):
    inner = GELU_C * (x + GELU_A * x * x * x)
    t = jnp.tanh(inner)
    half = 0.5 * (1.0 + t)
    slope = half + 0.5 * x * (1.0 - t * t) * (GELU_C * (1.0 + 3.0 * GELU_A * x * x))
    return x * half, slope


def gelu_tanh(x):
    return x * (0.5 * (1.0 + jnp.tanh(GELU_C * (x + GELU_A * x * x * x))))


def sigmoid(x):
    return 0.5 * jnp.tanh(0.5 * x) + 0.5


def softplus(x):
    return jnp.maximum(x, 0.0) + jnp.log1p(jnp.exp(-jnp.abs(x)))


def lane_groups(width):
    return [slice(g * LANES, (g + 1) * LANES) for g in range(width // LANES)]


def put(ref, rows, value):
    for g, lanes in enumerate(lane_groups(value.shape[1])):
        ref[g, rows, :] = value[:, lanes]


def take(ref, rows):
    return jnp.concatenate([ref[g, rows, :] for g in range(ref.shape[0])], axis=1)


def strided_scan(steps, groups, load, store):
    def step(k, carry):
        i = steps(k)
        out = []
        for g in range(groups):
            state, total = carry[g]
            factor, term = load(g, i)
            state = factor * state + term
            total = factor * total
            store(g, i, state, total)
            out.append((state, total))
        return tuple(out)

    return step


TAP, CONV_B, RATE_B, ENTRY_B, DECAY = 0, 4, 5, 6, 7


def gate_values(pre, log_scale, width):
    r = sigmoid(pre[:, :width])
    e = sigmoid(pre[:, width:])
    a = jnp.exp(r * log_scale)
    room = 1.0 - a * a
    m = jnp.sqrt(jnp.maximum(room, MULT_FLOOR))
    return r, e, a, room, m


def scan_forward_kernel(
    parts, quarters, chunk, proj_ref, par_ref, gates_ref, z_ref, h_ref, v_ref, u_pad, a_s, b_s
):
    length, width = h_ref.shape
    seg = length // SEGMENTS
    chunks = length // chunk

    def place(c):
        q = c // parts
        s = c - q * parts
        return pl.multiple_of((s * quarters + q) * chunk, chunk)

    def time_of(c):
        return pl.multiple_of(c * chunk, chunk)

    log_scale = -DECAY_SCALE * softplus(-par_ref[DECAY : DECAY + 1, :])
    bias = jnp.concatenate(
        [par_ref[RATE_B : RATE_B + 1, :], par_ref[ENTRY_B : ENTRY_B + 1, :]], axis=1
    )
    u_pad[0:8, :] = jnp.zeros((8, width), F32)

    def first(c, carry):
        u = proj_ref[pl.ds(place(c), chunk), width : 2 * width].astype(BF16).astype(F32)
        u_pad[pl.ds(pl.multiple_of(time_of(c) + 8, 8), chunk), :] = u
        wide = u_pad[pl.ds(time_of(c), chunk + 8), :]
        v = par_ref[CONV_B : CONV_B + 1, :] + par_ref[0:1, :] * wide[8:]
        for k in range(1, 4):
            v = v + par_ref[k : k + 1, :] * wide[8 - k : 8 - k + chunk]
        v = v.astype(BF16)
        v_ref[pl.ds(time_of(c), chunk), :] = v
        pre = dot(v, gates_ref[...]) + bias
        r, e, a, room, m = gate_values(pre, log_scale, width)
        put(a_s, pl.ds(time_of(c), chunk), a)
        put(b_s, pl.ds(time_of(c), chunk), m * e * v.astype(F32))
        return carry

    lax.fori_loop(0, chunks, first, 0)

    def load(g, i):
        at = pl.ds(i, SEGMENTS, stride=seg)
        return a_s[g, at, :], b_s[g, at, :]

    def store(g, i, state, total):
        at = pl.ds(i, SEGMENTS, stride=seg)
        b_s[g, at, :] = state
        a_s[g, at, :] = total

    groups = width // LANES
    start = (jnp.zeros((SEGMENTS, LANES), F32), jnp.ones((SEGMENTS, LANES), F32))
    ends = lax.fori_loop(
        0, seg, strided_scan(lambda k: k, groups, load, store), (start,) * groups, unroll=8
    )
    final = jnp.concatenate([e[0] for e in ends], axis=1)
    totals = jnp.concatenate([e[1] for e in ends], axis=1)
    carries = [jnp.zeros((1, width), F32)]
    for j in range(SEGMENTS - 1):
        carries.append(totals[j : j + 1] * carries[j] + final[j : j + 1])
    for j in range(SEGMENTS):
        per = seg // chunk

        def last(k, carry, j=j, per=per):
            c = j * per + k
            rows = pl.ds(time_of(c), chunk)
            h = take(b_s, rows) + take(a_s, rows) * carries[j]
            h_ref[rows, :] = h
            y = gelu_tanh(proj_ref[pl.ds(place(c), chunk), 0:width])
            z_ref[pl.ds(place(c), chunk), :] = (h.astype(BF16).astype(F32) * y).astype(BF16)
            return carry

        lax.fori_loop(0, per, last, 0)


def scan_forward(parts, quarters, chunk, proj, params, gates):
    length, width = proj.shape[0], proj.shape[1] // 2
    return pl.pallas_call(
        functools.partial(scan_forward_kernel, parts, quarters, chunk),
        out_shape=(
            jax.ShapeDtypeStruct((length, width), BF16),
            jax.ShapeDtypeStruct((length, width), F32),
            jax.ShapeDtypeStruct((length, width), BF16),
        ),
        in_specs=[pl.BlockSpec(memory_space=pltpu.VMEM)] * 3,
        out_specs=[pl.BlockSpec(memory_space=pltpu.VMEM)] * 3,
        scratch_shapes=[
            pltpu.VMEM((length + 8, width), F32),
            pltpu.VMEM((width // LANES, length, LANES), F32),
            pltpu.VMEM((width // LANES, length, LANES), F32),
        ],
        compiler_params=pltpu.CompilerParams(vmem_limit_bytes=48 * 2**20),
        name="scan_forward",
    )(proj, params, gates)


def scan_backward_kernel(
    parts,
    quarters,
    chunk,
    dz_ref,
    proj_ref,
    h_ref,
    v_ref,
    par_ref,
    gates_ref,
    both_ref,
    gate_grad_ref,
    sums_ref,
    a_s,
    g_s,
    t_s,
    h_pad,
    pre_s,
    dpre_s,
    dv_s,
    u_pad,
):
    length, width = h_ref.shape
    seg = length // SEGMENTS
    chunks = length // chunk

    def place(c):
        q = c // parts
        s = c - q * parts
        return pl.multiple_of((s * quarters + q) * chunk, chunk)

    def time_of(c):
        return pl.multiple_of(c * chunk, chunk)

    softplus_decay = softplus(-par_ref[DECAY : DECAY + 1, :])
    log_scale = -DECAY_SCALE * softplus_decay
    bias = jnp.concatenate(
        [par_ref[RATE_B : RATE_B + 1, :], par_ref[ENTRY_B : ENTRY_B + 1, :]], axis=1
    )
    zeros8 = jnp.zeros((8, width), F32)
    put(a_s, pl.ds(length, 8), zeros8)
    h_pad[0:8, :] = zeros8
    u_pad[0:8, :] = zeros8
    dv_s[pl.ds(length, 8), :] = zeros8

    def first(c, carry):
        rows = pl.ds(time_of(c), chunk)
        later = pl.ds(pl.multiple_of(time_of(c) + 8, 8), chunk)
        there = pl.ds(place(c), chunk)
        h = h_ref[rows, :]
        h_pad[later, :] = h
        u_pad[later, :] = proj_ref[there, width : 2 * width].astype(BF16).astype(F32)
        y, slope = gelu_and_slope(proj_ref[there, 0:width])
        dz = dz_ref[there, :]
        put(g_s, rows, (dz * y).astype(BF16).astype(F32))
        both_ref[there, 0:width] = (dz * h.astype(BF16).astype(F32) * slope).astype(BF16)
        pre = dot(v_ref[rows, :], gates_ref[...]) + bias
        pre_s[rows, :] = pre
        put(a_s, rows, jnp.exp(sigmoid(pre[:, :width]) * log_scale))
        return carry

    lax.fori_loop(0, chunks, first, 0)

    def load(g, i):
        return (
            a_s[g, pl.ds(i + 1, SEGMENTS, stride=seg), :],
            g_s[g, pl.ds(i, SEGMENTS, stride=seg), :],
        )

    def store(g, i, state, total):
        g_s[g, pl.ds(i, SEGMENTS, stride=seg), :] = state
        t_s[g, pl.ds(i, SEGMENTS, stride=seg), :] = total

    groups = width // LANES
    start = (jnp.zeros((SEGMENTS, LANES), F32), jnp.ones((SEGMENTS, LANES), F32))
    ends = lax.fori_loop(
        0,
        seg,
        strided_scan(lambda k: seg - 1 - k, groups, load, store),
        (start,) * groups,
        unroll=8,
    )
    firsts = jnp.concatenate([e[0] for e in ends], axis=1)
    totals = jnp.concatenate([e[1] for e in ends], axis=1)
    carries = [None] * SEGMENTS
    carries[SEGMENTS - 1] = jnp.zeros((1, width), F32)
    for j in range(SEGMENTS - 2, -1, -1):
        carries[j] = totals[j + 1 : j + 2] * carries[j + 1] + firsts[j + 1 : j + 2]

    def fold(values):
        return jnp.sum(values.reshape(chunk // 8, 8, values.shape[1]), axis=0)

    sums_ref[...] = jnp.zeros(sums_ref.shape, F32)

    for j in range(SEGMENTS):
        per = seg // chunk

        def middle(k, carry, j=j, per=per):
            c = j * per + k
            rows = pl.ds(time_of(c), chunk)
            g = take(g_s, rows) + take(t_s, rows) * carries[j]
            before = h_pad[pl.ds(time_of(c), chunk + 8), :][7 : 7 + chunk]
            v = v_ref[rows, :].astype(F32)
            r, e, a, room, m = gate_values(pre_s[rows, :], log_scale, width)
            gv = g * v
            held = jnp.where(room > MULT_FLOOR, gv * e * a / m, 0.0)
            ta = (g * before - held) * a * r
            drpre = (ta * (log_scale * (1.0 - r))).astype(BF16)
            depre = (gv * m * e * (1.0 - e)).astype(BF16)
            dpre_s[rows, 0:width] = drpre
            dpre_s[rows, width : 2 * width] = depre
            sums_ref[0:8, :] += fold(ta)
            sums_ref[8:16, :] += fold(drpre.astype(F32))
            sums_ref[16:24, :] += fold(depre.astype(F32))
            dv = g * m * e + dot(dpre_s[rows, :], gates_ref[...], ((1,), (1,)))
            dv_s[rows, :] = dv
            sums_ref[24:32, :] += fold(dv)
            wide = u_pad[pl.ds(time_of(c), chunk + 8), :]
            for tap in range(4):
                at = 32 + 8 * tap
                sums_ref[at : at + 8, :] += fold(dv * wide[8 - tap : 8 - tap + chunk])
            return carry

        lax.fori_loop(0, per, middle, 0)
    sums_ref[0:8, :] = sums_ref[0:8, :] * (
        DECAY_SCALE * sigmoid(-par_ref[DECAY : DECAY + 1, :])
    )

    def last(c, carry):
        wide = dv_s[pl.ds(time_of(c), chunk + 8), :]
        du = par_ref[0:1, :] * wide[0:chunk]
        for tap in range(1, 4):
            du = du + par_ref[tap : tap + 1, :] * wide[tap : tap + chunk]
        both_ref[pl.ds(place(c), chunk), width : 2 * width] = du.astype(BF16)
        return carry

    lax.fori_loop(0, chunks, last, 0)
    gate_grad_ref[...] = dot(v_ref[...], dpre_s[...], ((0,), (0,)))


def scan_backward(parts, quarters, chunk, dz, proj, h, v, params, gates):
    length, width = h.shape
    return pl.pallas_call(
        functools.partial(scan_backward_kernel, parts, quarters, chunk),
        out_shape=(
            jax.ShapeDtypeStruct((length, 2 * width), BF16),
            jax.ShapeDtypeStruct((width, 2 * width), F32),
            jax.ShapeDtypeStruct((64, width), F32),
        ),
        in_specs=[pl.BlockSpec(memory_space=pltpu.VMEM)] * 6,
        out_specs=[pl.BlockSpec(memory_space=pltpu.VMEM)] * 3,
        scratch_shapes=[
            pltpu.VMEM((width // LANES, length + 8, LANES), F32),
            pltpu.VMEM((width // LANES, length, LANES), F32),
            pltpu.VMEM((width // LANES, length, LANES), F32),
            pltpu.VMEM((length + 8, width), F32),
            pltpu.VMEM((length, 2 * width), F32),
            pltpu.VMEM((length, 2 * width), BF16),
            pltpu.VMEM((length + 8, width), F32),
            pltpu.VMEM((length + 8, width), F32),
        ],
        compiler_params=pltpu.CompilerParams(vmem_limit_bytes=52 * 2**20),
        name="scan_backward",
    )(dz, proj, h, v, params, gates)


def rms_parts(values):
    return lax.rsqrt(jnp.mean(values * values, axis=-1, keepdims=True) + EPSILON)


def rms_back(values, scale, gain, grad):
    k = grad * gain
    return scale * k - scale * scale * scale * values * jnp.mean(
        k * values, axis=-1, keepdims=True
    )


def body(
    tokens,
    first_gain,
    branch_weight,
    input_weight,
    conv_weight,
    conv_bias,
    rate_weight,
    rate_bias,
    entry_weight,
    entry_bias,
    decay_param,
    output_weight,
    second_gain,
    hidden_gate,
    hidden_up,
    hidden_down,
    cotangent,
):
    quarters, _, chunk, model = tokens.shape
    rows = quarters * chunk
    parts = lax.axis_size("seq")
    shards = lax.axis_size("shard")
    inner = 2
    outer = parts // inner
    seq_at = lax.axis_index("seq")
    inner_at = lax.rem(seq_at, inner)
    lru = branch_weight.shape[1]
    channels = lru // parts
    width = (channels + LANES) // LANES * LANES
    spare = width - channels
    blocks, block_width = rate_weight.shape[0], rate_weight.shape[1]
    piece = model // (parts * shards)
    pairs = [[o * inner + i for i in range(inner)] for o in range(outer)]
    columns = [[o * inner + i for o in range(outer)] for i in range(inner)]

    def gather_seq(x):
        return lax.all_gather(x, "seq", axis=0, tiled=True)

    def scatter_seq(x):
        return lax.psum_scatter(x, "seq", scatter_dimension=0, tiled=True)

    def gather_plane(x):
        x = lax.all_gather(x, "shard", axis=0, tiled=True)
        return lax.all_gather(x, "seq", axis=0, tiled=True, axis_index_groups=pairs)

    def scatter_plane(x):
        x = lax.psum_scatter(x, "seq", scatter_dimension=0, tiled=True, axis_index_groups=pairs)
        return lax.psum_scatter(x, "shard", scatter_dimension=0, tiled=True)

    def own(weight, axis):
        part = lax.dynamic_slice_in_dim(weight, seq_at * channels, channels, axis)
        pads = [(0, 0), (0, 0)]
        pads[axis] = (0, spare)
        return jnp.pad(part, pads)

    w_in = lax.all_gather(
        jnp.concatenate([own(branch_weight, 1), own(input_weight, 1)], axis=1),
        "shard",
        axis=0,
        tiled=True,
    )
    w_out = lax.all_gather(own(output_weight, 0), "shard", axis=1, tiled=True)
    params = jnp.pad(
        jnp.concatenate(
            [
                conv_weight.astype(F32),
                conv_bias[None],
                rate_bias[None],
                entry_bias[None],
                decay_param[None],
            ],
            axis=0,
        ),
        ((0, 0), (0, spare)),
    )

    def spread(weight):
        out = jnp.zeros((width, width), BF16)
        for j in range(blocks):
            at = j * block_width
            out = out.at[at : at + block_width, at : at + block_width].set(weight[j])
        return out

    gates = jnp.concatenate([spread(rate_weight), spread(entry_weight)], axis=1)

    xs = tokens.reshape(rows, model).astype(F32)
    scale1 = rms_parts(xs)
    n1 = gather_seq((xs * scale1 * first_gain).astype(BF16))
    proj = dot(n1, w_in)
    z, h, v = scan_forward(parts, quarters, chunk, proj, params, gates)
    mid = xs + scatter_seq(dot(z, w_out).astype(BF16)).astype(F32)
    scale2 = rms_parts(mid)
    n2 = gather_plane((mid * scale2 * second_gain).astype(BF16))
    cot = cotangent.reshape(rows, model)
    cot_all = gather_plane(cot)
    hidden = hidden_gate.shape[1] // inner
    wg = lax.dynamic_slice_in_dim(hidden_gate, inner_at * hidden, hidden, 1)
    wu = lax.dynamic_slice_in_dim(hidden_up, inner_at * hidden, hidden, 1)
    wd = lax.dynamic_slice_in_dim(hidden_down, inner_at * hidden, hidden, 0)
    gm = dot(n2, wg)
    um = dot(n2, wu)
    act, slope = gelu_and_slope(gm)
    mm = (act * um).astype(BF16)
    result = (mid + scatter_plane(dot(mm, wd).astype(BF16)).astype(F32)).astype(BF16)
    dmm = dot(cot_all, wd, ((1,), (1,)))
    dgm = (dmm * um * slope).astype(BF16)
    dum = (dmm * act).astype(BF16)
    ffn_grads = jnp.concatenate(
        [
            dot(n2, dgm, ((0,), (0,))).astype(BF16),
            dot(n2, dum, ((0,), (0,))).astype(BF16),
            dot(cot_all, mm, ((0,), (0,))).astype(BF16),
        ],
        axis=1,
    )
    ffn_sum = lax.psum_scatter(
        ffn_grads, "seq", scatter_dimension=0, tiled=True, axis_index_groups=columns
    )
    dn2 = scatter_plane(
        (dot(dgm, wg, ((1,), (1,))) + dot(dum, wu, ((1,), (1,)))).astype(BF16)
    ).astype(F32)
    dmid = cot.astype(F32) + rms_back(mid, scale2, second_gain, dn2)
    second_gain_grad = jnp.sum(dn2 * mid * scale2, axis=0)
    dout = gather_seq(dmid.astype(BF16))
    dz = dot(dout, w_out, ((1,), (1,)))
    both, gate_grad, sums = scan_backward(
        parts, quarters, chunk, dz, proj, h, v, params, gates
    )
    dn1 = scatter_seq(dot(both, w_in, ((1,), (1,))).astype(BF16)).astype(F32)
    tokens_grad = (dmid + rms_back(xs, scale1, first_gain, dn1)).reshape(tokens.shape)
    first_gain_grad = jnp.sum(dn1 * xs * scale1, axis=0)
    mix_grads = jnp.concatenate(
        [dot(n1, both, ((0,), (0,))).astype(BF16), dot(dout, z, ((0,), (0,))).astype(BF16)],
        axis=1,
    )
    mix_cols = 3 * width
    mix_sum = lax.psum_scatter(
        mix_grads.reshape(parts, shards, piece, mix_cols).transpose(1, 0, 2, 3),
        "shard",
        scatter_dimension=0,
        tiled=True,
    )
    mix = lax.all_to_all(
        mix_sum.reshape(parts, piece, mix_cols), "seq", split_axis=0, concat_axis=0, tiled=True
    )
    mix = mix.reshape(parts, piece, 3, width)[..., :channels].astype(F32)
    mix = mix.transpose(2, 1, 0, 3).reshape(3, piece, lru)
    ffn = lax.all_to_all(
        ffn_sum.reshape(inner, shards, piece, 3 * hidden),
        "shard",
        split_axis=1,
        concat_axis=1,
        tiled=True,
    )
    ffn = lax.all_to_all(
        ffn, "seq", split_axis=0, concat_axis=0, tiled=True, axis_index_groups=pairs
    )
    ffn = ffn.reshape(inner, shards, piece, 3, hidden).transpose(3, 2, 1, 0, 4)
    ffn = ffn.reshape(3, piece, inner * shards * hidden).astype(F32)
    first_gain_sum, second_gain_sum = (
        lax.psum_scatter(x, ("seq", "shard"), scatter_dimension=0, tiled=True)
        for x in (first_gain_grad, second_gain_grad)
    )
    sums = sums.reshape(8, 8, width).sum(axis=1)[:, :channels]

    def blocks_of(at):
        return jnp.stack(
            [
                gate_grad[
                    j * block_width : (j + 1) * block_width,
                    at + j * block_width : at + (j + 1) * block_width,
                ]
                for j in range(blocks)
            ]
        )

    sums, rate_grad, entry_grad = lax.psum((sums, blocks_of(0), blocks_of(width)), "shard")
    return (
        result.reshape(tokens.shape),
        tokens_grad,
        first_gain_sum,
        mix[0],
        mix[1],
        sums[4:8],
        sums[3],
        rate_grad,
        sums[1],
        entry_grad,
        sums[2],
        sums[0],
        mix[2].T,
        second_gain_sum,
        ffn[0],
        ffn[1],
        ffn[2].T,
    )


def solution(mesh):
    placed = (
        P(None, "shard", "seq", None),
        P(),
        P("shard", None),
        P("shard", None),
        P(None, "seq"),
        P("seq"),
        P("seq", None, None),
        P("seq"),
        P("seq", None, None),
        P("seq"),
        P("seq"),
        P(None, "shard"),
        P(),
        P(None, "shard"),
        P(None, "shard"),
        P("shard", None),
        P(None, "shard", "seq", None),
    )
    return jax.shard_map(
        body,
        mesh=mesh,
        in_specs=placed,
        out_specs=(
            P(None, "shard", "seq", None),
            P(None, "shard", "seq", None),
            P(("seq", "shard")),
            P(("seq", "shard"), None),
            P(("seq", "shard"), None),
            P(None, "seq"),
            P("seq"),
            P("seq", None, None),
            P("seq"),
            P("seq", None, None),
            P("seq"),
            P("seq"),
            P(None, ("seq", "shard")),
            P(("seq", "shard")),
            P(("seq", "shard"), None),
            P(("seq", "shard"), None),
            P(None, ("seq", "shard")),
        ),
        check_vma=False,
    )
```

```python
import functools

import jax
import jax.numpy as jnp
from jax import lax
from jax.experimental import pallas as pl
from jax.experimental.pallas import tpu as pltpu
from jax.sharding import PartitionSpec as P

EPSILON = 1e-06
DECAY_SCALE = 8.0
MULT_FLOOR = 0.01
LANES = 128
SEGMENTS = 8
GELU_C = 0.7978845608028654
GELU_A = 0.044715
F32 = jnp.float32
BF16 = jnp.bfloat16


MESH = pl.DeviceIdType.MESH
ANY = pl.BlockSpec(memory_space=pl.ANY)
IN_VMEM = pl.BlockSpec(memory_space=pltpu.VMEM)
DMA = pltpu.SemaphoreType.DMA


def cost(us):
    return pl.CostEstimate(flops=0, bytes_accessed=int(us * 3.3e6), transcendentals=0)


def dot(left, right, dims=((1,), (0,))):
    return lax.dot_general(left, right, (dims, ((), ())), preferred_element_type=F32)


def gelu_and_slope(x):
    inner = GELU_C * (x + GELU_A * x * x * x)
    t = jnp.tanh(inner)
    half = 0.5 * (1.0 + t)
    slope = half + 0.5 * x * (1.0 - t * t) * (GELU_C * (1.0 + 3.0 * GELU_A * x * x))
    return x * half, slope


def gelu_tanh(x):
    return x * (0.5 * (1.0 + jnp.tanh(GELU_C * (x + GELU_A * x * x * x))))


def sigmoid(x):
    return 0.5 * jnp.tanh(0.5 * x) + 0.5


def softplus(x):
    return jnp.maximum(x, 0.0) + jnp.log1p(jnp.exp(-jnp.abs(x)))


def lane_groups(width):
    return [slice(g * LANES, (g + 1) * LANES) for g in range(width // LANES)]


def put(ref, rows, value):
    for g, lanes in enumerate(lane_groups(value.shape[1])):
        ref[g, rows, :] = value[:, lanes]


def take(ref, rows):
    return jnp.concatenate([ref[g, rows, :] for g in range(ref.shape[0])], axis=1)


def strided_scan(steps, groups, load, store):
    def step(k, carry):
        i = steps(k)
        out = []
        for g in range(groups):
            state, total = carry[g]
            factor, term = load(g, i)
            state = factor * state + term
            total = factor * total
            store(g, i, state, total)
            out.append((state, total))
        return tuple(out)

    return step


TAP, CONV_B, RATE_B, ENTRY_B, DECAY = 0, 4, 5, 6, 7


def gate_values(pre, log_scale, width):
    r = sigmoid(pre[:, :width])
    e = sigmoid(pre[:, width:])
    a = jnp.exp(r * log_scale)
    room = 1.0 - a * a
    m = jnp.sqrt(jnp.maximum(room, MULT_FLOOR))
    return r, e, a, room, m


def scan_forward_kernel(
    parts, quarters, chunk, proj_ref, par_ref, gates_ref, z_ref, h_ref, v_ref, u_pad, a_s, b_s
):
    length, width = h_ref.shape
    seg = length // SEGMENTS
    chunks = length // chunk

    def place(c):
        q = c // parts
        s = c - q * parts
        return pl.multiple_of((s * quarters + q) * chunk, chunk)

    def time_of(c):
        return pl.multiple_of(c * chunk, chunk)

    log_scale = -DECAY_SCALE * softplus(-par_ref[DECAY : DECAY + 1, :])
    bias = jnp.concatenate(
        [par_ref[RATE_B : RATE_B + 1, :], par_ref[ENTRY_B : ENTRY_B + 1, :]], axis=1
    )
    u_pad[0:8, :] = jnp.zeros((8, width), F32)

    def first(c, carry):
        u = proj_ref[pl.ds(place(c), chunk), width : 2 * width].astype(BF16).astype(F32)
        u_pad[pl.ds(pl.multiple_of(time_of(c) + 8, 8), chunk), :] = u
        wide = u_pad[pl.ds(time_of(c), chunk + 8), :]
        v = par_ref[CONV_B : CONV_B + 1, :] + par_ref[0:1, :] * wide[8:]
        for k in range(1, 4):
            v = v + par_ref[k : k + 1, :] * wide[8 - k : 8 - k + chunk]
        v = v.astype(BF16)
        v_ref[pl.ds(time_of(c), chunk), :] = v
        pre = dot(v, gates_ref[...]) + bias
        r, e, a, room, m = gate_values(pre, log_scale, width)
        put(a_s, pl.ds(time_of(c), chunk), a)
        put(b_s, pl.ds(time_of(c), chunk), m * e * v.astype(F32))
        return carry

    lax.fori_loop(0, chunks, first, 0)

    def load(g, i):
        at = pl.ds(i, SEGMENTS, stride=seg)
        return a_s[g, at, :], b_s[g, at, :]

    def store(g, i, state, total):
        at = pl.ds(i, SEGMENTS, stride=seg)
        b_s[g, at, :] = state
        a_s[g, at, :] = total

    groups = width // LANES
    start = (jnp.zeros((SEGMENTS, LANES), F32), jnp.ones((SEGMENTS, LANES), F32))
    ends = lax.fori_loop(
        0, seg, strided_scan(lambda k: k, groups, load, store), (start,) * groups, unroll=8
    )
    final = jnp.concatenate([e[0] for e in ends], axis=1)
    totals = jnp.concatenate([e[1] for e in ends], axis=1)
    carries = [jnp.zeros((1, width), F32)]
    for j in range(SEGMENTS - 1):
        carries.append(totals[j : j + 1] * carries[j] + final[j : j + 1])
    for j in range(SEGMENTS):
        per = seg // chunk

        def last(k, carry, j=j, per=per):
            c = j * per + k
            rows = pl.ds(time_of(c), chunk)
            h = take(b_s, rows) + take(a_s, rows) * carries[j]
            h_ref[rows, :] = h
            y = gelu_tanh(proj_ref[pl.ds(place(c), chunk), 0:width])
            z_ref[pl.ds(place(c), chunk), :] = (h.astype(BF16).astype(F32) * y).astype(BF16)
            return carry

        lax.fori_loop(0, per, last, 0)


def scan_forward(parts, quarters, chunk, proj, params, gates):
    length, width = proj.shape[0], proj.shape[1] // 2
    return pl.pallas_call(
        functools.partial(scan_forward_kernel, parts, quarters, chunk),
        out_shape=(
            jax.ShapeDtypeStruct((length, width), BF16),
            jax.ShapeDtypeStruct((length, width), F32),
            jax.ShapeDtypeStruct((length, width), BF16),
        ),
        in_specs=[pl.BlockSpec(memory_space=pltpu.VMEM)] * 3,
        out_specs=[pl.BlockSpec(memory_space=pltpu.VMEM)] * 3,
        scratch_shapes=[
            pltpu.VMEM((length + 8, width), F32),
            pltpu.VMEM((width // LANES, length, LANES), F32),
            pltpu.VMEM((width // LANES, length, LANES), F32),
        ],
        compiler_params=pltpu.CompilerParams(vmem_limit_bytes=48 * 2**20),
        cost_estimate=cost(12),
        name="scan_forward",
    )(proj, params, gates)


def scan_backward_kernel(
    parts,
    quarters,
    chunk,
    blocks,
    block_width,
    dz_ref,
    proj_ref,
    h_ref,
    v_ref,
    par_ref,
    gates_ref,
    both_ref,
    blocks_ref,
    totals_ref,
    sums_ref,
    gate_grad_ref,
    a_s,
    g_s,
    t_s,
    h_pad,
    pre_s,
    dpre_s,
    dv_s,
    u_pad,
):
    length, width = h_ref.shape
    seg = length // SEGMENTS
    chunks = length // chunk

    def place(c):
        q = c // parts
        s = c - q * parts
        return pl.multiple_of((s * quarters + q) * chunk, chunk)

    def time_of(c):
        return pl.multiple_of(c * chunk, chunk)

    softplus_decay = softplus(-par_ref[DECAY : DECAY + 1, :])
    log_scale = -DECAY_SCALE * softplus_decay
    bias = jnp.concatenate(
        [par_ref[RATE_B : RATE_B + 1, :], par_ref[ENTRY_B : ENTRY_B + 1, :]], axis=1
    )
    zeros8 = jnp.zeros((8, width), F32)
    put(a_s, pl.ds(length, 8), zeros8)
    h_pad[0:8, :] = zeros8
    u_pad[0:8, :] = zeros8
    dv_s[pl.ds(length, 8), :] = zeros8

    def first(c, carry):
        rows = pl.ds(time_of(c), chunk)
        later = pl.ds(pl.multiple_of(time_of(c) + 8, 8), chunk)
        there = pl.ds(place(c), chunk)
        h = h_ref[rows, :]
        h_pad[later, :] = h
        u_pad[later, :] = proj_ref[there, width : 2 * width].astype(BF16).astype(F32)
        y, slope = gelu_and_slope(proj_ref[there, 0:width])
        dz = dz_ref[there, :]
        put(g_s, rows, (dz * y).astype(BF16).astype(F32))
        both_ref[there, 0:width] = (dz * h.astype(BF16).astype(F32) * slope).astype(BF16)
        pre = dot(v_ref[rows, :], gates_ref[...]) + bias
        pre_s[rows, :] = pre
        put(a_s, rows, jnp.exp(sigmoid(pre[:, :width]) * log_scale))
        return carry

    lax.fori_loop(0, chunks, first, 0)

    def load(g, i):
        return (
            a_s[g, pl.ds(i + 1, SEGMENTS, stride=seg), :],
            g_s[g, pl.ds(i, SEGMENTS, stride=seg), :],
        )

    def store(g, i, state, total):
        g_s[g, pl.ds(i, SEGMENTS, stride=seg), :] = state
        t_s[g, pl.ds(i, SEGMENTS, stride=seg), :] = total

    groups = width // LANES
    start = (jnp.zeros((SEGMENTS, LANES), F32), jnp.ones((SEGMENTS, LANES), F32))
    ends = lax.fori_loop(
        0,
        seg,
        strided_scan(lambda k: seg - 1 - k, groups, load, store),
        (start,) * groups,
        unroll=8,
    )
    firsts = jnp.concatenate([e[0] for e in ends], axis=1)
    totals = jnp.concatenate([e[1] for e in ends], axis=1)
    carries = [None] * SEGMENTS
    carries[SEGMENTS - 1] = jnp.zeros((1, width), F32)
    for j in range(SEGMENTS - 2, -1, -1):
        carries[j] = totals[j + 1 : j + 2] * carries[j + 1] + firsts[j + 1 : j + 2]

    def fold(values):
        return jnp.sum(values.reshape(chunk // 8, 8, values.shape[1]), axis=0)

    sums_ref[...] = jnp.zeros(sums_ref.shape, F32)

    for j in range(SEGMENTS):
        per = seg // chunk

        def middle(k, carry, j=j, per=per):
            c = j * per + k
            rows = pl.ds(time_of(c), chunk)
            g = take(g_s, rows) + take(t_s, rows) * carries[j]
            before = h_pad[pl.ds(time_of(c), chunk + 8), :][7 : 7 + chunk]
            v = v_ref[rows, :].astype(F32)
            r, e, a, room, m = gate_values(pre_s[rows, :], log_scale, width)
            gv = g * v
            held = jnp.where(room > MULT_FLOOR, gv * e * a / m, 0.0)
            ta = (g * before - held) * a * r
            drpre = (ta * (log_scale * (1.0 - r))).astype(BF16)
            depre = (gv * m * e * (1.0 - e)).astype(BF16)
            dpre_s[rows, 0:width] = drpre
            dpre_s[rows, width : 2 * width] = depre
            sums_ref[0:8, :] += fold(ta)
            sums_ref[8:16, :] += fold(drpre.astype(F32))
            sums_ref[16:24, :] += fold(depre.astype(F32))
            dv = g * m * e + dot(dpre_s[rows, :], gates_ref[...], ((1,), (1,)))
            dv_s[rows, :] = dv
            sums_ref[24:32, :] += fold(dv)
            wide = u_pad[pl.ds(time_of(c), chunk + 8), :]
            for tap in range(4):
                at = 32 + 8 * tap
                sums_ref[at : at + 8, :] += fold(dv * wide[8 - tap : 8 - tap + chunk])
            return carry

        lax.fori_loop(0, per, middle, 0)
    sums_ref[0:8, :] = sums_ref[0:8, :] * (
        DECAY_SCALE * sigmoid(-par_ref[DECAY : DECAY + 1, :])
    )

    def last(c, carry):
        wide = dv_s[pl.ds(time_of(c), chunk + 8), :]
        du = par_ref[0:1, :] * wide[0:chunk]
        for tap in range(1, 4):
            du = du + par_ref[tap : tap + 1, :] * wide[tap : tap + chunk]
        both_ref[pl.ds(place(c), chunk), width : 2 * width] = du.astype(BF16)
        return carry

    lax.fori_loop(0, chunks, last, 0)
    gate_grad_ref[...] = dot(v_ref[...], dpre_s[...], ((0,), (0,)))
    blocks_ref[...] = jnp.zeros(blocks_ref.shape, F32)
    tall = blocks_ref.shape[0] // (2 * blocks)
    for gate in range(2):
        for j in range(blocks):
            at, lanes = (gate * blocks + j) * tall, gate * width + j * block_width
            rows = slice(j * block_width, (j + 1) * block_width)
            blocks_ref[at : at + block_width, :block_width] = gate_grad_ref[
                rows, lanes : lanes + block_width
            ]
    for k in range(8):
        totals_ref[k : k + 1, :] = jnp.sum(sums_ref[8 * k : 8 * k + 8, :], axis=0, keepdims=True)


def scan_backward(parts, quarters, chunk, blocks, block_width, dz, proj, h, v, params, gates):
    length, width = h.shape
    tall, wide = -(-block_width // 8) * 8, -(-block_width // LANES) * LANES
    return pl.pallas_call(
        functools.partial(scan_backward_kernel, parts, quarters, chunk, blocks, block_width),
        out_shape=(
            jax.ShapeDtypeStruct((length, 2 * width), BF16),
            jax.ShapeDtypeStruct((2 * blocks * tall, wide), F32),
            jax.ShapeDtypeStruct((8, width), F32),
        ),
        in_specs=[pl.BlockSpec(memory_space=pltpu.VMEM)] * 6,
        out_specs=[pl.BlockSpec(memory_space=pltpu.VMEM)] * 3,
        scratch_shapes=[
            pltpu.VMEM((64, width), F32),
            pltpu.VMEM((width, 2 * width), F32),
            pltpu.VMEM((width // LANES, length + 8, LANES), F32),
            pltpu.VMEM((width // LANES, length, LANES), F32),
            pltpu.VMEM((width // LANES, length, LANES), F32),
            pltpu.VMEM((length + 8, width), F32),
            pltpu.VMEM((length, 2 * width), F32),
            pltpu.VMEM((length, 2 * width), BF16),
            pltpu.VMEM((length + 8, width), F32),
            pltpu.VMEM((length + 8, width), F32),
        ],
        compiler_params=pltpu.CompilerParams(vmem_limit_bytes=52 * 2**20),
        cost_estimate=cost(21),
        name="scan_backward",
    )(dz, proj, h, v, params, gates)


def remote(src, dst, send, recv, to):
    return pltpu.make_async_remote_copy(
        src_ref=src, dst_ref=dst, send_sem=send, recv_sem=recv, device_id=to, device_id_type=MESH
    )


def greet(others):
    barrier = pltpu.get_barrier_semaphore()
    for to in others:
        pl.semaphore_signal(barrier, inc=1, device_id=to, device_id_type=MESH)
    pl.semaphore_wait(barrier, len(others))


def add_rows(rows, fn):
    def one(k, carry):
        fn(pl.ds(pl.multiple_of(k * 16, 16), 16))
        return carry

    lax.fori_loop(0, rows // 16, one, 0)


def line_gather_kernel(outer, inner, x_ref, out_ref, local_sem, across, up, down):
    s, h = lax.axis_index("seq"), lax.axis_index("shard")
    o, i = s // inner, lax.rem(s, inner)
    beside = (o * inner + 1 - i, h)
    above, below = (s + inner, h), (s - inner, h)

    def at(row):
        return out_ref.at[row * inner + i]

    def branch(o0):
        others = [beside] + ([above] if o0 < outer - 1 else []) + ([below] if o0 > 0 else [])
        greet(others)
        mine = pltpu.make_async_copy(x_ref, out_ref.at[s], local_sem)
        mine.start()
        sent = []

        def send(row, sems, to):
            src = x_ref if row == o0 else at(row)
            copy = remote(src, at(row), sems.at[0, row], sems.at[1, row], to)
            copy.start()
            sent.append(copy)

        def came(row, sems, to):
            remote(x_ref, at(row), sems.at[0, row], sems.at[1, row], to).wait_recv()

        for k in range(outer):
            lower, upper = o0 - k, o0 + k
            if k > 0 and lower >= 0:
                came(lower, up, below)
            if lower >= 0 and o0 < outer - 1:
                send(lower, up, above)
            if lower >= 0:
                send(lower, across, beside)
            if k > 0 and upper < outer:
                came(upper, down, above)
            if upper < outer and o0 > 0:
                send(upper, down, below)
            if k > 0 and upper < outer:
                send(upper, across, beside)
        for row in range(outer):
            there = out_ref.at[row * inner + 1 - i]
            remote(x_ref, there, across.at[0, row], across.at[1, row], beside).wait_recv()
        for copy in sent:
            copy.wait_send()
        mine.wait()

    for o0 in range(outer):
        pl.when(o == o0)(functools.partial(branch, o0))


def line_gather(x, outer, inner, collective):
    rows, cols = x.shape
    return pl.pallas_call(
        functools.partial(line_gather_kernel, outer, inner),
        out_shape=jax.ShapeDtypeStruct((outer * inner, rows, cols), x.dtype),
        in_specs=[ANY],
        out_specs=ANY,
        scratch_shapes=[DMA] + [DMA((2, outer))] * 3,
        compiler_params=pltpu.CompilerParams(collective_id=collective, has_side_effects=True),
        cost_estimate=cost(52),
        name="line_gather",
    )(x)


def line_scatter_kernel(
    outer, inner, p_ref, out_ref, x_in, up_in, down_in, up_out, down_out, across, up, down
):
    s, h = lax.axis_index("seq"), lax.axis_index("shard")
    o, i = s // inner, lax.rem(s, inner)
    beside = (o * inner + 1 - i, h)
    above, below = (s + inner, h), (s - inner, h)
    rows = p_ref.shape[1]

    def branch(o0):
        first, last = o0 == 0, o0 == outer - 1
        greet([beside] + ([] if last else [above]) + ([] if first else [below]))
        order = sorted(range(outer), key=lambda d: (-abs(d - o0), d))
        sent = []
        for d in order:
            copy = remote(
                p_ref.at[d * inner + 1 - i], x_in.at[d], across.at[0, d], across.at[1, d], beside
            )
            copy.start()
            sent.append(copy)
        for d in order:
            mine = p_ref.at[d * inner + i]
            remote(mine, x_in.at[d], across.at[0, d], across.at[1, d], beside).wait_recv()
            terms = [mine, x_in.at[d]]
            if d >= o0 and not first:
                remote(mine, up_in.at[d], up.at[0, d], up.at[1, d], below).wait_recv()
                terms.append(up_in.at[d])
            if d <= o0 and not last:
                remote(mine, down_in.at[d], down.at[0, d], down.at[1, d], above).wait_recv()
                terms.append(down_in.at[d])
            target = out_ref if d == o0 else (up_out.at[d] if d > o0 else down_out.at[d])

            def add(at, terms=terms, target=target):
                total = terms[0][at, :].astype(F32)
                for term in terms[1:]:
                    total = total + term[at, :].astype(F32)
                target[at, :] = total.astype(target.dtype)

            add_rows(rows, add)
            if d != o0:
                sems, to, land = (up, above, up_in) if d > o0 else (down, below, down_in)
                copy = remote(target, land.at[d], sems.at[0, d], sems.at[1, d], to)
                copy.start()
                sent.append(copy)
        for copy in sent:
            copy.wait_send()

    for o0 in range(outer):
        pl.when(o == o0)(functools.partial(branch, o0))


def line_scatter(p, outer, inner, collective):
    parts, rows, cols = p.shape
    slots = pltpu.VMEM((outer, rows, cols), p.dtype)
    return pl.pallas_call(
        functools.partial(line_scatter_kernel, outer, inner),
        out_shape=jax.ShapeDtypeStruct((rows, cols), F32),
        in_specs=[IN_VMEM],
        out_specs=IN_VMEM,
        scratch_shapes=[slots] * 5 + [DMA((2, outer))] * 3,
        compiler_params=pltpu.CompilerParams(
            collective_id=collective, has_side_effects=True, vmem_limit_bytes=48 * 2**20
        ),
        cost_estimate=cost(57),
        name="line_scatter",
    )(p)


def plane_steps(inner, ys):
    steps = [(di, dy) for di in range(inner) for dy in range(ys) if (di, dy) != (0, 0)]
    return sorted(steps, key=lambda d: -((d[0] > 0) + (d[1] > 0)))


def plane_place(inner, shards):
    s, h = lax.axis_index("seq"), lax.axis_index("shard")
    o, i = s // inner, lax.rem(s, inner)
    y, core = h // 2, lax.rem(h, 2)
    ys = shards // 2

    def device(di, dy, other=False):
        to_i = lax.rem(i + di + inner, inner)
        to_y = lax.rem(y + dy + ys, ys)
        to_core = 1 - core if other else core
        to_h = to_y * 2 + to_core
        return (o * inner + to_i, to_h), to_i * shards + to_h

    return device


def plane_gather_kernel(inner, shards, x_ref, out_ref, local_sem, far, near):
    device = plane_place(inner, shards)
    steps = plane_steps(inner, shards // 2)
    sibling, sibling_slot = device(0, 0, True)
    _, me = device(0, 0)
    greet([sibling] + [device(*d)[0] for d in steps])
    mine = pltpu.make_async_copy(x_ref, out_ref.at[me], local_sem)
    mine.start()
    sent = []
    for k, d in enumerate(steps):
        copy = remote(x_ref, out_ref.at[me], far.at[0, k], far.at[1, k], device(*d)[0])
        copy.start()
        sent.append(copy)
    last = len(steps)
    copy = remote(x_ref, out_ref.at[me], near.at[0, last], near.at[1, last], sibling)
    copy.start()
    sent.append(copy)
    for k in reversed(range(len(steps))):
        di, dy = steps[k]
        source, slot = device(-di, -dy)
        here = out_ref.at[slot]
        remote(x_ref, here, far.at[0, k], far.at[1, k], source).wait_recv()
        copy = remote(here, here, near.at[0, k], near.at[1, k], sibling)
        copy.start()
        sent.append(copy)
    for k, d in enumerate(steps + [(0, 0)]):
        _, slot = device(-d[0], -d[1], True)
        remote(x_ref, out_ref.at[slot], near.at[0, k], near.at[1, k], sibling).wait_recv()
    for copy in sent:
        copy.wait_send()
    mine.wait()


def plane_gather(x, inner, shards, collective):
    rows, cols = x.shape
    chips = inner * shards // 2
    return pl.pallas_call(
        functools.partial(plane_gather_kernel, inner, shards),
        out_shape=jax.ShapeDtypeStruct((inner * shards, rows, cols), x.dtype),
        in_specs=[ANY],
        out_specs=ANY,
        scratch_shapes=[DMA, DMA((2, chips)), DMA((2, chips))],
        compiler_params=pltpu.CompilerParams(collective_id=collective, has_side_effects=True),
        cost_estimate=cost(29),
        name="plane_gather",
    )(x)


class Sent:
    def __init__(self):
        self.copies = []

    def __call__(self, *copy):
        copy = remote(*copy)
        copy.start()
        self.copies.append(copy)

    def finish(self):
        for copy in self.copies:
            copy.wait_send()


def received(like, here, sem, source):
    remote(like, here, sem, sem, source).wait_recv()


def shard_place(shards):
    s, h = lax.axis_index("seq"), lax.axis_index("shard")
    y, core, ys = h // 2, lax.rem(h, 2), shards // 2

    def along(dy, other=False):
        return lax.rem(y + dy + ys, ys) * 2 + (1 - core if other else core)

    return s, h, along, list(range(1, ys))


def opening_kernel(
    outer,
    inner,
    shards,
    x_ref,
    wi_ref,
    wo_ref,
    cot_ref,
    n_out,
    wi_out,
    wo_out,
    cot_out,
    local,
    across,
    up,
    down,
    w_far,
    w_near,
    c_side,
    c_far,
    c_near,
):
    s, h, along, far_steps = shard_place(shards)
    o, i = s // inner, lax.rem(s, inner)
    beside = (o * inner + 1 - i, h)
    above, below = (s + inner, h), (s - inner, h)
    sibling = (s, along(0, True))
    weights = ((wi_ref, wi_out), (wo_ref, wo_out))
    ys = shards // 2

    def at(row):
        return n_out.at[row * inner + i]

    def slot(side, dy, other=False):
        return (1 - i if side else i) * shards + along(dy, other)

    def branch(o0):
        greet(
            [beside, sibling]
            + ([above] if o0 < outer - 1 else [])
            + ([below] if o0 > 0 else [])
            + [(s, along(dy)) for dy in far_steps]
        )
        keep = [
            pltpu.make_async_copy(x_ref, n_out.at[s], local.at[0]),
            pltpu.make_async_copy(wi_ref, wi_out.at[h], local.at[1]),
            pltpu.make_async_copy(wo_ref, wo_out.at[h], local.at[2]),
            pltpu.make_async_copy(cot_ref, cot_out.at[slot(0, 0)], local.at[3]),
        ]
        send = Sent()

        def pass_on(row, sems, to):
            src = x_ref if row == o0 else at(row)
            send(src, at(row), sems.at[0, row], sems.at[1, row], to)

        def came(row, sems, source):
            received(x_ref, at(row), sems.at[1, row], source)

        def steps(k):
            lower, upper = o0 - k, o0 + k
            if k > 0 and lower >= 0:
                came(lower, up, below)
            if lower >= 0 and o0 < outer - 1:
                pass_on(lower, up, above)
            if lower >= 0:
                pass_on(lower, across, beside)
            if k > 0 and upper < outer:
                came(upper, down, above)
            if upper < outer and o0 > 0:
                pass_on(upper, down, below)
            if k > 0 and upper < outer:
                pass_on(upper, across, beside)

        steps(0)
        for n, (src, dst) in enumerate(weights):
            for dy in far_steps:
                send(src, dst.at[h], w_far.at[0, n, dy], w_far.at[1, n, dy], (s, along(dy)))
            send(src, dst.at[h], w_near.at[0, n, 0], w_near.at[1, n, 0], sibling)
        me = cot_out.at[slot(0, 0)]
        send(cot_ref, me, c_side.at[0], c_side.at[1], beside)
        for dy in far_steps:
            send(cot_ref, me, c_far.at[0, 0, dy], c_far.at[1, 0, dy], (s, along(dy)))
        send(cot_ref, me, c_near.at[0, 0, 0], c_near.at[1, 0, 0], sibling)
        for copy in keep:
            copy.start()
        for k in range(1, outer):
            steps(k)
            if k == 1:
                for n, (src, dst) in enumerate(weights):
                    for dy in far_steps:
                        source = along(-dy)
                        here = dst.at[source]
                        received(src, here, w_far.at[1, n, dy], (s, source))
                        send(here, here, w_near.at[0, n, dy], w_near.at[1, n, dy], sibling)
                here = cot_out.at[slot(1, 0)]
                received(cot_ref, here, c_side.at[1], beside)
                for dy in far_steps:
                    send(here, here, c_far.at[0, 1, dy], c_far.at[1, 1, dy], (s, along(dy)))
                send(here, here, c_near.at[0, 1, 0], c_near.at[1, 1, 0], sibling)
        for side in range(2):
            for dy in far_steps:
                here = cot_out.at[slot(side, -dy)]
                received(cot_ref, here, c_far.at[1, side, dy], (s, along(-dy)))
                send(here, here, c_near.at[0, side, dy], c_near.at[1, side, dy], sibling)
        for row in range(outer):
            received(x_ref, n_out.at[row * inner + 1 - i], across.at[1, row], beside)
        for dy in range(ys):
            for n, (src, dst) in enumerate(weights):
                received(src, dst.at[along(-dy, True)], w_near.at[1, n, dy], sibling)
            for side in range(2):
                received(cot_ref, cot_out.at[slot(side, -dy, True)], c_near.at[1, side, dy], sibling)
        send.finish()
        for copy in keep:
            copy.wait()

    for o0 in range(outer):
        pl.when(o == o0)(functools.partial(branch, o0))


def opening(x, w_in, w_out, cot, outer, inner, shards, collective):
    ys = shards // 2
    return pl.pallas_call(
        functools.partial(opening_kernel, outer, inner, shards),
        out_shape=(
            jax.ShapeDtypeStruct((outer * inner,) + x.shape, x.dtype),
            jax.ShapeDtypeStruct((shards,) + w_in.shape, w_in.dtype),
            jax.ShapeDtypeStruct((shards,) + w_out.shape, w_out.dtype),
            jax.ShapeDtypeStruct((inner * shards,) + cot.shape, cot.dtype),
        ),
        in_specs=[ANY] * 4,
        out_specs=[ANY] * 4,
        scratch_shapes=[DMA((4,))]
        + [DMA((2, outer))] * 3
        + [DMA((2, 2, ys))] * 2
        + [DMA((2,)), DMA((2, 2, ys)), DMA((2, 2, ys))],
        compiler_params=pltpu.CompilerParams(collective_id=collective, has_side_effects=True),
        cost_estimate=cost(62),
        name="opening",
    )(x, w_in, w_out, cot)


def closing_kernel(
    outer,
    inner,
    shards,
    p_ref,
    g_ref,
    blocks_ref,
    sums_ref,
    dn_ref,
    mix_ref,
    blocks_out,
    sums_out,
    x_in,
    up_in,
    down_in,
    up_out,
    down_out,
    near_in,
    far_in,
    far_out,
    done,
    block_slots,
    sum_slots,
    across,
    up,
    down,
    near,
    far,
    final,
    s_far,
    s_near,
    local,
):
    s, h, along, far_steps = shard_place(shards)
    parts = outer * inner
    o, i = s // inner, lax.rem(s, inner)
    beside = (o * inner + 1 - i, h)
    above, below = (s + inner, h), (s - inner, h)
    sibling = (s, along(0, True))
    rows, piece, ys = p_ref.shape[1], g_ref.shape[2], shards // 2
    order = [lax.rem(s + k, parts) for k in range(1, parts + 1)]
    small = ((blocks_ref, block_slots, blocks_out), (sums_ref, sum_slots, sums_out))

    def branch(o0):
        first, last = o0 == 0, o0 == outer - 1
        greet(
            [sibling]
            + [(s, along(dy)) for dy in far_steps]
            + [(lax.rem(s + k, parts), h) for k in range(1, parts)]
        )
        send = Sent()
        line = sorted(range(outer), key=lambda d: (-abs(d - o0), d))
        for d in line:
            send(p_ref.at[d * inner + 1 - i], x_in.at[d], across.at[0, d], across.at[1, d], beside)
        for k, p in enumerate(order):
            for dy in far_steps + [0]:
                src = g_ref.at[p, along(dy, True)]
                send(src, near_in.at[dy, p], near.at[0, dy, k], near.at[1, dy, k], sibling)
        for k, p in enumerate(order):
            for dy in far_steps:
                mine = g_ref.at[p, along(dy)]
                received(mine, near_in.at[dy, p], near.at[1, dy, k], sibling)

                def add(at, p=p, dy=dy, mine=mine):
                    total = mine[at, :].astype(F32) + near_in[dy, p, at, :].astype(F32)
                    far_out[dy - 1, p, at, :] = total.astype(BF16)

                add_rows(piece, add)
                send(
                    far_out.at[dy - 1, p],
                    far_in.at[dy - 1, p],
                    far.at[0, dy, k],
                    far.at[1, dy, k],
                    (s, along(dy)),
                )
        for n, (src, slots, _) in enumerate(small):
            for dy in far_steps:
                send(src, slots.at[h], s_far.at[0, n, dy], s_far.at[1, n, dy], (s, along(dy)))
            send(src, slots.at[h], s_near.at[0, n, 0], s_near.at[1, n, 0], sibling)
            slots[h] = src[...]

        def line_step(d):
            mine = p_ref.at[d * inner + i]
            received(mine, x_in.at[d], across.at[1, d], beside)
            terms = [mine, x_in.at[d]]
            if d >= o0 and not first:
                received(mine, up_in.at[d], up.at[1, d], below)
                terms.append(up_in.at[d])
            if d <= o0 and not last:
                received(mine, down_in.at[d], down.at[1, d], above)
                terms.append(down_in.at[d])
            target = dn_ref if d == o0 else (up_out.at[d] if d > o0 else down_out.at[d])

            def add(at):
                total = terms[0][at, :].astype(F32)
                for term in terms[1:]:
                    total = total + term[at, :].astype(F32)
                target[at, :] = total.astype(target.dtype)

            add_rows(rows, add)
            if d != o0:
                sems, to, land = (up, above, up_in) if d > o0 else (down, below, down_in)
                send(target, land.at[d], sems.at[0, d], sems.at[1, d], to)

        def mix_step(k):
            p = order[k]
            mine = g_ref.at[p, h]
            received(mine, near_in.at[0, p], near.at[1, 0, k], sibling)
            for dy in far_steps:
                received(mine, far_in.at[dy - 1, p], far.at[1, dy, k], (s, along(-dy)))

            def add(at):
                total = mine[at, :].astype(F32) + near_in[0, p, at, :].astype(F32)
                for dy in far_steps:
                    total = total + far_in[dy - 1, p, at, :].astype(F32)
                done[p, at, :] = total.astype(BF16)

            add_rows(piece, add)
            if k < parts - 1:
                send(done.at[p], mix_ref.at[s], final.at[0, k], final.at[1, k], (p, h))

        for n, d in enumerate(line):
            line_step(d)
            for k in range(n * inner, (n + 1) * inner):
                mix_step(k)
        mine = pltpu.make_async_copy(done.at[s], mix_ref.at[s], local)
        mine.start()
        for n, (src, slots, out) in enumerate(small):
            for dy in far_steps:
                here = slots.at[along(-dy)]
                received(src, here, s_far.at[1, n, dy], (s, along(-dy)))
                send(here, here, s_near.at[0, n, dy], s_near.at[1, n, dy], sibling)
        for n, (src, slots, out) in enumerate(small):
            for dy in [0] + far_steps:
                received(src, slots.at[along(-dy, True)], s_near.at[1, n, dy], sibling)

            def add(k, carry, slots=slots, out=out):
                at = pl.ds(pl.multiple_of(k * 8, 8), 8)
                total = slots[0, at, :]
                for j in range(1, shards):
                    total = total + slots[j, at, :]
                out[at, :] = total
                return carry

            lax.fori_loop(0, src.shape[0] // 8, add, 0)
        for k in range(parts - 1):
            source = lax.rem(s + parts - (k + 1), parts)
            received(done.at[s], mix_ref.at[source], final.at[1, k], (source, h))
        send.finish()
        mine.wait()

    for o0 in range(outer):
        pl.when(o == o0)(functools.partial(branch, o0))


def closing(p, g, blocks, sums, outer, inner, collective):
    parts, rows, cols = p.shape
    _, shards, piece, mix_cols = g.shape
    ys = shards // 2
    slots = pltpu.VMEM((outer, rows, cols), BF16)
    far = pltpu.VMEM((max(ys - 1, 1), parts, piece, mix_cols), BF16)
    return pl.pallas_call(
        functools.partial(closing_kernel, outer, inner, shards),
        out_shape=(
            jax.ShapeDtypeStruct((rows, cols), F32),
            jax.ShapeDtypeStruct((parts, piece, mix_cols), BF16),
            jax.ShapeDtypeStruct(blocks.shape, F32),
            jax.ShapeDtypeStruct(sums.shape, F32),
        ),
        in_specs=[IN_VMEM] * 4,
        out_specs=[IN_VMEM] * 4,
        scratch_shapes=[slots] * 5
        + [
            pltpu.VMEM((ys, parts, piece, mix_cols), BF16),
            far,
            far,
            pltpu.VMEM((parts, piece, mix_cols), BF16),
            pltpu.VMEM((shards,) + blocks.shape, F32),
            pltpu.VMEM((shards,) + sums.shape, F32),
        ]
        + [DMA((2, outer))] * 3
        + [DMA((2, ys, parts))] * 2
        + [DMA((2, parts))]
        + [DMA((2, 2, ys))] * 2
        + [DMA],
        compiler_params=pltpu.CompilerParams(
            collective_id=collective, has_side_effects=True, vmem_limit_bytes=56 * 2**20
        ),
        cost_estimate=cost(75),
        name="closing",
    )(p, g, blocks, sums)


def finish_kernel(
    inner, parts, shards, g_ref, u_ref, d_ref, x_ref, g_out, u_out, d_out, x_out, slots, sems, gs, local
):
    device = plane_place(inner, shards)
    steps = [(di, dy, False) for di, dy in plane_steps(inner, shards // 2)]
    steps = steps + [(di, dy, True) for di, dy, _ in steps] + [(0, 0, True)]
    _, slot_me = device(0, 0)
    s, h = lax.axis_index("seq"), lax.axis_index("shard")
    count = parts * shards
    me = s * shards + h
    barrier = pltpu.get_barrier_semaphore()
    arrays = ((d_ref, d_out), (g_ref, g_out), (u_ref, u_out))

    def other(k):
        to = lax.rem(me + k, count)
        return (to // shards, lax.rem(to, shards)), to

    def hello(k, carry):
        pl.semaphore_signal(barrier, inc=1, device_id=other(k)[0], device_id_type=MESH)
        return carry

    lax.fori_loop(1, count, hello, 0)
    pl.semaphore_wait(barrier, count - 1)
    send = Sent()
    for n, (src, dst) in enumerate(arrays):
        for k, d in enumerate(steps):
            to, slot = device(*d)
            send(src.at[slot], dst.at[slot_me], sems.at[0, n, k], sems.at[1, n, k], to)

    def gain(k):
        to, row = other(k)
        return remote(x_ref.at[row], slots.at[k], gs.at[0, k], gs.at[1, k], to)

    def start(k, carry):
        gain(k).start()
        return carry

    def arrive(k, total):
        gain(k).wait_recv()
        return total + slots[k]

    def leave(k, carry):
        gain(k).wait_send()
        return carry

    lax.fori_loop(1, count, start, 0)
    keep = [
        pltpu.make_async_copy(src.at[slot_me], dst.at[slot_me], local.at[n])
        for n, (src, dst) in enumerate(arrays)
    ]
    for copy in keep:
        copy.start()
    x_out[...] = lax.fori_loop(1, count, arrive, x_ref[me])
    lax.fori_loop(1, count, leave, 0)
    for n, (src, dst) in enumerate(arrays):
        for k, (di, dy, far) in enumerate(steps):
            source, slot = device(-di, -dy, far)
            received(src.at[slot_me], dst.at[slot], sems.at[1, n, k], source)
    send.finish()
    for copy in keep:
        copy.wait()


def finish(gate, up, down, gains, inner, parts, shards, collective):
    slots = gate.shape[0]
    count, _, lanes = gains.shape
    same = jax.ShapeDtypeStruct(gate.shape, gate.dtype)
    return pl.pallas_call(
        functools.partial(finish_kernel, inner, parts, shards),
        out_shape=(same, same, same, jax.ShapeDtypeStruct((1, lanes), F32)),
        in_specs=[ANY, ANY, ANY, IN_VMEM],
        out_specs=[ANY, ANY, ANY, IN_VMEM],
        scratch_shapes=[
            pltpu.VMEM((count, 1, lanes), F32),
            DMA((2, 3, slots)),
            DMA((2, count)),
            DMA((3,)),
        ],
        compiler_params=pltpu.CompilerParams(collective_id=collective, has_side_effects=True),
        cost_estimate=cost(30),
        name="finish",
    )(gate, up, down, gains)


def twin_scatter_kernel(inner, shards, *refs):
    p_refs, out_refs, (near_in, far_in, far_out, near, far) = refs[:2], refs[2:4], refs[4:]
    device = plane_place(inner, shards)
    steps = plane_steps(inner, shards // 2) + [(0, 0)]
    sibling, _ = device(0, 0, True)
    greet([sibling] + [device(*d)[0] for d in steps[:-1]])
    rows = p_refs[0].shape[1]
    send = Sent()
    for n, p_ref in enumerate(p_refs):
        for k, d in enumerate(steps):
            _, slot = device(*d, True)
            send(p_ref.at[slot], near_in.at[n, k], near.at[0, n, k], near.at[1, n, k], sibling)
    for n, (p_ref, out_ref) in enumerate(zip(p_refs, out_refs, strict=True)):
        for k, d in enumerate(steps):
            to, slot = device(*d)
            received(p_ref.at[slot], near_in.at[n, k], near.at[1, n, k], sibling)
            home = k == len(steps) - 1
            target = out_ref if home else far_out.at[n, k]

            def add(at, n=n, k=k, slot=slot, target=target, p_ref=p_ref):
                total = p_ref[slot, at, :].astype(F32) + near_in[n, k, at, :].astype(F32)
                target[at, :] = total.astype(target.dtype)

            add_rows(rows, add)
            if not home:
                send(far_out.at[n, k], far_in.at[n, k], far.at[0, n, k], far.at[1, n, k], to)
    for n, out_ref in enumerate(out_refs):
        for k, d in enumerate(steps[:-1]):
            source, _ = device(-d[0], -d[1])
            received(far_out.at[n, k], far_in.at[n, k], far.at[1, n, k], source)

        def total_of(at, n=n, out_ref=out_ref):
            total = out_ref[at, :]
            for k in range(len(steps) - 1):
                total = total + far_in[n, k, at, :].astype(F32)
            out_ref[at, :] = total

        add_rows(rows, total_of)
    send.finish()


def twin_scatter(p, q, inner, shards, collective):
    slots, rows, cols = p.shape
    chips = slots // 2
    buffers = pltpu.VMEM((2, chips, rows, cols), p.dtype)
    return pl.pallas_call(
        functools.partial(twin_scatter_kernel, inner, shards),
        out_shape=(jax.ShapeDtypeStruct((rows, cols), F32),) * 2,
        in_specs=[IN_VMEM] * 2,
        out_specs=[IN_VMEM] * 2,
        scratch_shapes=[buffers] * 3 + [DMA((2, 2, chips))] * 2,
        compiler_params=pltpu.CompilerParams(
            collective_id=collective, has_side_effects=True, vmem_limit_bytes=48 * 2**20
        ),
        cost_estimate=cost(52),
        name="twin_scatter",
    )(p, q)


def unpack_kernel(
    inner, channels, gate_ref, up_ref, down_ref, mix_ref, gate, up, down, branch, enter, leave
):
    slots, piece, hidden = gate_ref.shape
    shards = slots // inner
    parts, width = mix_ref.shape[0], mix_ref.shape[2] // 3
    for i in range(inner):
        for h in range(shards):
            at = (h * inner + i) * hidden
            slot = i * shards + h
            gate[:, at : at + hidden] = gate_ref[slot].astype(F32)
            up[:, at : at + hidden] = up_ref[slot].astype(F32)
            down[at : at + hidden, :] = down_ref[slot].astype(F32).T

    def row(k):
        lanes = slice(k * width, k * width + width)
        return jnp.concatenate(
            [mix_ref[p][:, lanes].astype(F32)[:, :channels] for p in range(parts)], axis=1
        )

    branch[...] = row(0)
    enter[...] = row(1)
    total = parts * channels
    padded = (total + LANES - 1) // LANES * LANES
    wide = jnp.concatenate([row(2), jnp.zeros((piece, padded - total), F32)], axis=1)
    leave[...] = wide.T[:total, :]


def unpack(ffn_gate, ffn_up, ffn_down, mix, inner, channels):
    slots, piece, hidden = ffn_gate.shape
    lru = mix.shape[0] * channels
    across = jax.ShapeDtypeStruct((piece, slots * hidden), F32)
    along = jax.ShapeDtypeStruct((slots * hidden, piece), F32)
    wide = jax.ShapeDtypeStruct((piece, lru), F32)
    tall = jax.ShapeDtypeStruct((lru, piece), F32)
    return pl.pallas_call(
        functools.partial(unpack_kernel, inner, channels),
        out_shape=(across, across, along, wide, wide, tall),
        in_specs=[IN_VMEM] * 4,
        out_specs=[IN_VMEM] * 6,
        compiler_params=pltpu.CompilerParams(vmem_limit_bytes=48 * 2**20),
        cost_estimate=cost(5),
        name="unpack",
    )(ffn_gate, ffn_up, ffn_down, mix)


def rms_parts(values):
    return lax.rsqrt(jnp.mean(values * values, axis=-1, keepdims=True) + EPSILON)


def rms_back(values, scale, gain, grad):
    k = grad * gain
    return scale * k - scale * scale * scale * values * jnp.mean(
        k * values, axis=-1, keepdims=True
    )


def body(
    tokens,
    first_gain,
    branch_weight,
    input_weight,
    conv_weight,
    conv_bias,
    rate_weight,
    rate_bias,
    entry_weight,
    entry_bias,
    decay_param,
    output_weight,
    second_gain,
    hidden_gate,
    hidden_up,
    hidden_down,
    cotangent,
):
    quarters, _, chunk, model = tokens.shape
    rows = quarters * chunk
    parts = lax.axis_size("seq")
    shards = lax.axis_size("shard")
    inner = 2
    outer = parts // inner
    seq_at = lax.axis_index("seq")
    inner_at = lax.rem(seq_at, inner)
    lru = branch_weight.shape[1]
    channels = lru // parts
    width = (channels + LANES) // LANES * LANES
    spare = width - channels
    blocks, block_width = rate_weight.shape[0], rate_weight.shape[1]
    piece = model // (parts * shards)
    columns = [[o * inner + i for o in range(outer)] for i in range(inner)]

    def own(weight, axis):
        part = lax.dynamic_slice_in_dim(weight, seq_at * channels, channels, axis)
        pads = [(0, 0), (0, 0)]
        pads[axis] = (0, spare)
        return jnp.pad(part, pads)

    params = jnp.pad(
        jnp.concatenate(
            [
                conv_weight.astype(F32),
                conv_bias[None],
                rate_bias[None],
                entry_bias[None],
                decay_param[None],
            ],
            axis=0,
        ),
        ((0, 0), (0, spare)),
    )

    def spread(weight):
        out = jnp.zeros((width, width), BF16)
        for j in range(blocks):
            at = j * block_width
            out = out.at[at : at + block_width, at : at + block_width].set(weight[j])
        return out

    gates = jnp.concatenate([spread(rate_weight), spread(entry_weight)], axis=1)

    xs = tokens.reshape(rows, model).astype(F32)
    cot = cotangent.reshape(rows, model)
    scale1 = rms_parts(xs)
    n1, w_in, w_out, cot_all = opening(
        (xs * scale1 * first_gain).astype(BF16),
        jnp.concatenate([own(branch_weight, 1), own(input_weight, 1)], axis=1),
        own(output_weight, 0),
        cot,
        outer,
        inner,
        shards,
        0,
    )
    n1 = n1.reshape(parts * rows, model)
    w_in = w_in.reshape(model, 2 * width)
    w_out = w_out.transpose(1, 0, 2).reshape(width, model)
    cot_all = cot_all.reshape(inner * shards * rows, model)
    proj = dot(n1, w_in)
    z, h, v = scan_forward(parts, quarters, chunk, proj, params, gates)
    mid = xs + line_scatter(
        dot(z, w_out).astype(BF16).reshape(parts, rows, model), outer, inner, 1
    )
    scale2 = rms_parts(mid)
    n2 = plane_gather((mid * scale2 * second_gain).astype(BF16), inner, shards, 2)
    n2 = n2.reshape(inner * shards * rows, model)
    hidden = hidden_gate.shape[1] // inner
    wg = lax.dynamic_slice_in_dim(hidden_gate, inner_at * hidden, hidden, 1)
    wu = lax.dynamic_slice_in_dim(hidden_up, inner_at * hidden, hidden, 1)
    wd = lax.dynamic_slice_in_dim(hidden_down, inner_at * hidden, hidden, 0)

    def sum_tokens(x):
        return lax.psum_scatter(
            x.astype(BF16), "seq", scatter_dimension=0, tiled=True, axis_index_groups=columns
        ).reshape(inner * shards, piece, hidden)

    gm = dot(n2, wg)
    um = dot(n2, wu)
    act, slope = gelu_and_slope(gm)
    mm = (act * um).astype(BF16)
    down_sum = sum_tokens(dot(cot_all, mm, ((0,), (0,))))
    dmm = dot(cot_all, wd, ((1,), (1,)))
    dgm = (dmm * um * slope).astype(BF16)
    dum = (dmm * act).astype(BF16)
    gate_sum = sum_tokens(dot(n2, dgm, ((0,), (0,))))
    up_terms = dot(n2, dum, ((0,), (0,)))
    dn2_terms = dot(dgm, wg, ((1,), (1,))) + dot(dum, wu, ((1,), (1,)))
    dn2, ffn_out = twin_scatter(
        dn2_terms.astype(BF16).reshape(inner * shards, rows, model),
        dot(mm, wd).astype(BF16).reshape(inner * shards, rows, model),
        inner,
        shards,
        3,
    )
    result = (mid + ffn_out).astype(BF16)
    dmid = cot.astype(F32) + rms_back(mid, scale2, second_gain, dn2)
    second_gain_grad = jnp.sum(dn2 * mid * scale2, axis=0)
    dout = line_gather(dmid.astype(BF16), outer, inner, 4).reshape(parts * rows, model)
    dout, up_terms = lax.optimization_barrier((dout, up_terms.astype(BF16)))
    up_sum = sum_tokens(up_terms)
    dz = dot(dout, w_out, ((1,), (1,)))
    both, small, sums = scan_backward(
        parts, quarters, chunk, blocks, block_width, dz, proj, h, v, params, gates
    )
    mix_grads = jnp.concatenate(
        [dot(n1, both, ((0,), (0,))).astype(BF16), dot(dout, z, ((0,), (0,))).astype(BF16)],
        axis=1,
    )
    dn1, mix, small, sums = closing(
        dot(both, w_in, ((1,), (1,))).astype(BF16).reshape(parts, rows, model),
        mix_grads.reshape(parts, shards, piece, 3 * width),
        small,
        sums,
        outer,
        inner,
        5,
    )
    tokens_grad = (dmid + rms_back(xs, scale1, first_gain, dn1)).reshape(tokens.shape)
    first_gain_grad = jnp.sum(dn1 * xs * scale1, axis=0)
    gains = jnp.concatenate(
        [x.reshape(parts * shards, 1, piece) for x in (first_gain_grad, second_gain_grad)], axis=2
    )
    gain_lanes = -(-2 * piece // LANES) * LANES
    gains = jnp.pad(gains, ((0, 0), (0, 0), (0, gain_lanes - 2 * piece)))
    gate_sum, up_sum, down_sum, gains = finish(
        gate_sum, up_sum, down_sum, gains, inner, parts, shards, 6
    )
    gains = gains[0]
    gate_sum, up_sum, down_sum, branch_sum, input_sum, output_sum = unpack(
        gate_sum, up_sum, down_sum, mix, inner, channels
    )
    sums = sums[:, :channels]
    small = small.reshape(2, blocks, -1, small.shape[1])[:, :, :block_width, :block_width]
    rate_grad, entry_grad = small[0], small[1]
    return (
        result.reshape(tokens.shape),
        tokens_grad,
        gains[:piece],
        branch_sum,
        input_sum,
        sums[4:8],
        sums[3],
        rate_grad,
        sums[1],
        entry_grad,
        sums[2],
        sums[0],
        output_sum,
        gains[piece : 2 * piece],
        gate_sum,
        up_sum,
        down_sum,
    )


def solution(mesh):
    placed = (
        P(None, "shard", "seq", None),
        P(),
        P("shard", None),
        P("shard", None),
        P(None, "seq"),
        P("seq"),
        P("seq", None, None),
        P("seq"),
        P("seq", None, None),
        P("seq"),
        P("seq"),
        P(None, "shard"),
        P(),
        P(None, "shard"),
        P(None, "shard"),
        P("shard", None),
        P(None, "shard", "seq", None),
    )
    return jax.shard_map(
        body,
        mesh=mesh,
        in_specs=placed,
        out_specs=(
            P(None, "shard", "seq", None),
            P(None, "shard", "seq", None),
            P(("seq", "shard")),
            P(("seq", "shard"), None),
            P(("seq", "shard"), None),
            P(None, "seq"),
            P("seq"),
            P("seq", None, None),
            P("seq"),
            P("seq", None, None),
            P("seq"),
            P("seq"),
            P(None, ("seq", "shard")),
            P(("seq", "shard")),
            P(("seq", "shard"), None),
            P(("seq", "shard"), None),
            P(None, ("seq", "shard")),
        ),
        check_vma=False,
    )
```

```python
import functools

import jax
import jax.numpy as jnp
from jax import lax
from jax.experimental import pallas as pl
from jax.experimental.pallas import tpu as pltpu
from jax.sharding import PartitionSpec as P

EPSILON = 1e-06
DECAY_SCALE = 8.0
MULT_FLOOR = 0.01
LANES = 128
SEGMENTS = 8
GELU_C = 0.7978845608028654
GELU_A = 0.044715
F32 = jnp.float32
BF16 = jnp.bfloat16


MESH = pl.DeviceIdType.MESH
ANY = pl.BlockSpec(memory_space=pl.ANY)
IN_VMEM = pl.BlockSpec(memory_space=pltpu.VMEM)
DMA = pltpu.SemaphoreType.DMA


def cost(us):
    return pl.CostEstimate(flops=0, bytes_accessed=int(us * 3.3e6), transcendentals=0)


def dot(left, right, dims=((1,), (0,))):
    return lax.dot_general(left, right, (dims, ((), ())), preferred_element_type=F32)


def gelu_and_slope(x):
    inner = GELU_C * (x + GELU_A * x * x * x)
    t = jnp.tanh(inner)
    half = 0.5 * (1.0 + t)
    slope = half + 0.5 * x * (1.0 - t * t) * (GELU_C * (1.0 + 3.0 * GELU_A * x * x))
    return x * half, slope


def gelu_tanh(x):
    return x * (0.5 * (1.0 + jnp.tanh(GELU_C * (x + GELU_A * x * x * x))))


def sigmoid(x):
    return 0.5 * jnp.tanh(0.5 * x) + 0.5


def softplus(x):
    return jnp.maximum(x, 0.0) + jnp.log1p(jnp.exp(-jnp.abs(x)))


def lane_groups(width):
    return [slice(g * LANES, (g + 1) * LANES) for g in range(width // LANES)]


def put(ref, rows, value):
    for g, lanes in enumerate(lane_groups(value.shape[1])):
        ref[g, rows, :] = value[:, lanes]


def take(ref, rows):
    return jnp.concatenate([ref[g, rows, :] for g in range(ref.shape[0])], axis=1)


def strided_scan(steps, groups, load, store):
    def step(k, carry):
        i = steps(k)
        out = []
        for g in range(groups):
            state, total = carry[g]
            factor, term = load(g, i)
            state = factor * state + term
            total = factor * total
            store(g, i, state, total)
            out.append((state, total))
        return tuple(out)

    return step


TAP, CONV_B, RATE_B, ENTRY_B, DECAY = 0, 4, 5, 6, 7


def gate_values(pre, log_scale, width):
    r = sigmoid(pre[:, :width])
    e = sigmoid(pre[:, width:])
    a = jnp.exp(r * log_scale)
    room = 1.0 - a * a
    m = jnp.sqrt(jnp.maximum(room, MULT_FLOOR))
    return r, e, a, room, m


def scan_forward_kernel(
    parts,
    quarters,
    chunk,
    n1_ref,
    wi_ref,
    par_ref,
    rate_ref,
    entry_ref,
    z_ref,
    h_ref,
    v_ref,
    proj_ref,
    gates_ref,
    n1_s,
    wi_s,
    gates_s,
    u_pad,
    a_s,
    b_s,
    sems,
):
    length, width = h_ref.shape
    rows = quarters * chunk

    def load(p):
        return pltpu.make_async_copy(
            n1_ref.at[p], n1_s.at[pl.ds(pl.multiple_of(p * rows, rows), rows)], sems.at[p]
        )

    weights = pltpu.make_async_copy(wi_ref, wi_s, sems.at[parts])
    weights.start()
    for p in range(parts):
        load(p).start()
    gates_s[...] = jnp.zeros(gates_s.shape, F32)
    blocks, block_width = rate_ref.shape[0], rate_ref.shape[1]
    for gate, src in enumerate((rate_ref, entry_ref)):
        for j in range(blocks):
            at, lane = j * block_width, gate * width + j * block_width
            gates_s[at : at + block_width, lane : lane + block_width] = src[j].astype(F32)
    gates_ref[...] = gates_s[...].astype(BF16)
    weights.wait()

    def project(k, carry):
        load(2 * k).wait()
        load(2 * k + 1).wait()
        at = pl.ds(pl.multiple_of(k * 2 * rows, 2 * rows), 2 * rows)
        proj_ref[at, :] = dot(n1_s[at, :], wi_s[...])
        return carry

    lax.fori_loop(0, parts // 2, project, 0)
    seg = length // SEGMENTS
    chunks = length // chunk

    def place(c):
        q = c // parts
        s = c - q * parts
        return pl.multiple_of((s * quarters + q) * chunk, chunk)

    def time_of(c):
        return pl.multiple_of(c * chunk, chunk)

    log_scale = -DECAY_SCALE * softplus(-par_ref[DECAY : DECAY + 1, :])
    bias = jnp.concatenate(
        [par_ref[RATE_B : RATE_B + 1, :], par_ref[ENTRY_B : ENTRY_B + 1, :]], axis=1
    )
    u_pad[0:8, :] = jnp.zeros((8, width), F32)

    def first(c, carry):
        u = proj_ref[pl.ds(place(c), chunk), width : 2 * width].astype(BF16).astype(F32)
        u_pad[pl.ds(pl.multiple_of(time_of(c) + 8, 8), chunk), :] = u
        wide = u_pad[pl.ds(time_of(c), chunk + 8), :]
        v = par_ref[CONV_B : CONV_B + 1, :] + par_ref[0:1, :] * wide[8:]
        for k in range(1, 4):
            v = v + par_ref[k : k + 1, :] * wide[8 - k : 8 - k + chunk]
        v = v.astype(BF16)
        v_ref[pl.ds(time_of(c), chunk), :] = v
        pre = dot(v, gates_ref[...]) + bias
        r, e, a, room, m = gate_values(pre, log_scale, width)
        put(a_s, pl.ds(time_of(c), chunk), a)
        put(b_s, pl.ds(time_of(c), chunk), m * e * v.astype(F32))
        return carry

    lax.fori_loop(0, chunks, first, 0)

    def load(g, i):
        at = pl.ds(i, SEGMENTS, stride=seg)
        return a_s[g, at, :], b_s[g, at, :]

    def store(g, i, state, total):
        at = pl.ds(i, SEGMENTS, stride=seg)
        b_s[g, at, :] = state
        a_s[g, at, :] = total

    groups = width // LANES
    start = (jnp.zeros((SEGMENTS, LANES), F32), jnp.ones((SEGMENTS, LANES), F32))
    ends = lax.fori_loop(
        0, seg, strided_scan(lambda k: k, groups, load, store), (start,) * groups, unroll=8
    )
    final = jnp.concatenate([e[0] for e in ends], axis=1)
    totals = jnp.concatenate([e[1] for e in ends], axis=1)
    carries = [jnp.zeros((1, width), F32)]
    for j in range(SEGMENTS - 1):
        carries.append(totals[j : j + 1] * carries[j] + final[j : j + 1])
    for j in range(SEGMENTS):
        per = seg // chunk

        def last(k, carry, j=j, per=per):
            c = j * per + k
            rows = pl.ds(time_of(c), chunk)
            h = take(b_s, rows) + take(a_s, rows) * carries[j]
            h_ref[rows, :] = h
            y = gelu_tanh(proj_ref[pl.ds(place(c), chunk), 0:width])
            z_ref[pl.ds(place(c), chunk), :] = (h.astype(BF16).astype(F32) * y).astype(BF16)
            return carry

        lax.fori_loop(0, per, last, 0)


def scan_forward(quarters, chunk, n1, w_in, params, rate, entry):
    parts, rows, model = n1.shape
    length, width = parts * rows, w_in.shape[1] // 2
    return pl.pallas_call(
        functools.partial(scan_forward_kernel, parts, quarters, chunk),
        out_shape=(
            jax.ShapeDtypeStruct((length, width), BF16),
            jax.ShapeDtypeStruct((length, width), F32),
            jax.ShapeDtypeStruct((length, width), BF16),
            jax.ShapeDtypeStruct((length, 2 * width), F32),
            jax.ShapeDtypeStruct((width, 2 * width), BF16),
        ),
        in_specs=[ANY] * 2 + [IN_VMEM] * 3,
        out_specs=[IN_VMEM] * 5,
        scratch_shapes=[
            pltpu.VMEM((length, model), BF16),
            pltpu.VMEM(w_in.shape, BF16),
            pltpu.VMEM((width, 2 * width), F32),
            pltpu.VMEM((length + 8, width), F32),
            pltpu.VMEM((width // LANES, length, LANES), F32),
            pltpu.VMEM((width // LANES, length, LANES), F32),
            DMA((parts + 1,)),
        ],
        compiler_params=pltpu.CompilerParams(vmem_limit_bytes=48 * 2**20),
        cost_estimate=cost(18),
        name="scan_forward",
    )(n1, w_in, params, rate, entry)


def scan_backward_kernel(
    parts,
    quarters,
    chunk,
    blocks,
    block_width,
    dout_ref,
    wo_ref,
    proj_ref,
    h_ref,
    v_ref,
    par_ref,
    gates_ref,
    both_ref,
    blocks_ref,
    totals_ref,
    dout_s,
    dz_s,
    sems,
    sums_ref,
    gate_grad_ref,
    a_s,
    g_s,
    t_s,
    h_pad,
    pre_s,
    dpre_s,
    dv_s,
    u_pad,
):
    length, width = h_ref.shape
    seg = length // SEGMENTS
    chunks = length // chunk

    def place(c):
        q = c // parts
        s = c - q * parts
        return pl.multiple_of((s * quarters + q) * chunk, chunk)

    def time_of(c):
        return pl.multiple_of(c * chunk, chunk)

    span = quarters * chunk

    def load(p):
        return pltpu.make_async_copy(
            dout_ref.at[p], dout_s.at[pl.ds(pl.multiple_of(p * span, span), span)], sems.at[p]
        )

    for p in range(parts):
        load(p).start()

    def back_project(k, carry):
        load(2 * k).wait()
        load(2 * k + 1).wait()
        at = pl.ds(pl.multiple_of(k * 2 * span, 2 * span), 2 * span)
        depth = wo_ref.shape[2]
        total = dot(dout_s[at, 0:depth], wo_ref[0], ((1,), (1,)))
        for p in range(1, wo_ref.shape[0]):
            lanes = slice(p * depth, (p + 1) * depth)
            total = total + dot(dout_s[at, lanes], wo_ref[p], ((1,), (1,)))
        dz_s[at, :] = total
        return carry

    lax.fori_loop(0, parts // 2, back_project, 0)
    log_scale = -DECAY_SCALE * softplus(-par_ref[DECAY : DECAY + 1, :])
    bias = jnp.concatenate(
        [par_ref[RATE_B : RATE_B + 1, :], par_ref[ENTRY_B : ENTRY_B + 1, :]], axis=1
    )
    zeros8 = jnp.zeros((8, width), F32)
    put(a_s, pl.ds(length, 8), zeros8)
    h_pad[0:8, :] = zeros8
    u_pad[0:8, :] = zeros8
    dv_s[pl.ds(length, 8), :] = zeros8

    def first(c, carry):
        rows = pl.ds(time_of(c), chunk)
        later = pl.ds(pl.multiple_of(time_of(c) + 8, 8), chunk)
        there = pl.ds(place(c), chunk)
        h = h_ref[rows, :]
        h_pad[later, :] = h
        u_pad[later, :] = proj_ref[there, width : 2 * width].astype(BF16).astype(F32)
        y, slope = gelu_and_slope(proj_ref[there, 0:width])
        dz = dz_s[there, :]
        put(g_s, rows, (dz * y).astype(BF16).astype(F32))
        both_ref[there, 0:width] = (dz * h.astype(BF16).astype(F32) * slope).astype(BF16)
        pre = dot(v_ref[rows, :], gates_ref[...]) + bias
        pre_s[rows, :] = pre
        put(a_s, rows, jnp.exp(sigmoid(pre[:, :width]) * log_scale))
        return carry

    lax.fori_loop(0, chunks, first, 0)

    def load(g, i):
        return (
            a_s[g, pl.ds(i + 1, SEGMENTS, stride=seg), :],
            g_s[g, pl.ds(i, SEGMENTS, stride=seg), :],
        )

    def store(g, i, state, total):
        g_s[g, pl.ds(i, SEGMENTS, stride=seg), :] = state
        t_s[g, pl.ds(i, SEGMENTS, stride=seg), :] = total

    groups = width // LANES
    start = (jnp.zeros((SEGMENTS, LANES), F32), jnp.ones((SEGMENTS, LANES), F32))
    ends = lax.fori_loop(
        0,
        seg,
        strided_scan(lambda k: seg - 1 - k, groups, load, store),
        (start,) * groups,
        unroll=8,
    )
    firsts = jnp.concatenate([e[0] for e in ends], axis=1)
    totals = jnp.concatenate([e[1] for e in ends], axis=1)
    carries = [None] * SEGMENTS
    carries[SEGMENTS - 1] = jnp.zeros((1, width), F32)
    for j in range(SEGMENTS - 2, -1, -1):
        carries[j] = totals[j + 1 : j + 2] * carries[j + 1] + firsts[j + 1 : j + 2]

    def fold(values):
        return jnp.sum(values.reshape(chunk // 8, 8, values.shape[1]), axis=0)

    sums_ref[...] = jnp.zeros(sums_ref.shape, F32)

    for j in range(SEGMENTS):
        per = seg // chunk

        def middle(k, carry, j=j, per=per):
            c = j * per + k
            rows = pl.ds(time_of(c), chunk)
            g = take(g_s, rows) + take(t_s, rows) * carries[j]
            before = h_pad[pl.ds(time_of(c), chunk + 8), :][7 : 7 + chunk]
            v = v_ref[rows, :].astype(F32)
            r, e, a, room, m = gate_values(pre_s[rows, :], log_scale, width)
            gv = g * v
            held = jnp.where(room > MULT_FLOOR, gv * e * a / m, 0.0)
            ta = (g * before - held) * a * r
            drpre = (ta * (log_scale * (1.0 - r))).astype(BF16)
            depre = (gv * m * e * (1.0 - e)).astype(BF16)
            dpre_s[rows, 0:width] = drpre
            dpre_s[rows, width : 2 * width] = depre
            sums_ref[0:8, :] += fold(ta)
            sums_ref[8:16, :] += fold(drpre.astype(F32))
            sums_ref[16:24, :] += fold(depre.astype(F32))
            dv = g * m * e + dot(dpre_s[rows, :], gates_ref[...], ((1,), (1,)))
            dv_s[rows, :] = dv
            sums_ref[24:32, :] += fold(dv)
            wide = u_pad[pl.ds(time_of(c), chunk + 8), :]
            for tap in range(4):
                at = 32 + 8 * tap
                sums_ref[at : at + 8, :] += fold(dv * wide[8 - tap : 8 - tap + chunk])
            return carry

        lax.fori_loop(0, per, middle, 0)
    sums_ref[0:8, :] = sums_ref[0:8, :] * (
        DECAY_SCALE * sigmoid(-par_ref[DECAY : DECAY + 1, :])
    )

    def last(c, carry):
        wide = dv_s[pl.ds(time_of(c), chunk + 8), :]
        du = par_ref[0:1, :] * wide[0:chunk]
        for tap in range(1, 4):
            du = du + par_ref[tap : tap + 1, :] * wide[tap : tap + chunk]
        both_ref[pl.ds(place(c), chunk), width : 2 * width] = du.astype(BF16)
        return carry

    lax.fori_loop(0, chunks, last, 0)
    gate_grad_ref[...] = dot(v_ref[...], dpre_s[...], ((0,), (0,)))
    blocks_ref[...] = jnp.zeros(blocks_ref.shape, F32)
    tall = blocks_ref.shape[0] // (2 * blocks)
    for gate in range(2):
        for j in range(blocks):
            at, lanes = (gate * blocks + j) * tall, gate * width + j * block_width
            rows = slice(j * block_width, (j + 1) * block_width)
            blocks_ref[at : at + block_width, :block_width] = gate_grad_ref[
                rows, lanes : lanes + block_width
            ]
    for k in range(8):
        totals_ref[k : k + 1, :] = jnp.sum(sums_ref[8 * k : 8 * k + 8, :], axis=0, keepdims=True)


def scan_backward(
    quarters, chunk, blocks, block_width, dout, w_out, proj, h, v, params, gates
):
    parts = dout.shape[0]
    length, width = h.shape
    tall, wide = -(-block_width // 8) * 8, -(-block_width // LANES) * LANES
    return pl.pallas_call(
        functools.partial(scan_backward_kernel, parts, quarters, chunk, blocks, block_width),
        out_shape=(
            jax.ShapeDtypeStruct((length, 2 * width), BF16),
            jax.ShapeDtypeStruct((2 * blocks * tall, wide), F32),
            jax.ShapeDtypeStruct((8, width), F32),
        ),
        in_specs=[ANY] + [IN_VMEM] * 6,
        out_specs=[IN_VMEM] * 3,
        scratch_shapes=[
            pltpu.VMEM((length, dout.shape[2]), BF16),
            pltpu.VMEM((length, width), F32),
            DMA((parts,)),
            pltpu.VMEM((64, width), F32),
            pltpu.VMEM((width, 2 * width), F32),
            pltpu.VMEM((width // LANES, length + 8, LANES), F32),
            pltpu.VMEM((width // LANES, length, LANES), F32),
            pltpu.VMEM((width // LANES, length, LANES), F32),
            pltpu.VMEM((length + 8, width), F32),
            pltpu.VMEM((length, 2 * width), F32),
            pltpu.VMEM((length, 2 * width), BF16),
            pltpu.VMEM((length + 8, width), F32),
            pltpu.VMEM((length + 8, width), F32),
        ],
        compiler_params=pltpu.CompilerParams(vmem_limit_bytes=56 * 2**20),
        cost_estimate=cost(21),
        name="scan_backward",
    )(dout, w_out, proj, h, v, params, gates)


def remote(src, dst, send, recv, to):
    return pltpu.make_async_remote_copy(
        src_ref=src, dst_ref=dst, send_sem=send, recv_sem=recv, device_id=to, device_id_type=MESH
    )


def add_rows(rows, fn):
    def one(k, carry):
        fn(pl.ds(pl.multiple_of(k * 16, 16), 16))
        return carry

    lax.fori_loop(0, rows // 16, one, 0)


class Place:
    def __init__(self, outer, inner, shards):
        self.outer, self.inner, self.shards = outer, inner, shards
        self.parts, self.ys, self.count = outer * inner, shards // 2, outer * inner * shards
        self.chips = inner * self.ys
        self.s, self.h = lax.axis_index("seq"), lax.axis_index("shard")
        self.o, self.i = self.s // inner, lax.rem(self.s, inner)
        self.y, self.core = self.h // 2, lax.rem(self.h, 2)
        self.beside = (self.o * inner + 1 - self.i, self.h)
        self.above, self.below = (self.s + inner, self.h), (self.s - inner, self.h)
        self.sibling = (self.s, self.along(0, 1))

    def along(self, dy, other=0):
        y = lax.rem(self.y + dy + self.ys, self.ys)
        return y * 2 + lax.rem(self.core + other, 2)

    def chip(self, q, back=False):
        di, dy = q // self.ys, q - q // self.ys * self.ys
        if back:
            di, dy = self.inner - di, self.ys - dy
        return lax.rem(self.i + di, self.inner), lax.rem(self.y + dy, self.ys)

    def near(self, q, other=0, back=False):
        i, y = self.chip(q, back)
        h = y * 2 + lax.rem(self.core + other, 2)
        return (self.o * self.inner + i, h), i * self.shards + h

    def far_first(self, n):
        sign = 2 * ((2 * self.o) // self.outer) - 1
        return lax.rem(self.o + sign * (n + 1) + 2 * self.outer, self.outer)

    def branches(self, fn):
        for o0 in range(self.outer):
            pl.when(self.o == o0)(functools.partial(fn, o0))


def hello(to):
    barrier = pltpu.get_barrier_semaphore()
    pl.semaphore_signal(barrier, inc=1, device_id=to, device_id_type=MESH)


def welcome(n):
    pl.semaphore_wait(pltpu.get_barrier_semaphore(), n)


def greet(others):
    for to in others:
        hello(to)
    welcome(len(others))


def greet_with_line(at, others):
    up, down = at.o < at.outer - 1, at.o > 0
    for to in others:
        hello(to)
    pl.when(up)(lambda: hello(at.above))
    pl.when(down)(lambda: hello(at.below))
    ends = lax.rem(at.o, at.outer - 1) == 0
    pl.when(ends)(lambda: welcome(len(others) + 1))
    pl.when(jnp.logical_not(ends))(lambda: welcome(len(others) + 2))


class Sent:
    def __init__(self):
        self.copies = []

    def __call__(self, src, dst, sems, at, to):
        copy = remote(src, dst, sems.at[(0,) + at], sems.at[(1,) + at], to)
        copy.start()
        self.copies.append(copy)

    def finish(self):
        for copy in self.copies:
            copy.wait_send()


def received(like, here, sems, at, source):
    remote(like, here, sems.at[(0,) + at], sems.at[(1,) + at], source).wait_recv()


def line_gather(at, o0, x_ref, out, across, up, down, between=lambda k: None):
    send = Sent()

    def slot(row):
        return out.at[row * at.inner + at.i]

    def pass_on(row, sems, to):
        send(x_ref if row == o0 else slot(row), slot(row), sems, (row,), to)

    for k in range(at.outer):
        lower, upper = o0 - k, o0 + k
        if k > 0 and lower >= 0:
            received(x_ref, slot(lower), up, (lower,), at.below)
        if lower >= 0 and o0 < at.outer - 1:
            pass_on(lower, up, at.above)
        if lower >= 0:
            pass_on(lower, across, at.beside)
        if k > 0 and upper < at.outer:
            received(x_ref, slot(upper), down, (upper,), at.above)
        if upper < at.outer and o0 > 0:
            pass_on(upper, down, at.below)
        if k > 0 and upper < at.outer:
            pass_on(upper, across, at.beside)
        between(k)
    for row in range(at.outer):
        received(x_ref, out.at[row * at.inner + 1 - at.i], across, (row,), at.beside)
    send.finish()


class LineSum:
    def __init__(self, at, p, bufs, sems):
        self.at, self.p = at, p
        self.x_in, self.up_in, self.down_in, self.sums = bufs
        self.across, self.up, self.down = sems
        self.rows = self.x_in.shape[1]

    def block(self, d, i):
        return self.p.at[d, pl.ds(pl.multiple_of(i * self.rows, self.rows), self.rows)]

    def cross(self, d):
        return remote(
            self.block(d, 1 - self.at.i),
            self.x_in.at[d],
            self.across.at[0, d],
            self.across.at[1, d],
            self.at.beside,
        )

    def steps(self, o0, last_add, between=lambda n: None):
        at = self.at
        send = Sent()
        order = sorted(range(at.outer), key=lambda d: (-abs(d - o0), d))
        for n, d in enumerate(order):
            mine = self.block(d, at.i)
            self.cross(d).wait_recv()
            terms = [mine, self.x_in.at[d]]
            if d >= o0 > 0:
                received(mine, self.up_in.at[d], self.up, (d,), at.below)
                terms.append(self.up_in.at[d])
            if d <= o0 < at.outer - 1:
                received(mine, self.down_in.at[d], self.down, (d,), at.above)
                terms.append(self.down_in.at[d])
            target = self.sums.at[d]

            def add(rows, terms=terms, target=target, d=d):
                total = terms[0][rows, :].astype(F32)
                for term in terms[1:]:
                    total = total + term[rows, :].astype(F32)
                if d == o0:
                    last_add(rows, total)
                else:
                    target[rows, :] = total.astype(target.dtype)

            add_rows(self.rows, add)
            if d > o0:
                send(target, self.up_in.at[d], self.up, (d,), at.above)
            if d < o0:
                send(target, self.down_in.at[d], self.down, (d,), at.below)
            between(n)
        for d in range(at.outer):
            self.cross(d).wait_send()
        send.finish()


def line_sum_scratch(outer, rows, cols):
    return [pltpu.VMEM((outer, rows, cols), BF16)] * 4, [DMA((2, outer))] * 3


def opening_kernel(
    outer, inner, shards, x_ref, wi_ref, wo_ref, n_out, wi_out, wo_out, local, across, up, down, far, near
):
    at = Place(outer, inner, shards)
    steps = list(range(1, at.ys))
    weights = ((wi_ref, wi_out), (wo_ref, wo_out))
    greet_with_line(at, [at.beside, at.sibling] + [(at.s, at.along(dy)) for dy in steps])
    keep = [
        pltpu.make_async_copy(x_ref, n_out.at[at.s], local.at[0]),
        pltpu.make_async_copy(wi_ref, wi_out.at[at.h], local.at[1]),
        pltpu.make_async_copy(wo_ref, wo_out.at[at.h], local.at[2]),
    ]
    for copy in keep:
        copy.start()
    send = Sent()
    for n, (src, dst) in enumerate(weights):
        for dy in steps:
            send(src, dst.at[at.h], far, (n, dy), (at.s, at.along(dy)))
        send(src, dst.at[at.h], near, (n, 0), at.sibling)

    def branch(o0):
        forward = Sent()

        def between(k):
            if k != 1:
                return
            for n, (src, dst) in enumerate(weights):
                for dy in steps:
                    source = at.along(-dy)
                    received(src, dst.at[source], far, (n, dy), (at.s, source))
                    forward(dst.at[source], dst.at[source], near, (n, dy), at.sibling)

        line_gather(at, o0, x_ref, n_out, across, up, down, between)
        forward.finish()

    at.branches(branch)
    for n, (src, dst) in enumerate(weights):
        for dy in range(at.ys):
            received(src, dst.at[at.along(-dy, 1)], near, (n, dy), at.sibling)
    send.finish()
    for copy in keep:
        copy.wait()


def opening(x, w_in, w_out, outer, inner, shards, collective):
    ys = shards // 2
    return pl.pallas_call(
        functools.partial(opening_kernel, outer, inner, shards),
        out_shape=(
            jax.ShapeDtypeStruct((outer * inner,) + x.shape, x.dtype),
            jax.ShapeDtypeStruct((shards,) + w_in.shape, w_in.dtype),
            jax.ShapeDtypeStruct((shards,) + w_out.shape, w_out.dtype),
        ),
        in_specs=[ANY] * 3,
        out_specs=[ANY] * 3,
        scratch_shapes=[DMA((3,))] + [DMA((2, outer))] * 3 + [DMA((2, 2, ys))] * 2,
        compiler_params=pltpu.CompilerParams(collective_id=collective, has_side_effects=True),
        cost_estimate=cost(55),
        name="opening",
    )(x, w_in, w_out)


def row_rms(values):
    return lax.rsqrt(jnp.mean(values * values, axis=-1, keepdims=True) + EPSILON)


def rms_back(values, scale, gain, grad):
    k = grad * gain
    mean = jnp.mean(k * values, axis=-1, keepdims=True)
    return scale * k - scale * scale * scale * values * mean


def middle_kernel(
    outer,
    inner,
    shards,
    z_ref,
    wo_ref,
    x_ref,
    gain_ref,
    cot_ref,
    cot_beside_ref,
    mid_ref,
    n2_out,
    cot_out,
    p_s,
    n2_s,
    x_in,
    up_in,
    down_in,
    line_out,
    across,
    up,
    down,
    far,
    near,
    c_far,
    c_near,
    local,
):
    at = Place(outer, inner, shards)
    line = LineSum(at, p_s, (x_in, up_in, down_in, line_out), (across, up, down))
    steps = list(range(1, at.ys))
    cols = wo_ref.shape[2]
    greet_with_line(at, [at.sibling] + [at.near(q)[0] for q in range(1, at.chips)])
    send = Sent()

    def project(n, carry):
        d = at.far_first(n)
        for k in range(shards):
            block = dot(z_ref[d], wo_ref[k]).astype(BF16)
            p_s[d, :, k * cols : (k + 1) * cols] = block
        line.cross(d).start()
        return carry

    lax.fori_loop(0, outer, project, 0)

    def slot(side, dy, other=0):
        i = 1 - at.i if side else at.i
        return cot_out.at[i * shards + at.along(dy, other)]

    mine = (cot_ref, cot_beside_ref)
    keep = []
    for side in range(2):
        keep.append(pltpu.make_async_copy(mine[side], slot(side, 0), local.at[side]))
        keep[-1].start()
        for dy in steps:
            send(mine[side], slot(side, 0), c_far, (side, dy), (at.s, at.along(dy)))
        send(mine[side], slot(side, 0), c_near, (side, 0), at.sibling)

    def last_add(rows, total):
        mid = x_ref[rows, :].astype(F32) + total
        mid_ref[rows, :] = mid
        n2_s[rows, :] = (mid * row_rms(mid) * gain_ref[...]).astype(BF16)

    def branch(o0):
        forward = Sent()

        def between(n):
            if n != outer - 2:
                return
            for side in range(2):
                for dy in steps:
                    here = slot(side, -dy)
                    received(cot_ref, here, c_far, (side, dy), (at.s, at.along(-dy)))
                    forward(here, here, c_near, (side, dy), at.sibling)

        line.steps(o0, last_add, between)
        forward.finish()

    at.branches(branch)
    _, me = at.near(0)
    keep.append(pltpu.make_async_copy(n2_s, n2_out.at[me], local.at[2]))
    keep[-1].start()
    for q in reversed(range(1, at.chips)):
        send(n2_s, n2_out.at[me], far, (q,), at.near(q)[0])
    send(n2_s, n2_out.at[me], near, (0,), at.sibling)
    for q in range(1, at.chips):
        source, there = at.near(q, back=True)
        here = n2_out.at[there]
        received(n2_s, here, far, (q,), source)
        send(here, here, near, (q,), at.sibling)
    for q in range(at.chips):
        received(n2_s, n2_out.at[at.near(q, 1, True)[1]], near, (q,), at.sibling)
    for side in range(2):
        for dy in range(at.ys):
            received(cot_ref, slot(side, -dy, 1), c_near, (side, dy), at.sibling)
    send.finish()
    for copy in keep:
        copy.wait()


def middle(z, w_out, x, gain, cot, cot_beside, outer, inner, shards, collective):
    rows, cols = x.shape
    ys, chips = shards // 2, inner * shards // 2
    bufs, sems = line_sum_scratch(outer, rows, cols)
    plane = jax.ShapeDtypeStruct((inner * shards, rows, cols), BF16)
    return pl.pallas_call(
        functools.partial(middle_kernel, outer, inner, shards),
        out_shape=(jax.ShapeDtypeStruct((rows, cols), F32), plane, plane),
        in_specs=[IN_VMEM] * 4 + [ANY] * 2,
        out_specs=[IN_VMEM, ANY, ANY],
        scratch_shapes=[
            pltpu.VMEM((outer, inner * rows, cols), BF16),
            pltpu.VMEM((rows, cols), BF16),
        ]
        + bufs
        + sems
        + [DMA((2, chips))] * 2
        + [DMA((2, 2, ys))] * 2
        + [DMA((3,))],
        compiler_params=pltpu.CompilerParams(
            collective_id=collective, has_side_effects=True, vmem_limit_bytes=48 * 2**20
        ),
        cost_estimate=cost(80),
        name="middle",
    )(z.reshape(outer, inner * rows, z.shape[1]), w_out, x, gain, cot, cot_beside)


class PlaneSum:
    def __init__(self, at, n, p, near_in, far_in, far_out, near, far):
        self.at, self.n, self.p = at, n, p
        self.near_in, self.far_in, self.far_out = near_in, far_in, far_out
        self.near, self.far = near, far
        self.rows = near_in.shape[2]

    def block(self, q, other):
        i, y = self.at.chip(q)
        core = lax.rem(self.at.core + other, 2)
        rows = pl.ds(pl.multiple_of(core * self.rows, self.rows), self.rows)
        return self.p.at[i * self.at.ys + y, rows]

    def to_sibling(self, q):
        n = self.n
        return remote(
            self.block(q, 1),
            self.near_in.at[n, q],
            self.near.at[0, n, q],
            self.near.at[1, n, q],
            self.at.sibling,
        )

    def onward(self, q, back=False):
        n = self.n
        return remote(
            self.far_out.at[n, q],
            self.far_in.at[n, q],
            self.far.at[0, n, q],
            self.far.at[1, n, q],
            self.at.near(q, 0, back)[0],
        )

    def combine(self):
        def one(k, carry):
            q = self.at.chips - 1 - k
            self.to_sibling(q).wait_recv()
            mine = self.block(q, 0)

            def add(rows):
                total = mine[rows, :].astype(F32) + self.near_in[self.n, q, rows, :].astype(F32)
                self.far_out[self.n, q, rows, :] = total.astype(BF16)

            add_rows(self.rows, add)
            self.onward(q).start()
            return carry

        lax.fori_loop(0, self.at.chips - 1, one, 0)
        self.to_sibling(0).wait_recv()

    def total(self, rows):
        n = self.n
        value = self.block(0, 0)[rows, :].astype(F32) + self.near_in[n, 0, rows, :].astype(F32)
        for q in range(1, self.at.chips):
            value = value + self.far_in[n, q, rows, :].astype(F32)
        return value

    def arrive(self):
        for q in range(1, self.at.chips):
            self.onward(q, True).wait_recv()

    def finish(self):
        for q in range(self.at.chips):
            self.to_sibling(q).wait_send()
        for q in range(1, self.at.chips):
            self.onward(q).wait_send()


def turn_kernel(
    outer,
    inner,
    shards,
    dgm_ref,
    dum_ref,
    mm_ref,
    wg_ref,
    wu_ref,
    wd_ref,
    mid_ref,
    cot_ref,
    gain_ref,
    dmid_ref,
    dout_ref,
    result_ref,
    gain_grad_ref,
    p_s,
    q_s,
    dout_s,
    gain_s,
    wg_s,
    wu_s,
    wd_s,
    near_in,
    far_in,
    far_out,
    near,
    far,
    across,
    up,
    down,
    local,
):
    at = Place(outer, inner, shards)
    model, hidden = wg_s.shape
    own = pl.ds(pl.multiple_of(at.i * hidden, hidden), hidden)
    load = [
        pltpu.make_async_copy(wg_ref.at[:, own], wg_s, local.at[1]),
        pltpu.make_async_copy(wu_ref.at[:, own], wu_s, local.at[2]),
        pltpu.make_async_copy(wd_ref.at[own, :], wd_s, local.at[3]),
    ]
    for copy in load:
        copy.start()
    tile = min(512, model)
    greet_with_line(at, [at.sibling] + [at.near(q)[0] for q in range(1, at.chips)])
    grad = PlaneSum(at, 0, p_s, near_in, far_in, far_out, near, far)
    value = PlaneSum(at, 1, q_s, near_in, far_in, far_out, near, far)

    load[0].wait()
    load[1].wait()

    def back(k, carry):
        q = at.chips - 1 - k
        i, y = at.chip(q)
        c = i * at.ys + y
        for lane in range(0, model, tile):
            lanes = slice(lane, lane + tile)
            block = dot(dgm_ref[c], wg_s[lanes, :], ((1,), (1,)))
            block = block + dot(dum_ref[c], wu_s[lanes, :], ((1,), (1,)))
            p_s[c, :, lanes] = block.astype(BF16)
        grad.to_sibling(q).start()
        return carry

    lax.fori_loop(0, at.chips, back, 0)
    grad.combine()

    load[2].wait()

    def ahead(k, carry):
        q = at.chips - 1 - k
        i, y = at.chip(q)
        c = i * at.ys + y
        for lane in range(0, model, tile):
            lanes = slice(lane, lane + tile)
            q_s[c, :, lanes] = dot(mm_ref[c], wd_s[:, lanes]).astype(BF16)
        value.to_sibling(q).start()
        return carry

    lax.fori_loop(0, at.chips, ahead, 0)
    gain_s[...] = jnp.zeros(gain_s.shape, F32)
    grad.arrive()

    def norm_back(rows):
        dn2 = grad.total(rows)
        mid = mid_ref[rows, :]
        scale = row_rms(mid)
        gain_s[...] += dn2 * mid * scale
        dmid = cot_ref[rows, :].astype(F32) + rms_back(mid, scale, gain_ref[...], dn2)
        dmid_ref[rows, :] = dmid
        dout_s[rows, :] = dmid.astype(BF16)

    add_rows(dout_s.shape[0], norm_back)
    gain_grad_ref[...] = jnp.sum(gain_s[...], axis=0, keepdims=True)
    keep = pltpu.make_async_copy(dout_s, dout_ref.at[at.s], local.at[0])
    keep.start()

    def branch(o0):
        def between(k):
            if k == 0:
                value.combine()

        line_gather(at, o0, dout_s, dout_ref, across, up, down, between)

    at.branches(branch)
    value.arrive()

    def output(rows):
        result_ref[rows, :] = (mid_ref[rows, :] + value.total(rows)).astype(BF16)

    add_rows(result_ref.shape[0], output)
    grad.finish()
    value.finish()
    keep.wait()


def turn(dgm, dum, mm, wg, wu, wd, mid, cot, gain, outer, inner, shards, collective):
    rows, cols = mid.shape
    hidden = dgm.shape[1]
    chips = inner * shards // 2
    buffers = pltpu.VMEM((2, chips, rows, cols), BF16)
    partial = pltpu.VMEM((chips, 2 * rows, cols), BF16)
    dgm, dum, mm = (x.reshape(chips, 2 * rows, hidden) for x in (dgm, dum, mm))
    return pl.pallas_call(
        functools.partial(turn_kernel, outer, inner, shards),
        out_shape=(
            jax.ShapeDtypeStruct((rows, cols), F32),
            jax.ShapeDtypeStruct((outer * inner, rows, cols), BF16),
            jax.ShapeDtypeStruct((rows, cols), BF16),
            jax.ShapeDtypeStruct((1, cols), F32),
        ),
        in_specs=[IN_VMEM] * 3 + [ANY] * 3 + [IN_VMEM] * 3,
        out_specs=[IN_VMEM, ANY, IN_VMEM, IN_VMEM],
        scratch_shapes=[
            partial,
            partial,
            pltpu.VMEM((rows, cols), BF16),
            pltpu.VMEM((16, cols), F32),
            pltpu.VMEM((cols, hidden), BF16),
            pltpu.VMEM((cols, hidden), BF16),
            pltpu.VMEM((hidden, cols), BF16),
        ]
        + [buffers] * 3
        + [DMA((2, 2, chips))] * 2
        + [DMA((2, outer))] * 3
        + [DMA((4,))],
        compiler_params=pltpu.CompilerParams(
            collective_id=collective, has_side_effects=True, vmem_limit_bytes=56 * 2**20
        ),
        cost_estimate=cost(120),
        name="turn",
    )(dgm, dum, mm, wg, wu, wd, mid, cot, gain)


class PlaneExchange:
    def __init__(self, at, n, x, out, sems, local):
        self.at, self.n, self.x, self.out, self.sems = at, n, x, out, sems
        _, self.me = at.near(0)
        self.keep = pltpu.make_async_copy(x.at[self.me], out.at[self.me], local)
        self.hops = [(q, other) for q in reversed(range(at.chips)) for other in range(2)][:-2] + [(0, 1)]

    def others(self):
        return [self.at.near(q, other)[0] for q, other in self.hops]

    def start(self):
        self.send = Sent()
        for k, (q, other) in enumerate(self.hops):
            to, slot = self.at.near(q, other)
            self.send(self.x.at[slot], self.out.at[self.me], self.sems, (self.n, k), to)
        self.keep.start()

    def finish(self):
        for k, (q, other) in enumerate(self.hops):
            source, slot = self.at.near(q, other, True)
            received(self.x.at[self.me], self.out.at[slot], self.sems, (self.n, k), source)
        self.send.finish()
        self.keep.wait()


def closing_kernel(
    outer,
    inner,
    shards,
    both_ref,
    wi_ref,
    z_ref,
    x_ref,
    dmid_ref,
    gain_ref,
    gain2_ref,
    blocks_ref,
    sums_ref,
    n1_ref,
    dout_ref,
    down_ref,
    gate_ref,
    grad_ref,
    mix_ref,
    blocks_out,
    sums_out,
    gains_out,
    down_out,
    gate_out,
    p_s,
    n1_s,
    dout_s,
    g_s,
    gain_s,
    gain_rows,
    gain_slots,
    near_in,
    far_in,
    far_out,
    done,
    block_slots,
    sum_slots,
    x_in,
    up_in,
    down_in,
    line_out,
    across,
    up,
    low,
    near,
    far,
    final,
    s_far,
    s_near,
    swap,
    g_sem,
    local,
):
    at = Place(outer, inner, shards)
    s, h, parts, ys = at.s, at.h, at.parts, at.ys
    steps = list(range(1, ys))
    line = LineSum(at, p_s, (x_in, up_in, down_in, line_out), (across, up, low))
    model = x_ref.shape[1]
    tile = min(512, model)
    piece = done.shape[1]
    span = shards * piece
    width2 = both_ref.shape[1]
    me = s * shards + h
    small = ((blocks_ref, block_slots, blocks_out), (sums_ref, sum_slots, sums_out))
    load = [
        pltpu.make_async_copy(n1_ref, n1_s, local.at[0]),
        pltpu.make_async_copy(dout_ref, dout_s, local.at[1]),
    ]
    for copy in load:
        copy.start()

    def anyone(k):
        to = lax.rem(me + k, at.count)
        return (to // shards, lax.rem(to, shards)), to

    def greet_one(k, carry):
        hello(anyone(k)[0])
        return carry

    lax.fori_loop(1, at.count, greet_one, 0)
    welcome(at.count - 1)

    def back(n, carry):
        d = at.far_first(n)
        rows = pl.ds(pl.multiple_of(d * p_s.shape[1], p_s.shape[1]), p_s.shape[1])
        for lane in range(0, model, tile):
            lanes = slice(lane, lane + tile)
            p_s[d, :, lanes] = dot(both_ref[rows, :], wi_ref[lanes, :], ((1,), (1,))).astype(BF16)
        line.cross(d).start()
        return carry

    lax.fori_loop(0, outer, back, 0)
    send = Sent()
    for n, (src, slots, _) in enumerate(small):
        for dy in steps:
            send(src, slots.at[h], s_far, (n, dy), (s, at.along(dy)))
        send(src, slots.at[h], s_near, (n, 0), at.sibling)
        slots[h] = src[...]
    for copy in load:
        copy.wait()

    def owner(k):
        return lax.rem(s + k + 1, parts)

    def mix_rows(p, shard):
        return g_s.at[p, pl.ds(pl.multiple_of(shard * piece, piece), piece)]

    def to_sibling(k, dy):
        p = owner(k)
        return remote(
            mix_rows(p, at.along(dy, 1)),
            near_in.at[dy, p],
            near.at[0, dy, k],
            near.at[1, dy, k],
            at.sibling,
        )

    def to_shard(k, dy, source=False):
        p = owner(k)
        return remote(
            far_out.at[dy - 1, p],
            far_in.at[dy - 1, p],
            far.at[0, dy, k],
            far.at[1, dy, k],
            (s, at.along(-dy if source else dy)),
        )

    def to_owner(k, source=False):
        p = lax.rem(s + parts - k - 1, parts) if source else owner(k)
        return remote(
            done.at[owner(k)],
            mix_ref.at[p if source else s],
            final.at[0, k],
            final.at[1, k],
            (p, h),
        )

    def weight_grads(k, carry):
        p = owner(k)
        lanes = pl.ds(pl.multiple_of(p * span, span), span)
        g_s[p, :, 0:width2] = dot(n1_s[:, lanes], both_ref[...], ((0,), (0,))).astype(BF16)
        g_s[p, :, width2:] = dot(dout_s[:, lanes], z_ref[...], ((0,), (0,))).astype(BF16)
        for dy in steps + [0]:
            to_sibling(k, dy).start()
        return carry

    lax.fori_loop(0, parts, weight_grads, 0)
    exchanges = [
        PlaneExchange(at, 0, down_ref, down_out, swap, local.at[2]),
        PlaneExchange(at, 1, gate_ref, gate_out, swap, local.at[3]),
    ]

    def sibling_sums(k, carry):
        p = owner(k)
        for dy in steps:
            to_sibling(k, dy).wait_recv()
            mine = mix_rows(p, at.along(dy))

            def add(rows, dy=dy, mine=mine):
                total = mine[rows, :].astype(F32) + near_in[dy, p, rows, :].astype(F32)
                far_out[dy - 1, p, rows, :] = total.astype(BF16)

            add_rows(piece, add)
            to_shard(k, dy).start()
        return carry

    lax.fori_loop(0, parts, sibling_sums, 0)
    for exchange in exchanges:
        exchange.start()
    gain_s[...] = jnp.zeros(gain_s.shape, F32)

    def mix_step(k):
        p = owner(k)
        mine = mix_rows(p, h)
        to_sibling(k, 0).wait_recv()
        for dy in steps:
            to_shard(k, dy, True).wait_recv()

        def add(rows):
            total = mine[rows, :].astype(F32) + near_in[0, p, rows, :].astype(F32)
            for dy in steps:
                total = total + far_in[dy - 1, p, rows, :].astype(F32)
            done[p, rows, :] = total.astype(BF16)

        add_rows(piece, add)
        if k < parts - 1:
            to_owner(k).start()

    def last_add(rows, dn1):
        x = x_ref[rows, :].astype(F32)
        scale = row_rms(x)
        gain_s[...] += dn1 * x * scale
        grad_ref[rows, :] = dmid_ref[rows, :] + rms_back(x, scale, gain_ref[...], dn1)

    def branch(o0):
        def between(n):
            for k in range(n * inner, (n + 1) * inner):
                mix_step(k)

        line.steps(o0, last_add, between)

    at.branches(branch)
    keep = pltpu.make_async_copy(done.at[s], mix_ref.at[s], local.at[4])
    keep.start()
    gain1, gain2 = jnp.sum(gain_s[...], axis=0, keepdims=True), gain2_ref[...]
    spare = gain_rows.shape[2] - 2 * piece
    for k in range(at.count):
        lanes = slice(k * piece, (k + 1) * piece)
        parts_of = [gain1[:, lanes], gain2[:, lanes]]
        if spare:
            parts_of.append(jnp.zeros((1, spare), F32))
        gain_rows[k] = jnp.concatenate(parts_of, axis=1)

    def gain(k):
        to, row = anyone(k)
        return remote(gain_rows.at[row], gain_slots.at[k], g_sem.at[0, k], g_sem.at[1, k], to)

    def gain_start(k, carry):
        gain(k).start()
        return carry

    def gain_arrive(k, total):
        gain(k).wait_recv()
        return total + gain_slots[k]

    def gain_leave(k, carry):
        gain(k).wait_send()
        return carry

    lax.fori_loop(1, at.count, gain_start, 0)
    for n, (src, slots, out) in enumerate(small):
        for dy in steps:
            here = slots.at[at.along(-dy)]
            received(src, here, s_far, (n, dy), (s, at.along(-dy)))
            send(here, here, s_near, (n, dy), at.sibling)
    for n, (src, slots, out) in enumerate(small):
        for dy in range(ys):
            received(src, slots.at[at.along(-dy, 1)], s_near, (n, dy), at.sibling)

        def add(k, carry, slots=slots, out=out):
            rows = pl.ds(pl.multiple_of(k * 8, 8), 8)
            total = slots[0, rows, :]
            for j in range(1, shards):
                total = total + slots[j, rows, :]
            out[rows, :] = total
            return carry

        lax.fori_loop(0, src.shape[0] // 8, add, 0)
    gains_out[...] = lax.fori_loop(1, at.count, gain_arrive, gain_rows[me])
    for k in range(parts - 1):
        to_owner(k, True).wait_recv()
    for exchange in exchanges:
        exchange.finish()
    for k in range(parts):
        for dy in range(ys):
            to_sibling(k, dy).wait_send()
        for dy in steps:
            to_shard(k, dy).wait_send()
        if k < parts - 1:
            to_owner(k).wait_send()
    lax.fori_loop(1, at.count, gain_leave, 0)
    send.finish()
    keep.wait()


def closing(
    both, w_in, z, x, dmid, gain, gain2, small, sums, n1, dout, down, gate, outer, inner, shards, collective
):
    rows, cols = x.shape
    parts, ys, count = outer * inner, shards // 2, outer * inner * shards
    piece = cols // count
    width = z.shape[1]
    lanes = -(-2 * piece // LANES) * LANES
    bufs, sems = line_sum_scratch(outer, rows, cols)
    pieces = pltpu.VMEM((max(ys - 1, 1), parts, piece, 3 * width), BF16)
    whole = pltpu.VMEM((parts * rows, cols), BF16)
    same = jax.ShapeDtypeStruct(down.shape, down.dtype)
    return pl.pallas_call(
        functools.partial(closing_kernel, outer, inner, shards),
        out_shape=(
            jax.ShapeDtypeStruct((rows, cols), F32),
            jax.ShapeDtypeStruct((parts, piece, 3 * width), BF16),
            jax.ShapeDtypeStruct(small.shape, F32),
            jax.ShapeDtypeStruct(sums.shape, F32),
            jax.ShapeDtypeStruct((1, lanes), F32),
            same,
            same,
        ),
        in_specs=[IN_VMEM] * 9 + [ANY] * 4,
        out_specs=[IN_VMEM] * 5 + [ANY] * 2,
        scratch_shapes=[
            pltpu.VMEM((outer, inner * rows, cols), BF16),
            whole,
            whole,
            pltpu.VMEM((parts, shards * piece, 3 * width), BF16),
            pltpu.VMEM((16, cols), F32),
            pltpu.VMEM((count, 1, lanes), F32),
            pltpu.VMEM((count, 1, lanes), F32),
            pltpu.VMEM((ys, parts, piece, 3 * width), BF16),
            pieces,
            pieces,
            pltpu.VMEM((parts, piece, 3 * width), BF16),
            pltpu.VMEM((shards,) + small.shape, F32),
            pltpu.VMEM((shards,) + sums.shape, F32),
        ]
        + bufs
        + sems
        + [DMA((2, ys, parts))] * 2
        + [DMA((2, parts))]
        + [DMA((2, 2, ys))] * 2
        + [DMA((2, 2, inner * shards)), DMA((2, count)), DMA((5,))],
        compiler_params=pltpu.CompilerParams(
            collective_id=collective, has_side_effects=True, vmem_limit_bytes=60 * 2**20
        ),
        cost_estimate=cost(80),
        name="closing",
    )(
        both,
        w_in,
        z,
        x,
        dmid,
        gain,
        gain2,
        small,
        sums,
        n1,
        dout,
        down,
        gate,
    )


def finish_kernel(outer, inner, shards, x_ref, out_ref, sems, local):
    at = Place(outer, inner, shards)
    exchange = PlaneExchange(at, 0, x_ref, out_ref, sems, local)
    greet(exchange.others())
    exchange.start()
    exchange.finish()


def finish(x, outer, inner, shards, collective):
    return pl.pallas_call(
        functools.partial(finish_kernel, outer, inner, shards),
        out_shape=jax.ShapeDtypeStruct(x.shape, x.dtype),
        in_specs=[ANY],
        out_specs=ANY,
        scratch_shapes=[DMA((2, 1, inner * shards)), DMA],
        compiler_params=pltpu.CompilerParams(collective_id=collective, has_side_effects=True),
        cost_estimate=cost(12),
        name="finish",
    )(x)


def unpack_kernel(
    inner, channels, gate_ref, up_ref, down_ref, mix_ref, gate, up, down, branch, enter, leave
):
    slots, piece, hidden = gate_ref.shape
    shards = slots // inner
    parts, width = mix_ref.shape[0], mix_ref.shape[2] // 3
    for i in range(inner):
        for h in range(shards):
            lanes = slice((h * inner + i) * hidden, (h * inner + i + 1) * hidden)
            slot = i * shards + h
            for src, dst in ((gate_ref, gate), (up_ref, up), (down_ref, down)):
                dst[:, lanes] = src[slot].astype(F32)
    for k, dst in enumerate((branch, enter, leave)):
        lanes = slice(k * width, k * width + width)
        dst[...] = jnp.concatenate(
            [mix_ref[p][:, lanes].astype(F32)[:, :channels] for p in range(parts)], axis=1
        )


def unpack(ffn_gate, ffn_up, ffn_down, mix, inner, channels):
    slots, piece, hidden = ffn_gate.shape
    across = jax.ShapeDtypeStruct((piece, slots * hidden), F32)
    wide = jax.ShapeDtypeStruct((piece, mix.shape[0] * channels), F32)
    return pl.pallas_call(
        functools.partial(unpack_kernel, inner, channels),
        out_shape=(across,) * 3 + (wide,) * 3,
        in_specs=[IN_VMEM] * 4,
        out_specs=[IN_VMEM] * 6,
        compiler_params=pltpu.CompilerParams(vmem_limit_bytes=48 * 2**20),
        cost_estimate=cost(4),
        name="unpack",
    )(ffn_gate, ffn_up, ffn_down, mix)


def body(
    tokens,
    first_gain,
    branch_weight,
    input_weight,
    conv_weight,
    conv_bias,
    rate_weight,
    rate_bias,
    entry_weight,
    entry_bias,
    decay_param,
    output_weight,
    second_gain,
    hidden_gate,
    hidden_up,
    hidden_down,
    cotangent,
):
    quarters, _, chunk, model = tokens.shape
    rows = quarters * chunk
    parts = lax.axis_size("seq")
    shards = lax.axis_size("shard")
    inner = 2
    outer = parts // inner
    seq_at = lax.axis_index("seq")
    inner_at = lax.rem(seq_at, inner)
    lru = branch_weight.shape[1]
    channels = lru // parts
    width = (channels + LANES) // LANES * LANES
    spare = width - channels
    blocks, block_width = rate_weight.shape[0], rate_weight.shape[1]
    piece = model // (parts * shards)
    columns = [[o * inner + i for o in range(outer)] for i in range(inner)]

    def own(weight, axis):
        part = lax.dynamic_slice_in_dim(weight, seq_at * channels, channels, axis)
        pads = [(0, 0), (0, 0)]
        pads[axis] = (0, spare)
        return jnp.pad(part, pads)

    params = jnp.pad(
        jnp.concatenate(
            [
                conv_weight.astype(F32),
                conv_bias[None],
                rate_bias[None],
                entry_bias[None],
                decay_param[None],
            ],
            axis=0,
        ),
        ((0, 0), (0, spare)),
    )

    x = tokens.reshape(rows, model)
    cot = cotangent.reshape(rows, model)
    gain1, gain2 = first_gain[None], second_gain[None]
    xs = x.astype(F32)
    n1, w_in, w_out = opening(
        (xs * row_rms(xs) * gain1).astype(BF16),
        jnp.concatenate([own(branch_weight, 1), own(input_weight, 1)], axis=1),
        own(output_weight, 0),
        outer,
        inner,
        shards,
        0,
    )
    n1, cot = lax.optimization_barrier((n1, cot))
    beside = [(o * inner + i, o * inner + 1 - i) for o in range(outer) for i in range(inner)]
    cot_beside = lax.ppermute(cot, "seq", beside)
    w_in = w_in.reshape(model, 2 * width)
    z, h, v, proj, gates = scan_forward(
        quarters, chunk, n1, w_in, params, rate_weight, entry_weight
    )
    mid, n2, cot_all = middle(
        z, w_out, x, gain2, cot, cot_beside, outer, inner, shards, 1
    )
    n2 = n2.reshape(inner * shards * rows, model)
    cot_all = cot_all.reshape(inner * shards * rows, model)
    hidden = hidden_gate.shape[1] // inner
    wg = lax.dynamic_slice_in_dim(hidden_gate, inner_at * hidden, hidden, 1)
    wu = lax.dynamic_slice_in_dim(hidden_up, inner_at * hidden, hidden, 1)
    wd = lax.dynamic_slice_in_dim(hidden_down, inner_at * hidden, hidden, 0)

    def sum_tokens(x):
        return lax.psum_scatter(
            x.astype(BF16), "seq", scatter_dimension=0, tiled=True, axis_index_groups=columns
        ).reshape(inner * shards, piece, hidden)

    gm = dot(n2, wg)
    um = dot(n2, wu)
    act, slope = gelu_and_slope(gm)
    mm = (act * um).astype(BF16)
    down_sum = sum_tokens(dot(cot_all, mm, ((0,), (0,))))
    dmm = dot(cot_all, wd, ((1,), (1,)))
    dgm = (dmm * um * slope).astype(BF16)
    dum = (dmm * act).astype(BF16)
    gate_sum = sum_tokens(dot(n2, dgm, ((0,), (0,))))
    up_terms = dot(n2, dum, ((0,), (0,)))
    dmid, dout, result, gain2_grad = turn(
        dgm, dum, mm, hidden_gate, hidden_up, hidden_down, mid, cot, gain2, outer, inner, shards, 2
    )
    dout, up_terms = lax.optimization_barrier((dout, up_terms.astype(BF16)))
    up_sum = sum_tokens(up_terms)
    both, small, sums = scan_backward(
        quarters, chunk, blocks, block_width, dout, w_out, proj, h, v, params, gates
    )
    tokens_grad, mix, small, sums, gains, down_sum, gate_sum = closing(
        both,
        w_in,
        z,
        x,
        dmid,
        gain1,
        gain2_grad,
        small,
        sums,
        n1.reshape(parts * rows, model),
        dout.reshape(parts * rows, model),
        down_sum,
        gate_sum,
        outer,
        inner,
        shards,
        3,
    )
    gains = gains[0]
    up_sum = finish(up_sum, outer, inner, shards, 4)
    gate_sum, up_sum, down_sum, branch_sum, input_sum, output_sum = unpack(
        gate_sum, up_sum, down_sum, mix, inner, channels
    )
    sums = sums[:, :channels]
    small = small.reshape(2, blocks, -1, small.shape[1])[:, :, :block_width, :block_width]
    rate_grad, entry_grad = small[0], small[1]
    return (
        result.reshape(tokens.shape),
        tokens_grad.reshape(tokens.shape),
        gains[:piece],
        branch_sum,
        input_sum,
        sums[4:8],
        sums[3],
        rate_grad,
        sums[1],
        entry_grad,
        sums[2],
        sums[0],
        output_sum.T,
        gains[piece : 2 * piece],
        gate_sum,
        up_sum,
        down_sum.T,
    )


def solution(mesh):
    placed = (
        P(None, "shard", "seq", None),
        P(),
        P("shard", None),
        P("shard", None),
        P(None, "seq"),
        P("seq"),
        P("seq", None, None),
        P("seq"),
        P("seq", None, None),
        P("seq"),
        P("seq"),
        P(None, "shard"),
        P(),
        P(None, "shard"),
        P(None, "shard"),
        P("shard", None),
        P(None, "shard", "seq", None),
    )
    return jax.shard_map(
        body,
        mesh=mesh,
        in_specs=placed,
        out_specs=(
            P(None, "shard", "seq", None),
            P(None, "shard", "seq", None),
            P(("seq", "shard")),
            P(("seq", "shard"), None),
            P(("seq", "shard"), None),
            P(None, "seq"),
            P("seq"),
            P("seq", None, None),
            P("seq"),
            P("seq", None, None),
            P("seq"),
            P("seq"),
            P(None, ("seq", "shard")),
            P(("seq", "shard")),
            P(("seq", "shard"), None),
            P(("seq", "shard"), None),
            P(None, ("seq", "shard")),
        ),
        check_vma=False,
    )
```

```python
import functools

import jax
import jax.numpy as jnp
from jax import lax
from jax.experimental import pallas as pl
from jax.experimental.pallas import tpu as pltpu
from jax.sharding import PartitionSpec as P

EPSILON = 1e-06
DECAY_SCALE = 8.0
MULT_FLOOR = 0.01
LANES = 128
SEGMENTS = 8
GELU_C = 0.7978845608028654
GELU_A = 0.044715
F32 = jnp.float32
BF16 = jnp.bfloat16


MESH = pl.DeviceIdType.MESH
ANY = pl.BlockSpec(memory_space=pl.ANY)
IN_VMEM = pl.BlockSpec(memory_space=pltpu.VMEM)
DMA = pltpu.SemaphoreType.DMA


def cost(us):
    return pl.CostEstimate(flops=0, bytes_accessed=int(us * 3.3e6), transcendentals=0)


def dot(left, right, dims=((1,), (0,))):
    return lax.dot_general(left, right, (dims, ((), ())), preferred_element_type=F32)


def gelu_and_slope(x):
    inner = GELU_C * (x + GELU_A * x * x * x)
    t = jnp.tanh(inner)
    half = 0.5 * (1.0 + t)
    slope = half + 0.5 * x * (1.0 - t * t) * (GELU_C * (1.0 + 3.0 * GELU_A * x * x))
    return x * half, slope


def gelu_tanh(x):
    return x * (0.5 * (1.0 + jnp.tanh(GELU_C * (x + GELU_A * x * x * x))))


def sigmoid(x):
    return 0.5 * jnp.tanh(0.5 * x) + 0.5


def softplus(x):
    return jnp.maximum(x, 0.0) + jnp.log1p(jnp.exp(-jnp.abs(x)))


def lane_groups(width):
    return [slice(g * LANES, (g + 1) * LANES) for g in range(width // LANES)]


def put(ref, rows, value):
    for g, lanes in enumerate(lane_groups(value.shape[1])):
        ref[g, rows, :] = value[:, lanes]


def take(ref, rows):
    return jnp.concatenate([ref[g, rows, :] for g in range(ref.shape[0])], axis=1)


def strided_scan(steps, groups, load, store):
    def step(k, carry):
        i = steps(k)
        out = []
        for g in range(groups):
            state, total = carry[g]
            factor, term = load(g, i)
            state = factor * state + term
            total = factor * total
            store(g, i, state, total)
            out.append((state, total))
        return tuple(out)

    return step


TAP, CONV_B, RATE_B, ENTRY_B, DECAY = 0, 4, 5, 6, 7


def gate_values(pre, log_scale, width):
    r = sigmoid(pre[:, :width])
    e = sigmoid(pre[:, width:])
    a = jnp.exp(r * log_scale)
    room = 1.0 - a * a
    m = jnp.sqrt(jnp.maximum(room, MULT_FLOOR))
    return r, e, a, room, m


def scan_forward_kernel(
    parts,
    quarters,
    chunk,
    n1_ref,
    wi_ref,
    par_ref,
    rate_ref,
    entry_ref,
    z_ref,
    h_ref,
    v_ref,
    proj_ref,
    gates_ref,
    n1_s,
    wi_s,
    gates_s,
    u_pad,
    a_s,
    b_s,
    sems,
):
    length, width = h_ref.shape
    rows = quarters * chunk

    def load(p):
        return pltpu.make_async_copy(
            n1_ref.at[p], n1_s.at[pl.ds(pl.multiple_of(p * rows, rows), rows)], sems.at[p]
        )

    weights = pltpu.make_async_copy(wi_ref, wi_s, sems.at[parts])
    weights.start()
    for p in range(parts):
        load(p).start()
    gates_s[...] = jnp.zeros(gates_s.shape, F32)
    blocks, block_width = rate_ref.shape[0], rate_ref.shape[1]
    for gate, src in enumerate((rate_ref, entry_ref)):
        for j in range(blocks):
            at, lane = j * block_width, gate * width + j * block_width
            gates_s[at : at + block_width, lane : lane + block_width] = src[j].astype(F32)
    gates_ref[...] = gates_s[...].astype(BF16)
    weights.wait()

    def project(k, carry):
        load(2 * k).wait()
        load(2 * k + 1).wait()
        at = pl.ds(pl.multiple_of(k * 2 * rows, 2 * rows), 2 * rows)
        proj_ref[at, :] = dot(n1_s[at, :], wi_s[...])
        return carry

    lax.fori_loop(0, parts // 2, project, 0)
    seg = length // SEGMENTS
    chunks = length // chunk

    def place(c):
        q = c // parts
        s = c - q * parts
        return pl.multiple_of((s * quarters + q) * chunk, chunk)

    def time_of(c):
        return pl.multiple_of(c * chunk, chunk)

    log_scale = -DECAY_SCALE * softplus(-par_ref[DECAY : DECAY + 1, :])
    bias = jnp.concatenate(
        [par_ref[RATE_B : RATE_B + 1, :], par_ref[ENTRY_B : ENTRY_B + 1, :]], axis=1
    )
    u_pad[0:8, :] = jnp.zeros((8, width), F32)

    def first(c, carry):
        u = proj_ref[pl.ds(place(c), chunk), width : 2 * width].astype(BF16).astype(F32)
        u_pad[pl.ds(pl.multiple_of(time_of(c) + 8, 8), chunk), :] = u
        wide = u_pad[pl.ds(time_of(c), chunk + 8), :]
        v = par_ref[CONV_B : CONV_B + 1, :] + par_ref[0:1, :] * wide[8:]
        for k in range(1, 4):
            v = v + par_ref[k : k + 1, :] * wide[8 - k : 8 - k + chunk]
        v = v.astype(BF16)
        v_ref[pl.ds(time_of(c), chunk), :] = v
        pre = dot(v, gates_ref[...]) + bias
        r, e, a, room, m = gate_values(pre, log_scale, width)
        put(a_s, pl.ds(time_of(c), chunk), a)
        put(b_s, pl.ds(time_of(c), chunk), m * e * v.astype(F32))
        return carry

    lax.fori_loop(0, chunks, first, 0)

    def load(g, i):
        at = pl.ds(i, SEGMENTS, stride=seg)
        return a_s[g, at, :], b_s[g, at, :]

    def store(g, i, state, total):
        at = pl.ds(i, SEGMENTS, stride=seg)
        b_s[g, at, :] = state
        a_s[g, at, :] = total

    groups = width // LANES
    start = (jnp.zeros((SEGMENTS, LANES), F32), jnp.ones((SEGMENTS, LANES), F32))
    ends = lax.fori_loop(
        0, seg, strided_scan(lambda k: k, groups, load, store), (start,) * groups, unroll=8
    )
    final = jnp.concatenate([e[0] for e in ends], axis=1)
    totals = jnp.concatenate([e[1] for e in ends], axis=1)
    carries = [jnp.zeros((1, width), F32)]
    for j in range(SEGMENTS - 1):
        carries.append(totals[j : j + 1] * carries[j] + final[j : j + 1])
    for j in range(SEGMENTS):
        per = seg // chunk

        def last(k, carry, j=j, per=per):
            c = j * per + k
            rows = pl.ds(time_of(c), chunk)
            h = take(b_s, rows) + take(a_s, rows) * carries[j]
            h_ref[rows, :] = h
            y = gelu_tanh(proj_ref[pl.ds(place(c), chunk), 0:width])
            z_ref[pl.ds(place(c), chunk), :] = (h.astype(BF16).astype(F32) * y).astype(BF16)
            return carry

        lax.fori_loop(0, per, last, 0)


def scan_forward(quarters, chunk, n1, w_in, params, rate, entry):
    parts, rows, model = n1.shape
    length, width = parts * rows, w_in.shape[1] // 2
    return pl.pallas_call(
        functools.partial(scan_forward_kernel, parts, quarters, chunk),
        out_shape=(
            jax.ShapeDtypeStruct((length, width), BF16),
            jax.ShapeDtypeStruct((length, width), F32),
            jax.ShapeDtypeStruct((length, width), BF16),
            jax.ShapeDtypeStruct((length, 2 * width), F32),
            jax.ShapeDtypeStruct((width, 2 * width), BF16),
        ),
        in_specs=[ANY] * 2 + [IN_VMEM] * 3,
        out_specs=[IN_VMEM] * 5,
        scratch_shapes=[
            pltpu.VMEM((length, model), BF16),
            pltpu.VMEM(w_in.shape, BF16),
            pltpu.VMEM((width, 2 * width), F32),
            pltpu.VMEM((length + 8, width), F32),
            pltpu.VMEM((width // LANES, length, LANES), F32),
            pltpu.VMEM((width // LANES, length, LANES), F32),
            DMA((parts + 1,)),
        ],
        compiler_params=pltpu.CompilerParams(vmem_limit_bytes=48 * 2**20),
        cost_estimate=cost(18),
        name="scan_forward",
    )(n1, w_in, params, rate, entry)


class Place:
    def __init__(self, outer, inner, shards):
        self.outer, self.inner, self.shards = outer, inner, shards
        self.parts, self.ys, self.count = outer * inner, shards // 2, outer * inner * shards
        self.chips = inner * self.ys
        self.s, self.h = lax.axis_index("seq"), lax.axis_index("shard")
        self.o, self.i = self.s // inner, lax.rem(self.s, inner)
        self.y, self.core = self.h // 2, lax.rem(self.h, 2)
        self.beside = (self.o * inner + 1 - self.i, self.h)
        self.above, self.below = (self.s + inner, self.h), (self.s - inner, self.h)
        self.sibling = (self.s, self.along(0, 1))

    def along(self, dy, other=0):
        y = lax.rem(self.y + dy + self.ys, self.ys)
        return y * 2 + lax.rem(self.core + other, 2)

    def chip(self, q, back=False):
        di, dy = q // self.ys, q - q // self.ys * self.ys
        if back:
            di, dy = self.inner - di, self.ys - dy
        return lax.rem(self.i + di, self.inner), lax.rem(self.y + dy, self.ys)

    def near(self, q, other=0, back=False):
        i, y = self.chip(q, back)
        h = y * 2 + lax.rem(self.core + other, 2)
        return (self.o * self.inner + i, h), i * self.shards + h

    def far_first(self, n):
        sign = 2 * ((2 * self.o) // self.outer) - 1
        return lax.rem(self.o + sign * (n + 1) + 2 * self.outer, self.outer)

    def branches(self, fn):
        for o0 in range(self.outer):
            pl.when(self.o == o0)(functools.partial(fn, o0))


def hello(to):
    barrier = pltpu.get_barrier_semaphore()
    pl.semaphore_signal(barrier, inc=1, device_id=to, device_id_type=MESH)


def welcome(n):
    pl.semaphore_wait(pltpu.get_barrier_semaphore(), n)


def greet(others):
    for to in others:
        hello(to)
    welcome(len(others))


def greet_with_line(at, others):
    up, down = at.o < at.outer - 1, at.o > 0
    for to in others:
        hello(to)
    pl.when(up)(lambda: hello(at.above))
    pl.when(down)(lambda: hello(at.below))
    ends = lax.rem(at.o, at.outer - 1) == 0
    pl.when(ends)(lambda: welcome(len(others) + 1))
    pl.when(jnp.logical_not(ends))(lambda: welcome(len(others) + 2))


class Sent:
    def __init__(self):
        self.copies = []

    def __call__(self, src, dst, sems, at, to):
        copy = remote(src, dst, sems.at[(0,) + at], sems.at[(1,) + at], to)
        copy.start()
        self.copies.append(copy)

    def finish(self):
        for copy in self.copies:
            copy.wait_send()


def received(like, here, sems, at, source):
    remote(like, here, sems.at[(0,) + at], sems.at[(1,) + at], source).wait_recv()


def line_gather(at, o0, x_ref, out, across, up, down, between=lambda k: None):
    send = Sent()

    def slot(row):
        return out.at[row * at.inner + at.i]

    def pass_on(row, sems, to):
        send(x_ref if row == o0 else slot(row), slot(row), sems, (row,), to)

    for k in range(at.outer):
        lower, upper = o0 - k, o0 + k
        if k > 0 and lower >= 0:
            received(x_ref, slot(lower), up, (lower,), at.below)
        if lower >= 0 and o0 < at.outer - 1:
            pass_on(lower, up, at.above)
        if lower >= 0:
            pass_on(lower, across, at.beside)
        if k > 0 and upper < at.outer:
            received(x_ref, slot(upper), down, (upper,), at.above)
        if upper < at.outer and o0 > 0:
            pass_on(upper, down, at.below)
        if k > 0 and upper < at.outer:
            pass_on(upper, across, at.beside)
        between(k)
    for row in range(at.outer):
        received(x_ref, out.at[row * at.inner + 1 - at.i], across, (row,), at.beside)
    send.finish()


class LineSum:
    def __init__(self, at, p, bufs, sems):
        self.at, self.p = at, p
        self.x_in, self.up_in, self.down_in, self.sums = bufs
        self.across, self.up, self.down = sems
        self.rows = self.x_in.shape[1]

    def block(self, d, i):
        return self.p.at[d, pl.ds(pl.multiple_of(i * self.rows, self.rows), self.rows)]

    def cross(self, d):
        return remote(
            self.block(d, 1 - self.at.i),
            self.x_in.at[d],
            self.across.at[0, d],
            self.across.at[1, d],
            self.at.beside,
        )

    def steps(self, o0, last_add, between=lambda n: None):
        at = self.at
        send = Sent()
        order = sorted(range(at.outer), key=lambda d: (-abs(d - o0), d))
        for n, d in enumerate(order):
            mine = self.block(d, at.i)
            self.cross(d).wait_recv()
            terms = [mine, self.x_in.at[d]]
            if d >= o0 > 0:
                received(mine, self.up_in.at[d], self.up, (d,), at.below)
                terms.append(self.up_in.at[d])
            if d <= o0 < at.outer - 1:
                received(mine, self.down_in.at[d], self.down, (d,), at.above)
                terms.append(self.down_in.at[d])
            target = self.sums.at[d]

            def add(rows, terms=terms, target=target, d=d):
                total = terms[0][rows, :].astype(F32)
                for term in terms[1:]:
                    total = total + term[rows, :].astype(F32)
                if d == o0:
                    last_add(rows, total)
                else:
                    target[rows, :] = total.astype(target.dtype)

            add_rows(self.rows, add)
            if d > o0:
                send(target, self.up_in.at[d], self.up, (d,), at.above)
            if d < o0:
                send(target, self.down_in.at[d], self.down, (d,), at.below)
            between(n)
        for d in range(at.outer):
            self.cross(d).wait_send()
        send.finish()


class LineReduce:
    def __init__(self, at, own, land, up, down):
        self.at, self.own, self.land, self.up, self.down = at, own, land, up, down

    def order(self, o0):
        return sorted(range(self.at.outer), key=lambda d: (-abs(d - o0), d))

    def ascent(self, d):
        at = self.at
        return remote(
            self.own.at[d], self.land.at[d], self.up.at[0, d], self.up.at[1, d], at.above
        )

    def descent(self, o0, d):
        slot = d if d != o0 - 1 else self.at.outer
        return remote(
            self.own.at[d], self.land.at[slot], self.down.at[0, d], self.down.at[1, d], self.at.below
        )

    def early(self, n, d, limit):
        at = self.at
        inside = n < limit
        last = at.outer - 1
        pl.when(jnp.logical_and(at.o == 0, inside))(lambda: self.ascent(d).start())
        far = remote(
            self.own.at[d], self.land.at[d], self.down.at[0, d], self.down.at[1, d], at.below
        )
        pl.when(jnp.logical_and(at.o == last, inside))(lambda: far.start())

    def push(self, o0, d):
        if d > o0:
            self.ascent(d).start()
        if d < o0:
            self.descent(o0, d).start()

    def absorb(self, o0, d):
        terms = []
        if d >= o0 > 0:
            self.ascent(d).wait_recv()
            terms.append(self.land.at[d])
        if d <= o0 < self.at.outer - 1:
            slot = d if d < o0 else self.at.outer
            self.descent(o0 + 1, d).wait_recv()
            terms.append(self.land.at[slot])
        mine = self.own.at[d]

        def add(rows):
            total = mine[rows, :].astype(F32)
            for term in terms:
                total = total + term[rows, :].astype(F32)
            mine[rows, :] = total.astype(BF16)

        if terms:
            add_rows(mine.shape[0], add)

    def step(self, o0, n):
        d = self.order(o0)[n]
        self.absorb(o0, d)
        self.push(o0, d)

    def finish(self, o0):
        for d in range(self.at.outer):
            if d > o0:
                self.ascent(d).wait_send()
            if d < o0:
                self.descent(o0, d).wait_send()


def first_half(hidden):
    return -(-(hidden // 2) // LANES) * LANES


def line_reduce_scratch(outer, rows, cols):
    blocks = [pltpu.VMEM((outer, rows, cols), BF16), pltpu.VMEM((outer + 1, rows, cols), BF16)]
    return blocks, [DMA((2, outer))] * 2


def line_sum_scratch(outer, rows, cols):
    return [pltpu.VMEM((outer, rows, cols), BF16)] * 4, [DMA((2, outer))] * 3


def opening_kernel(
    outer, inner, shards, x_ref, wi_ref, wo_ref, n_out, wi_out, wo_out, local, across, up, down, far, near
):
    at = Place(outer, inner, shards)
    steps = list(range(1, at.ys))
    weights = ((wi_ref, wi_out), (wo_ref, wo_out))
    greet_with_line(at, [at.beside, at.sibling] + [(at.s, at.along(dy)) for dy in steps])
    keep = [
        pltpu.make_async_copy(x_ref, n_out.at[at.s], local.at[0]),
        pltpu.make_async_copy(wi_ref, wi_out.at[at.h], local.at[1]),
        pltpu.make_async_copy(wo_ref, wo_out.at[at.h], local.at[2]),
    ]
    for copy in keep:
        copy.start()
    send = Sent()
    for n, (src, dst) in enumerate(weights):
        for dy in steps:
            send(src, dst.at[at.h], far, (n, dy), (at.s, at.along(dy)))
        send(src, dst.at[at.h], near, (n, 0), at.sibling)

    def branch(o0):
        forward = Sent()

        def between(k):
            if k != 1:
                return
            for n, (src, dst) in enumerate(weights):
                for dy in steps:
                    source = at.along(-dy)
                    received(src, dst.at[source], far, (n, dy), (at.s, source))
                    forward(dst.at[source], dst.at[source], near, (n, dy), at.sibling)

        line_gather(at, o0, x_ref, n_out, across, up, down, between)
        forward.finish()

    at.branches(branch)
    for n, (src, dst) in enumerate(weights):
        for dy in range(at.ys):
            received(src, dst.at[at.along(-dy, 1)], near, (n, dy), at.sibling)
    send.finish()
    for copy in keep:
        copy.wait()


def opening(x, w_in, w_out, outer, inner, shards, collective):
    ys = shards // 2
    return pl.pallas_call(
        functools.partial(opening_kernel, outer, inner, shards),
        out_shape=(
            jax.ShapeDtypeStruct((outer * inner,) + x.shape, x.dtype),
            jax.ShapeDtypeStruct((shards,) + w_in.shape, w_in.dtype),
            jax.ShapeDtypeStruct((shards,) + w_out.shape, w_out.dtype),
        ),
        in_specs=[ANY] * 3,
        out_specs=[ANY] * 3,
        scratch_shapes=[DMA((3,))] + [DMA((2, outer))] * 3 + [DMA((2, 2, ys))] * 2,
        compiler_params=pltpu.CompilerParams(collective_id=collective, has_side_effects=True),
        cost_estimate=cost(55),
        name="opening",
    )(x, w_in, w_out)


def row_rms(values):
    return lax.rsqrt(jnp.mean(values * values, axis=-1, keepdims=True) + EPSILON)


def rms_back(values, scale, gain, grad):
    k = grad * gain
    mean = jnp.mean(k * values, axis=-1, keepdims=True)
    return scale * k - scale * scale * scale * values * mean


def middle_kernel(
    outer,
    inner,
    shards,
    z_ref,
    wo_ref,
    x_ref,
    gain_ref,
    cot_ref,
    cot_beside_ref,
    mid_ref,
    n2_out,
    cot_out,
    p_s,
    n2_s,
    x_in,
    up_in,
    down_in,
    line_out,
    across,
    up,
    down,
    far,
    near,
    c_far,
    c_near,
    local,
):
    at = Place(outer, inner, shards)
    line = LineSum(at, p_s, (x_in, up_in, down_in, line_out), (across, up, down))
    steps = list(range(1, at.ys))
    cols = wo_ref.shape[2]
    greet_with_line(at, [at.sibling] + [at.near(q)[0] for q in range(1, at.chips)])
    send = Sent()

    def project(n, carry):
        d = at.far_first(n)
        for k in range(shards):
            block = dot(z_ref[d], wo_ref[k]).astype(BF16)
            p_s[d, :, k * cols : (k + 1) * cols] = block
        line.cross(d).start()
        return carry

    lax.fori_loop(0, outer, project, 0)

    def slot(side, dy, other=0):
        i = 1 - at.i if side else at.i
        return cot_out.at[i * shards + at.along(dy, other)]

    mine = (cot_ref, cot_beside_ref)
    keep = []
    for side in range(2):
        keep.append(pltpu.make_async_copy(mine[side], slot(side, 0), local.at[side]))
        keep[-1].start()
        for dy in steps:
            send(mine[side], slot(side, 0), c_far, (side, dy), (at.s, at.along(dy)))
        send(mine[side], slot(side, 0), c_near, (side, 0), at.sibling)

    def last_add(rows, total):
        mid = x_ref[rows, :].astype(F32) + total
        mid_ref[rows, :] = mid
        n2_s[rows, :] = (mid * row_rms(mid) * gain_ref[...]).astype(BF16)

    def branch(o0):
        forward = Sent()

        def between(n):
            if n != outer - 2:
                return
            for side in range(2):
                for dy in steps:
                    here = slot(side, -dy)
                    received(cot_ref, here, c_far, (side, dy), (at.s, at.along(-dy)))
                    forward(here, here, c_near, (side, dy), at.sibling)

        line.steps(o0, last_add, between)
        forward.finish()

    at.branches(branch)
    _, me = at.near(0)
    keep.append(pltpu.make_async_copy(n2_s, n2_out.at[me], local.at[2]))
    keep[-1].start()
    for q in reversed(range(1, at.chips)):
        send(n2_s, n2_out.at[me], far, (q,), at.near(q)[0])
    send(n2_s, n2_out.at[me], near, (0,), at.sibling)
    for q in range(1, at.chips):
        source, there = at.near(q, back=True)
        here = n2_out.at[there]
        received(n2_s, here, far, (q,), source)
        send(here, here, near, (q,), at.sibling)
    for q in range(at.chips):
        received(n2_s, n2_out.at[at.near(q, 1, True)[1]], near, (q,), at.sibling)
    for side in range(2):
        for dy in range(at.ys):
            received(cot_ref, slot(side, -dy, 1), c_near, (side, dy), at.sibling)
    send.finish()
    for copy in keep:
        copy.wait()


def middle(z, w_out, x, gain, cot, cot_beside, outer, inner, shards, collective):
    rows, cols = x.shape
    ys, chips = shards // 2, inner * shards // 2
    bufs, sems = line_sum_scratch(outer, rows, cols)
    plane = jax.ShapeDtypeStruct((inner * shards, rows, cols), BF16)
    return pl.pallas_call(
        functools.partial(middle_kernel, outer, inner, shards),
        out_shape=(jax.ShapeDtypeStruct((rows, cols), F32), plane, plane),
        in_specs=[IN_VMEM] * 4 + [ANY] * 2,
        out_specs=[IN_VMEM, ANY, ANY],
        scratch_shapes=[
            pltpu.VMEM((outer, inner * rows, cols), BF16),
            pltpu.VMEM((rows, cols), BF16),
        ]
        + bufs
        + sems
        + [DMA((2, chips))] * 2
        + [DMA((2, 2, ys))] * 2
        + [DMA((3,))],
        compiler_params=pltpu.CompilerParams(
            collective_id=collective, has_side_effects=True, vmem_limit_bytes=48 * 2**20
        ),
        cost_estimate=cost(80),
        name="middle",
    )(z.reshape(outer, inner * rows, z.shape[1]), w_out, x, gain, cot, cot_beside)


class PlaneSum:
    def __init__(self, at, n, p, near_in, far_in, far_out, near, far):
        self.at, self.n, self.p = at, n, p
        self.near_in, self.far_in, self.far_out = near_in, far_in, far_out
        self.near, self.far = near, far
        self.rows = near_in.shape[2]

    def block(self, q, other):
        i, y = self.at.chip(q)
        core = lax.rem(self.at.core + other, 2)
        rows = pl.ds(pl.multiple_of(core * self.rows, self.rows), self.rows)
        return self.p.at[i * self.at.ys + y, rows]

    def to_sibling(self, q):
        n = self.n
        return remote(
            self.block(q, 1),
            self.near_in.at[n, q],
            self.near.at[0, n, q],
            self.near.at[1, n, q],
            self.at.sibling,
        )

    def onward(self, q, back=False):
        n = self.n
        return remote(
            self.far_out.at[n, q],
            self.far_in.at[n, q],
            self.far.at[0, n, q],
            self.far.at[1, n, q],
            self.at.near(q, 0, back)[0],
        )

    def combine(self, own=None):
        def one(k, carry):
            q = self.at.chips - 1 - k
            self.to_sibling(q).wait_recv()
            mine = self.block(q, 0) if own is None else own.at[q]

            def add(rows):
                total = mine[rows, :].astype(F32) + self.near_in[self.n, q, rows, :].astype(F32)
                self.far_out[self.n, q, rows, :] = total.astype(BF16)

            add_rows(self.rows, add)
            self.onward(q).start()
            return carry

        lax.fori_loop(0, self.at.chips - 1, one, 0)
        self.to_sibling(0).wait_recv()

    def total(self, rows, own=None):
        n = self.n
        mine = self.block(0, 0) if own is None else own.at[0]
        value = mine[rows, :].astype(F32) + self.near_in[n, 0, rows, :].astype(F32)
        for q in range(1, self.at.chips):
            value = value + self.far_in[n, q, rows, :].astype(F32)
        return value

    def arrive(self):
        for q in range(1, self.at.chips):
            self.onward(q, True).wait_recv()

    def finish(self):
        for q in range(self.at.chips):
            self.to_sibling(q).wait_send()
        for q in range(1, self.at.chips):
            self.onward(q).wait_send()


def turn_kernel(
    outer,
    inner,
    shards,
    dgm_ref,
    dum_ref,
    mm_ref,
    mid_ref,
    cot_ref,
    gain_ref,
    wg_ref,
    wu_ref,
    wd_ref,
    n2_ref,
    cots_ref,
    dmid_ref,
    gain_grad_ref,
    dout_ref,
    q_ref,
    down_ref,
    gate_ref,
    rest_ref,
    up_ref,
    p_s,
    q_s,
    dout_s,
    gain_s,
    wg_s,
    wu_s,
    wd_s,
    n2_s,
    cots_s,
    u_s,
    r_s,
    near_in,
    far_in,
    far_out,
    down_own,
    down_land,
    gate_own,
    gate_land,
    near,
    far,
    across,
    up,
    low,
    down_up,
    down_low,
    gate_up,
    gate_low,
    local,
    q_sem,
    u_sem,
    r_sem,
):
    at = Place(outer, inner, shards)
    model, hidden = wg_s.shape
    tile = min(512, model)
    pair = p_s.shape[1]
    span = model // outer
    own = pl.ds(pl.multiple_of(at.i * hidden, hidden), hidden)
    load = [
        pltpu.make_async_copy(cots_ref, cots_s, local.at[1]),
        pltpu.make_async_copy(wg_ref.at[:, own], wg_s, local.at[2]),
        pltpu.make_async_copy(wu_ref.at[:, own], wu_s, local.at[3]),
        pltpu.make_async_copy(n2_ref, n2_s, local.at[4]),
        pltpu.make_async_copy(wd_ref.at[own, :], wd_s, local.at[5]),
    ]
    for copy in load:
        copy.start()
    greet_with_line(at, [at.sibling] + [at.near(q)[0] for q in range(1, at.chips)])
    grad = PlaneSum(at, 0, p_s, near_in, far_in, far_out, near, far)
    down = LineReduce(at, down_own, down_land, down_up, down_low)
    gate = LineReduce(at, gate_own, gate_land, gate_up, gate_low)

    def columns(d):
        return pl.ds(pl.multiple_of(d * span, span), span)

    load[0].wait()

    def down_grad(n, carry):
        d = at.far_first(n)
        down_own[d] = dot(cots_s[:, columns(d)], mm_ref[...], ((0,), (0,))).astype(BF16)
        down.early(n, d, outer - 2)
        return carry

    lax.fori_loop(0, outer, down_grad, 0)
    load[1].wait()
    load[2].wait()

    def back(k, carry):
        q = at.chips - 1 - k
        i, y = at.chip(q)
        c = i * at.ys + y
        rows = pl.ds(pl.multiple_of(c * pair, pair), pair)
        for lane in range(0, model, tile):
            lanes = slice(lane, lane + tile)
            block = dot(dgm_ref[rows, :], wg_s[lanes, :], ((1,), (1,)))
            block = block + dot(dum_ref[rows, :], wu_s[lanes, :], ((1,), (1,)))
            p_s[c, :, lanes] = block.astype(BF16)
        grad.to_sibling(q).start()
        return carry

    lax.fori_loop(0, at.chips, back, 0)
    grad.combine()
    load[3].wait()

    cut = gate_own.shape[2]

    def keep_r(n):
        slot = lax.rem(n, 2)
        return pltpu.make_async_copy(r_s.at[slot], rest_ref.at[at.far_first(n)], r_sem.at[slot])

    def gate_grad(n, carry):
        d = at.far_first(n)
        pl.when(n >= 2)(lambda: keep_r(n - 2).wait())
        block = dot(n2_s[:, columns(d)], dgm_ref[...], ((0,), (0,))).astype(BF16)
        gate_own[d] = block[:, :cut]
        r_s[lax.rem(n, 2)] = block[:, cut:]
        keep_r(n).start()
        return carry

    lax.fori_loop(0, outer, gate_grad, 0)
    for n in range(max(outer - 2, 0), outer):
        keep_r(n).wait()

    def first_down(o0):
        if 0 < o0 < outer - 1:
            down.step(o0, 0)

    at.branches(first_down)
    load[4].wait()

    def keep_q(c):
        slot = lax.rem(c, 2)
        return pltpu.make_async_copy(q_s.at[slot], q_ref.at[c], q_sem.at[slot])

    def ahead(c, carry):
        rows = pl.ds(pl.multiple_of(c * pair, pair), pair)
        pl.when(c >= 2)(lambda: keep_q(c - 2).wait())
        for lane in range(0, model, tile):
            lanes = slice(lane, lane + tile)
            q_s[lax.rem(c, 2), :, lanes] = dot(mm_ref[rows, :], wd_s[:, lanes]).astype(BF16)
        keep_q(c).start()
        return carry

    lax.fori_loop(0, at.chips, ahead, 0)
    for c in range(max(at.chips - 2, 0), at.chips):
        keep_q(c).wait()
    gain_s[...] = jnp.zeros(gain_s.shape, F32)
    grad.arrive()

    def norm_back(rows):
        dn2 = grad.total(rows)
        mid = mid_ref[rows, :]
        scale = row_rms(mid)
        gain_s[...] += dn2 * mid * scale
        dmid = cot_ref[rows, :].astype(F32) + rms_back(mid, scale, gain_ref[...], dn2)
        dmid_ref[rows, :] = dmid
        dout_s[rows, :] = dmid.astype(BF16)

    add_rows(dout_s.shape[0], norm_back)
    gain_grad_ref[...] = jnp.sum(gain_s[...], axis=0, keepdims=True)
    keep = pltpu.make_async_copy(dout_s, dout_ref.at[at.s], local.at[0])
    keep.start()

    def keep_u(n):
        slot = lax.rem(n, 2)
        return pltpu.make_async_copy(u_s.at[slot], up_ref.at[at.far_first(n)], u_sem.at[slot])

    def up_grad(n, carry):
        pl.when(n >= 2)(lambda: keep_u(n - 2).wait())
        u_s[lax.rem(n, 2)] = dot(
            n2_s[:, columns(at.far_first(n))], dum_ref[...], ((0,), (0,))
        ).astype(BF16)
        keep_u(n).start()
        return carry

    def branch(o0):
        ends = o0 in (0, outer - 1)

        def between(k):
            if k == 0:
                if ends:
                    down.push(o0, down.order(o0)[outer - 2])
                    for d in gate.order(o0)[:-1]:
                        gate.push(o0, d)
                else:
                    for n in range(1, outer - 1):
                        down.step(o0, n)
                lax.fori_loop(0, outer, up_grad, 0)
            if k == outer - 1:
                down.absorb(o0, o0)

        line_gather(at, o0, dout_s, dout_ref, across, up, low, between)
        if not ends:
            for n in range(outer - 1):
                gate.step(o0, n)
        gate.absorb(o0, o0)
        down.finish(o0)
        gate.finish(o0)

    at.branches(branch)
    last = [
        pltpu.make_async_copy(down_own.at[at.o], down_ref, local.at[1]),
        pltpu.make_async_copy(gate_own.at[at.o], gate_ref, local.at[2]),
    ]
    for copy in last:
        copy.start()
    for n in range(max(outer - 2, 0), outer):
        keep_u(n).wait()
    grad.finish()
    keep.wait()
    for copy in last:
        copy.wait()


def turn(
    dgm, dum, mm, mid, cot, gain, wg, wu, wd, n2, cots, outer, inner, shards, collective
):
    rows, cols = mid.shape
    tokens, hidden = dgm.shape
    chips, span = inner * shards // 2, cols // outer
    buffers = pltpu.VMEM((1, chips, rows, cols), BF16)
    cut = first_half(hidden)
    down_vmem, reduce_sems = line_reduce_scratch(outer, span, hidden)
    gate_vmem, _ = line_reduce_scratch(outer, span, cut)
    return pl.pallas_call(
        functools.partial(turn_kernel, outer, inner, shards),
        out_shape=(
            jax.ShapeDtypeStruct((rows, cols), F32),
            jax.ShapeDtypeStruct((1, cols), F32),
            jax.ShapeDtypeStruct((outer * inner, rows, cols), BF16),
            jax.ShapeDtypeStruct((chips, 2 * rows, cols), BF16),
            jax.ShapeDtypeStruct((span, hidden), BF16),
            jax.ShapeDtypeStruct((span, cut), BF16),
            jax.ShapeDtypeStruct((outer, span, hidden - cut), BF16),
            jax.ShapeDtypeStruct((outer, span, hidden), BF16),
        ),
        in_specs=[IN_VMEM] * 6 + [ANY] * 5,
        out_specs=[IN_VMEM] * 2 + [ANY] * 6,
        scratch_shapes=[
            pltpu.VMEM((chips, 2 * rows, cols), BF16),
            pltpu.VMEM((2, 2 * rows, cols), BF16),
            pltpu.VMEM((rows, cols), BF16),
            pltpu.VMEM((16, cols), F32),
            pltpu.VMEM((cols, hidden), BF16),
            pltpu.VMEM((cols, hidden), BF16),
            pltpu.VMEM((hidden, cols), BF16),
            pltpu.VMEM((tokens, cols), BF16),
            pltpu.VMEM((tokens, cols), BF16),
            pltpu.VMEM((2, span, hidden), BF16),
            pltpu.VMEM((2, span, hidden - cut), BF16),
        ]
        + [buffers] * 3
        + down_vmem
        + gate_vmem
        + [DMA((2, 1, chips))] * 2
        + [DMA((2, outer))] * 3
        + reduce_sems * 2
        + [DMA((6,)), DMA((2,)), DMA((2,)), DMA((2,))],
        compiler_params=pltpu.CompilerParams(
            collective_id=collective, has_side_effects=True, vmem_limit_bytes=60 * 2**20
        ),
        cost_estimate=cost(110),
        name="turn",
    )(dgm, dum, mm, mid, cot, gain, wg, wu, wd, n2, cots)


def scan_backward_kernel(
    outer,
    inner,
    shards,
    quarters,
    chunk,
    blocks,
    block_width,
    dout_ref,
    wo_ref,
    proj_ref,
    h_ref,
    v_ref,
    par_ref,
    gates_ref,
    mid_ref,
    q_ref,
    rest_ref,
    both_ref,
    blocks_ref,
    totals_ref,
    result_ref,
    rest_out,
    q_s,
    near_in,
    far_in,
    far_out,
    rest_own,
    rest_land,
    near,
    far,
    q_sem,
    r_up,
    r_low,
    r_sem,
    dout_s,
    dz_s,
    sems,
    sums_ref,
    gate_grad_ref,
    a_s,
    g_s,
    t_s,
    h_pad,
    pre_s,
    dpre_s,
    dv_s,
    u_pad,
):
    length, width = h_ref.shape
    seg = length // SEGMENTS
    chunks = length // chunk

    def place(c):
        q = c // parts
        s = c - q * parts
        return pl.multiple_of((s * quarters + q) * chunk, chunk)

    def time_of(c):
        return pl.multiple_of(c * chunk, chunk)

    at = Place(outer, inner, shards)
    parts = at.parts
    rest = LineReduce(at, rest_own, rest_land, r_up, r_low)
    fetch = pltpu.make_async_copy(rest_ref, rest_own, r_sem)
    fetch.start()
    greet_with_line(at, [at.sibling] + [at.near(q)[0] for q in range(1, at.chips)])
    fetch.wait()

    def rest_early(o0):
        if o0 in (0, outer - 1):
            for d in rest.order(o0)[:-1]:
                rest.push(o0, d)

    def rest_step(n, o0):
        if 0 < o0 < outer - 1:
            rest.step(o0, n)

    def rest_last(o0):
        rest.absorb(o0, o0)
        rest.finish(o0)

    at.branches(rest_early)
    value = PlaneSum(at, 0, q_ref, near_in, far_in, far_out, near, far)

    def keep(q):
        return pltpu.make_async_copy(value.block(q, 0), q_s.at[q], q_sem.at[q])

    for q in reversed(range(at.chips)):
        value.to_sibling(q).start()
        keep(q).start()
    span = quarters * chunk

    def load(p):
        return pltpu.make_async_copy(
            dout_ref.at[p], dout_s.at[pl.ds(pl.multiple_of(p * span, span), span)], sems.at[p]
        )

    for p in range(parts):
        load(p).start()

    def back_project(k, carry):
        load(2 * k).wait()
        load(2 * k + 1).wait()
        some = pl.ds(pl.multiple_of(k * 2 * span, 2 * span), 2 * span)
        depth = wo_ref.shape[2]
        total = dot(dout_s[some, 0:depth], wo_ref[0], ((1,), (1,)))
        for p in range(1, wo_ref.shape[0]):
            lanes = slice(p * depth, (p + 1) * depth)
            total = total + dot(dout_s[some, lanes], wo_ref[p], ((1,), (1,)))
        dz_s[some, :] = total
        return carry

    lax.fori_loop(0, parts // 2, back_project, 0)
    for q in range(at.chips):
        keep(q).wait()
    value.combine(q_s)
    at.branches(functools.partial(rest_step, 0))
    log_scale = -DECAY_SCALE * softplus(-par_ref[DECAY : DECAY + 1, :])
    bias = jnp.concatenate(
        [par_ref[RATE_B : RATE_B + 1, :], par_ref[ENTRY_B : ENTRY_B + 1, :]], axis=1
    )
    zeros8 = jnp.zeros((8, width), F32)
    put(a_s, pl.ds(length, 8), zeros8)
    h_pad[0:8, :] = zeros8
    u_pad[0:8, :] = zeros8
    dv_s[pl.ds(length, 8), :] = zeros8

    def first(c, carry):
        rows = pl.ds(time_of(c), chunk)
        later = pl.ds(pl.multiple_of(time_of(c) + 8, 8), chunk)
        there = pl.ds(place(c), chunk)
        h = h_ref[rows, :]
        h_pad[later, :] = h
        u_pad[later, :] = proj_ref[there, width : 2 * width].astype(BF16).astype(F32)
        y, slope = gelu_and_slope(proj_ref[there, 0:width])
        dz = dz_s[there, :]
        put(g_s, rows, (dz * y).astype(BF16).astype(F32))
        both_ref[there, 0:width] = (dz * h.astype(BF16).astype(F32) * slope).astype(BF16)
        pre = dot(v_ref[rows, :], gates_ref[...]) + bias
        pre_s[rows, :] = pre
        put(a_s, rows, jnp.exp(sigmoid(pre[:, :width]) * log_scale))
        return carry

    lax.fori_loop(0, chunks, first, 0)

    def load(g, i):
        return (
            a_s[g, pl.ds(i + 1, SEGMENTS, stride=seg), :],
            g_s[g, pl.ds(i, SEGMENTS, stride=seg), :],
        )

    def store(g, i, state, total):
        g_s[g, pl.ds(i, SEGMENTS, stride=seg), :] = state
        t_s[g, pl.ds(i, SEGMENTS, stride=seg), :] = total

    groups = width // LANES
    start = (jnp.zeros((SEGMENTS, LANES), F32), jnp.ones((SEGMENTS, LANES), F32))
    ends = lax.fori_loop(
        0,
        seg,
        strided_scan(lambda k: seg - 1 - k, groups, load, store),
        (start,) * groups,
        unroll=8,
    )
    firsts = jnp.concatenate([e[0] for e in ends], axis=1)
    totals = jnp.concatenate([e[1] for e in ends], axis=1)
    carries = [None] * SEGMENTS
    carries[SEGMENTS - 1] = jnp.zeros((1, width), F32)
    for j in range(SEGMENTS - 2, -1, -1):
        carries[j] = totals[j + 1 : j + 2] * carries[j + 1] + firsts[j + 1 : j + 2]

    def fold(values):
        return jnp.sum(values.reshape(chunk // 8, 8, values.shape[1]), axis=0)

    sums_ref[...] = jnp.zeros(sums_ref.shape, F32)

    for j in range(SEGMENTS):
        per = seg // chunk

        def middle(k, carry, j=j, per=per):
            c = j * per + k
            rows = pl.ds(time_of(c), chunk)
            g = take(g_s, rows) + take(t_s, rows) * carries[j]
            before = h_pad[pl.ds(time_of(c), chunk + 8), :][7 : 7 + chunk]
            v = v_ref[rows, :].astype(F32)
            r, e, a, room, m = gate_values(pre_s[rows, :], log_scale, width)
            gv = g * v
            held = jnp.where(room > MULT_FLOOR, gv * e * a / m, 0.0)
            ta = (g * before - held) * a * r
            drpre = (ta * (log_scale * (1.0 - r))).astype(BF16)
            depre = (gv * m * e * (1.0 - e)).astype(BF16)
            dpre_s[rows, 0:width] = drpre
            dpre_s[rows, width : 2 * width] = depre
            sums_ref[0:8, :] += fold(ta)
            sums_ref[8:16, :] += fold(drpre.astype(F32))
            sums_ref[16:24, :] += fold(depre.astype(F32))
            dv = g * m * e + dot(dpre_s[rows, :], gates_ref[...], ((1,), (1,)))
            dv_s[rows, :] = dv
            sums_ref[24:32, :] += fold(dv)
            wide = u_pad[pl.ds(time_of(c), chunk + 8), :]
            for tap in range(4):
                top = 32 + 8 * tap
                sums_ref[top : top + 8, :] += fold(dv * wide[8 - tap : 8 - tap + chunk])
            return carry

        lax.fori_loop(0, per, middle, 0)
        if j == 3:
            for n in range(1, outer - 1):
                at.branches(functools.partial(rest_step, n))
    at.branches(rest_last)
    out = pltpu.make_async_copy(rest_own.at[at.o], rest_out, r_sem)
    out.start()
    sums_ref[0:8, :] = sums_ref[0:8, :] * (
        DECAY_SCALE * sigmoid(-par_ref[DECAY : DECAY + 1, :])
    )

    def last(c, carry):
        wide = dv_s[pl.ds(time_of(c), chunk + 8), :]
        du = par_ref[0:1, :] * wide[0:chunk]
        for tap in range(1, 4):
            du = du + par_ref[tap : tap + 1, :] * wide[tap : tap + chunk]
        both_ref[pl.ds(place(c), chunk), width : 2 * width] = du.astype(BF16)
        return carry

    lax.fori_loop(0, chunks, last, 0)
    gate_grad_ref[...] = dot(v_ref[...], dpre_s[...], ((0,), (0,)))
    blocks_ref[...] = jnp.zeros(blocks_ref.shape, F32)
    tall = blocks_ref.shape[0] // (2 * blocks)
    for gate in range(2):
        for j in range(blocks):
            top, lanes = (gate * blocks + j) * tall, gate * width + j * block_width
            rows = slice(j * block_width, (j + 1) * block_width)
            blocks_ref[top : top + block_width, :block_width] = gate_grad_ref[
                rows, lanes : lanes + block_width
            ]
    for k in range(8):
        totals_ref[k : k + 1, :] = jnp.sum(sums_ref[8 * k : 8 * k + 8, :], axis=0, keepdims=True)
    value.arrive()

    def output(rows):
        result_ref[rows, :] = (mid_ref[rows, :] + value.total(rows, q_s)).astype(BF16)

    add_rows(span, output)
    value.finish()
    out.wait()


def scan_backward(
    quarters,
    chunk,
    blocks,
    block_width,
    dout,
    w_out,
    proj,
    h,
    v,
    params,
    gates,
    mid,
    q,
    rest,
    outer,
    inner,
    shards,
    collective,
):
    parts = dout.shape[0]
    rows, cols = mid.shape
    chips = q.shape[0]
    rest_vmem, rest_sems = line_reduce_scratch(*rest.shape)
    buffers = pltpu.VMEM((1, chips, rows, cols), BF16)
    length, width = h.shape
    tall, wide = -(-block_width // 8) * 8, -(-block_width // LANES) * LANES
    return pl.pallas_call(
        functools.partial(
            scan_backward_kernel, outer, inner, shards, quarters, chunk, blocks, block_width
        ),
        out_shape=(
            jax.ShapeDtypeStruct((length, 2 * width), BF16),
            jax.ShapeDtypeStruct((2 * blocks * tall, wide), F32),
            jax.ShapeDtypeStruct((8, width), F32),
            jax.ShapeDtypeStruct((rows, cols), BF16),
            jax.ShapeDtypeStruct(rest.shape[1:], BF16),
        ),
        in_specs=[ANY] + [IN_VMEM] * 7 + [ANY] * 2,
        out_specs=[IN_VMEM] * 4 + [ANY],
        scratch_shapes=[
            pltpu.VMEM((chips, rows, cols), BF16),
            buffers,
            buffers,
            buffers,
            *rest_vmem,
            DMA((2, 1, chips)),
            DMA((2, 1, chips)),
            DMA((chips,)),
            *rest_sems,
            DMA,
            pltpu.VMEM((length, dout.shape[2]), BF16),
            pltpu.VMEM((length, width), F32),
            DMA((parts,)),
            pltpu.VMEM((64, width), F32),
            pltpu.VMEM((width, 2 * width), F32),
            pltpu.VMEM((width // LANES, length + 8, LANES), F32),
            pltpu.VMEM((width // LANES, length, LANES), F32),
            pltpu.VMEM((width // LANES, length, LANES), F32),
            pltpu.VMEM((length + 8, width), F32),
            pltpu.VMEM((length, 2 * width), F32),
            pltpu.VMEM((length, 2 * width), BF16),
            pltpu.VMEM((length + 8, width), F32),
            pltpu.VMEM((length + 8, width), F32),
        ],
        compiler_params=pltpu.CompilerParams(
            collective_id=collective, has_side_effects=True, vmem_limit_bytes=60 * 2**20
        ),
        cost_estimate=cost(21),
        name="scan_backward",
    )(dout, w_out, proj, h, v, params, gates, mid, q, rest)


def remote(src, dst, send, recv, to):
    return pltpu.make_async_remote_copy(
        src_ref=src, dst_ref=dst, send_sem=send, recv_sem=recv, device_id=to, device_id_type=MESH
    )


def add_rows(rows, fn):
    def one(k, carry):
        fn(pl.ds(pl.multiple_of(k * 16, 16), 16))
        return carry

    lax.fori_loop(0, rows // 16, one, 0)


class PlaneExchange:
    def __init__(self, at, n, x, out, sems, local):
        self.at, self.n, self.x, self.out, self.sems, self.local = at, n, x, out, sems, local
        _, self.me = at.near(0)
        self.hops = [(q, c) for q in reversed(range(1, at.chips)) for c in range(2)] + [(0, 1)]

    def rows(self, slot):
        piece = self.out.shape[1]
        return self.x.at[pl.ds(pl.multiple_of(slot * piece, piece), piece)]

    def mine(self):
        return pltpu.make_async_copy(self.rows(self.me), self.out.at[self.me], self.local)

    def start(self):
        self.send = Sent()
        for k, (q, other) in enumerate(self.hops):
            to, slot = self.at.near(q, other)
            self.send(self.rows(slot), self.out.at[self.me], self.sems, (self.n, k), to)
        self.mine().start()

    def finish(self):
        for k, (q, other) in enumerate(self.hops):
            source, slot = self.at.near(q, other, True)
            received(self.rows(self.me), self.out.at[slot], self.sems, (self.n, k), source)
        self.send.finish()
        self.mine().wait()


def closing_kernel(
    outer,
    inner,
    shards,
    both_ref,
    wi_ref,
    z_ref,
    x_ref,
    dmid_ref,
    gain_ref,
    gain2_ref,
    blocks_ref,
    sums_ref,
    n1_ref,
    dout_ref,
    down_ref,
    gate_ref,
    rest_ref,
    up_ref,
    grad_ref,
    mix_ref,
    blocks_out,
    sums_out,
    gains_out,
    down_out,
    gate_out,
    rest_out,
    up_out,
    p_s,
    up_own,
    up_land,
    up_sum,
    n1_s,
    dout_s,
    g_s,
    gain_s,
    gain_rows,
    gain_slots,
    near_in,
    far_in,
    far_out,
    done,
    block_slots,
    sum_slots,
    x_in,
    up_in,
    down_in,
    line_out,
    across,
    up,
    low,
    near,
    far,
    final,
    s_far,
    s_near,
    swap,
    g_sem,
    stripe,
    u_up,
    u_low,
    local,
):
    at = Place(outer, inner, shards)
    s, h, parts, ys = at.s, at.h, at.parts, at.ys
    steps = list(range(1, ys))
    line = LineSum(at, p_s, (x_in, up_in, down_in, line_out), (across, up, low))
    model = x_ref.shape[1]
    tile = min(512, model)
    piece = done.shape[1]
    span = shards * piece
    width2 = both_ref.shape[1]
    me = s * shards + h
    small = ((blocks_ref, block_slots, blocks_out), (sums_ref, sum_slots, sums_out))
    fetch = pltpu.make_async_copy(up_ref, up_own, local.at[0])
    fetch.start()

    def stripes(k):
        lanes = pl.ds(pl.multiple_of(owner(k) * span, span), span)
        slot = lax.rem(k, 2)
        return (
            pltpu.make_async_copy(n1_ref.at[:, lanes], n1_s.at[slot], stripe.at[0, slot]),
            pltpu.make_async_copy(dout_ref.at[:, lanes], dout_s.at[slot], stripe.at[1, slot]),
        )

    def owner(k):
        return lax.rem(s + k + 1, parts)

    for copy in stripes(0):
        copy.start()

    def anyone(k):
        to = lax.rem(me + k, at.count)
        return (to // shards, lax.rem(to, shards)), to

    def greet_one(k, carry):
        hello(anyone(k)[0])
        return carry

    lax.fori_loop(1, at.count, greet_one, 0)
    welcome(at.count - 1)
    ups = LineReduce(at, up_own, up_land, u_up, u_low)
    fetch.wait()

    ups.early(0, at.far_first(0), min(1, outer - 2))

    def back(n, carry):
        d = at.far_first(n)
        rows = pl.ds(pl.multiple_of(d * p_s.shape[1], p_s.shape[1]), p_s.shape[1])
        for lane in range(0, model, tile):
            lanes = slice(lane, lane + tile)
            p_s[d, :, lanes] = dot(both_ref[rows, :], wi_ref[lanes, :], ((1,), (1,))).astype(BF16)
        line.cross(d).start()
        return carry

    lax.fori_loop(0, outer, back, 0)
    send = Sent()
    for n, (src, slots, _) in enumerate(small):
        for dy in steps:
            send(src, slots.at[h], s_far, (n, dy), (s, at.along(dy)))
        send(src, slots.at[h], s_near, (n, 0), at.sibling)
        slots[h] = src[...]

    def mix_rows(p, shard):
        return g_s.at[p, pl.ds(pl.multiple_of(shard * piece, piece), piece)]

    def to_sibling(k, dy):
        p = owner(k)
        return remote(
            mix_rows(p, at.along(dy, 1)),
            near_in.at[dy, p],
            near.at[0, dy, k],
            near.at[1, dy, k],
            at.sibling,
        )

    def to_shard(k, dy, source=False):
        p = owner(k)
        return remote(
            far_out.at[dy - 1, p],
            far_in.at[dy - 1, p],
            far.at[0, dy, k],
            far.at[1, dy, k],
            (s, at.along(-dy if source else dy)),
        )

    def to_owner(k, source=False):
        p = lax.rem(s + parts - k - 1, parts) if source else owner(k)
        return remote(
            done.at[owner(k)],
            mix_ref.at[p if source else s],
            final.at[0, k],
            final.at[1, k],
            (p, h),
        )

    def weight_grads(k, carry):
        p, slot = owner(k), lax.rem(k, 2)
        for copy in stripes(k):
            copy.wait()

        @pl.when(k < parts - 1)
        def _():
            for copy in stripes(k + 1):
                copy.start()

        g_s[p, :, 0:width2] = dot(n1_s[slot], both_ref[...], ((0,), (0,))).astype(BF16)
        g_s[p, :, width2:] = dot(dout_s[slot], z_ref[...], ((0,), (0,))).astype(BF16)
        for dy in steps + [0]:
            to_sibling(k, dy).start()
        return carry

    lax.fori_loop(0, parts, weight_grads, 0)
    exchanges = [
        PlaneExchange(at, 0, down_ref, down_out, swap, local.at[2]),
        PlaneExchange(at, 1, gate_ref, gate_out, swap, local.at[3]),
        PlaneExchange(at, 3, rest_ref, rest_out, swap, local.at[5]),
    ]
    up_exchange = PlaneExchange(at, 2, up_sum, up_out, swap, local.at[1])

    def sibling_sums(k, carry):
        p = owner(k)
        for dy in steps:
            to_sibling(k, dy).wait_recv()
            mine = mix_rows(p, at.along(dy))

            def add(rows, dy=dy, mine=mine):
                total = mine[rows, :].astype(F32) + near_in[dy, p, rows, :].astype(F32)
                far_out[dy - 1, p, rows, :] = total.astype(BF16)

            add_rows(piece, add)
            to_shard(k, dy).start()
        return carry

    lax.fori_loop(0, parts, sibling_sums, 0)
    for exchange in exchanges:
        exchange.start()
    gain_s[...] = jnp.zeros(gain_s.shape, F32)

    def mix_step(k):
        p = owner(k)
        mine = mix_rows(p, h)
        to_sibling(k, 0).wait_recv()
        for dy in steps:
            to_shard(k, dy, True).wait_recv()

        def add(rows):
            total = mine[rows, :].astype(F32) + near_in[0, p, rows, :].astype(F32)
            for dy in steps:
                total = total + far_in[dy - 1, p, rows, :].astype(F32)
            done[p, rows, :] = total.astype(BF16)

        add_rows(piece, add)
        if k < parts - 1:
            to_owner(k).start()

    def last_add(rows, dn1):
        x = x_ref[rows, :].astype(F32)
        scale = row_rms(x)
        gain_s[...] += dn1 * x * scale
        grad_ref[rows, :] = dmid_ref[rows, :] + rms_back(x, scale, gain_ref[...], dn1)

    def branch(o0):
        ends = o0 in (0, outer - 1)

        sooner = min(1, outer - 2) if ends else 0

        def between(n):
            if n + sooner < outer - 1 and ends:
                ups.push(o0, ups.order(o0)[n + sooner])
            for k in range(n * inner, (n + 1) * inner):
                mix_step(k)
            if n + 1 < outer - 1 and not ends:
                ups.step(o0, n + 1)

        if not ends:
            ups.step(o0, 0)
        line.steps(o0, last_add, between)

    at.branches(branch)
    keep = pltpu.make_async_copy(done.at[s], mix_ref.at[s], local.at[4])
    keep.start()
    gain1, gain2 = jnp.sum(gain_s[...], axis=0, keepdims=True), gain2_ref[...]
    spare = gain_rows.shape[2] - 2 * piece
    for k in range(at.count):
        lanes = slice(k * piece, (k + 1) * piece)
        parts_of = [gain1[:, lanes], gain2[:, lanes]]
        if spare:
            parts_of.append(jnp.zeros((1, spare), F32))
        gain_rows[k] = jnp.concatenate(parts_of, axis=1)

    def gain(k):
        to, row = anyone(k)
        return remote(gain_rows.at[row], gain_slots.at[k], g_sem.at[0, k], g_sem.at[1, k], to)

    def gain_start(k, carry):
        gain(k).start()
        return carry

    def gain_arrive(k, total):
        gain(k).wait_recv()
        return total + gain_slots[k]

    def gain_leave(k, carry):
        gain(k).wait_send()
        return carry

    lax.fori_loop(1, at.count, gain_start, 0)

    def last_up(o0):
        ups.absorb(o0, o0)
        ups.finish(o0)

    at.branches(last_up)

    def keep_up(rows):
        up_sum[rows, :] = up_own[at.o, rows, :]

    add_rows(up_sum.shape[0], keep_up)
    up_exchange.start()
    for n, (src, slots, out) in enumerate(small):
        for dy in steps:
            here = slots.at[at.along(-dy)]
            received(src, here, s_far, (n, dy), (s, at.along(-dy)))
            send(here, here, s_near, (n, dy), at.sibling)
    for n, (src, slots, out) in enumerate(small):
        for dy in range(ys):
            received(src, slots.at[at.along(-dy, 1)], s_near, (n, dy), at.sibling)

        def add(k, carry, slots=slots, out=out):
            rows = pl.ds(pl.multiple_of(k * 8, 8), 8)
            total = slots[0, rows, :]
            for j in range(1, shards):
                total = total + slots[j, rows, :]
            out[rows, :] = total
            return carry

        lax.fori_loop(0, src.shape[0] // 8, add, 0)
    gains_out[...] = lax.fori_loop(1, at.count, gain_arrive, gain_rows[me])
    for k in range(parts - 1):
        to_owner(k, True).wait_recv()
    for exchange in exchanges + [up_exchange]:
        exchange.finish()
    for k in range(parts):
        for dy in range(ys):
            to_sibling(k, dy).wait_send()
        for dy in steps:
            to_shard(k, dy).wait_send()
        if k < parts - 1:
            to_owner(k).wait_send()
    lax.fori_loop(1, at.count, gain_leave, 0)
    send.finish()
    keep.wait()


def closing(
    both,
    w_in,
    z,
    x,
    dmid,
    gain,
    gain2,
    small,
    sums,
    n1,
    dout,
    down,
    gate,
    rest,
    ups,
    outer,
    inner,
    shards,
    collective,
):
    rows, cols = x.shape
    parts, ys, count = outer * inner, shards // 2, outer * inner * shards
    piece = cols // count
    width = z.shape[1]
    lanes = -(-2 * piece // LANES) * LANES
    bufs, sems = line_sum_scratch(outer, rows, cols)
    pieces = pltpu.VMEM((max(ys - 1, 1), parts, piece, 3 * width), BF16)
    stripes = pltpu.VMEM((2, parts * rows, cols // parts), BF16)
    span, hidden = down.shape

    def swapped(array):
        shape = (inner * shards, span // (inner * shards), array.shape[-1])
        return jax.ShapeDtypeStruct(shape, BF16)

    reduce_vmem, reduce_sems = line_reduce_scratch(outer, span, hidden)
    return pl.pallas_call(
        functools.partial(closing_kernel, outer, inner, shards),
        out_shape=(
            jax.ShapeDtypeStruct((rows, cols), F32),
            jax.ShapeDtypeStruct((parts, piece, 3 * width), BF16),
            jax.ShapeDtypeStruct(small.shape, F32),
            jax.ShapeDtypeStruct(sums.shape, F32),
            jax.ShapeDtypeStruct((1, lanes), F32),
            *[swapped(array) for array in (down, gate, rest, ups)],
        ),
        in_specs=[IN_VMEM] * 9 + [ANY] * 6,
        out_specs=[IN_VMEM] * 5 + [ANY] * 4,
        scratch_shapes=[
            pltpu.VMEM((outer, inner * rows, cols), BF16),
            *reduce_vmem,
            pltpu.VMEM((span, hidden), BF16),
            stripes,
            stripes,
            pltpu.VMEM((parts, shards * piece, 3 * width), BF16),
            pltpu.VMEM((16, cols), F32),
            pltpu.VMEM((count, 1, lanes), F32),
            pltpu.VMEM((count, 1, lanes), F32),
            pltpu.VMEM((ys, parts, piece, 3 * width), BF16),
            pieces,
            pieces,
            pltpu.VMEM((parts, piece, 3 * width), BF16),
            pltpu.VMEM((shards,) + small.shape, F32),
            pltpu.VMEM((shards,) + sums.shape, F32),
        ]
        + bufs
        + sems
        + [DMA((2, ys, parts))] * 2
        + [DMA((2, parts))]
        + [DMA((2, 2, ys))] * 2
        + [DMA((2, 4, inner * shards)), DMA((2, count)), DMA((2, 2))]
        + reduce_sems
        + [DMA((6,))],
        compiler_params=pltpu.CompilerParams(
            collective_id=collective, has_side_effects=True, vmem_limit_bytes=60 * 2**20
        ),
        cost_estimate=cost(80),
        name="closing",
    )(
        both,
        w_in,
        z,
        x,
        dmid,
        gain,
        gain2,
        small,
        sums,
        n1,
        dout,
        down,
        gate,
        rest,
        ups,
    )


def unpack_kernel(
    inner,
    channels,
    gate_ref,
    rest_ref,
    up_ref,
    down_ref,
    mix_ref,
    gate,
    up,
    down,
    branch,
    enter,
    leave,
):
    slots, piece, hidden = up_ref.shape
    cut = gate_ref.shape[2]
    shards = slots // inner
    parts, width = mix_ref.shape[0], mix_ref.shape[2] // 3
    for i in range(inner):
        for h in range(shards):
            first = (h * inner + i) * hidden
            slot = i * shards + h
            gate[:, first : first + cut] = gate_ref[slot].astype(F32)
            gate[:, first + cut : first + hidden] = rest_ref[slot].astype(F32)
            up[:, first : first + hidden] = up_ref[slot].astype(F32)
            down[:, first : first + hidden] = down_ref[slot].astype(F32)
    for k, dst in enumerate((branch, enter, leave)):
        lanes = slice(k * width, k * width + width)
        dst[...] = jnp.concatenate(
            [mix_ref[p][:, lanes].astype(F32)[:, :channels] for p in range(parts)], axis=1
        )


def unpack(ffn_gate, ffn_rest, ffn_up, ffn_down, mix, inner, channels):
    slots, piece, hidden = ffn_up.shape
    across = jax.ShapeDtypeStruct((piece, slots * hidden), F32)
    wide = jax.ShapeDtypeStruct((piece, mix.shape[0] * channels), F32)
    return pl.pallas_call(
        functools.partial(unpack_kernel, inner, channels),
        out_shape=(across,) * 3 + (wide,) * 3,
        in_specs=[IN_VMEM] * 5,
        out_specs=[IN_VMEM] * 6,
        compiler_params=pltpu.CompilerParams(vmem_limit_bytes=48 * 2**20),
        cost_estimate=cost(4),
        name="unpack",
    )(ffn_gate, ffn_rest, ffn_up, ffn_down, mix)


def body(
    tokens,
    first_gain,
    branch_weight,
    input_weight,
    conv_weight,
    conv_bias,
    rate_weight,
    rate_bias,
    entry_weight,
    entry_bias,
    decay_param,
    output_weight,
    second_gain,
    hidden_gate,
    hidden_up,
    hidden_down,
    cotangent,
):
    quarters, _, chunk, model = tokens.shape
    rows = quarters * chunk
    parts = lax.axis_size("seq")
    shards = lax.axis_size("shard")
    inner = 2
    outer = parts // inner
    seq_at = lax.axis_index("seq")
    inner_at = lax.rem(seq_at, inner)
    lru = branch_weight.shape[1]
    channels = lru // parts
    width = (channels + LANES) // LANES * LANES
    spare = width - channels
    blocks, block_width = rate_weight.shape[0], rate_weight.shape[1]
    piece = model // (parts * shards)

    def own(weight, axis):
        part = lax.dynamic_slice_in_dim(weight, seq_at * channels, channels, axis)
        pads = [(0, 0), (0, 0)]
        pads[axis] = (0, spare)
        return jnp.pad(part, pads)

    params = jnp.pad(
        jnp.concatenate(
            [
                conv_weight.astype(F32),
                conv_bias[None],
                rate_bias[None],
                entry_bias[None],
                decay_param[None],
            ],
            axis=0,
        ),
        ((0, 0), (0, spare)),
    )

    x = tokens.reshape(rows, model)
    cot = cotangent.reshape(rows, model)
    gain1, gain2 = first_gain[None], second_gain[None]
    xs = x.astype(F32)
    n1, w_in, w_out = opening(
        (xs * row_rms(xs) * gain1).astype(BF16),
        jnp.concatenate([own(branch_weight, 1), own(input_weight, 1)], axis=1),
        own(output_weight, 0),
        outer,
        inner,
        shards,
        0,
    )
    n1, cot = lax.optimization_barrier((n1, cot))
    beside = [(o * inner + i, o * inner + 1 - i) for o in range(outer) for i in range(inner)]
    cot_beside = lax.ppermute(cot, "seq", beside)
    w_in = w_in.reshape(model, 2 * width)
    z, h, v, proj, gates = scan_forward(
        quarters, chunk, n1, w_in, params, rate_weight, entry_weight
    )
    mid, n2, cot_all = middle(
        z, w_out, x, gain2, cot, cot_beside, outer, inner, shards, 1
    )
    n2 = n2.reshape(inner * shards * rows, model)
    cot_all = cot_all.reshape(inner * shards * rows, model)
    hidden = hidden_gate.shape[1] // inner
    wg = lax.dynamic_slice_in_dim(hidden_gate, inner_at * hidden, hidden, 1)
    wu = lax.dynamic_slice_in_dim(hidden_up, inner_at * hidden, hidden, 1)
    wd = lax.dynamic_slice_in_dim(hidden_down, inner_at * hidden, hidden, 0)

    gm = dot(n2, wg)
    um = dot(n2, wu)
    act, slope = gelu_and_slope(gm)
    mm = (act * um).astype(BF16)
    dmm = dot(cot_all, wd, ((1,), (1,)))
    dgm = (dmm * um * slope).astype(BF16)
    dum = (dmm * act).astype(BF16)
    dmid, gain2_grad, dout, partial, down_sum, gate_sum, rest_terms, up_terms = turn(
        dgm,
        dum,
        mm,
        mid,
        cot,
        gain2,
        hidden_gate,
        hidden_up,
        hidden_down,
        n2,
        cot_all,
        outer,
        inner,
        shards,
        2,
    )
    both, small, sums, result, rest_sum = scan_backward(
        quarters,
        chunk,
        blocks,
        block_width,
        dout,
        w_out,
        proj,
        h,
        v,
        params,
        gates,
        mid,
        partial,
        rest_terms,
        outer,
        inner,
        shards,
        3,
    )
    tokens_grad, mix, small, sums, gains, down_sum, gate_sum, rest_sum, up_sum = closing(
        both,
        w_in,
        z,
        x,
        dmid,
        gain1,
        gain2_grad,
        small,
        sums,
        n1.reshape(parts * rows, model),
        dout.reshape(parts * rows, model),
        down_sum,
        gate_sum,
        rest_sum,
        up_terms,
        outer,
        inner,
        shards,
        4,
    )
    gains = gains[0]
    gate_sum, up_sum, down_sum, branch_sum, input_sum, output_sum = unpack(
        gate_sum, rest_sum, up_sum, down_sum, mix, inner, channels
    )
    sums = sums[:, :channels]
    small = small.reshape(2, blocks, -1, small.shape[1])[:, :, :block_width, :block_width]
    rate_grad, entry_grad = small[0], small[1]
    return (
        result.reshape(tokens.shape),
        tokens_grad.reshape(tokens.shape),
        gains[:piece],
        branch_sum,
        input_sum,
        sums[4:8],
        sums[3],
        rate_grad,
        sums[1],
        entry_grad,
        sums[2],
        sums[0],
        output_sum.T,
        gains[piece : 2 * piece],
        gate_sum,
        up_sum,
        down_sum.T,
    )


def solution(mesh):
    placed = (
        P(None, "shard", "seq", None),
        P(),
        P("shard", None),
        P("shard", None),
        P(None, "seq"),
        P("seq"),
        P("seq", None, None),
        P("seq"),
        P("seq", None, None),
        P("seq"),
        P("seq"),
        P(None, "shard"),
        P(),
        P(None, "shard"),
        P(None, "shard"),
        P("shard", None),
        P(None, "shard", "seq", None),
    )
    return jax.shard_map(
        body,
        mesh=mesh,
        in_specs=placed,
        out_specs=(
            P(None, "shard", "seq", None),
            P(None, "shard", "seq", None),
            P(("seq", "shard")),
            P(("seq", "shard"), None),
            P(("seq", "shard"), None),
            P(None, "seq"),
            P("seq"),
            P("seq", None, None),
            P("seq"),
            P("seq", None, None),
            P("seq"),
            P("seq"),
            P(None, ("seq", "shard")),
            P(("seq", "shard")),
            P(("seq", "shard"), None),
            P(("seq", "shard"), None),
            P(None, ("seq", "shard")),
        ),
        check_vma=False,
    )
```

```python
import functools

import jax
import jax.numpy as jnp
from jax import lax
from jax.experimental import pallas as pl
from jax.experimental.pallas import tpu as pltpu
from jax.sharding import PartitionSpec as P

EPSILON = 1e-06
DECAY_SCALE = 8.0
MULT_FLOOR = 0.01
LANES = 128
SEGMENTS = 8
GELU_C = 0.7978845608028654
GELU_A = 0.044715
F32 = jnp.float32
BF16 = jnp.bfloat16


MESH = pl.DeviceIdType.MESH
IN_HBM = pl.BlockSpec(memory_space=pltpu.HBM)
IN_VMEM = pl.BlockSpec(memory_space=pltpu.VMEM)
DMA = pltpu.SemaphoreType.DMA


def cost(us):
    return pl.CostEstimate(flops=0, bytes_accessed=int(us * 3.3e6), transcendentals=0)


def dot(left, right, dims=((1,), (0,))):
    return lax.dot_general(left, right, (dims, ((), ())), preferred_element_type=F32)


def gelu_and_slope(x):
    inner = GELU_C * (x + GELU_A * x * x * x)
    t = jnp.tanh(inner)
    half = 0.5 * (1.0 + t)
    slope = half + 0.5 * x * (1.0 - t * t) * (GELU_C * (1.0 + 3.0 * GELU_A * x * x))
    return x * half, slope


def gelu_tanh(x):
    return x * (0.5 * (1.0 + jnp.tanh(GELU_C * (x + GELU_A * x * x * x))))


def sigmoid(x):
    return 0.5 * jnp.tanh(0.5 * x) + 0.5


def softplus(x):
    return jnp.maximum(x, 0.0) + jnp.log1p(jnp.exp(-jnp.abs(x)))


def lane_groups(width):
    return [slice(g * LANES, (g + 1) * LANES) for g in range(width // LANES)]


def put(ref, rows, value):
    for g, lanes in enumerate(lane_groups(value.shape[1])):
        ref[g, rows, :] = value[:, lanes]


def take(ref, rows):
    return jnp.concatenate([ref[g, rows, :] for g in range(ref.shape[0])], axis=1)


def strided_scan(steps, groups, load, store):
    def step(k, carry):
        i = steps(k)
        out = []
        for g in range(groups):
            state, total = carry[g]
            factor, term = load(g, i)
            state = factor * state + term
            total = factor * total
            store(g, i, state, total)
            out.append((state, total))
        return tuple(out)

    return step


TAP, CONV_B, RATE_B, ENTRY_B, DECAY = 0, 4, 5, 6, 7


def gate_values(pre, log_scale, width):
    r = sigmoid(pre[:, :width])
    e = sigmoid(pre[:, width:])
    a = jnp.exp(r * log_scale)
    room = 1.0 - a * a
    m = jnp.sqrt(jnp.maximum(room, MULT_FLOOR))
    return r, e, a, room, m


class Place:
    def __init__(self, outer, inner, shards):
        self.outer, self.inner, self.shards = outer, inner, shards
        self.parts, self.ys, self.count = outer * inner, shards // 2, outer * inner * shards
        self.chips = inner * self.ys
        self.s, self.h = lax.axis_index("seq"), lax.axis_index("shard")
        self.o, self.i = self.s // inner, lax.rem(self.s, inner)
        self.y, self.core = self.h // 2, lax.rem(self.h, 2)
        self.beside = (self.o * inner + 1 - self.i, self.h)
        self.above, self.below = (self.s + inner, self.h), (self.s - inner, self.h)
        self.sibling = (self.s, self.along(0, 1))

    def along(self, dy, other=0):
        y = lax.rem(self.y + dy + self.ys, self.ys)
        return y * 2 + lax.rem(self.core + other, 2)

    def chip(self, q, back=False):
        di, dy = q // self.ys, q - q // self.ys * self.ys
        if back:
            di, dy = self.inner - di, self.ys - dy
        return lax.rem(self.i + di, self.inner), lax.rem(self.y + dy, self.ys)

    def near(self, q, other=0, back=False):
        i, y = self.chip(q, back)
        h = y * 2 + lax.rem(self.core + other, 2)
        return (self.o * self.inner + i, h), i * self.shards + h

    def far_first(self, n):
        sign = 2 * ((2 * self.o) // self.outer) - 1
        return lax.rem(self.o + sign * (n + 1) + 2 * self.outer, self.outer)

    def branches(self, fn):
        for o0 in range(self.outer):
            pl.when(self.o == o0)(functools.partial(fn, o0))


def hello(to):
    barrier = pltpu.get_barrier_semaphore()
    pl.semaphore_signal(barrier, inc=1, device_id=to, device_id_type=MESH)


def welcome(n):
    pl.semaphore_wait(pltpu.get_barrier_semaphore(), n)


def greet(others):
    for to in others:
        hello(to)
    welcome(len(others))


def greet_with_line(at, others):
    up, down = at.o < at.outer - 1, at.o > 0
    for to in others:
        hello(to)
    pl.when(up)(lambda: hello(at.above))
    pl.when(down)(lambda: hello(at.below))
    ends = lax.rem(at.o, at.outer - 1) == 0
    pl.when(ends)(lambda: welcome(len(others) + 1))
    pl.when(jnp.logical_not(ends))(lambda: welcome(len(others) + 2))


class Sent:
    def __init__(self):
        self.copies = []

    def __call__(self, src, dst, sems, at, to):
        copy = remote(src, dst, sems.at[(0,) + at], sems.at[(1,) + at], to)
        copy.start()
        self.copies.append(copy)

    def finish(self):
        for copy in self.copies:
            copy.wait_send()


def received(like, here, sems, at, source):
    remote(like, here, sems.at[(0,) + at], sems.at[(1,) + at], source).wait_recv()


def line_gather(
    at, o0, x_ref, out, across, up, down, between=lambda k: None, each=lambda row: None
):
    send = Sent()

    def slot(row):
        return out.at[row * at.inner + at.i]

    def pass_on(row, sems, to):
        send(x_ref if row == o0 else slot(row), slot(row), sems, (row,), to)

    for k in range(at.outer):
        lower, upper = o0 - k, o0 + k
        if k > 0 and lower >= 0:
            received(x_ref, slot(lower), up, (lower,), at.below)
        if lower >= 0 and o0 < at.outer - 1:
            pass_on(lower, up, at.above)
        if lower >= 0:
            pass_on(lower, across, at.beside)
        if k > 0 and upper < at.outer:
            received(x_ref, slot(upper), down, (upper,), at.above)
        if upper < at.outer and o0 > 0:
            pass_on(upper, down, at.below)
        if k > 0 and upper < at.outer:
            pass_on(upper, across, at.beside)
        between(k)
    between(at.outer)
    for row in sorted(range(at.outer), key=lambda row: abs(row - o0)):
        received(x_ref, out.at[row * at.inner + 1 - at.i], across, (row,), at.beside)
        each(row)
    send.finish()


class LineSum:
    def __init__(self, at, p, bufs, sems):
        self.at, self.p = at, p
        self.x_in, self.up_in, self.down_in, self.sums = bufs
        self.across, self.up, self.down = sems
        self.rows = self.x_in.shape[1]

    def block(self, d, i):
        return self.p.at[d, pl.ds(pl.multiple_of(i * self.rows, self.rows), self.rows)]

    def cross(self, d):
        return remote(
            self.block(d, 1 - self.at.i),
            self.x_in.at[d],
            self.across.at[0, d],
            self.across.at[1, d],
            self.at.beside,
        )

    def steps(self, o0, last_add, between=lambda n: None):
        at = self.at
        send = Sent()
        order = sorted(range(at.outer), key=lambda d: (-abs(d - o0), d))
        for n, d in enumerate(order):
            mine = self.block(d, at.i)
            self.cross(d).wait_recv()
            terms = [mine, self.x_in.at[d]]
            if d >= o0 > 0:
                received(mine, self.up_in.at[d], self.up, (d,), at.below)
                terms.append(self.up_in.at[d])
            if d <= o0 < at.outer - 1:
                received(mine, self.down_in.at[d], self.down, (d,), at.above)
                terms.append(self.down_in.at[d])
            target = self.sums.at[d]

            def add(rows, terms=terms, target=target, d=d):
                total = terms[0][rows, :].astype(F32)
                for term in terms[1:]:
                    total = total + term[rows, :].astype(F32)
                if d == o0:
                    last_add(rows, total)
                else:
                    target[rows, :] = total.astype(target.dtype)

            add_rows(self.rows, add)
            if d > o0:
                send(target, self.up_in.at[d], self.up, (d,), at.above)
            if d < o0:
                send(target, self.down_in.at[d], self.down, (d,), at.below)
            between(n)
        for d in range(at.outer):
            self.cross(d).wait_send()
        send.finish()


class LineReduce:
    def __init__(self, at, own, land, up, down):
        self.at, self.own, self.land, self.up, self.down = at, own, land, up, down

    def order(self, o0):
        return sorted(range(self.at.outer), key=lambda d: (-abs(d - o0), d))

    def ascent(self, d):
        at = self.at
        return remote(
            self.own.at[d], self.land.at[d], self.up.at[0, d], self.up.at[1, d], at.above
        )

    def descent(self, o0, d):
        slot = d if d != o0 - 1 else self.at.outer
        return remote(
            self.own.at[d], self.land.at[slot], self.down.at[0, d], self.down.at[1, d], self.at.below
        )

    def early(self, n, d, limit):
        at = self.at
        inside = n < limit
        last = at.outer - 1
        pl.when(jnp.logical_and(at.o == 0, inside))(lambda: self.ascent(d).start())
        far = remote(
            self.own.at[d], self.land.at[d], self.down.at[0, d], self.down.at[1, d], at.below
        )
        pl.when(jnp.logical_and(at.o == last, inside))(lambda: far.start())

    def push(self, o0, d):
        if d > o0:
            self.ascent(d).start()
        if d < o0:
            self.descent(o0, d).start()

    def absorb(self, o0, d):
        terms = []
        if d >= o0 > 0:
            self.ascent(d).wait_recv()
            terms.append(self.land.at[d])
        if d <= o0 < self.at.outer - 1:
            slot = d if d < o0 else self.at.outer
            self.descent(o0 + 1, d).wait_recv()
            terms.append(self.land.at[slot])
        mine = self.own.at[d]

        def add(rows):
            total = mine[rows, :].astype(F32)
            for term in terms:
                total = total + term[rows, :].astype(F32)
            mine[rows, :] = total.astype(BF16)

        if terms:
            add_rows(mine.shape[0], add)

    def step(self, o0, n):
        d = self.order(o0)[n]
        self.absorb(o0, d)
        self.push(o0, d)

    def finish(self, o0):
        for d in range(self.at.outer):
            if d > o0:
                self.ascent(d).wait_send()
            if d < o0:
                self.descent(o0, d).wait_send()


def first_half(hidden):
    return -(-(hidden // 2) // LANES) * LANES


def line_reduce_scratch(outer, rows, cols):
    blocks = [pltpu.VMEM((outer, rows, cols), BF16), pltpu.VMEM((outer + 1, rows, cols), BF16)]
    return blocks, [DMA((2, outer))] * 2


def line_sum_scratch(outer, rows, cols):
    return [pltpu.VMEM((outer, rows, cols), BF16)] * 4, [DMA((2, outer))] * 3


def row_rms(values):
    return lax.rsqrt(jnp.mean(values * values, axis=-1, keepdims=True) + EPSILON)


def rms_back(values, scale, gain, grad):
    k = grad * gain
    mean = jnp.mean(k * values, axis=-1, keepdims=True)
    return scale * k - scale * scale * scale * values * mean


def run_scan(
    parts, quarters, chunk, proj_ref, par_ref, gates_ref, z_ref, h_ref, v_ref, u_pad, a_s, b_s
):
    length, width = h_ref.shape
    seg = length // SEGMENTS
    chunks = length // chunk

    def place(c):
        q = c // parts
        s = c - q * parts
        return pl.multiple_of((s * quarters + q) * chunk, chunk)

    def time_of(c):
        return pl.multiple_of(c * chunk, chunk)

    log_scale = -DECAY_SCALE * softplus(-par_ref[DECAY : DECAY + 1, :])
    bias = jnp.concatenate(
        [par_ref[RATE_B : RATE_B + 1, :], par_ref[ENTRY_B : ENTRY_B + 1, :]], axis=1
    )
    u_pad[0:8, :] = jnp.zeros((8, width), F32)

    def first(c, carry):
        u = proj_ref[pl.ds(place(c), chunk), width : 2 * width].astype(BF16).astype(F32)
        u_pad[pl.ds(pl.multiple_of(time_of(c) + 8, 8), chunk), :] = u
        wide = u_pad[pl.ds(time_of(c), chunk + 8), :]
        v = par_ref[CONV_B : CONV_B + 1, :] + par_ref[0:1, :] * wide[8:]
        for k in range(1, 4):
            v = v + par_ref[k : k + 1, :] * wide[8 - k : 8 - k + chunk]
        v = v.astype(BF16)
        v_ref[pl.ds(time_of(c), chunk), :] = v
        pre = dot(v, gates_ref[...]) + bias
        r, e, a, room, m = gate_values(pre, log_scale, width)
        put(a_s, pl.ds(time_of(c), chunk), a)
        put(b_s, pl.ds(time_of(c), chunk), m * e * v.astype(F32))
        return carry

    lax.fori_loop(0, chunks, first, 0)

    def load(g, i):
        at = pl.ds(i, SEGMENTS, stride=seg)
        return a_s[g, at, :], b_s[g, at, :]

    def store(g, i, state, total):
        at = pl.ds(i, SEGMENTS, stride=seg)
        b_s[g, at, :] = state
        a_s[g, at, :] = total

    groups = width // LANES
    start = (jnp.zeros((SEGMENTS, LANES), F32), jnp.ones((SEGMENTS, LANES), F32))
    ends = lax.fori_loop(
        0, seg, strided_scan(lambda k: k, groups, load, store), (start,) * groups, unroll=8
    )
    final = jnp.concatenate([e[0] for e in ends], axis=1)
    totals = jnp.concatenate([e[1] for e in ends], axis=1)
    carries = [jnp.zeros((1, width), F32)]
    for j in range(SEGMENTS - 1):
        carries.append(totals[j : j + 1] * carries[j] + final[j : j + 1])
    for j in range(SEGMENTS):
        per = seg // chunk

        def last(k, carry, j=j, per=per):
            c = j * per + k
            rows = pl.ds(time_of(c), chunk)
            h = take(b_s, rows) + take(a_s, rows) * carries[j]
            h_ref[rows, :] = h
            y = gelu_tanh(proj_ref[pl.ds(place(c), chunk), 0:width])
            z_ref[pl.ds(place(c), chunk), :] = (h.astype(BF16).astype(F32) * y).astype(BF16)
            return carry

        lax.fori_loop(0, per, last, 0)


def forward_kernel(
    outer,
    inner,
    shards,
    quarters,
    chunk,
    x_ref,
    gain1_ref,
    gain2_ref,
    taps_ref,
    conv_b_ref,
    rate_b_ref,
    entry_b_ref,
    decay_ref,
    rate_ref,
    entry_ref,
    cot_ref,
    wi_ref,
    wo_ref,
    par_ref,
    mid_ref,
    z_out,
    h_out,
    v_out,
    proj_out,
    gates_out,
    n1_out,
    wi_out,
    wo_out,
    n2_out,
    cot_out,
    own_s,
    n1_s,
    wi_s,
    wo_s,
    gates_s,
    u_pad,
    a_s,
    b_s,
    z_ref,
    h_ref,
    v_ref,
    proj_ref,
    gates_ref,
    p_s,
    cot_s,
    x_in,
    up_in,
    down_in,
    line_out,
    g_across,
    g_up,
    g_down,
    w_far,
    w_near,
    across,
    up,
    down,
    far,
    near,
    c_side,
    c_far,
    c_near,
    local,
):
    at = Place(outer, inner, shards)
    parts, rows = at.parts, x_ref.shape[0]
    steps = list(range(1, at.ys))
    width2 = wi_ref.shape[1]
    width, depth, cols = width2 // 2, wi_ref.shape[0], wo_ref.shape[1]

    def normalize(some):
        x = x_ref[some, :].astype(F32)
        own_s[some, :] = (x * row_rms(x) * gain1_ref[...]).astype(BF16)

    add_rows(rows, normalize)
    greet_with_line(at, [at.sibling] + [at.near(q)[0] for q in range(1, at.chips)])
    weights = ((wi_ref, wi_s), (wo_ref, wo_s))
    keep = [
        pltpu.make_async_copy(own_s, n1_s.at[at.s], local.at[0]),
        pltpu.make_async_copy(wi_ref, wi_s.at[at.h], local.at[1]),
        pltpu.make_async_copy(wo_ref, wo_s.at[at.h], local.at[2]),
    ]
    for copy in keep:
        copy.start()
    send = Sent()

    def send_weights():
        for n, (src, dst) in enumerate(weights):
            for dy in steps:
                send(src, dst.at[at.h], w_far, (n, dy), (at.s, at.along(dy)))
            send(src, dst.at[at.h], w_near, (n, 0), at.sibling)

    send_weights()
    channels = decay_ref.shape[0]
    par_ref[...] = jnp.zeros(par_ref.shape, F32)
    par_ref[0:4, :channels] = taps_ref[...].astype(F32)
    for row, src in (
        (CONV_B, conv_b_ref),
        (RATE_B, rate_b_ref),
        (ENTRY_B, entry_b_ref),
        (DECAY, decay_ref),
    ):
        par_ref[row, :channels] = src[...]
    gates_s[...] = jnp.zeros(gates_s.shape, F32)
    block_width, blocks = rate_ref.shape[0], rate_ref.shape[1]
    for gate, src in enumerate((rate_ref, entry_ref)):
        for j in range(blocks):
            top, lane = j * block_width, gate * width + j * block_width
            gates_s[top : top + block_width, lane : lane + block_width] = src[:, j, :].astype(F32)
    gates_ref[...] = gates_s[...].astype(BF16)

    def project(d):
        total = None
        for k in range(shards):
            lanes = slice(k * depth, (k + 1) * depth)
            pair = jnp.concatenate([n1_s[d * inner + i, :, lanes] for i in range(inner)], axis=0)
            term = dot(pair, wi_s[k])
            total = term if total is None else total + term
        proj_ref[d * inner * rows : (d + 1) * inner * rows, :] = total

    def gather(o0):
        forward = Sent()

        def between(k):
            if k != 1:
                return
            for n, (src, dst) in enumerate(weights):
                for dy in steps:
                    source = at.along(-dy)
                    received(src, dst.at[source], w_far, (n, dy), (at.s, source))
                    forward(dst.at[source], dst.at[source], w_near, (n, dy), at.sibling)
            for n, (src, dst) in enumerate(weights):
                for dy in range(at.ys):
                    received(src, dst.at[at.along(-dy, 1)], w_near, (n, dy), at.sibling)
            for copy in keep:
                copy.wait()

        def each(row):
            project(row)

        line_gather(at, o0, own_s, n1_s, g_across, g_up, g_down, between, each)
        forward.finish()

    at.branches(gather)
    send(cot_ref, cot_s, c_side, (), at.beside)
    keep = [
        pltpu.make_async_copy(n1_s, n1_out, local.at[0]),
        pltpu.make_async_copy(wi_s, wi_out, local.at[1]),
        pltpu.make_async_copy(wo_s, wo_out, local.at[2]),
    ]
    for copy in keep:
        copy.start()
    run_scan(
        parts, quarters, chunk, proj_ref, par_ref, gates_ref, z_ref, h_ref, v_ref, u_pad, a_s, b_s
    )
    made = (
        (z_ref, z_out),
        (h_ref, h_out),
        (v_ref, v_out),
        (proj_ref, proj_out),
        (gates_ref, gates_out),
    )
    for n, (src, dst) in enumerate(made):
        keep.append(pltpu.make_async_copy(src, dst, local.at[6 + n]))
        keep[-1].start()
    line = LineSum(at, p_s, (x_in, up_in, down_in, line_out), (across, up, down))

    def back_project(n, carry):
        d = at.far_first(n)
        some = pl.ds(pl.multiple_of(d * inner * rows, inner * rows), inner * rows)
        for k in range(shards):
            p_s[d, :, k * cols : (k + 1) * cols] = dot(z_ref[some, :], wo_s[k]).astype(BF16)
        line.cross(d).start()
        return carry

    lax.fori_loop(0, outer, back_project, 0)
    received(cot_ref, cot_s, c_side, (), at.beside)

    def slot(side, dy, other=0):
        i = 1 - at.i if side else at.i
        return cot_out.at[i * shards + at.along(dy, other)]

    mine = (cot_ref, cot_s)
    for side in range(2):
        keep.append(pltpu.make_async_copy(mine[side], slot(side, 0), local.at[3 + side]))
        keep[-1].start()
        for dy in steps:
            send(mine[side], slot(side, 0), c_far, (side, dy), (at.s, at.along(dy)))
        send(mine[side], slot(side, 0), c_near, (side, 0), at.sibling)

    def last_add(some, total):
        mid = x_ref[some, :].astype(F32) + total
        mid_ref[some, :] = mid
        own_s[some, :] = (mid * row_rms(mid) * gain2_ref[...]).astype(BF16)

    def branch(o0):
        forward = Sent()

        def between(n):
            if n != outer - 2:
                return
            for side in range(2):
                for dy in steps:
                    here = slot(side, -dy)
                    received(cot_ref, here, c_far, (side, dy), (at.s, at.along(-dy)))
                    forward(here, here, c_near, (side, dy), at.sibling)

        line.steps(o0, last_add, between)
        forward.finish()

    at.branches(branch)
    _, me = at.near(0)
    keep.append(pltpu.make_async_copy(own_s, n2_out.at[me], local.at[5]))
    keep[-1].start()
    for q in reversed(range(1, at.chips)):
        send(own_s, n2_out.at[me], far, (q,), at.near(q)[0])
    send(own_s, n2_out.at[me], near, (0,), at.sibling)
    for q in range(1, at.chips):
        source, there = at.near(q, back=True)
        here = n2_out.at[there]
        received(own_s, here, far, (q,), source)
        send(here, here, near, (q,), at.sibling)
    for q in range(at.chips):
        received(own_s, n2_out.at[at.near(q, 1, True)[1]], near, (q,), at.sibling)
    for side in range(2):
        for dy in range(at.ys):
            received(cot_ref, slot(side, -dy, 1), c_near, (side, dy), at.sibling)
    send.finish()
    for copy in keep:
        copy.wait()


def forward(
    x,
    gain1,
    gain2,
    channel,
    rate,
    entry,
    cot,
    w_in,
    w_out,
    quarters,
    chunk,
    outer,
    inner,
    shards,
    collective,
):
    rows, cols = x.shape
    parts, ys, chips = outer * inner, shards // 2, inner * shards // 2
    length, width = parts * rows, w_in.shape[1] // 2
    bufs, sems = line_sum_scratch(outer, rows, cols)
    plane = jax.ShapeDtypeStruct((inner * shards, rows, cols), BF16)
    lanes = pltpu.VMEM((width // LANES, length, LANES), F32)
    made = (
        ((length, width), BF16),
        ((length, width), F32),
        ((length, width), BF16),
        ((length, 2 * width), F32),
        ((width, 2 * width), BF16),
    )
    return pl.pallas_call(
        functools.partial(forward_kernel, outer, inner, shards, quarters, chunk),
        out_shape=(
            jax.ShapeDtypeStruct((8, width), F32),
            jax.ShapeDtypeStruct((rows, cols), F32),
            *[jax.ShapeDtypeStruct(shape, dtype) for shape, dtype in made],
            jax.ShapeDtypeStruct((parts, rows, cols), BF16),
            jax.ShapeDtypeStruct((shards,) + w_in.shape, BF16),
            jax.ShapeDtypeStruct((shards,) + w_out.shape, BF16),
            plane,
            plane,
        ),
        in_specs=[IN_VMEM] * 11 + [IN_HBM] * 2,
        out_specs=[IN_VMEM] * 2 + [IN_HBM] * 10,
        scratch_shapes=[
            pltpu.VMEM((rows, cols), BF16),
            pltpu.VMEM((parts, rows, cols), BF16),
            pltpu.VMEM((shards,) + w_in.shape, BF16),
            pltpu.VMEM((shards,) + w_out.shape, BF16),
            pltpu.VMEM((width, 2 * width), F32),
            pltpu.VMEM((length + 8, width), F32),
            lanes,
            lanes,
            *[pltpu.VMEM(shape, dtype) for shape, dtype in made],
            pltpu.VMEM((outer, inner * rows, cols), BF16),
            pltpu.VMEM((rows, cols), BF16),
        ]
        + bufs
        + [DMA((2, outer))] * 3
        + [DMA((2, 2, ys))] * 2
        + sems
        + [DMA((2, chips))] * 2
        + [DMA((2,))]
        + [DMA((2, 2, ys))] * 2
        + [DMA((11,))],
        compiler_params=pltpu.CompilerParams(
            collective_id=collective, has_side_effects=True, vmem_limit_bytes=60 * 2**20
        ),
        cost_estimate=cost(140),
        name="forward",
    )(x, gain1, gain2, *channel, rate, entry, cot, w_in, w_out)


class PlaneSum:
    def __init__(self, at, n, p, near_in, far_in, far_out, near, far):
        self.at, self.n, self.p = at, n, p
        self.near_in, self.far_in, self.far_out = near_in, far_in, far_out
        self.near, self.far = near, far
        self.rows = near_in.shape[2]

    def block(self, q, other):
        i, y = self.at.chip(q)
        core = lax.rem(self.at.core + other, 2)
        rows = pl.ds(pl.multiple_of(core * self.rows, self.rows), self.rows)
        return self.p.at[i * self.at.ys + y, rows]

    def to_sibling(self, q):
        n = self.n
        return remote(
            self.block(q, 1),
            self.near_in.at[n, q],
            self.near.at[0, n, q],
            self.near.at[1, n, q],
            self.at.sibling,
        )

    def onward(self, q, back=False):
        n = self.n
        return remote(
            self.far_out.at[n, q],
            self.far_in.at[n, q],
            self.far.at[0, n, q],
            self.far.at[1, n, q],
            self.at.near(q, 0, back)[0],
        )

    def combine_one(self, k, own=None):
        q = self.at.chips - 1 - k
        self.to_sibling(q).wait_recv()
        mine = self.block(q, 0) if own is None else own.at[q]

        def add(rows):
            total = mine[rows, :].astype(F32) + self.near_in[self.n, q, rows, :].astype(F32)
            self.far_out[self.n, q, rows, :] = total.astype(BF16)

        add_rows(self.rows, add)
        self.onward(q).start()

    def combine(self, own=None):
        def one(k, carry):
            self.combine_one(k, own)
            return carry

        lax.fori_loop(0, self.at.chips - 1, one, 0)
        self.to_sibling(0).wait_recv()

    def total(self, rows, own=None):
        n = self.n
        mine = self.block(0, 0) if own is None else own.at[0]
        value = mine[rows, :].astype(F32) + self.near_in[n, 0, rows, :].astype(F32)
        for q in range(1, self.at.chips):
            value = value + self.far_in[n, q, rows, :].astype(F32)
        return value

    def arrive(self):
        for q in range(1, self.at.chips):
            self.onward(q, True).wait_recv()

    def finish(self):
        for q in range(self.at.chips):
            self.to_sibling(q).wait_send()
        for q in range(1, self.at.chips):
            self.onward(q).wait_send()


def turn_kernel(
    outer,
    inner,
    shards,
    dgm_ref,
    dum_ref,
    mm_ref,
    mid_ref,
    cot_ref,
    gain_ref,
    wg_ref,
    wu_ref,
    wd_ref,
    n2_ref,
    cots_ref,
    dmid_ref,
    gain_grad_ref,
    dout_ref,
    q_ref,
    down_ref,
    gate_ref,
    rest_ref,
    up_ref,
    p_s,
    q_s,
    dout_s,
    gain_s,
    wg_s,
    wu_s,
    wd_s,
    n2_s,
    cots_s,
    u_s,
    r_s,
    near_in,
    far_in,
    far_out,
    down_own,
    down_land,
    gate_own,
    gate_land,
    near,
    far,
    across,
    up,
    low,
    down_up,
    down_low,
    gate_up,
    gate_low,
    local,
    q_sem,
    u_sem,
    r_sem,
):
    at = Place(outer, inner, shards)
    model, hidden = wg_s.shape
    tile = min(512, model)
    pair = p_s.shape[1]
    span = model // outer
    own = pl.ds(pl.multiple_of(at.i * hidden, hidden), hidden)
    load = [
        pltpu.make_async_copy(cots_ref, cots_s, local.at[1]),
        pltpu.make_async_copy(wg_ref.at[:, own], wg_s, local.at[2]),
        pltpu.make_async_copy(wu_ref.at[:, own], wu_s, local.at[3]),
        pltpu.make_async_copy(n2_ref, n2_s, local.at[4]),
        pltpu.make_async_copy(wd_ref.at[own, :], wd_s, local.at[5]),
    ]
    for copy in load:
        copy.start()
    greet_with_line(at, [at.sibling] + [at.near(q)[0] for q in range(1, at.chips)])
    grad = PlaneSum(at, 0, p_s, near_in, far_in, far_out, near, far)
    down = LineReduce(at, down_own, down_land, down_up, down_low)
    gate = LineReduce(at, gate_own, gate_land, gate_up, gate_low)

    def columns(d):
        return pl.ds(pl.multiple_of(d * span, span), span)

    load[0].wait()

    def down_grad(n, carry):
        d = at.far_first(n)
        down_own[d] = dot(cots_s[:, columns(d)], mm_ref[...], ((0,), (0,))).astype(BF16)
        down.early(n, d, outer - 2)
        return carry

    down_grad(0, 0)
    load[1].wait()
    load[2].wait()

    def back(k, carry):
        q = at.chips - 1 - k
        i, y = at.chip(q)
        c = i * at.ys + y
        rows = pl.ds(pl.multiple_of(c * pair, pair), pair)
        for lane in range(0, model, tile):
            lanes = slice(lane, lane + tile)
            block = dot(dgm_ref[rows, :], wg_s[lanes, :], ((1,), (1,)))
            block = block + dot(dum_ref[rows, :], wu_s[lanes, :], ((1,), (1,)))
            p_s[c, :, lanes] = block.astype(BF16)
        grad.to_sibling(q).start()
        pl.when(k > 0)(lambda: grad.combine_one(k - 1))
        return carry

    lax.fori_loop(0, at.chips, back, 0)
    grad.to_sibling(0).wait_recv()
    lax.fori_loop(1, outer, down_grad, 0)
    load[3].wait()

    cut = gate_own.shape[2]

    def keep_r(n):
        slot = lax.rem(n, 2)
        there = rest_ref.at[at.far_first(n), :, : hidden - cut]
        return pltpu.make_async_copy(r_s.at[slot], there, r_sem.at[slot])

    def gate_grad(n, carry):
        d = at.far_first(n)
        pl.when(n >= 2)(lambda: keep_r(n - 2).wait())
        block = dot(n2_s[:, columns(d)], dgm_ref[...], ((0,), (0,))).astype(BF16)
        gate_own[d] = block[:, :cut]
        r_s[lax.rem(n, 2)] = block[:, cut:]
        keep_r(n).start()
        return carry

    lax.fori_loop(0, outer, gate_grad, 0)
    for n in range(max(outer - 2, 0), outer):
        keep_r(n).wait()

    def first_down(o0):
        if 0 < o0 < outer - 1:
            down.step(o0, 0)

    at.branches(first_down)
    load[4].wait()

    def keep_q(c):
        slot = lax.rem(c, 2)
        return pltpu.make_async_copy(q_s.at[slot], q_ref.at[c], q_sem.at[slot])

    def ahead(c, carry):
        rows = pl.ds(pl.multiple_of(c * pair, pair), pair)
        pl.when(c >= 2)(lambda: keep_q(c - 2).wait())
        for lane in range(0, model, tile):
            lanes = slice(lane, lane + tile)
            q_s[lax.rem(c, 2), :, lanes] = dot(mm_ref[rows, :], wd_s[:, lanes]).astype(BF16)
        keep_q(c).start()
        return carry

    lax.fori_loop(0, at.chips, ahead, 0)
    for c in range(max(at.chips - 2, 0), at.chips):
        keep_q(c).wait()
    gain_s[...] = jnp.zeros(gain_s.shape, F32)
    grad.arrive()

    def norm_back(rows):
        dn2 = grad.total(rows)
        mid = mid_ref[rows, :]
        scale = row_rms(mid)
        gain_s[...] += dn2 * mid * scale
        dmid = cot_ref[rows, :].astype(F32) + rms_back(mid, scale, gain_ref[...], dn2)
        dmid_ref[rows, :] = dmid
        dout_s[rows, :] = dmid.astype(BF16)

    add_rows(dout_s.shape[0], norm_back)
    gain_grad_ref[...] = jnp.sum(gain_s[...], axis=0, keepdims=True)
    keep = pltpu.make_async_copy(dout_s, dout_ref.at[at.s], local.at[0])
    keep.start()

    head = u_s.shape[2] - up_ref.shape[2]

    class keep_u:
        def __init__(self, n):
            slot, d = lax.rem(n, 2), at.far_first(n)
            block = u_s.at[slot]
            self.copies = (
                pltpu.make_async_copy(
                    block.at[:, :head], rest_ref.at[d, :, hidden - cut :], u_sem.at[0, slot]
                ),
                pltpu.make_async_copy(block.at[:, head:], up_ref.at[d], u_sem.at[1, slot]),
            )

        def start(self):
            for copy in self.copies:
                copy.start()

        def wait(self):
            for copy in self.copies:
                copy.wait()

    def up_grad(n, carry):
        pl.when(n >= 2)(lambda: keep_u(n - 2).wait())
        u_s[lax.rem(n, 2)] = dot(
            n2_s[:, columns(at.far_first(n))], dum_ref[...], ((0,), (0,))
        ).astype(BF16)
        keep_u(n).start()
        return carry

    def branch(o0):
        ends = o0 in (0, outer - 1)

        def between(k):
            if k == 0:
                if ends:
                    down.push(o0, down.order(o0)[outer - 2])
                    for d in gate.order(o0)[:-1]:
                        gate.push(o0, d)
                else:
                    for n in range(1, outer - 1):
                        down.step(o0, n)
                lax.fori_loop(0, outer, up_grad, 0)
            if k == outer - 1:
                down.absorb(o0, o0)
            if k == outer and not ends:
                for n in range(outer - 1):
                    gate.step(o0, n)

        line_gather(at, o0, dout_s, dout_ref, across, up, low, between)
        gate.absorb(o0, o0)
        down.finish(o0)
        gate.finish(o0)

    at.branches(branch)
    last = [
        pltpu.make_async_copy(down_own.at[at.o], down_ref, local.at[1]),
        pltpu.make_async_copy(gate_own.at[at.o], gate_ref, local.at[2]),
    ]
    for copy in last:
        copy.start()
    for n in range(max(outer - 2, 0), outer):
        keep_u(n).wait()
    grad.finish()
    keep.wait()
    for copy in last:
        copy.wait()


def turn(
    dgm, dum, mm, mid, cot, gain, wg, wu, wd, n2, cots, outer, inner, shards, collective
):
    rows, cols = mid.shape
    tokens, hidden = dgm.shape
    chips, span = inner * shards // 2, cols // outer
    buffers = pltpu.VMEM((1, chips, rows, cols), BF16)
    cut = first_half(hidden)
    down_vmem, reduce_sems = line_reduce_scratch(outer, span, hidden)
    gate_vmem, _ = line_reduce_scratch(outer, span, cut)
    return pl.pallas_call(
        functools.partial(turn_kernel, outer, inner, shards),
        out_shape=(
            jax.ShapeDtypeStruct((rows, cols), F32),
            jax.ShapeDtypeStruct((1, cols), F32),
            jax.ShapeDtypeStruct((outer * inner, rows, cols), BF16),
            jax.ShapeDtypeStruct((chips, 2 * rows, cols), BF16),
            jax.ShapeDtypeStruct((span, hidden), BF16),
            jax.ShapeDtypeStruct((span, cut), BF16),
            jax.ShapeDtypeStruct((outer, span, hidden - cut + LANES), BF16),
            jax.ShapeDtypeStruct((outer, span, hidden - LANES), BF16),
        ),
        in_specs=[IN_VMEM] * 6 + [IN_HBM] * 5,
        out_specs=[IN_VMEM] * 2 + [IN_HBM] * 6,
        scratch_shapes=[
            pltpu.VMEM((chips, 2 * rows, cols), BF16),
            pltpu.VMEM((2, 2 * rows, cols), BF16),
            pltpu.VMEM((rows, cols), BF16),
            pltpu.VMEM((16, cols), F32),
            pltpu.VMEM((cols, hidden), BF16),
            pltpu.VMEM((cols, hidden), BF16),
            pltpu.VMEM((hidden, cols), BF16),
            pltpu.VMEM((tokens, cols), BF16),
            pltpu.VMEM((tokens, cols), BF16),
            pltpu.VMEM((2, span, hidden), BF16),
            pltpu.VMEM((2, span, hidden - cut), BF16),
        ]
        + [buffers] * 3
        + down_vmem
        + gate_vmem
        + [DMA((2, 1, chips))] * 2
        + [DMA((2, outer))] * 3
        + reduce_sems * 2
        + [DMA((6,)), DMA((2,)), DMA((2, 2)), DMA((2,))],
        compiler_params=pltpu.CompilerParams(
            collective_id=collective, has_side_effects=True, vmem_limit_bytes=60 * 2**20
        ),
        cost_estimate=cost(110),
        name="turn",
    )(dgm, dum, mm, mid, cot, gain, wg, wu, wd, n2, cots)


def scan_backward_kernel(
    outer,
    inner,
    shards,
    quarters,
    chunk,
    blocks,
    block_width,
    dout_ref,
    wo_ref,
    proj_ref,
    h_ref,
    v_ref,
    par_ref,
    gates_ref,
    mid_ref,
    q_ref,
    rest_ref,
    both_ref,
    blocks_ref,
    totals_ref,
    result_ref,
    rest_out,
    q_s,
    near_in,
    far_in,
    far_out,
    rest_own,
    rest_land,
    near,
    far,
    q_sem,
    r_up,
    r_low,
    r_sem,
    dout_s,
    dz_s,
    sems,
    sums_ref,
    gate_grad_ref,
    a_s,
    g_s,
    t_s,
    h_pad,
    pre_s,
    dpre_s,
    dv_s,
    u_pad,
):
    length, width = h_ref.shape
    seg = length // SEGMENTS
    chunks = length // chunk

    def place(c):
        q = c // parts
        s = c - q * parts
        return pl.multiple_of((s * quarters + q) * chunk, chunk)

    def time_of(c):
        return pl.multiple_of(c * chunk, chunk)

    at = Place(outer, inner, shards)
    parts = at.parts
    rest = LineReduce(at, rest_own, rest_land, r_up, r_low)
    fetch = pltpu.make_async_copy(rest_ref, rest_own, r_sem)
    fetch.start()
    greet_with_line(at, [at.sibling] + [at.near(q)[0] for q in range(1, at.chips)])
    fetch.wait()

    def rest_early(o0):
        if o0 in (0, outer - 1):
            for d in rest.order(o0)[:-1]:
                rest.push(o0, d)

    def rest_step(n, o0):
        if 0 < o0 < outer - 1:
            rest.step(o0, n)

    def rest_last(o0):
        rest.absorb(o0, o0)
        rest.finish(o0)

    at.branches(rest_early)
    value = PlaneSum(at, 0, q_ref, near_in, far_in, far_out, near, far)

    def keep(q):
        return pltpu.make_async_copy(value.block(q, 0), q_s.at[q], q_sem.at[q])

    for q in reversed(range(at.chips)):
        value.to_sibling(q).start()
        keep(q).start()
    span = quarters * chunk

    def load(p):
        return pltpu.make_async_copy(
            dout_ref.at[p], dout_s.at[pl.ds(pl.multiple_of(p * span, span), span)], sems.at[p]
        )

    for p in range(parts):
        load(p).start()

    def back_project(k, carry):
        load(2 * k).wait()
        load(2 * k + 1).wait()
        some = pl.ds(pl.multiple_of(k * 2 * span, 2 * span), 2 * span)
        depth = wo_ref.shape[2]
        total = dot(dout_s[some, 0:depth], wo_ref[0], ((1,), (1,)))
        for p in range(1, wo_ref.shape[0]):
            lanes = slice(p * depth, (p + 1) * depth)
            total = total + dot(dout_s[some, lanes], wo_ref[p], ((1,), (1,)))
        dz_s[some, :] = total
        return carry

    lax.fori_loop(0, parts // 2, back_project, 0)
    for q in range(at.chips):
        keep(q).wait()
    value.combine(q_s)
    log_scale = -DECAY_SCALE * softplus(-par_ref[DECAY : DECAY + 1, :])
    bias = jnp.concatenate(
        [par_ref[RATE_B : RATE_B + 1, :], par_ref[ENTRY_B : ENTRY_B + 1, :]], axis=1
    )
    zeros8 = jnp.zeros((8, width), F32)
    put(a_s, pl.ds(length, 8), zeros8)
    h_pad[0:8, :] = zeros8
    u_pad[0:8, :] = zeros8
    dv_s[pl.ds(length, 8), :] = zeros8

    def first(c, carry):
        rows = pl.ds(time_of(c), chunk)
        later = pl.ds(pl.multiple_of(time_of(c) + 8, 8), chunk)
        there = pl.ds(place(c), chunk)
        h = h_ref[rows, :]
        h_pad[later, :] = h
        u_pad[later, :] = proj_ref[there, width : 2 * width].astype(BF16).astype(F32)
        y, slope = gelu_and_slope(proj_ref[there, 0:width])
        dz = dz_s[there, :]
        put(g_s, rows, (dz * y).astype(BF16).astype(F32))
        both_ref[there, 0:width] = (dz * h.astype(BF16).astype(F32) * slope).astype(BF16)
        pre = dot(v_ref[rows, :], gates_ref[...]) + bias
        pre_s[rows, :] = pre
        put(a_s, rows, jnp.exp(sigmoid(pre[:, :width]) * log_scale))
        return carry

    lax.fori_loop(0, chunks, first, 0)

    def load(g, i):
        return (
            a_s[g, pl.ds(i + 1, SEGMENTS, stride=seg), :],
            g_s[g, pl.ds(i, SEGMENTS, stride=seg), :],
        )

    def store(g, i, state, total):
        g_s[g, pl.ds(i, SEGMENTS, stride=seg), :] = state
        t_s[g, pl.ds(i, SEGMENTS, stride=seg), :] = total

    groups = width // LANES
    start = (jnp.zeros((SEGMENTS, LANES), F32), jnp.ones((SEGMENTS, LANES), F32))
    ends = lax.fori_loop(
        0,
        seg,
        strided_scan(lambda k: seg - 1 - k, groups, load, store),
        (start,) * groups,
        unroll=8,
    )
    firsts = jnp.concatenate([e[0] for e in ends], axis=1)
    totals = jnp.concatenate([e[1] for e in ends], axis=1)
    carries = [None] * SEGMENTS
    carries[SEGMENTS - 1] = jnp.zeros((1, width), F32)
    for j in range(SEGMENTS - 2, -1, -1):
        carries[j] = totals[j + 1 : j + 2] * carries[j + 1] + firsts[j + 1 : j + 2]

    def fold(values):
        return jnp.sum(values.reshape(chunk // 8, 8, values.shape[1]), axis=0)

    sums_ref[...] = jnp.zeros(sums_ref.shape, F32)

    for j in range(SEGMENTS):
        per = seg // chunk

        def middle(k, carry, j=j, per=per):
            c = j * per + k
            rows = pl.ds(time_of(c), chunk)
            g = take(g_s, rows) + take(t_s, rows) * carries[j]
            before = h_pad[pl.ds(time_of(c), chunk + 8), :][7 : 7 + chunk]
            v = v_ref[rows, :].astype(F32)
            r, e, a, room, m = gate_values(pre_s[rows, :], log_scale, width)
            gv = g * v
            held = jnp.where(room > MULT_FLOOR, gv * e * a / m, 0.0)
            ta = (g * before - held) * a * r
            drpre = (ta * (log_scale * (1.0 - r))).astype(BF16)
            depre = (gv * m * e * (1.0 - e)).astype(BF16)
            dpre_s[rows, 0:width] = drpre
            dpre_s[rows, width : 2 * width] = depre
            sums_ref[0:8, :] += fold(ta)
            sums_ref[8:16, :] += fold(drpre.astype(F32))
            sums_ref[16:24, :] += fold(depre.astype(F32))
            dv = g * m * e + dot(dpre_s[rows, :], gates_ref[...], ((1,), (1,)))
            dv_s[rows, :] = dv
            sums_ref[24:32, :] += fold(dv)
            wide = u_pad[pl.ds(time_of(c), chunk + 8), :]
            for tap in range(4):
                top = 32 + 8 * tap
                sums_ref[top : top + 8, :] += fold(dv * wide[8 - tap : 8 - tap + chunk])
            return carry

        lax.fori_loop(0, per, middle, 0)
        if j == 2:
            at.branches(functools.partial(rest_step, 0))
        if j == SEGMENTS - 2:
            at.branches(functools.partial(rest_step, 1))
    for n in range(2, outer - 1):
        at.branches(functools.partial(rest_step, n))
    sums_ref[0:8, :] = sums_ref[0:8, :] * (
        DECAY_SCALE * sigmoid(-par_ref[DECAY : DECAY + 1, :])
    )

    def last(c, carry):
        wide = dv_s[pl.ds(time_of(c), chunk + 8), :]
        du = par_ref[0:1, :] * wide[0:chunk]
        for tap in range(1, 4):
            du = du + par_ref[tap : tap + 1, :] * wide[tap : tap + chunk]
        both_ref[pl.ds(place(c), chunk), width : 2 * width] = du.astype(BF16)
        return carry

    lax.fori_loop(0, chunks, last, 0)
    gate_grad_ref[...] = dot(v_ref[...], dpre_s[...], ((0,), (0,)))
    blocks_ref[...] = jnp.zeros(blocks_ref.shape, F32)
    tall = blocks_ref.shape[0] // (2 * blocks)
    for gate in range(2):
        for j in range(blocks):
            top, lanes = (gate * blocks + j) * tall, gate * width + j * block_width
            rows = slice(j * block_width, (j + 1) * block_width)
            blocks_ref[top : top + block_width, :block_width] = gate_grad_ref[
                rows, lanes : lanes + block_width
            ]
    for k in range(8):
        totals_ref[k : k + 1, :] = jnp.sum(sums_ref[8 * k : 8 * k + 8, :], axis=0, keepdims=True)
    value.arrive()

    def output(rows):
        result_ref[rows, :] = (mid_ref[rows, :] + value.total(rows, q_s)).astype(BF16)

    add_rows(span, output)
    value.finish()
    at.branches(rest_last)
    out = pltpu.make_async_copy(rest_own.at[at.o], rest_out, r_sem)
    out.start()
    out.wait()


def scan_backward(
    quarters,
    chunk,
    blocks,
    block_width,
    dout,
    w_out,
    proj,
    h,
    v,
    params,
    gates,
    mid,
    q,
    rest,
    outer,
    inner,
    shards,
    collective,
):
    parts = dout.shape[0]
    rows, cols = mid.shape
    chips = q.shape[0]
    rest_vmem, rest_sems = line_reduce_scratch(*rest.shape)
    buffers = pltpu.VMEM((1, chips, rows, cols), BF16)
    length, width = h.shape
    tall, wide = -(-block_width // 8) * 8, -(-block_width // LANES) * LANES
    return pl.pallas_call(
        functools.partial(
            scan_backward_kernel, outer, inner, shards, quarters, chunk, blocks, block_width
        ),
        out_shape=(
            jax.ShapeDtypeStruct((length, 2 * width), BF16),
            jax.ShapeDtypeStruct((2 * blocks * tall, wide), F32),
            jax.ShapeDtypeStruct((8, width), F32),
            jax.ShapeDtypeStruct((rows, cols), BF16),
            jax.ShapeDtypeStruct(rest.shape[1:], BF16),
        ),
        in_specs=[IN_HBM] + [IN_VMEM] * 7 + [IN_HBM] * 2,
        out_specs=[IN_VMEM] * 4 + [IN_HBM],
        scratch_shapes=[
            pltpu.VMEM((chips, rows, cols), BF16),
            buffers,
            buffers,
            buffers,
            *rest_vmem,
            DMA((2, 1, chips)),
            DMA((2, 1, chips)),
            DMA((chips,)),
            *rest_sems,
            DMA,
            pltpu.VMEM((length, dout.shape[2]), BF16),
            pltpu.VMEM((length, width), F32),
            DMA((parts,)),
            pltpu.VMEM((64, width), F32),
            pltpu.VMEM((width, 2 * width), F32),
            pltpu.VMEM((width // LANES, length + 8, LANES), F32),
            pltpu.VMEM((width // LANES, length, LANES), F32),
            pltpu.VMEM((width // LANES, length, LANES), F32),
            pltpu.VMEM((length + 8, width), F32),
            pltpu.VMEM((length, 2 * width), F32),
            pltpu.VMEM((length, 2 * width), BF16),
            pltpu.VMEM((length + 8, width), F32),
            pltpu.VMEM((length + 8, width), F32),
        ],
        compiler_params=pltpu.CompilerParams(
            collective_id=collective, has_side_effects=True, vmem_limit_bytes=60 * 2**20
        ),
        cost_estimate=cost(21),
        name="scan_backward",
    )(dout, w_out, proj, h, v, params, gates, mid, q, rest)


def remote(src, dst, send, recv, to):
    return pltpu.make_async_remote_copy(
        src_ref=src, dst_ref=dst, send_sem=send, recv_sem=recv, device_id=to, device_id_type=MESH
    )


def add_rows(rows, fn):
    def one(k, carry):
        fn(pl.ds(pl.multiple_of(k * 16, 16), 16))
        return carry

    lax.fori_loop(0, rows // 16, one, 0)


class PlaneExchange:
    def __init__(self, at, n, x, out, sems, local):
        self.at, self.n, self.x, self.out, self.sems, self.local = at, n, x, out, sems, local
        _, self.me = at.near(0)
        self.hops = [(q, c) for q in reversed(range(1, at.chips)) for c in range(2)] + [(0, 1)]

    def rows(self, slot):
        piece = self.out.shape[1]
        return self.x.at[pl.ds(pl.multiple_of(slot * piece, piece), piece)]

    def mine(self):
        return pltpu.make_async_copy(self.rows(self.me), self.out.at[self.me], self.local)

    def start(self):
        self.send = Sent()
        for k, (q, other) in enumerate(self.hops):
            to, slot = self.at.near(q, other)
            self.send(self.rows(slot), self.out.at[self.me], self.sems, (self.n, k), to)
        self.mine().start()

    def finish(self):
        for k, (q, other) in enumerate(self.hops):
            source, slot = self.at.near(q, other, True)
            received(self.rows(self.me), self.out.at[slot], self.sems, (self.n, k), source)
        self.send.finish()
        self.mine().wait()


def closing_kernel(
    outer,
    inner,
    shards,
    both_ref,
    wi_ref,
    z_ref,
    x_ref,
    dmid_ref,
    gain_ref,
    gain2_ref,
    blocks_ref,
    sums_ref,
    n1_ref,
    dout_ref,
    down_ref,
    gate_ref,
    rest_ref,
    up_ref,
    grad_ref,
    mix_ref,
    blocks_out,
    sums_out,
    gains_out,
    down_out,
    gate_out,
    rest_out,
    up_out,
    p_s,
    up_own,
    up_land,
    up_sum,
    n1_s,
    dout_s,
    g_s,
    gain_s,
    gain_rows,
    gain_slots,
    near_in,
    far_in,
    far_out,
    done,
    block_slots,
    sum_slots,
    x_in,
    up_in,
    down_in,
    line_out,
    across,
    up,
    low,
    near,
    far,
    final,
    s_far,
    s_near,
    swap,
    g_sem,
    stripe,
    u_up,
    u_low,
    local,
):
    at = Place(outer, inner, shards)
    s, h, parts, ys = at.s, at.h, at.parts, at.ys
    steps = list(range(1, ys))
    line = LineSum(at, p_s, (x_in, up_in, down_in, line_out), (across, up, low))
    model = x_ref.shape[1]
    tile = min(512, model)
    piece = done.shape[1]
    span = shards * piece
    width2 = both_ref.shape[1]
    me = s * shards + h
    small = ((blocks_ref, block_slots, blocks_out), (sums_ref, sum_slots, sums_out))
    fetch = pltpu.make_async_copy(up_ref, up_own, local.at[0])
    fetch.start()

    def stripes(k):
        lanes = pl.ds(pl.multiple_of(owner(k) * span, span), span)
        slot = lax.rem(k, 2)
        return (
            pltpu.make_async_copy(n1_ref.at[:, lanes], n1_s.at[slot], stripe.at[0, slot]),
            pltpu.make_async_copy(dout_ref.at[:, lanes], dout_s.at[slot], stripe.at[1, slot]),
        )

    def owner(k):
        return lax.rem(s + k + 1, parts)

    for copy in stripes(0):
        copy.start()

    def anyone(k):
        to = lax.rem(me + k, at.count)
        return (to // shards, lax.rem(to, shards)), to

    def greet_one(k, carry):
        hello(anyone(k)[0])
        return carry

    lax.fori_loop(1, at.count, greet_one, 0)
    welcome(at.count - 1)
    ups = LineReduce(at, up_own, up_land, u_up, u_low)
    fetch.wait()

    ups.early(0, at.far_first(0), min(1, outer - 2))

    def back(n, carry):
        d = at.far_first(n)
        rows = pl.ds(pl.multiple_of(d * p_s.shape[1], p_s.shape[1]), p_s.shape[1])
        for lane in range(0, model, tile):
            lanes = slice(lane, lane + tile)
            p_s[d, :, lanes] = dot(both_ref[rows, :], wi_ref[lanes, :], ((1,), (1,))).astype(BF16)
        line.cross(d).start()
        return carry

    lax.fori_loop(0, outer, back, 0)
    send = Sent()
    for n, (src, slots, _) in enumerate(small):
        for dy in steps:
            send(src, slots.at[h], s_far, (n, dy), (s, at.along(dy)))
        send(src, slots.at[h], s_near, (n, 0), at.sibling)
        slots[h] = src[...]

    def mix_rows(p, shard):
        return g_s.at[p, pl.ds(pl.multiple_of(shard * piece, piece), piece)]

    def to_sibling(k, dy):
        p = owner(k)
        return remote(
            mix_rows(p, at.along(dy, 1)),
            near_in.at[dy, p],
            near.at[0, dy, k],
            near.at[1, dy, k],
            at.sibling,
        )

    def to_shard(k, dy, source=False):
        p = owner(k)
        return remote(
            far_out.at[dy - 1, p],
            far_in.at[dy - 1, p],
            far.at[0, dy, k],
            far.at[1, dy, k],
            (s, at.along(-dy if source else dy)),
        )

    def to_owner(k, source=False):
        p = lax.rem(s + parts - k - 1, parts) if source else owner(k)
        return remote(
            done.at[owner(k)],
            mix_ref.at[p if source else s],
            final.at[0, k],
            final.at[1, k],
            (p, h),
        )

    def weight_grads(k, carry):
        p, slot = owner(k), lax.rem(k, 2)
        for copy in stripes(k):
            copy.wait()

        @pl.when(k < parts - 1)
        def _():
            for copy in stripes(k + 1):
                copy.start()

        g_s[p, :, 0:width2] = dot(n1_s[slot], both_ref[...], ((0,), (0,))).astype(BF16)
        g_s[p, :, width2:] = dot(dout_s[slot], z_ref[...], ((0,), (0,))).astype(BF16)
        for dy in steps + [0]:
            to_sibling(k, dy).start()
        return carry

    lax.fori_loop(0, parts, weight_grads, 0)
    exchanges = [
        PlaneExchange(at, 0, down_ref, down_out, swap, local.at[2]),
        PlaneExchange(at, 1, gate_ref, gate_out, swap, local.at[3]),
        PlaneExchange(at, 3, rest_ref, rest_out, swap, local.at[5]),
    ]
    up_exchange = PlaneExchange(at, 2, up_sum, up_out, swap, local.at[1])

    def sibling_sums(k, carry):
        p = owner(k)
        for dy in steps:
            to_sibling(k, dy).wait_recv()
            mine = mix_rows(p, at.along(dy))

            def add(rows, dy=dy, mine=mine):
                total = mine[rows, :].astype(F32) + near_in[dy, p, rows, :].astype(F32)
                far_out[dy - 1, p, rows, :] = total.astype(BF16)

            add_rows(piece, add)
            to_shard(k, dy).start()
        return carry

    lax.fori_loop(0, parts, sibling_sums, 0)
    for exchange in exchanges:
        exchange.start()
    gain_s[...] = jnp.zeros(gain_s.shape, F32)

    def mix_step(k):
        p = owner(k)
        mine = mix_rows(p, h)
        to_sibling(k, 0).wait_recv()
        for dy in steps:
            to_shard(k, dy, True).wait_recv()

        def add(rows):
            total = mine[rows, :].astype(F32) + near_in[0, p, rows, :].astype(F32)
            for dy in steps:
                total = total + far_in[dy - 1, p, rows, :].astype(F32)
            done[p, rows, :] = total.astype(BF16)

        add_rows(piece, add)
        if k < parts - 1:
            to_owner(k).start()

    def last_add(rows, dn1):
        x = x_ref[rows, :].astype(F32)
        scale = row_rms(x)
        gain_s[...] += dn1 * x * scale
        grad_ref[rows, :] = dmid_ref[rows, :] + rms_back(x, scale, gain_ref[...], dn1)

    def branch(o0):
        ends = o0 in (0, outer - 1)

        sooner = min(1, outer - 2) if ends else 0

        def between(n):
            if n + sooner < outer - 1 and ends:
                ups.push(o0, ups.order(o0)[n + sooner])
            for k in range(n * inner, (n + 1) * inner):
                mix_step(k)
            if n + 1 < outer - 1 and not ends:
                ups.step(o0, n + 1)

        if not ends:
            ups.step(o0, 0)
        line.steps(o0, last_add, between)

    at.branches(branch)
    keep = pltpu.make_async_copy(done.at[s], mix_ref.at[s], local.at[4])
    keep.start()
    gain1, gain2 = jnp.sum(gain_s[...], axis=0, keepdims=True), gain2_ref[...]
    spare = gain_rows.shape[2] - 2 * piece
    for k in range(at.count):
        lanes = slice(k * piece, (k + 1) * piece)
        parts_of = [gain1[:, lanes], gain2[:, lanes]]
        if spare:
            parts_of.append(jnp.zeros((1, spare), F32))
        gain_rows[k] = jnp.concatenate(parts_of, axis=1)

    def gain(k):
        to, row = anyone(k)
        return remote(gain_rows.at[row], gain_slots.at[k], g_sem.at[0, k], g_sem.at[1, k], to)

    def gain_start(k, carry):
        gain(k).start()
        return carry

    def gain_arrive(k, total):
        gain(k).wait_recv()
        return total + gain_slots[k]

    def gain_leave(k, carry):
        gain(k).wait_send()
        return carry

    lax.fori_loop(1, at.count, gain_start, 0)

    def last_up(o0):
        ups.absorb(o0, o0)
        ups.finish(o0)

    at.branches(last_up)

    def keep_up(rows):
        up_sum[rows, :] = up_own[at.o, rows, :]

    add_rows(up_sum.shape[0], keep_up)
    up_exchange.start()
    for n, (src, slots, out) in enumerate(small):
        for dy in steps:
            here = slots.at[at.along(-dy)]
            received(src, here, s_far, (n, dy), (s, at.along(-dy)))
            send(here, here, s_near, (n, dy), at.sibling)
    for n, (src, slots, out) in enumerate(small):
        for dy in range(ys):
            received(src, slots.at[at.along(-dy, 1)], s_near, (n, dy), at.sibling)

        def add(k, carry, slots=slots, out=out):
            rows = pl.ds(pl.multiple_of(k * 8, 8), 8)
            total = slots[0, rows, :]
            for j in range(1, shards):
                total = total + slots[j, rows, :]
            out[rows, :] = total
            return carry

        lax.fori_loop(0, src.shape[0] // 8, add, 0)
    gains_out[...] = lax.fori_loop(1, at.count, gain_arrive, gain_rows[me])
    for k in range(parts - 1):
        to_owner(k, True).wait_recv()
    for exchange in exchanges + [up_exchange]:
        exchange.finish()
    for k in range(parts):
        for dy in range(ys):
            to_sibling(k, dy).wait_send()
        for dy in steps:
            to_shard(k, dy).wait_send()
        if k < parts - 1:
            to_owner(k).wait_send()
    lax.fori_loop(1, at.count, gain_leave, 0)
    send.finish()
    keep.wait()


def closing(
    both,
    w_in,
    z,
    x,
    dmid,
    gain,
    gain2,
    small,
    sums,
    n1,
    dout,
    down,
    gate,
    rest,
    ups,
    outer,
    inner,
    shards,
    collective,
):
    rows, cols = x.shape
    parts, ys, count = outer * inner, shards // 2, outer * inner * shards
    piece = cols // count
    width = z.shape[1]
    lanes = -(-2 * piece // LANES) * LANES
    bufs, sems = line_sum_scratch(outer, rows, cols)
    pieces = pltpu.VMEM((max(ys - 1, 1), parts, piece, 3 * width), BF16)
    stripes = pltpu.VMEM((2, parts * rows, cols // parts), BF16)
    span, hidden = ups.shape[1:]

    def swapped(array):
        shape = (inner * shards, span // (inner * shards), array.shape[-1])
        return jax.ShapeDtypeStruct(shape, BF16)

    reduce_vmem, reduce_sems = line_reduce_scratch(outer, span, hidden)
    return pl.pallas_call(
        functools.partial(closing_kernel, outer, inner, shards),
        out_shape=(
            jax.ShapeDtypeStruct((rows, cols), F32),
            jax.ShapeDtypeStruct((parts, piece, 3 * width), BF16),
            jax.ShapeDtypeStruct(small.shape, F32),
            jax.ShapeDtypeStruct(sums.shape, F32),
            jax.ShapeDtypeStruct((1, lanes), F32),
            *[swapped(array) for array in (down, gate, rest, ups)],
        ),
        in_specs=[IN_VMEM] * 9 + [IN_HBM] * 6,
        out_specs=[IN_VMEM] * 5 + [IN_HBM] * 4,
        scratch_shapes=[
            pltpu.VMEM((outer, inner * rows, cols), BF16),
            *reduce_vmem,
            pltpu.VMEM((span, hidden), BF16),
            stripes,
            stripes,
            pltpu.VMEM((parts, shards * piece, 3 * width), BF16),
            pltpu.VMEM((16, cols), F32),
            pltpu.VMEM((count, 1, lanes), F32),
            pltpu.VMEM((count, 1, lanes), F32),
            pltpu.VMEM((ys, parts, piece, 3 * width), BF16),
            pieces,
            pieces,
            pltpu.VMEM((parts, piece, 3 * width), BF16),
            pltpu.VMEM((shards,) + small.shape, F32),
            pltpu.VMEM((shards,) + sums.shape, F32),
        ]
        + bufs
        + sems
        + [DMA((2, ys, parts))] * 2
        + [DMA((2, parts))]
        + [DMA((2, 2, ys))] * 2
        + [DMA((2, 4, inner * shards)), DMA((2, count)), DMA((2, 2))]
        + reduce_sems
        + [DMA((6,))],
        compiler_params=pltpu.CompilerParams(
            collective_id=collective, has_side_effects=True, vmem_limit_bytes=60 * 2**20
        ),
        cost_estimate=cost(80),
        name="closing",
    )(
        both,
        w_in,
        z,
        x,
        dmid,
        gain,
        gain2,
        small,
        sums,
        n1,
        dout,
        down,
        gate,
        rest,
        ups,
    )


def unpack_kernel(inner, channels, block_width, *refs):
    sources, targets = refs[:10], refs[10:27]
    held, made, in_sem, out_sem = refs[27:36], refs[36:42], refs[42], refs[43]
    gate_ref, rest_ref, up_ref, down_ref, mix_ref, blocks_ref, sums_ref = held[:7]
    fetch = [
        pltpu.make_async_copy(sources[k], held[k], in_sem.at[k]) for k in range(len(held))
    ]
    for copy in fetch:
        copy.start()
    store = []
    gains_ref = sources[9]
    rate, entry, taps, conv_b, rate_b, entry_b, decay, first_gain, second_gain = targets[8:]
    for copy in fetch:
        copy.wait()
    for k in range(2):
        copy = pltpu.make_async_copy(held[7 + k], targets[6 + k], out_sem.at[6 + k])
        copy.start()
        store.append(copy)
    gate, up, down = made[:3]
    slots, piece, hidden = down_ref.shape
    cut = gate_ref.shape[2]
    tail = hidden - cut
    head = hidden - up_ref.shape[2]
    shards = slots // inner
    parts, width = mix_ref.shape[0], mix_ref.shape[2] // 3
    places = [
        ((h * inner + i) * hidden, i * shards + h) for i in range(inner) for h in range(shards)
    ]

    def ship(k):
        copy = pltpu.make_async_copy(made[k], targets[k], out_sem.at[k])
        copy.start()
        store.append(copy)

    for first, slot in places:
        gate[:, first : first + cut] = gate_ref[slot].astype(F32)
        gate[:, first + cut : first + hidden] = rest_ref[slot][:, :tail].astype(F32)
    ship(0)
    for first, slot in places:
        up[:, first : first + head] = rest_ref[slot][:, tail:].astype(F32)
        up[:, first + head : first + hidden] = up_ref[slot].astype(F32)
    ship(1)
    for first, slot in places:
        down[:, first : first + hidden] = down_ref[slot].astype(F32)
    ship(2)
    for k in range(3):
        lanes = slice(k * width, k * width + width)
        made[3 + k][...] = jnp.concatenate(
            [mix_ref[p][:, lanes].astype(F32)[:, :channels] for p in range(parts)], axis=1
        )
        ship(3 + k)
    blocks = rate.shape[1]
    tall = blocks_ref.shape[0] // (2 * blocks)
    for k, dst in enumerate((rate, entry)):
        for j in range(blocks):
            top = (k * blocks + j) * tall
            dst[:, j, :] = blocks_ref[top : top + block_width, :block_width]
    taps[...] = sums_ref[4:8, :channels]
    for row, dst in ((3, conv_b), (1, rate_b), (2, entry_b), (0, decay)):
        dst[...] = sums_ref[row, :channels]
    first_gain[...] = gains_ref[0, :piece]
    second_gain[...] = gains_ref[0, piece : 2 * piece]
    for copy in store:
        copy.wait()


def unpack(
    gate, rest, up, down, mix, small, sums, result, grad, gains, inner, channels, blocks, block_width
):
    slots, piece, hidden = down.shape
    across = jax.ShapeDtypeStruct((piece, slots * hidden), F32)
    wide = jax.ShapeDtypeStruct((piece, mix.shape[0] * channels), F32)
    square = jax.ShapeDtypeStruct((block_width, blocks, block_width), F32)
    vector = jax.ShapeDtypeStruct((channels,), F32)
    taps = jax.ShapeDtypeStruct((4, channels), F32)
    gain = jax.ShapeDtypeStruct((piece,), F32)
    held = (gate, rest, up, down, mix, small, sums, result, grad)
    made = (across,) * 3 + (wide,) * 3
    return pl.pallas_call(
        functools.partial(unpack_kernel, inner, channels, block_width),
        out_shape=made
        + tuple(jax.ShapeDtypeStruct(x.shape, x.dtype) for x in (result, grad))
        + (square,) * 2
        + (taps,)
        + (vector,) * 4
        + (gain,) * 2,
        in_specs=[IN_HBM] * 9 + [IN_VMEM],
        out_specs=[IN_HBM] * 8 + [IN_VMEM] * 9,
        scratch_shapes=[pltpu.VMEM(x.shape, x.dtype) for x in held + made]
        + [DMA((len(held),)), DMA((8,))],
        compiler_params=pltpu.CompilerParams(vmem_limit_bytes=60 * 2**20),
        cost_estimate=cost(5),
        name="unpack",
    )(*held, gains)


def body(
    tokens,
    first_gain,
    branch_weight,
    input_weight,
    conv_weight,
    conv_bias,
    rate_weight,
    rate_bias,
    entry_weight,
    entry_bias,
    decay_param,
    output_weight,
    second_gain,
    hidden_gate,
    hidden_up,
    hidden_down,
    cotangent,
):
    quarters, _, chunk, model = tokens.shape
    rows = quarters * chunk
    parts = lax.axis_size("seq")
    shards = lax.axis_size("shard")
    inner = 2
    outer = parts // inner
    seq_at = lax.axis_index("seq")
    inner_at = lax.rem(seq_at, inner)
    lru = branch_weight.shape[1]
    channels = lru // parts
    width = (channels + LANES) // LANES * LANES
    spare = width - channels
    blocks, block_width = rate_weight.shape[0], rate_weight.shape[1]
    piece = model // (parts * shards)

    def own(weight, axis):
        part = lax.dynamic_slice_in_dim(weight, seq_at * channels, channels, axis)
        pads = [(0, 0), (0, 0)]
        pads[axis] = (0, spare)
        return jnp.pad(part, pads)

    x = tokens.reshape(rows, model)
    cot = cotangent.reshape(rows, model)
    gain1, gain2 = first_gain[None], second_gain[None]
    params, mid, z, h, v, proj, gates, n1, w_in, w_out, n2, cot_all = forward(
        x,
        gain1,
        gain2,
        (conv_weight, conv_bias, rate_bias, entry_bias, decay_param),
        rate_weight.transpose(1, 0, 2),
        entry_weight.transpose(1, 0, 2),
        cot,
        jnp.concatenate([own(branch_weight, 1), own(input_weight, 1)], axis=1),
        own(output_weight, 0),
        quarters,
        chunk,
        outer,
        inner,
        shards,
        0,
    )
    w_in = w_in.reshape(model, 2 * width)
    n2 = n2.reshape(inner * shards * rows, model)
    cot_all = cot_all.reshape(inner * shards * rows, model)
    hidden = hidden_gate.shape[1] // inner
    wg = lax.dynamic_slice_in_dim(hidden_gate, inner_at * hidden, hidden, 1)
    wu = lax.dynamic_slice_in_dim(hidden_up, inner_at * hidden, hidden, 1)
    wd = lax.dynamic_slice_in_dim(hidden_down, inner_at * hidden, hidden, 0)

    gm = dot(n2, wg)
    um = dot(n2, wu)
    act, slope = gelu_and_slope(gm)
    mm = (act * um).astype(BF16)
    dmm = dot(cot_all, wd, ((1,), (1,)))
    dgm = (dmm * um * slope).astype(BF16)
    dum = (dmm * act).astype(BF16)
    dmid, gain2_grad, dout, partial, down_sum, gate_sum, rest_terms, up_terms = turn(
        dgm,
        dum,
        mm,
        mid,
        cot,
        gain2,
        hidden_gate,
        hidden_up,
        hidden_down,
        n2,
        cot_all,
        outer,
        inner,
        shards,
        1,
    )
    both, small, sums, result, rest_sum = scan_backward(
        quarters,
        chunk,
        blocks,
        block_width,
        dout,
        w_out,
        proj,
        h,
        v,
        params,
        gates,
        mid,
        partial,
        rest_terms,
        outer,
        inner,
        shards,
        2,
    )
    tokens_grad, mix, small, sums, gains, down_sum, gate_sum, rest_sum, up_sum = closing(
        both,
        w_in,
        z,
        x,
        dmid,
        gain1,
        gain2_grad,
        small,
        sums,
        n1.reshape(parts * rows, model),
        dout.reshape(parts * rows, model),
        down_sum,
        gate_sum,
        rest_sum,
        up_terms,
        outer,
        inner,
        shards,
        3,
    )
    (
        gate_grad,
        up_grad,
        down_grad,
        branch_grad,
        input_grad,
        output_grad,
        result,
        tokens_grad,
        rate_grad,
        entry_grad,
        tap_grad,
        conv_bias_grad,
        rate_bias_grad,
        entry_bias_grad,
        decay_grad,
        gain1_grad,
        gain2_grad,
    ) = unpack(
        gate_sum,
        rest_sum,
        up_sum,
        down_sum,
        mix,
        small,
        sums,
        result,
        tokens_grad,
        gains,
        inner,
        channels,
        blocks,
        block_width,
    )
    return (
        result.reshape(tokens.shape),
        tokens_grad.reshape(tokens.shape),
        gain1_grad,
        branch_grad,
        input_grad,
        tap_grad,
        conv_bias_grad,
        rate_grad.transpose(1, 0, 2),
        rate_bias_grad,
        entry_grad.transpose(1, 0, 2),
        entry_bias_grad,
        decay_grad,
        output_grad.T,
        gain2_grad,
        gate_grad,
        up_grad,
        down_grad.T,
    )


def solution(mesh):
    placed = (
        P(None, "shard", "seq", None),
        P(),
        P("shard", None),
        P("shard", None),
        P(None, "seq"),
        P("seq"),
        P("seq", None, None),
        P("seq"),
        P("seq", None, None),
        P("seq"),
        P("seq"),
        P(None, "shard"),
        P(),
        P(None, "shard"),
        P(None, "shard"),
        P("shard", None),
        P(None, "shard", "seq", None),
    )
    return jax.shard_map(
        body,
        mesh=mesh,
        in_specs=placed,
        out_specs=(
            P(None, "shard", "seq", None),
            P(None, "shard", "seq", None),
            P(("seq", "shard")),
            P(("seq", "shard"), None),
            P(("seq", "shard"), None),
            P(None, "seq"),
            P("seq"),
            P("seq", None, None),
            P("seq"),
            P("seq", None, None),
            P("seq"),
            P("seq"),
            P(None, ("seq", "shard")),
            P(("seq", "shard")),
            P(("seq", "shard"), None),
            P(("seq", "shard"), None),
            P(None, ("seq", "shard")),
        ),
        check_vma=False,
    )
```

```python
import functools

import jax
import jax.numpy as jnp
from jax import lax
from jax.experimental import pallas as pl
from jax.experimental.pallas import tpu as pltpu
from jax.sharding import PartitionSpec as P

EPSILON = 1e-06
DECAY_SCALE = 8.0
MULT_FLOOR = 0.01
LANES = 128
SEGMENTS = 8
GELU_C = 0.7978845608028654
GELU_A = 0.044715
F32 = jnp.float32
BF16 = jnp.bfloat16


MESH = pl.DeviceIdType.MESH
IN_HBM = pl.BlockSpec(memory_space=pltpu.HBM)
IN_VMEM = pl.BlockSpec(memory_space=pltpu.VMEM)
DMA = pltpu.SemaphoreType.DMA


def cost(us):
    return pl.CostEstimate(flops=0, bytes_accessed=int(us * 3.3e6), transcendentals=0)


def dot(left, right, dims=((1,), (0,))):
    return lax.dot_general(left, right, (dims, ((), ())), preferred_element_type=F32)


def gelu_and_slope(x):
    inner = GELU_C * (x + GELU_A * x * x * x)
    t = jnp.tanh(inner)
    half = 0.5 * (1.0 + t)
    slope = half + 0.5 * x * (1.0 - t * t) * (GELU_C * (1.0 + 3.0 * GELU_A * x * x))
    return x * half, slope


def gelu_tanh(x):
    return x * (0.5 * (1.0 + jnp.tanh(GELU_C * (x + GELU_A * x * x * x))))


def sigmoid(x):
    return 0.5 * jnp.tanh(0.5 * x) + 0.5


def softplus(x):
    return jnp.maximum(x, 0.0) + jnp.log1p(jnp.exp(-jnp.abs(x)))


def lane_groups(width):
    return [slice(g * LANES, (g + 1) * LANES) for g in range(width // LANES)]


def put(ref, rows, value):
    for g, lanes in enumerate(lane_groups(value.shape[1])):
        ref[g, rows, :] = value[:, lanes]


def take(ref, rows):
    return jnp.concatenate([ref[g, rows, :] for g in range(ref.shape[0])], axis=1)


def strided_scan(steps, groups, load, store):
    def step(k, carry):
        i = steps(k)
        out = []
        for g in range(groups):
            state, total = carry[g]
            factor, term = load(g, i)
            state = factor * state + term
            total = factor * total
            store(g, i, state, total)
            out.append((state, total))
        return tuple(out)

    return step


TAP, CONV_B, RATE_B, ENTRY_B, DECAY = 0, 4, 5, 6, 7


def gate_values(pre, log_scale, width):
    r = sigmoid(pre[:, :width])
    e = sigmoid(pre[:, width:])
    a = jnp.exp(r * log_scale)
    room = 1.0 - a * a
    m = jnp.sqrt(jnp.maximum(room, MULT_FLOOR))
    return r, e, a, room, m


class Place:
    def __init__(self, outer, inner, shards):
        self.outer, self.inner, self.shards = outer, inner, shards
        self.parts, self.ys, self.count = outer * inner, shards // 2, outer * inner * shards
        self.chips = inner * self.ys
        self.s, self.h = lax.axis_index("seq"), lax.axis_index("shard")
        self.o, self.i = self.s // inner, lax.rem(self.s, inner)
        self.y, self.core = self.h // 2, lax.rem(self.h, 2)
        self.beside = (self.o * inner + 1 - self.i, self.h)
        self.above, self.below = (self.s + inner, self.h), (self.s - inner, self.h)
        self.sibling = (self.s, self.along(0, 1))

    def along(self, dy, other=0):
        y = lax.rem(self.y + dy + self.ys, self.ys)
        return y * 2 + lax.rem(self.core + other, 2)

    def chip(self, q, back=False):
        di, dy = q // self.ys, q - q // self.ys * self.ys
        if back:
            di, dy = self.inner - di, self.ys - dy
        return lax.rem(self.i + di, self.inner), lax.rem(self.y + dy, self.ys)

    def near(self, q, other=0, back=False):
        i, y = self.chip(q, back)
        h = y * 2 + lax.rem(self.core + other, 2)
        return (self.o * self.inner + i, h), i * self.shards + h

    def far_first(self, n):
        sign = 2 * ((2 * self.o) // self.outer) - 1
        return lax.rem(self.o + sign * (n + 1) + 2 * self.outer, self.outer)

    def branches(self, fn):
        for o0 in range(self.outer):
            pl.when(self.o == o0)(functools.partial(fn, o0))


def hello(to):
    barrier = pltpu.get_barrier_semaphore()
    pl.semaphore_signal(barrier, inc=1, device_id=to, device_id_type=MESH)


def welcome(n):
    pl.semaphore_wait(pltpu.get_barrier_semaphore(), n)


def greet(others):
    for to in others:
        hello(to)
    welcome(len(others))


def greet_with_line(at, others):
    up, down = at.o < at.outer - 1, at.o > 0
    for to in others:
        hello(to)
    pl.when(up)(lambda: hello(at.above))
    pl.when(down)(lambda: hello(at.below))
    ends = lax.rem(at.o, at.outer - 1) == 0
    pl.when(ends)(lambda: welcome(len(others) + 1))
    pl.when(jnp.logical_not(ends))(lambda: welcome(len(others) + 2))


class Sent:
    def __init__(self):
        self.copies = []

    def __call__(self, src, dst, sems, at, to):
        copy = remote(src, dst, sems.at[(0,) + at], sems.at[(1,) + at], to)
        copy.start()
        self.copies.append(copy)

    def finish(self):
        for copy in self.copies:
            copy.wait_send()


def received(like, here, sems, at, source):
    remote(like, here, sems.at[(0,) + at], sems.at[(1,) + at], source).wait_recv()


def line_gather(
    at,
    o0,
    x_ref,
    out,
    across,
    up,
    down,
    between=lambda k: None,
    each=lambda row: None,
    side=None,
    slim=0,
):
    send = Sent()
    rows = x_ref.shape[0]
    half = rows // HALVES
    low = pl.ds(rows - slim, slim)

    def slot(row, other=False):
        return out.at[row * at.inner + (1 - at.i if other else at.i)]

    def some(row, part):
        less = slim if slim and row != o0 and part == HALVES - 1 else 0
        return pl.ds(part * half, half - less)

    def pass_on(row, part, sems, to):
        some_rows = pl.ds(part * half, half)
        src = x_ref if row == o0 else slot(row)
        send(src.at[some_rows], slot(row).at[some_rows], sems, (row, part), to)

    def cross(row, part):
        src = x_ref if row == o0 else slot(row)
        send(src.at[some(row, part)], slot(row).at[some(row, part)], across, (row, part), at.beside)

    def crossed(row):
        for part in range(HALVES):
            here = slot(row, True).at[some(row, part)]
            received(here, here, across, (row, part), at.beside)

    def slim_on(row):
        here = slot(row, True).at[low]
        if row <= o0 < at.outer - 1:
            send(here, here, side[0], (row,), at.above)
        if row >= o0 > 0:
            send(here, here, side[1], (row,), at.below)

    def slim_came(row, sems, source):
        here = slot(row, True).at[low]
        received(here, here, sems, (row,), source)

    for k in range(at.outer):
        lower, upper = o0 - k, o0 + k
        for part in range(HALVES):
            here = x_ref.at[pl.ds(part * half, half)]
            if lower >= 0:
                if k > 0:
                    received(here, here, up, (lower, part), at.below)
                if o0 < at.outer - 1:
                    pass_on(lower, part, up, at.above)
                cross(lower, part)
            if upper < at.outer:
                if k > 0:
                    received(here, here, down, (upper, part), at.above)
                if o0 > 0:
                    pass_on(upper, part, down, at.below)
                if k > 0:
                    cross(upper, part)
        if slim and k == 1:
            crossed(o0)
            slim_on(o0)
        if slim and k > 1:
            for row, sems, source in (
                (o0 - k + 1, side[0], at.below),
                (o0 + k - 1, side[1], at.above),
            ):
                if 0 <= row < at.outer:
                    slim_came(row, sems, source)
                    slim_on(row)
        between(k)
    between(at.outer)
    for row in sorted(range(at.outer), key=lambda row: abs(row - o0)):
        if row != o0 or not slim:
            crossed(row)
        if slim and row != o0 and abs(row - o0) == at.outer - 1:
            slim_came(row, side[0] if row < o0 else side[1], at.below if row < o0 else at.above)
        each(row)
    send.finish()


class LineSum:
    def __init__(self, at, p, bufs, sems, side=None):
        self.at, self.p = at, p
        self.x_in, self.up_in, self.down_in, self.sums = bufs
        self.across, self.up, self.down = sems
        self.rows = self.x_in.shape[1]
        self.slim = 0
        if side is not None:
            self.s_up_in, self.s_down_in, self.s_sums, self.s_in = side[:4]
            self.s_up, self.s_down, self.s_across = side[4:]
            self.slim = self.s_in.shape[0]

    def block(self, d, i):
        return self.p.at[d, pl.ds(pl.multiple_of(i * self.rows, self.rows), self.rows)]

    def cross(self, d, part):
        half = self.rows // HALVES
        some = pl.ds(part * half, half - (self.slim if part == HALVES - 1 else 0))
        return remote(
            self.block(d, 1 - self.at.i).at[some],
            self.x_in.at[d].at[some],
            self.across.at[0, d, part],
            self.across.at[1, d, part],
            self.at.beside,
        )

    def start(self, d):
        for part in range(HALVES):
            self.cross(d, part).start()

    def steps(self, o0, last_add, between=lambda n: None):
        at, rows, slim = self.at, self.rows, self.slim
        send = Sent()
        order = sorted(range(at.outer), key=lambda d: (-abs(d - o0), d))
        low, half = rows - slim, rows // HALVES

        def arrivals(d, index, mine, up_in, down_in, up, down):
            terms = []
            if d >= o0 > 0:
                received(mine, mine, up, index, at.below)
                terms.append(up_in.at[d])
            if d <= o0 < at.outer - 1:
                received(mine, mine, down, index, at.above)
                terms.append(down_in.at[d])
            return terms

        def total_of(terms, some):
            total = terms[0][some, :].astype(F32)
            for term in terms[1:]:
                total = total + term[some, :].astype(F32)
            return total

        for n, d in enumerate(order):
            mine = self.block(d, at.i)
            target = self.sums.at[d]
            for part in range(HALVES):
                part_rows = pl.ds(part * half, half)
                self.cross(d, part).wait_recv()
                along = [mine] + arrivals(
                    d,
                    (d, part),
                    mine.at[part_rows],
                    self.up_in,
                    self.down_in,
                    self.up,
                    self.down,
                )
                both = along + [self.x_in.at[d]]

                def add(some, both=both, target=target, d=d):
                    total = total_of(both, some)
                    if d == o0:
                        last_add(some, total)
                    else:
                        target[some, :] = total.astype(BF16)

                def add_low(some, along=along, target=target):
                    target[some, :] = total_of(along, some).astype(BF16)

                add_rows(min((part + 1) * half, low), add, part * half)
                if slim and d != o0 and part == HALVES - 1:
                    add_rows(rows, add_low, low)
                if d > o0:
                    here, there = target.at[part_rows], self.up_in.at[d].at[part_rows]
                    send(here, there, self.up, (d, part), at.above)
                if d < o0:
                    here, there = target.at[part_rows], self.down_in.at[d].at[part_rows]
                    send(here, there, self.down, (d, part), at.below)
            if slim:
                theirs = self.block(d, 1 - at.i).at[pl.ds(low, slim)]
                extra = [theirs] + arrivals(
                    d, (d,), theirs, self.s_up_in, self.s_down_in, self.s_up, self.s_down
                )
                aside = self.s_sums.at[d]

                def add_aside(some, extra=extra, aside=aside):
                    aside[some, :] = total_of(extra, some).astype(BF16)

                add_rows(slim, add_aside)
                if d > o0:
                    send(aside, self.s_up_in.at[d], self.s_up, (d,), at.above)
                if d < o0:
                    send(aside, self.s_down_in.at[d], self.s_down, (d,), at.below)
                if d == o0:
                    send(aside, self.s_in, self.s_across, (), at.beside)
                    received(aside, self.s_in, self.s_across, (), at.beside)
                    for k in range(slim // 16):
                        some, here = pl.ds(low + 16 * k, 16), pl.ds(16 * k, 16)
                        last_add(some, total_of(along, some) + self.s_in[here, :].astype(F32))
            between(n)
        for d in range(at.outer):
            for part in range(HALVES):
                self.cross(d, part).wait_send()
        send.finish()


class LineReduce:
    def __init__(self, at, own, land, up, down):
        self.at, self.own, self.land, self.up, self.down = at, own, land, up, down

    def order(self, o0):
        return sorted(range(self.at.outer), key=lambda d: (-abs(d - o0), d))

    def ascent(self, d):
        at = self.at
        return remote(
            self.own.at[d], self.land.at[d], self.up.at[0, d], self.up.at[1, d], at.above
        )

    def descent(self, o0, d):
        slot = d if d != o0 - 1 else self.at.outer
        return remote(
            self.own.at[d], self.land.at[slot], self.down.at[0, d], self.down.at[1, d], self.at.below
        )

    def early(self, n, d, limit):
        at = self.at
        inside = n < limit
        last = at.outer - 1
        pl.when(jnp.logical_and(at.o == 0, inside))(lambda: self.ascent(d).start())
        far = remote(
            self.own.at[d], self.land.at[d], self.down.at[0, d], self.down.at[1, d], at.below
        )
        pl.when(jnp.logical_and(at.o == last, inside))(lambda: far.start())

    def push(self, o0, d):
        if d > o0:
            self.ascent(d).start()
        if d < o0:
            self.descent(o0, d).start()

    def absorb(self, o0, d):
        terms = []
        if d >= o0 > 0:
            self.ascent(d).wait_recv()
            terms.append(self.land.at[d])
        if d <= o0 < self.at.outer - 1:
            slot = d if d < o0 else self.at.outer
            self.descent(o0 + 1, d).wait_recv()
            terms.append(self.land.at[slot])
        mine = self.own.at[d]

        def add(rows):
            total = mine[rows, :].astype(F32)
            for term in terms:
                total = total + term[rows, :].astype(F32)
            mine[rows, :] = total.astype(BF16)

        if terms:
            add_rows(mine.shape[0], add)

    def step(self, o0, n):
        d = self.order(o0)[n]
        self.absorb(o0, d)
        self.push(o0, d)

    def finish(self, o0):
        for d in range(self.at.outer):
            if d > o0:
                self.ascent(d).wait_send()
            if d < o0:
                self.descent(o0, d).wait_send()


def first_half(hidden):
    return -(-(hidden // 2) // LANES) * LANES


def line_reduce_scratch(outer, rows, cols):
    blocks = [pltpu.VMEM((outer, rows, cols), BF16), pltpu.VMEM((outer + 1, rows, cols), BF16)]
    return blocks, [DMA((2, outer))] * 2


SLIM = 16
HALVES = 2


def slim_scratch(outer, cols):
    blocks = [pltpu.VMEM((outer, SLIM, cols), BF16)] * 3 + [pltpu.VMEM((SLIM, cols), BF16)]
    return blocks, [DMA((2, outer))] * 2 + [DMA((2,))]


def line_sum_scratch(outer, rows, cols):
    return [pltpu.VMEM((outer, rows, cols), BF16)] * 4, [DMA((2, outer, HALVES))] * 3


def row_rms(values):
    return lax.rsqrt(jnp.mean(values * values, axis=-1, keepdims=True) + EPSILON)


def rms_back(values, scale, gain, grad):
    k = grad * gain
    mean = jnp.mean(k * values, axis=-1, keepdims=True)
    return scale * k - scale * scale * scale * values * mean


def run_scan(
    parts, quarters, chunk, proj_ref, par_ref, gates_ref, z_ref, h_ref, v_ref, u_pad, a_s, b_s
):
    length, width = h_ref.shape
    seg = length // SEGMENTS
    chunks = length // chunk

    def place(c):
        q = c // parts
        s = c - q * parts
        return pl.multiple_of((s * quarters + q) * chunk, chunk)

    def time_of(c):
        return pl.multiple_of(c * chunk, chunk)

    log_scale = -DECAY_SCALE * softplus(-par_ref[DECAY : DECAY + 1, :])
    bias = jnp.concatenate(
        [par_ref[RATE_B : RATE_B + 1, :], par_ref[ENTRY_B : ENTRY_B + 1, :]], axis=1
    )
    u_pad[0:8, :] = jnp.zeros((8, width), F32)

    def first(c, carry):
        u = proj_ref[pl.ds(place(c), chunk), width : 2 * width].astype(BF16).astype(F32)
        u_pad[pl.ds(pl.multiple_of(time_of(c) + 8, 8), chunk), :] = u
        wide = u_pad[pl.ds(time_of(c), chunk + 8), :]
        v = par_ref[CONV_B : CONV_B + 1, :] + par_ref[0:1, :] * wide[8:]
        for k in range(1, 4):
            v = v + par_ref[k : k + 1, :] * wide[8 - k : 8 - k + chunk]
        v = v.astype(BF16)
        v_ref[pl.ds(time_of(c), chunk), :] = v
        pre = dot(v, gates_ref[...]) + bias
        r, e, a, room, m = gate_values(pre, log_scale, width)
        put(a_s, pl.ds(time_of(c), chunk), a)
        put(b_s, pl.ds(time_of(c), chunk), m * e * v.astype(F32))
        return carry

    lax.fori_loop(0, chunks, first, 0)

    def load(g, i):
        at = pl.ds(i, SEGMENTS, stride=seg)
        return a_s[g, at, :], b_s[g, at, :]

    def store(g, i, state, total):
        at = pl.ds(i, SEGMENTS, stride=seg)
        b_s[g, at, :] = state
        a_s[g, at, :] = total

    groups = width // LANES
    start = (jnp.zeros((SEGMENTS, LANES), F32), jnp.ones((SEGMENTS, LANES), F32))
    ends = lax.fori_loop(
        0, seg, strided_scan(lambda k: k, groups, load, store), (start,) * groups, unroll=8
    )
    final = jnp.concatenate([e[0] for e in ends], axis=1)
    totals = jnp.concatenate([e[1] for e in ends], axis=1)
    carries = [jnp.zeros((1, width), F32)]
    for j in range(SEGMENTS - 1):
        carries.append(totals[j : j + 1] * carries[j] + final[j : j + 1])
    for j in range(SEGMENTS):
        per = seg // chunk

        def last(k, carry, j=j, per=per):
            c = j * per + k
            rows = pl.ds(time_of(c), chunk)
            h = take(b_s, rows) + take(a_s, rows) * carries[j]
            h_ref[rows, :] = h
            y = gelu_tanh(proj_ref[pl.ds(place(c), chunk), 0:width])
            z_ref[pl.ds(place(c), chunk), :] = (h.astype(BF16).astype(F32) * y).astype(BF16)
            return carry

        lax.fori_loop(0, per, last, 0)


def forward_kernel(
    outer,
    inner,
    shards,
    quarters,
    chunk,
    x_ref,
    gain1_ref,
    gain2_ref,
    taps_ref,
    conv_b_ref,
    rate_b_ref,
    entry_b_ref,
    decay_ref,
    rate_ref,
    entry_ref,
    cot_ref,
    wi_ref,
    wo_ref,
    par_ref,
    mid_ref,
    z_out,
    h_out,
    v_out,
    proj_out,
    gates_out,
    n1_out,
    wi_out,
    wo_out,
    n2_out,
    cot_out,
    own_s,
    n1_s,
    wi_s,
    wo_s,
    gates_s,
    u_pad,
    a_s,
    b_s,
    z_ref,
    h_ref,
    v_ref,
    proj_ref,
    gates_ref,
    p_s,
    cot_s,
    x_in,
    up_in,
    down_in,
    line_out,
    g_across,
    g_up,
    g_down,
    w_far,
    w_near,
    across,
    up,
    down,
    far,
    near,
    c_side,
    c_far,
    c_near,
    local,
    s_up_in,
    s_down_in,
    s_sums,
    s_in,
    s_up,
    s_down,
    s_across,
    g_side_up,
    g_side_down,
):
    at = Place(outer, inner, shards)
    parts, rows = at.parts, x_ref.shape[0]
    steps = list(range(1, at.ys))
    width2 = wi_ref.shape[1]
    width, depth, cols = width2 // 2, wi_ref.shape[0], wo_ref.shape[1]

    def normalize(some):
        x = x_ref[some, :].astype(F32)
        own_s[some, :] = (x * row_rms(x) * gain1_ref[...]).astype(BF16)

    add_rows(rows, normalize)
    greet_with_line(at, [at.sibling] + [at.near(q)[0] for q in range(1, at.chips)])
    weights = ((wi_ref, wi_s), (wo_ref, wo_s))
    keep = [
        pltpu.make_async_copy(own_s, n1_s.at[at.s], local.at[0]),
        pltpu.make_async_copy(wi_ref, wi_s.at[at.h], local.at[1]),
        pltpu.make_async_copy(wo_ref, wo_s.at[at.h], local.at[2]),
    ]
    for copy in keep:
        copy.start()
    send = Sent()

    def send_weights():
        for n, (src, dst) in enumerate(weights):
            for dy in steps:
                send(src, dst.at[at.h], w_far, (n, dy), (at.s, at.along(dy)))
            send(src, dst.at[at.h], w_near, (n, 0), at.sibling)

    send_weights()
    def build_gates():
        channels = decay_ref.shape[0]
        par_ref[...] = jnp.zeros(par_ref.shape, F32)
        par_ref[0:4, :channels] = taps_ref[...].astype(F32)
        for row, src in (
            (CONV_B, conv_b_ref),
            (RATE_B, rate_b_ref),
            (ENTRY_B, entry_b_ref),
            (DECAY, decay_ref),
        ):
            par_ref[row, :channels] = src[...]
        gates_s[...] = jnp.zeros(gates_s.shape, F32)
        block_width, blocks = rate_ref.shape[0], rate_ref.shape[1]
        for gate, src in enumerate((rate_ref, entry_ref)):
            for j in range(blocks):
                top, lane = j * block_width, gate * width + j * block_width
                gates_s[top : top + block_width, lane : lane + block_width] = src[:, j, :].astype(F32)
        gates_ref[...] = gates_s[...].astype(BF16)

    def project(d):
        total = None
        for k in range(shards):
            lanes = slice(k * depth, (k + 1) * depth)
            pair = jnp.concatenate([n1_s[d * inner + i, :, lanes] for i in range(inner)], axis=0)
            term = dot(pair, wi_s[k])
            total = term if total is None else total + term
        proj_ref[d * inner * rows : (d + 1) * inner * rows, :] = total

    def gather(o0):
        forward = Sent()

        def between(k):
            if k == 0:
                build_gates()
            if k != outer - 1:
                return
            for n, (src, dst) in enumerate(weights):
                for dy in steps:
                    source = at.along(-dy)
                    received(src, dst.at[source], w_far, (n, dy), (at.s, source))
                    forward(dst.at[source], dst.at[source], w_near, (n, dy), at.sibling)
            for n, (src, dst) in enumerate(weights):
                for dy in range(at.ys):
                    received(src, dst.at[at.along(-dy, 1)], w_near, (n, dy), at.sibling)
            for copy in keep:
                copy.wait()

        def each(row):
            project(row)

        side = (g_side_up, g_side_down)
        line_gather(at, o0, own_s, n1_s, g_across, g_up, g_down, between, each, side, SLIM)
        forward.finish()

    at.branches(gather)
    send(cot_ref, cot_s, c_side, (), at.beside)
    keep = [
        pltpu.make_async_copy(n1_s, n1_out, local.at[0]),
        pltpu.make_async_copy(wi_s, wi_out, local.at[1]),
        pltpu.make_async_copy(wo_s, wo_out, local.at[2]),
    ]
    for copy in keep:
        copy.start()
    run_scan(
        parts, quarters, chunk, proj_ref, par_ref, gates_ref, z_ref, h_ref, v_ref, u_pad, a_s, b_s
    )
    made = (
        (z_ref, z_out),
        (h_ref, h_out),
        (v_ref, v_out),
        (proj_ref, proj_out),
        (gates_ref, gates_out),
    )
    for n, (src, dst) in enumerate(made):
        keep.append(pltpu.make_async_copy(src, dst, local.at[6 + n]))
        keep[-1].start()
    side = (s_up_in, s_down_in, s_sums, s_in, s_up, s_down, s_across)
    line = LineSum(at, p_s, (x_in, up_in, down_in, line_out), (across, up, down), side)

    def back_project(n, carry):
        d = at.far_first(n)
        some = pl.ds(pl.multiple_of(d * inner * rows, inner * rows), inner * rows)
        for k in range(shards):
            p_s[d, :, k * cols : (k + 1) * cols] = dot(z_ref[some, :], wo_s[k]).astype(BF16)
        line.start(d)
        return carry

    lax.fori_loop(0, outer, back_project, 0)
    received(cot_ref, cot_s, c_side, (), at.beside)

    def slot(side, dy, other=0):
        i = 1 - at.i if side else at.i
        return cot_out.at[i * shards + at.along(dy, other)]

    mine = (cot_ref, cot_s)
    for side in range(2):
        keep.append(pltpu.make_async_copy(mine[side], slot(side, 0), local.at[3 + side]))
        keep[-1].start()
        for dy in steps:
            send(mine[side], slot(side, 0), c_far, (side, dy), (at.s, at.along(dy)))
        send(mine[side], slot(side, 0), c_near, (side, 0), at.sibling)

    def last_add(some, total):
        mid = x_ref[some, :].astype(F32) + total
        mid_ref[some, :] = mid
        own_s[some, :] = (mid * row_rms(mid) * gain2_ref[...]).astype(BF16)

    def branch(o0):
        forward = Sent()

        def between(n):
            if n != outer - 2:
                return
            for side in range(2):
                for dy in steps:
                    here = slot(side, -dy)
                    received(cot_ref, here, c_far, (side, dy), (at.s, at.along(-dy)))
                    forward(here, here, c_near, (side, dy), at.sibling)

        line.steps(o0, last_add, between)
        forward.finish()

    at.branches(branch)
    _, me = at.near(0)
    keep.append(pltpu.make_async_copy(own_s, n2_out.at[me], local.at[5]))
    keep[-1].start()
    quad = inner == 2 and at.ys == 2
    for q in (1, 2) if quad else reversed(range(1, at.chips)):
        send(own_s, n2_out.at[me], far, (q,), at.near(q)[0])
    send(own_s, n2_out.at[me], near, (0,), at.sibling)
    for q in (1, 2) if quad else range(1, at.chips):
        source, there = at.near(q, back=True)
        here = n2_out.at[there]
        received(own_s, here, far, (q,), source)
        if quad:
            half = here.at[pl.ds((2 - q) * (rows // 2), rows // 2)]
            send(half, half, far, (3 if q == 2 else 0,), at.near(3 - q)[0])
        send(here, here, near, (q,), at.sibling)
    if quad:
        here = n2_out.at[at.near(3)[1]]
        for q in (1, 2):
            half = here.at[pl.ds((q - 1) * (rows // 2), rows // 2)]
            received(half, half, far, (3 if q == 1 else 0,), at.near(q)[0])
        send(here, here, near, (3,), at.sibling)
    for q in range(at.chips):
        received(own_s, n2_out.at[at.near(q, 1, True)[1]], near, (q,), at.sibling)
    for side in range(2):
        for dy in range(at.ys):
            received(cot_ref, slot(side, -dy, 1), c_near, (side, dy), at.sibling)
    send.finish()
    for copy in keep:
        copy.wait()


def forward(
    x,
    gain1,
    gain2,
    channel,
    rate,
    entry,
    cot,
    w_in,
    w_out,
    quarters,
    chunk,
    outer,
    inner,
    shards,
    collective,
):
    rows, cols = x.shape
    parts, ys, chips = outer * inner, shards // 2, inner * shards // 2
    length, width = parts * rows, w_in.shape[1] // 2
    bufs, sems = line_sum_scratch(outer, rows, cols)
    side_vmem, side_sems = slim_scratch(outer, cols)
    plane = jax.ShapeDtypeStruct((inner * shards, rows, cols), BF16)
    lanes = pltpu.VMEM((width // LANES, length, LANES), F32)
    made = (
        ((length, width), BF16),
        ((length, width), F32),
        ((length, width), BF16),
        ((length, 2 * width), F32),
        ((width, 2 * width), BF16),
    )
    return pl.pallas_call(
        functools.partial(forward_kernel, outer, inner, shards, quarters, chunk),
        out_shape=(
            jax.ShapeDtypeStruct((8, width), F32),
            jax.ShapeDtypeStruct((rows, cols), F32),
            *[jax.ShapeDtypeStruct(shape, dtype) for shape, dtype in made],
            jax.ShapeDtypeStruct((parts, rows, cols), BF16),
            jax.ShapeDtypeStruct((shards,) + w_in.shape, BF16),
            jax.ShapeDtypeStruct((shards,) + w_out.shape, BF16),
            plane,
            plane,
        ),
        in_specs=[IN_VMEM] * 11 + [IN_HBM] * 2,
        out_specs=[IN_VMEM] * 2 + [IN_HBM] * 10,
        scratch_shapes=[
            pltpu.VMEM((rows, cols), BF16),
            pltpu.VMEM((parts, rows, cols), BF16),
            pltpu.VMEM((shards,) + w_in.shape, BF16),
            pltpu.VMEM((shards,) + w_out.shape, BF16),
            pltpu.VMEM((width, 2 * width), F32),
            pltpu.VMEM((length + 8, width), F32),
            lanes,
            lanes,
            *[pltpu.VMEM(shape, dtype) for shape, dtype in made],
            pltpu.VMEM((outer, inner * rows, cols), BF16),
            pltpu.VMEM((rows, cols), BF16),
        ]
        + bufs
        + [DMA((2, outer, HALVES))] * 3
        + [DMA((2, 2, ys))] * 2
        + sems
        + [DMA((2, chips))] * 2
        + [DMA((2,))]
        + [DMA((2, 2, ys))] * 2
        + [DMA((11,))]
        + side_vmem
        + side_sems
        + [DMA((2, outer))] * 2,
        compiler_params=pltpu.CompilerParams(
            collective_id=collective, has_side_effects=True, vmem_limit_bytes=60 * 2**20
        ),
        cost_estimate=cost(140),
        name="forward",
    )(x, gain1, gain2, *channel, rate, entry, cot, w_in, w_out)


class PlaneSum:
    def __init__(self, at, n, p, near_in, far_in, far_out, near, far):
        self.at, self.n, self.p = at, n, p
        self.near_in, self.far_in, self.far_out = near_in, far_in, far_out
        self.near, self.far = near, far
        self.rows = near_in.shape[2]

    def block(self, q, other):
        i, y = self.at.chip(q)
        core = lax.rem(self.at.core + other, 2)
        rows = pl.ds(pl.multiple_of(core * self.rows, self.rows), self.rows)
        return self.p.at[i * self.at.ys + y, rows]

    def to_sibling(self, q):
        n = self.n
        return remote(
            self.block(q, 1),
            self.near_in.at[n, q],
            self.near.at[0, n, q],
            self.near.at[1, n, q],
            self.at.sibling,
        )

    def onward(self, q, back=False):
        n = self.n
        return remote(
            self.far_out.at[n, q],
            self.far_in.at[n, q],
            self.far.at[0, n, q],
            self.far.at[1, n, q],
            self.at.near(q, 0, back)[0],
        )

    def combine_one(self, k, own=None):
        q = self.at.chips - 1 - k
        self.to_sibling(q).wait_recv()
        mine = self.block(q, 0) if own is None else own.at[q]

        def add(rows):
            total = mine[rows, :].astype(F32) + self.near_in[self.n, q, rows, :].astype(F32)
            self.far_out[self.n, q, rows, :] = total.astype(BF16)

        add_rows(self.rows, add)
        self.onward(q).start()

    def combine(self, own=None):
        def one(k, carry):
            self.combine_one(k, own)
            return carry

        lax.fori_loop(0, self.at.chips - 1, one, 0)
        self.to_sibling(0).wait_recv()

    def total(self, rows, own=None):
        n = self.n
        mine = self.block(0, 0) if own is None else own.at[0]
        value = mine[rows, :].astype(F32) + self.near_in[n, 0, rows, :].astype(F32)
        for q in range(1, self.at.chips):
            value = value + self.far_in[n, q, rows, :].astype(F32)
        return value

    def arrive(self):
        for q in range(1, self.at.chips):
            self.onward(q, True).wait_recv()

    def finish(self):
        for q in range(self.at.chips):
            self.to_sibling(q).wait_send()
        for q in range(1, self.at.chips):
            self.onward(q).wait_send()


def turn_kernel(
    outer,
    inner,
    shards,
    dgm_ref,
    dum_ref,
    mm_ref,
    mid_ref,
    cot_ref,
    gain_ref,
    wg_ref,
    wu_ref,
    wd_ref,
    n2_ref,
    cots_ref,
    dmid_ref,
    gain_grad_ref,
    dout_ref,
    q_ref,
    down_ref,
    gate_ref,
    rest_ref,
    up_ref,
    p_s,
    q_s,
    dout_s,
    gain_s,
    wg_s,
    wu_s,
    wd_s,
    n2_s,
    cots_s,
    u_s,
    r_s,
    near_in,
    far_in,
    far_out,
    down_own,
    down_land,
    gate_own,
    gate_land,
    near,
    far,
    across,
    up,
    low,
    down_up,
    down_low,
    gate_up,
    gate_low,
    local,
    q_sem,
    u_sem,
    r_sem,
):
    at = Place(outer, inner, shards)
    model, hidden = wg_s.shape
    tile = min(512, model)
    pair = p_s.shape[1]
    span = model // outer
    own = pl.ds(pl.multiple_of(at.i * hidden, hidden), hidden)
    load = [
        pltpu.make_async_copy(cots_ref, cots_s, local.at[1]),
        pltpu.make_async_copy(wg_ref.at[:, own], wg_s, local.at[2]),
        pltpu.make_async_copy(wu_ref.at[:, own], wu_s, local.at[3]),
        pltpu.make_async_copy(n2_ref, n2_s, local.at[4]),
        pltpu.make_async_copy(wd_ref.at[own, :], wd_s, local.at[5]),
    ]
    for copy in load:
        copy.start()
    greet_with_line(at, [at.sibling] + [at.near(q)[0] for q in range(1, at.chips)])
    grad = PlaneSum(at, 0, p_s, near_in, far_in, far_out, near, far)
    down = LineReduce(at, down_own, down_land, down_up, down_low)
    gate = LineReduce(at, gate_own, gate_land, gate_up, gate_low)

    def columns(d):
        return pl.ds(pl.multiple_of(d * span, span), span)

    load[0].wait()

    def down_grad(n, carry):
        d = at.far_first(n)
        down_own[d] = dot(cots_s[:, columns(d)], mm_ref[...], ((0,), (0,))).astype(BF16)
        down.early(n, d, outer - 2)
        return carry

    down_grad(0, 0)
    load[1].wait()
    load[2].wait()

    def back(k, carry):
        q = at.chips - 1 - k
        i, y = at.chip(q)
        c = i * at.ys + y
        rows = pl.ds(pl.multiple_of(c * pair, pair), pair)
        for lane in range(0, model, tile):
            lanes = slice(lane, lane + tile)
            block = dot(dgm_ref[rows, :], wg_s[lanes, :], ((1,), (1,)))
            block = block + dot(dum_ref[rows, :], wu_s[lanes, :], ((1,), (1,)))
            p_s[c, :, lanes] = block.astype(BF16)
        grad.to_sibling(q).start()
        pl.when(k > 0)(lambda: grad.combine_one(k - 1))
        return carry

    lax.fori_loop(0, at.chips, back, 0)
    grad.to_sibling(0).wait_recv()
    lax.fori_loop(1, outer, down_grad, 0)
    load[3].wait()

    cut = gate_own.shape[2]

    def keep_r(n):
        slot = lax.rem(n, 2)
        there = rest_ref.at[at.far_first(n), :, : hidden - cut]
        return pltpu.make_async_copy(r_s.at[slot], there, r_sem.at[slot])

    def gate_grad(n, carry):
        d = at.far_first(n)
        pl.when(n >= 2)(lambda: keep_r(n - 2).wait())
        block = dot(n2_s[:, columns(d)], dgm_ref[...], ((0,), (0,))).astype(BF16)
        gate_own[d] = block[:, :cut]
        r_s[lax.rem(n, 2)] = block[:, cut:]
        keep_r(n).start()
        return carry

    lax.fori_loop(0, outer, gate_grad, 0)
    for n in range(max(outer - 2, 0), outer):
        keep_r(n).wait()

    def first_down(o0):
        if 0 < o0 < outer - 1:
            down.step(o0, 0)

    at.branches(first_down)
    load[4].wait()

    def keep_q(c):
        slot = lax.rem(c, 2)
        return pltpu.make_async_copy(q_s.at[slot], q_ref.at[c], q_sem.at[slot])

    def ahead(c, carry):
        rows = pl.ds(pl.multiple_of(c * pair, pair), pair)
        pl.when(c >= 2)(lambda: keep_q(c - 2).wait())
        for lane in range(0, model, tile):
            lanes = slice(lane, lane + tile)
            q_s[lax.rem(c, 2), :, lanes] = dot(mm_ref[rows, :], wd_s[:, lanes]).astype(BF16)
        keep_q(c).start()
        return carry

    lax.fori_loop(0, at.chips, ahead, 0)
    for c in range(max(at.chips - 2, 0), at.chips):
        keep_q(c).wait()
    gain_s[...] = jnp.zeros(gain_s.shape, F32)
    grad.arrive()

    def norm_back(rows):
        dn2 = grad.total(rows)
        mid = mid_ref[rows, :]
        scale = row_rms(mid)
        gain_s[...] += dn2 * mid * scale
        dmid = cot_ref[rows, :].astype(F32) + rms_back(mid, scale, gain_ref[...], dn2)
        dmid_ref[rows, :] = dmid
        dout_s[rows, :] = dmid.astype(BF16)

    add_rows(dout_s.shape[0], norm_back)
    gain_grad_ref[...] = jnp.sum(gain_s[...], axis=0, keepdims=True)
    keep = pltpu.make_async_copy(dout_s, dout_ref.at[at.s], local.at[0])
    keep.start()

    head = u_s.shape[2] - up_ref.shape[2]

    class keep_u:
        def __init__(self, n):
            slot, d = lax.rem(n, 2), at.far_first(n)
            block = u_s.at[slot]
            self.copies = (
                pltpu.make_async_copy(
                    block.at[:, :head], rest_ref.at[d, :, hidden - cut :], u_sem.at[0, slot]
                ),
                pltpu.make_async_copy(block.at[:, head:], up_ref.at[d], u_sem.at[1, slot]),
            )

        def start(self):
            for copy in self.copies:
                copy.start()

        def wait(self):
            for copy in self.copies:
                copy.wait()

    def up_grad(n, carry):
        pl.when(n >= 2)(lambda: keep_u(n - 2).wait())
        u_s[lax.rem(n, 2)] = dot(
            n2_s[:, columns(at.far_first(n))], dum_ref[...], ((0,), (0,))
        ).astype(BF16)
        keep_u(n).start()
        return carry

    def branch(o0):
        ends = o0 in (0, outer - 1)

        def between(k):
            if k == 0:
                if ends:
                    down.push(o0, down.order(o0)[outer - 2])
                    for d in gate.order(o0)[:-1]:
                        gate.push(o0, d)
                else:
                    for n in range(1, outer - 1):
                        down.step(o0, n)
                lax.fori_loop(0, outer, up_grad, 0)
            if k == outer - 1:
                down.absorb(o0, o0)
            if k == outer and not ends:
                for n in range(outer - 1):
                    gate.step(o0, n)

        line_gather(at, o0, dout_s, dout_ref, across, up, low, between)
        gate.absorb(o0, o0)
        down.finish(o0)
        gate.finish(o0)

    at.branches(branch)
    last = [
        pltpu.make_async_copy(down_own.at[at.o], down_ref, local.at[1]),
        pltpu.make_async_copy(gate_own.at[at.o], gate_ref, local.at[2]),
    ]
    for copy in last:
        copy.start()
    for n in range(max(outer - 2, 0), outer):
        keep_u(n).wait()
    grad.finish()
    keep.wait()
    for copy in last:
        copy.wait()


def turn(
    dgm, dum, mm, mid, cot, gain, wg, wu, wd, n2, cots, outer, inner, shards, collective
):
    rows, cols = mid.shape
    tokens, hidden = dgm.shape
    chips, span = inner * shards // 2, cols // outer
    buffers = pltpu.VMEM((1, chips, rows, cols), BF16)
    cut = first_half(hidden)
    down_vmem, reduce_sems = line_reduce_scratch(outer, span, hidden)
    gate_vmem, _ = line_reduce_scratch(outer, span, cut)
    return pl.pallas_call(
        functools.partial(turn_kernel, outer, inner, shards),
        out_shape=(
            jax.ShapeDtypeStruct((rows, cols), F32),
            jax.ShapeDtypeStruct((1, cols), F32),
            jax.ShapeDtypeStruct((outer * inner, rows, cols), BF16),
            jax.ShapeDtypeStruct((chips, 2 * rows, cols), BF16),
            jax.ShapeDtypeStruct((span, hidden), BF16),
            jax.ShapeDtypeStruct((span, cut), BF16),
            jax.ShapeDtypeStruct((outer, span, hidden - cut + LANES), BF16),
            jax.ShapeDtypeStruct((outer, span, hidden - LANES), BF16),
        ),
        in_specs=[IN_VMEM] * 6 + [IN_HBM] * 5,
        out_specs=[IN_VMEM] * 2 + [IN_HBM] * 6,
        scratch_shapes=[
            pltpu.VMEM((chips, 2 * rows, cols), BF16),
            pltpu.VMEM((2, 2 * rows, cols), BF16),
            pltpu.VMEM((rows, cols), BF16),
            pltpu.VMEM((16, cols), F32),
            pltpu.VMEM((cols, hidden), BF16),
            pltpu.VMEM((cols, hidden), BF16),
            pltpu.VMEM((hidden, cols), BF16),
            pltpu.VMEM((tokens, cols), BF16),
            pltpu.VMEM((tokens, cols), BF16),
            pltpu.VMEM((2, span, hidden), BF16),
            pltpu.VMEM((2, span, hidden - cut), BF16),
        ]
        + [buffers] * 3
        + down_vmem
        + gate_vmem
        + [DMA((2, 1, chips))] * 2
        + [DMA((2, outer, HALVES))] * 3
        + reduce_sems * 2
        + [DMA((6,)), DMA((2,)), DMA((2, 2)), DMA((2,))],
        compiler_params=pltpu.CompilerParams(
            collective_id=collective, has_side_effects=True, vmem_limit_bytes=60 * 2**20
        ),
        cost_estimate=cost(110),
        name="turn",
    )(dgm, dum, mm, mid, cot, gain, wg, wu, wd, n2, cots)


def scan_backward_kernel(
    outer,
    inner,
    shards,
    quarters,
    chunk,
    blocks,
    block_width,
    dout_ref,
    wo_ref,
    proj_ref,
    h_ref,
    v_ref,
    par_ref,
    gates_ref,
    mid_ref,
    q_ref,
    rest_ref,
    both_ref,
    blocks_ref,
    totals_ref,
    result_ref,
    rest_out,
    q_s,
    near_in,
    far_in,
    far_out,
    rest_own,
    rest_land,
    near,
    far,
    q_sem,
    r_up,
    r_low,
    r_sem,
    dout_s,
    dz_s,
    sems,
    sums_ref,
    gate_grad_ref,
    a_s,
    g_s,
    t_s,
    h_pad,
    pre_s,
    dpre_s,
    dv_s,
    u_pad,
):
    length, width = h_ref.shape
    seg = length // SEGMENTS
    chunks = length // chunk

    def place(c):
        q = c // parts
        s = c - q * parts
        return pl.multiple_of((s * quarters + q) * chunk, chunk)

    def time_of(c):
        return pl.multiple_of(c * chunk, chunk)

    at = Place(outer, inner, shards)
    parts = at.parts
    rest = LineReduce(at, rest_own, rest_land, r_up, r_low)
    fetch = pltpu.make_async_copy(rest_ref, rest_own, r_sem)
    fetch.start()
    greet_with_line(at, [at.sibling] + [at.near(q)[0] for q in range(1, at.chips)])
    fetch.wait()

    def rest_early(o0):
        if o0 in (0, outer - 1):
            for d in rest.order(o0)[:-1]:
                rest.push(o0, d)

    def rest_step(n, o0):
        if 0 < o0 < outer - 1:
            rest.step(o0, n)

    def rest_last(o0):
        rest.absorb(o0, o0)
        rest.finish(o0)

    at.branches(rest_early)
    value = PlaneSum(at, 0, q_ref, near_in, far_in, far_out, near, far)

    def keep(q):
        return pltpu.make_async_copy(value.block(q, 0), q_s.at[q], q_sem.at[q])

    for q in reversed(range(at.chips)):
        value.to_sibling(q).start()
        keep(q).start()
    span = quarters * chunk

    def load(p):
        return pltpu.make_async_copy(
            dout_ref.at[p], dout_s.at[pl.ds(pl.multiple_of(p * span, span), span)], sems.at[p]
        )

    for p in range(parts):
        load(p).start()

    def back_project(k, carry):
        load(2 * k).wait()
        load(2 * k + 1).wait()
        some = pl.ds(pl.multiple_of(k * 2 * span, 2 * span), 2 * span)
        depth = wo_ref.shape[2]
        total = dot(dout_s[some, 0:depth], wo_ref[0], ((1,), (1,)))
        for p in range(1, wo_ref.shape[0]):
            lanes = slice(p * depth, (p + 1) * depth)
            total = total + dot(dout_s[some, lanes], wo_ref[p], ((1,), (1,)))
        dz_s[some, :] = total
        return carry

    lax.fori_loop(0, parts // 2, back_project, 0)
    for q in range(at.chips):
        keep(q).wait()
    value.combine(q_s)
    log_scale = -DECAY_SCALE * softplus(-par_ref[DECAY : DECAY + 1, :])
    bias = jnp.concatenate(
        [par_ref[RATE_B : RATE_B + 1, :], par_ref[ENTRY_B : ENTRY_B + 1, :]], axis=1
    )
    zeros8 = jnp.zeros((8, width), F32)
    put(a_s, pl.ds(length, 8), zeros8)
    h_pad[0:8, :] = zeros8
    u_pad[0:8, :] = zeros8
    dv_s[pl.ds(length, 8), :] = zeros8

    def first(c, carry):
        rows = pl.ds(time_of(c), chunk)
        later = pl.ds(pl.multiple_of(time_of(c) + 8, 8), chunk)
        there = pl.ds(place(c), chunk)
        h = h_ref[rows, :]
        h_pad[later, :] = h
        u_pad[later, :] = proj_ref[there, width : 2 * width].astype(BF16).astype(F32)
        y, slope = gelu_and_slope(proj_ref[there, 0:width])
        dz = dz_s[there, :]
        put(g_s, rows, (dz * y).astype(BF16).astype(F32))
        both_ref[there, 0:width] = (dz * h.astype(BF16).astype(F32) * slope).astype(BF16)
        pre = dot(v_ref[rows, :], gates_ref[...]) + bias
        pre_s[rows, :] = pre
        put(a_s, rows, jnp.exp(sigmoid(pre[:, :width]) * log_scale))
        return carry

    lax.fori_loop(0, chunks, first, 0)

    def load(g, i):
        return (
            a_s[g, pl.ds(i + 1, SEGMENTS, stride=seg), :],
            g_s[g, pl.ds(i, SEGMENTS, stride=seg), :],
        )

    def store(g, i, state, total):
        g_s[g, pl.ds(i, SEGMENTS, stride=seg), :] = state
        t_s[g, pl.ds(i, SEGMENTS, stride=seg), :] = total

    groups = width // LANES
    start = (jnp.zeros((SEGMENTS, LANES), F32), jnp.ones((SEGMENTS, LANES), F32))
    ends = lax.fori_loop(
        0,
        seg,
        strided_scan(lambda k: seg - 1 - k, groups, load, store),
        (start,) * groups,
        unroll=8,
    )
    firsts = jnp.concatenate([e[0] for e in ends], axis=1)
    totals = jnp.concatenate([e[1] for e in ends], axis=1)
    carries = [None] * SEGMENTS
    carries[SEGMENTS - 1] = jnp.zeros((1, width), F32)
    for j in range(SEGMENTS - 2, -1, -1):
        carries[j] = totals[j + 1 : j + 2] * carries[j + 1] + firsts[j + 1 : j + 2]

    def fold(values):
        return jnp.sum(values.reshape(chunk // 8, 8, values.shape[1]), axis=0)

    sums_ref[...] = jnp.zeros(sums_ref.shape, F32)

    for j in range(SEGMENTS):
        per = seg // chunk

        def middle(k, carry, j=j, per=per):
            c = j * per + k
            rows = pl.ds(time_of(c), chunk)
            g = take(g_s, rows) + take(t_s, rows) * carries[j]
            before = h_pad[pl.ds(time_of(c), chunk + 8), :][7 : 7 + chunk]
            v = v_ref[rows, :].astype(F32)
            r, e, a, room, m = gate_values(pre_s[rows, :], log_scale, width)
            gv = g * v
            held = jnp.where(room > MULT_FLOOR, gv * e * a / m, 0.0)
            ta = (g * before - held) * a * r
            drpre = (ta * (log_scale * (1.0 - r))).astype(BF16)
            depre = (gv * m * e * (1.0 - e)).astype(BF16)
            dpre_s[rows, 0:width] = drpre
            dpre_s[rows, width : 2 * width] = depre
            sums_ref[0:8, :] += fold(ta)
            sums_ref[8:16, :] += fold(drpre.astype(F32))
            sums_ref[16:24, :] += fold(depre.astype(F32))
            dv = g * m * e + dot(dpre_s[rows, :], gates_ref[...], ((1,), (1,)))
            dv_s[rows, :] = dv
            sums_ref[24:32, :] += fold(dv)
            wide = u_pad[pl.ds(time_of(c), chunk + 8), :]
            for tap in range(4):
                top = 32 + 8 * tap
                sums_ref[top : top + 8, :] += fold(dv * wide[8 - tap : 8 - tap + chunk])
            return carry

        lax.fori_loop(0, per, middle, 0)
        if j == 2:
            at.branches(functools.partial(rest_step, 0))
        if j == SEGMENTS - 2:
            at.branches(functools.partial(rest_step, 1))
    for n in range(2, outer - 1):
        at.branches(functools.partial(rest_step, n))
    sums_ref[0:8, :] = sums_ref[0:8, :] * (
        DECAY_SCALE * sigmoid(-par_ref[DECAY : DECAY + 1, :])
    )

    def last(c, carry):
        wide = dv_s[pl.ds(time_of(c), chunk + 8), :]
        du = par_ref[0:1, :] * wide[0:chunk]
        for tap in range(1, 4):
            du = du + par_ref[tap : tap + 1, :] * wide[tap : tap + chunk]
        both_ref[pl.ds(place(c), chunk), width : 2 * width] = du.astype(BF16)
        return carry

    lax.fori_loop(0, chunks, last, 0)
    gate_grad_ref[...] = dot(v_ref[...], dpre_s[...], ((0,), (0,)))
    blocks_ref[...] = jnp.zeros(blocks_ref.shape, F32)
    tall = blocks_ref.shape[0] // (2 * blocks)
    for gate in range(2):
        for j in range(blocks):
            top, lanes = (gate * blocks + j) * tall, gate * width + j * block_width
            rows = slice(j * block_width, (j + 1) * block_width)
            blocks_ref[top : top + block_width, :block_width] = gate_grad_ref[
                rows, lanes : lanes + block_width
            ]
    for k in range(8):
        totals_ref[k : k + 1, :] = jnp.sum(sums_ref[8 * k : 8 * k + 8, :], axis=0, keepdims=True)
    value.arrive()

    def output(rows):
        result_ref[rows, :] = (mid_ref[rows, :] + value.total(rows, q_s)).astype(BF16)

    add_rows(span, output)
    value.finish()
    at.branches(rest_last)
    out = pltpu.make_async_copy(rest_own.at[at.o], rest_out, r_sem)
    out.start()
    out.wait()


def scan_backward(
    quarters,
    chunk,
    blocks,
    block_width,
    dout,
    w_out,
    proj,
    h,
    v,
    params,
    gates,
    mid,
    q,
    rest,
    outer,
    inner,
    shards,
    collective,
):
    parts = dout.shape[0]
    rows, cols = mid.shape
    chips = q.shape[0]
    rest_vmem, rest_sems = line_reduce_scratch(*rest.shape)
    buffers = pltpu.VMEM((1, chips, rows, cols), BF16)
    length, width = h.shape
    tall, wide = -(-block_width // 8) * 8, -(-block_width // LANES) * LANES
    return pl.pallas_call(
        functools.partial(
            scan_backward_kernel, outer, inner, shards, quarters, chunk, blocks, block_width
        ),
        out_shape=(
            jax.ShapeDtypeStruct((length, 2 * width), BF16),
            jax.ShapeDtypeStruct((2 * blocks * tall, wide), F32),
            jax.ShapeDtypeStruct((8, width), F32),
            jax.ShapeDtypeStruct((rows, cols), BF16),
            jax.ShapeDtypeStruct(rest.shape[1:], BF16),
        ),
        in_specs=[IN_HBM] + [IN_VMEM] * 7 + [IN_HBM] * 2,
        out_specs=[IN_VMEM] * 4 + [IN_HBM],
        scratch_shapes=[
            pltpu.VMEM((chips, rows, cols), BF16),
            buffers,
            buffers,
            buffers,
            *rest_vmem,
            DMA((2, 1, chips)),
            DMA((2, 1, chips)),
            DMA((chips,)),
            *rest_sems,
            DMA,
            pltpu.VMEM((length, dout.shape[2]), BF16),
            pltpu.VMEM((length, width), F32),
            DMA((parts,)),
            pltpu.VMEM((64, width), F32),
            pltpu.VMEM((width, 2 * width), F32),
            pltpu.VMEM((width // LANES, length + 8, LANES), F32),
            pltpu.VMEM((width // LANES, length, LANES), F32),
            pltpu.VMEM((width // LANES, length, LANES), F32),
            pltpu.VMEM((length + 8, width), F32),
            pltpu.VMEM((length, 2 * width), F32),
            pltpu.VMEM((length, 2 * width), BF16),
            pltpu.VMEM((length + 8, width), F32),
            pltpu.VMEM((length + 8, width), F32),
        ],
        compiler_params=pltpu.CompilerParams(
            collective_id=collective, has_side_effects=True, vmem_limit_bytes=60 * 2**20
        ),
        cost_estimate=cost(21),
        name="scan_backward",
    )(dout, w_out, proj, h, v, params, gates, mid, q, rest)


def remote(src, dst, send, recv, to):
    return pltpu.make_async_remote_copy(
        src_ref=src, dst_ref=dst, send_sem=send, recv_sem=recv, device_id=to, device_id_type=MESH
    )


def add_rows(rows, fn, start=0):
    def one(k, carry):
        fn(pl.ds(pl.multiple_of(k * 16, 16), 16))
        return carry

    lax.fori_loop(start // 16, rows // 16, one, 0)


def fetch(pairs, sems):
    copies = [
        pltpu.make_async_copy(src, dst, sems.at[k]) for k, (src, dst) in enumerate(pairs)
    ]
    for copy in copies:
        copy.start()
    return copies


class PlaneExchange:
    def __init__(self, at, n, x, out, sems, local):
        self.at, self.n, self.x, self.out, self.sems, self.local = at, n, x, out, sems, local
        _, self.me = at.near(0)
        self.hops = [(q, c) for q in reversed(range(1, at.chips)) for c in range(2)] + [(0, 1)]

    def rows(self, slot):
        piece = self.out.shape[1]
        return self.x.at[pl.ds(pl.multiple_of(slot * piece, piece), piece)]

    def mine(self):
        return pltpu.make_async_copy(self.rows(self.me), self.out.at[self.me], self.local)

    def start(self):
        self.send = Sent()
        for k, (q, other) in enumerate(self.hops):
            to, slot = self.at.near(q, other)
            self.send(self.rows(slot), self.out.at[self.me], self.sems, (self.n, k), to)
        self.mine().start()

    def finish(self):
        for k, (q, other) in enumerate(self.hops):
            source, slot = self.at.near(q, other, True)
            received(self.rows(self.me), self.out.at[slot], self.sems, (self.n, k), source)
        self.send.finish()
        self.mine().wait()


def closing_kernel(
    outer,
    inner,
    shards,
    both_ref,
    wi_ref,
    z_ref,
    x_ref,
    dmid_ref,
    gain_ref,
    gain2_ref,
    blocks_ref,
    sums_ref,
    n1_ref,
    dout_ref,
    down_ref,
    gate_ref,
    rest_ref,
    up_ref,
    grad_ref,
    mix_ref,
    blocks_out,
    sums_out,
    gains_out,
    down_out,
    gate_out,
    rest_out,
    up_out,
    p_s,
    up_own,
    up_land,
    up_sum,
    n1_s,
    dout_s,
    g_s,
    gain_s,
    gain_rows,
    gain_slots,
    near_in,
    far_in,
    far_out,
    done,
    block_slots,
    sum_slots,
    x_in,
    up_in,
    down_in,
    line_out,
    across,
    up,
    low,
    near,
    far,
    final,
    s_far,
    s_near,
    swap,
    g_sem,
    stripe,
    u_up,
    u_low,
    local,
):
    at = Place(outer, inner, shards)
    s, h, parts, ys = at.s, at.h, at.parts, at.ys
    steps = list(range(1, ys))
    line = LineSum(at, p_s, (x_in, up_in, down_in, line_out), (across, up, low))
    model = x_ref.shape[1]
    tile = min(512, model)
    piece = done.shape[1]
    span = shards * piece
    width2 = both_ref.shape[1]
    me = s * shards + h
    small = ((blocks_ref, block_slots, blocks_out), (sums_ref, sum_slots, sums_out))
    fetch = pltpu.make_async_copy(up_ref, up_own, local.at[0])
    fetch.start()

    def stripes(k):
        lanes = pl.ds(pl.multiple_of(owner(k) * span, span), span)
        slot = lax.rem(k, 2)
        return (
            pltpu.make_async_copy(n1_ref.at[:, lanes], n1_s.at[slot], stripe.at[0, slot]),
            pltpu.make_async_copy(dout_ref.at[:, lanes], dout_s.at[slot], stripe.at[1, slot]),
        )

    def owner(k):
        return lax.rem(s + k + 1, parts)

    for copy in stripes(0):
        copy.start()

    def anyone(k):
        to = lax.rem(me + k, at.count)
        return (to // shards, lax.rem(to, shards)), to

    def greet_one(k, carry):
        hello(anyone(k)[0])
        return carry

    lax.fori_loop(1, at.count, greet_one, 0)
    welcome(at.count - 1)
    ups = LineReduce(at, up_own, up_land, u_up, u_low)
    fetch.wait()

    ups.early(0, at.far_first(0), min(1, outer - 2))

    def back(n, carry):
        d = at.far_first(n)
        rows = pl.ds(pl.multiple_of(d * p_s.shape[1], p_s.shape[1]), p_s.shape[1])
        for lane in range(0, model, tile):
            lanes = slice(lane, lane + tile)
            p_s[d, :, lanes] = dot(both_ref[rows, :], wi_ref[lanes, :], ((1,), (1,))).astype(BF16)
        line.start(d)
        return carry

    lax.fori_loop(0, outer, back, 0)
    send = Sent()
    for n, (src, slots, _) in enumerate(small):
        for dy in steps:
            send(src, slots.at[h], s_far, (n, dy), (s, at.along(dy)))
        send(src, slots.at[h], s_near, (n, 0), at.sibling)
        slots[h] = src[...]

    def mix_rows(p, shard):
        return g_s.at[p, pl.ds(pl.multiple_of(shard * piece, piece), piece)]

    def to_sibling(k, dy):
        p = owner(k)
        return remote(
            mix_rows(p, at.along(dy, 1)),
            near_in.at[dy, p],
            near.at[0, dy, k],
            near.at[1, dy, k],
            at.sibling,
        )

    def to_shard(k, dy, source=False):
        p = owner(k)
        return remote(
            far_out.at[dy - 1, p],
            far_in.at[dy - 1, p],
            far.at[0, dy, k],
            far.at[1, dy, k],
            (s, at.along(-dy if source else dy)),
        )

    def to_owner(k, source=False):
        p = lax.rem(s + parts - k - 1, parts) if source else owner(k)
        return remote(
            done.at[owner(k)],
            mix_ref.at[p if source else s],
            final.at[0, k],
            final.at[1, k],
            (p, h),
        )

    def weight_grads(k, carry):
        p, slot = owner(k), lax.rem(k, 2)
        for copy in stripes(k):
            copy.wait()

        @pl.when(k < parts - 1)
        def _():
            for copy in stripes(k + 1):
                copy.start()

        g_s[p, :, 0:width2] = dot(n1_s[slot], both_ref[...], ((0,), (0,))).astype(BF16)
        g_s[p, :, width2:] = dot(dout_s[slot], z_ref[...], ((0,), (0,))).astype(BF16)
        for dy in steps + [0]:
            to_sibling(k, dy).start()
        return carry

    lax.fori_loop(0, parts, weight_grads, 0)
    exchanges = [
        PlaneExchange(at, 0, down_ref, down_out, swap, local.at[2]),
        PlaneExchange(at, 1, gate_ref, gate_out, swap, local.at[3]),
        PlaneExchange(at, 3, rest_ref, rest_out, swap, local.at[5]),
    ]
    up_exchange = PlaneExchange(at, 2, up_sum, up_out, swap, local.at[1])

    def sibling_sums(k, carry):
        p = owner(k)
        for dy in steps:
            to_sibling(k, dy).wait_recv()
            mine = mix_rows(p, at.along(dy))

            def add(rows, dy=dy, mine=mine):
                total = mine[rows, :].astype(F32) + near_in[dy, p, rows, :].astype(F32)
                far_out[dy - 1, p, rows, :] = total.astype(BF16)

            add_rows(piece, add)
            to_shard(k, dy).start()
        return carry

    lax.fori_loop(0, parts, sibling_sums, 0)
    for exchange in exchanges:
        exchange.start()
    gain_s[...] = jnp.zeros(gain_s.shape, F32)

    def mix_step(k):
        p = owner(k)
        mine = mix_rows(p, h)
        to_sibling(k, 0).wait_recv()
        for dy in steps:
            to_shard(k, dy, True).wait_recv()

        def add(rows):
            total = mine[rows, :].astype(F32) + near_in[0, p, rows, :].astype(F32)
            for dy in steps:
                total = total + far_in[dy - 1, p, rows, :].astype(F32)
            done[p, rows, :] = total.astype(BF16)

        add_rows(piece, add)
        if k < parts - 1:
            to_owner(k).start()

    def last_add(rows, dn1):
        x = x_ref[rows, :].astype(F32)
        scale = row_rms(x)
        gain_s[...] += dn1 * x * scale
        grad_ref[rows, :] = dmid_ref[rows, :] + rms_back(x, scale, gain_ref[...], dn1)

    def branch(o0):
        ends = o0 in (0, outer - 1)

        sooner = min(1, outer - 2) if ends else 0

        def between(n):
            if n + sooner < outer - 1 and ends:
                ups.push(o0, ups.order(o0)[n + sooner])
            for k in range(n * inner, (n + 1) * inner):
                mix_step(k)
            if n + 1 < outer - 1 and not ends:
                ups.step(o0, n + 1)

        if not ends:
            ups.step(o0, 0)
        line.steps(o0, last_add, between)

    at.branches(branch)
    keep = pltpu.make_async_copy(done.at[s], mix_ref.at[s], local.at[4])
    keep.start()
    gain1, gain2 = jnp.sum(gain_s[...], axis=0, keepdims=True), gain2_ref[...]
    spare = gain_rows.shape[2] - 2 * piece
    for k in range(at.count):
        lanes = slice(k * piece, (k + 1) * piece)
        parts_of = [gain1[:, lanes], gain2[:, lanes]]
        if spare:
            parts_of.append(jnp.zeros((1, spare), F32))
        gain_rows[k] = jnp.concatenate(parts_of, axis=1)

    def gain(k):
        to, row = anyone(k)
        return remote(gain_rows.at[row], gain_slots.at[k], g_sem.at[0, k], g_sem.at[1, k], to)

    def gain_start(k, carry):
        gain(k).start()
        return carry

    def gain_arrive(k, total):
        gain(k).wait_recv()
        return total + gain_slots[k]

    def gain_leave(k, carry):
        gain(k).wait_send()
        return carry

    lax.fori_loop(1, at.count, gain_start, 0)

    def last_up(o0):
        ups.absorb(o0, o0)
        ups.finish(o0)

    at.branches(last_up)

    def keep_up(rows):
        up_sum[rows, :] = up_own[at.o, rows, :]

    add_rows(up_sum.shape[0], keep_up)
    up_exchange.start()
    for n, (src, slots, out) in enumerate(small):
        for dy in steps:
            here = slots.at[at.along(-dy)]
            received(src, here, s_far, (n, dy), (s, at.along(-dy)))
            send(here, here, s_near, (n, dy), at.sibling)
    for n, (src, slots, out) in enumerate(small):
        for dy in range(ys):
            received(src, slots.at[at.along(-dy, 1)], s_near, (n, dy), at.sibling)

        def add(k, carry, slots=slots, out=out):
            rows = pl.ds(pl.multiple_of(k * 8, 8), 8)
            total = slots[0, rows, :]
            for j in range(1, shards):
                total = total + slots[j, rows, :]
            out[rows, :] = total
            return carry

        lax.fori_loop(0, src.shape[0] // 8, add, 0)
    gains_out[...] = lax.fori_loop(1, at.count, gain_arrive, gain_rows[me])
    for k in range(parts - 1):
        to_owner(k, True).wait_recv()
    for exchange in exchanges + [up_exchange]:
        exchange.finish()
    for k in range(parts):
        for dy in range(ys):
            to_sibling(k, dy).wait_send()
        for dy in steps:
            to_shard(k, dy).wait_send()
        if k < parts - 1:
            to_owner(k).wait_send()
    lax.fori_loop(1, at.count, gain_leave, 0)
    send.finish()
    keep.wait()


def closing(
    both,
    w_in,
    z,
    x,
    dmid,
    gain,
    gain2,
    small,
    sums,
    n1,
    dout,
    down,
    gate,
    rest,
    ups,
    outer,
    inner,
    shards,
    collective,
):
    rows, cols = x.shape
    parts, ys, count = outer * inner, shards // 2, outer * inner * shards
    piece = cols // count
    width = z.shape[1]
    lanes = -(-2 * piece // LANES) * LANES
    bufs, sems = line_sum_scratch(outer, rows, cols)
    pieces = pltpu.VMEM((max(ys - 1, 1), parts, piece, 3 * width), BF16)
    stripes = pltpu.VMEM((2, parts * rows, cols // parts), BF16)
    span, hidden = ups.shape[1:]

    def swapped(array):
        shape = (inner * shards, span // (inner * shards), array.shape[-1])
        return jax.ShapeDtypeStruct(shape, BF16)

    reduce_vmem, reduce_sems = line_reduce_scratch(outer, span, hidden)
    return pl.pallas_call(
        functools.partial(closing_kernel, outer, inner, shards),
        out_shape=(
            jax.ShapeDtypeStruct((rows, cols), F32),
            jax.ShapeDtypeStruct((parts, piece, 3 * width), BF16),
            jax.ShapeDtypeStruct(small.shape, F32),
            jax.ShapeDtypeStruct(sums.shape, F32),
            jax.ShapeDtypeStruct((1, lanes), F32),
            *[swapped(array) for array in (down, gate, rest, ups)],
        ),
        in_specs=[IN_VMEM] * 9 + [IN_HBM] * 6,
        out_specs=[IN_VMEM] * 5 + [IN_HBM] * 4,
        scratch_shapes=[
            pltpu.VMEM((outer, inner * rows, cols), BF16),
            *reduce_vmem,
            pltpu.VMEM((span, hidden), BF16),
            stripes,
            stripes,
            pltpu.VMEM((parts, shards * piece, 3 * width), BF16),
            pltpu.VMEM((16, cols), F32),
            pltpu.VMEM((count, 1, lanes), F32),
            pltpu.VMEM((count, 1, lanes), F32),
            pltpu.VMEM((ys, parts, piece, 3 * width), BF16),
            pieces,
            pieces,
            pltpu.VMEM((parts, piece, 3 * width), BF16),
            pltpu.VMEM((shards,) + small.shape, F32),
            pltpu.VMEM((shards,) + sums.shape, F32),
        ]
        + bufs
        + sems
        + [DMA((2, ys, parts))] * 2
        + [DMA((2, parts))]
        + [DMA((2, 2, ys))] * 2
        + [DMA((2, 4, inner * shards)), DMA((2, count)), DMA((2, 2))]
        + reduce_sems
        + [DMA((6,))],
        compiler_params=pltpu.CompilerParams(
            collective_id=collective, has_side_effects=True, vmem_limit_bytes=60 * 2**20
        ),
        cost_estimate=cost(80),
        name="closing",
    )(
        both,
        w_in,
        z,
        x,
        dmid,
        gain,
        gain2,
        small,
        sums,
        n1,
        dout,
        down,
        gate,
        rest,
        ups,
    )


def unpack_kernel(inner, channels, block_width, *refs):
    sources, targets = refs[:10], refs[10:27]
    held, made, in_sem, out_sem = refs[27:36], refs[36:42], refs[42], refs[43]
    gate_ref, rest_ref, up_ref, down_ref, mix_ref, blocks_ref, sums_ref = held[:7]
    fetch = [
        pltpu.make_async_copy(sources[k], held[k], in_sem.at[k]) for k in range(len(held))
    ]
    for copy in fetch:
        copy.start()
    store = []
    gains_ref = sources[9]
    rate, entry, taps, conv_b, rate_b, entry_b, decay, first_gain, second_gain = targets[8:]
    for copy in fetch:
        copy.wait()
    for k in range(2):
        copy = pltpu.make_async_copy(held[7 + k], targets[6 + k], out_sem.at[6 + k])
        copy.start()
        store.append(copy)
    gate, up, down = made[:3]
    slots, piece, hidden = down_ref.shape
    cut = gate_ref.shape[2]
    tail = hidden - cut
    head = hidden - up_ref.shape[2]
    shards = slots // inner
    parts, width = mix_ref.shape[0], mix_ref.shape[2] // 3
    places = [
        ((h * inner + i) * hidden, i * shards + h) for i in range(inner) for h in range(shards)
    ]

    def ship(k):
        copy = pltpu.make_async_copy(made[k], targets[k], out_sem.at[k])
        copy.start()
        store.append(copy)

    for first, slot in places:
        gate[:, first : first + cut] = gate_ref[slot].astype(F32)
        gate[:, first + cut : first + hidden] = rest_ref[slot][:, :tail].astype(F32)
    ship(0)
    for first, slot in places:
        up[:, first : first + head] = rest_ref[slot][:, tail:].astype(F32)
        up[:, first + head : first + hidden] = up_ref[slot].astype(F32)
    ship(1)
    for first, slot in places:
        down[:, first : first + hidden] = down_ref[slot].astype(F32)
    ship(2)
    for k in range(3):
        lanes = slice(k * width, k * width + width)
        made[3 + k][...] = jnp.concatenate(
            [mix_ref[p][:, lanes].astype(F32)[:, :channels] for p in range(parts)], axis=1
        )
        ship(3 + k)
    blocks = rate.shape[1]
    tall = blocks_ref.shape[0] // (2 * blocks)
    for k, dst in enumerate((rate, entry)):
        for j in range(blocks):
            top = (k * blocks + j) * tall
            dst[:, j, :] = blocks_ref[top : top + block_width, :block_width]
    taps[...] = sums_ref[4:8, :channels]
    for row, dst in ((3, conv_b), (1, rate_b), (2, entry_b), (0, decay)):
        dst[...] = sums_ref[row, :channels]
    first_gain[...] = gains_ref[0, :piece]
    second_gain[...] = gains_ref[0, piece : 2 * piece]
    for copy in store:
        copy.wait()


def unpack(
    gate, rest, up, down, mix, small, sums, result, grad, gains, inner, channels, blocks, block_width
):
    slots, piece, hidden = down.shape
    across = jax.ShapeDtypeStruct((piece, slots * hidden), F32)
    wide = jax.ShapeDtypeStruct((piece, mix.shape[0] * channels), F32)
    square = jax.ShapeDtypeStruct((block_width, blocks, block_width), F32)
    vector = jax.ShapeDtypeStruct((channels,), F32)
    taps = jax.ShapeDtypeStruct((4, channels), F32)
    gain = jax.ShapeDtypeStruct((piece,), F32)
    held = (gate, rest, up, down, mix, small, sums, result, grad)
    made = (across,) * 3 + (wide,) * 3
    return pl.pallas_call(
        functools.partial(unpack_kernel, inner, channels, block_width),
        out_shape=made
        + tuple(jax.ShapeDtypeStruct(x.shape, x.dtype) for x in (result, grad))
        + (square,) * 2
        + (taps,)
        + (vector,) * 4
        + (gain,) * 2,
        in_specs=[IN_HBM] * 9 + [IN_VMEM],
        out_specs=[IN_HBM] * 8 + [IN_VMEM] * 9,
        scratch_shapes=[pltpu.VMEM(x.shape, x.dtype) for x in held + made]
        + [DMA((len(held),)), DMA((8,))],
        compiler_params=pltpu.CompilerParams(vmem_limit_bytes=60 * 2**20),
        cost_estimate=cost(5),
        name="unpack",
    )(*held, gains)


def body(
    tokens,
    first_gain,
    branch_weight,
    input_weight,
    conv_weight,
    conv_bias,
    rate_weight,
    rate_bias,
    entry_weight,
    entry_bias,
    decay_param,
    output_weight,
    second_gain,
    hidden_gate,
    hidden_up,
    hidden_down,
    cotangent,
):
    quarters, _, chunk, model = tokens.shape
    rows = quarters * chunk
    parts = lax.axis_size("seq")
    shards = lax.axis_size("shard")
    inner = 2
    outer = parts // inner
    seq_at = lax.axis_index("seq")
    inner_at = lax.rem(seq_at, inner)
    lru = branch_weight.shape[1]
    channels = lru // parts
    width = (channels + LANES) // LANES * LANES
    spare = width - channels
    blocks, block_width = rate_weight.shape[0], rate_weight.shape[1]
    piece = model // (parts * shards)

    def own(weight, axis):
        part = lax.dynamic_slice_in_dim(weight, seq_at * channels, channels, axis)
        pads = [(0, 0), (0, 0)]
        pads[axis] = (0, spare)
        return jnp.pad(part, pads)

    x = tokens.reshape(rows, model)
    cot = cotangent.reshape(rows, model)
    gain1, gain2 = first_gain[None], second_gain[None]
    params, mid, z, h, v, proj, gates, n1, w_in, w_out, n2, cot_all = forward(
        x,
        gain1,
        gain2,
        (conv_weight, conv_bias, rate_bias, entry_bias, decay_param),
        rate_weight.transpose(1, 0, 2),
        entry_weight.transpose(1, 0, 2),
        cot,
        jnp.concatenate([own(branch_weight, 1), own(input_weight, 1)], axis=1),
        own(output_weight, 0),
        quarters,
        chunk,
        outer,
        inner,
        shards,
        0,
    )
    w_in = w_in.reshape(model, 2 * width)
    n2 = n2.reshape(inner * shards * rows, model)
    cot_all = cot_all.reshape(inner * shards * rows, model)
    hidden = hidden_gate.shape[1] // inner
    wg = lax.dynamic_slice_in_dim(hidden_gate, inner_at * hidden, hidden, 1)
    wu = lax.dynamic_slice_in_dim(hidden_up, inner_at * hidden, hidden, 1)
    wd = lax.dynamic_slice_in_dim(hidden_down, inner_at * hidden, hidden, 0)

    gm = dot(n2, wg)
    um = dot(n2, wu)
    act, slope = gelu_and_slope(gm)
    mm = (act * um).astype(BF16)
    dmm = dot(cot_all, wd, ((1,), (1,)))
    dgm = (dmm * um * slope).astype(BF16)
    dum = (dmm * act).astype(BF16)
    dmid, gain2_grad, dout, partial, down_sum, gate_sum, rest_terms, up_terms = turn(
        dgm,
        dum,
        mm,
        mid,
        cot,
        gain2,
        hidden_gate,
        hidden_up,
        hidden_down,
        n2,
        cot_all,
        outer,
        inner,
        shards,
        1,
    )
    both, small, sums, result, rest_sum = scan_backward(
        quarters,
        chunk,
        blocks,
        block_width,
        dout,
        w_out,
        proj,
        h,
        v,
        params,
        gates,
        mid,
        partial,
        rest_terms,
        outer,
        inner,
        shards,
        2,
    )
    tokens_grad, mix, small, sums, gains, down_sum, gate_sum, rest_sum, up_sum = closing(
        both,
        w_in,
        z,
        x,
        dmid,
        gain1,
        gain2_grad,
        small,
        sums,
        n1.reshape(parts * rows, model),
        dout.reshape(parts * rows, model),
        down_sum,
        gate_sum,
        rest_sum,
        up_terms,
        outer,
        inner,
        shards,
        3,
    )
    (
        gate_grad,
        up_grad,
        down_grad,
        branch_grad,
        input_grad,
        output_grad,
        result,
        tokens_grad,
        rate_grad,
        entry_grad,
        tap_grad,
        conv_bias_grad,
        rate_bias_grad,
        entry_bias_grad,
        decay_grad,
        gain1_grad,
        gain2_grad,
    ) = unpack(
        gate_sum,
        rest_sum,
        up_sum,
        down_sum,
        mix,
        small,
        sums,
        result,
        tokens_grad,
        gains,
        inner,
        channels,
        blocks,
        block_width,
    )
    return (
        result.reshape(tokens.shape),
        tokens_grad.reshape(tokens.shape),
        gain1_grad,
        branch_grad,
        input_grad,
        tap_grad,
        conv_bias_grad,
        rate_grad.transpose(1, 0, 2),
        rate_bias_grad,
        entry_grad.transpose(1, 0, 2),
        entry_bias_grad,
        decay_grad,
        output_grad.T,
        gain2_grad,
        gate_grad,
        up_grad,
        down_grad.T,
    )


def solution(mesh):
    placed = (
        P(None, "shard", "seq", None),
        P(),
        P("shard", None),
        P("shard", None),
        P(None, "seq"),
        P("seq"),
        P("seq", None, None),
        P("seq"),
        P("seq", None, None),
        P("seq"),
        P("seq"),
        P(None, "shard"),
        P(),
        P(None, "shard"),
        P(None, "shard"),
        P("shard", None),
        P(None, "shard", "seq", None),
    )
    return jax.shard_map(
        body,
        mesh=mesh,
        in_specs=placed,
        out_specs=(
            P(None, "shard", "seq", None),
            P(None, "shard", "seq", None),
            P(("seq", "shard")),
            P(("seq", "shard"), None),
            P(("seq", "shard"), None),
            P(None, "seq"),
            P("seq"),
            P("seq", None, None),
            P("seq"),
            P("seq", None, None),
            P("seq"),
            P("seq"),
            P(None, ("seq", "shard")),
            P(("seq", "shard")),
            P(("seq", "shard"), None),
            P(("seq", "shard"), None),
            P(None, ("seq", "shard")),
        ),
        check_vma=False,
    )
```

```python
import functools

import jax
import jax.numpy as jnp
from jax import lax
from jax.experimental import pallas as pl
from jax.experimental.pallas import tpu as pltpu
from jax.sharding import PartitionSpec as P

EPSILON = 1e-06
DECAY_SCALE = 8.0
MULT_FLOOR = 0.01
LANES = 128
SEGMENTS = 8
GELU_C = 0.7978845608028654
GELU_A = 0.044715
F32 = jnp.float32
BF16 = jnp.bfloat16


MESH = pl.DeviceIdType.MESH
IN_HBM = pl.BlockSpec(memory_space=pltpu.HBM)
IN_VMEM = pl.BlockSpec(memory_space=pltpu.VMEM)
DMA = pltpu.SemaphoreType.DMA


def cost(us):
    return pl.CostEstimate(flops=0, bytes_accessed=int(us * 3.3e6), transcendentals=0)


def dot(left, right, dims=((1,), (0,))):
    return lax.dot_general(left, right, (dims, ((), ())), preferred_element_type=F32)


def gelu_and_slope(x):
    inner = GELU_C * (x + GELU_A * x * x * x)
    t = jnp.tanh(inner)
    half = 0.5 * (1.0 + t)
    slope = half + 0.5 * x * (1.0 - t * t) * (GELU_C * (1.0 + 3.0 * GELU_A * x * x))
    return x * half, slope


def gelu_tanh(x):
    return x * (0.5 * (1.0 + jnp.tanh(GELU_C * (x + GELU_A * x * x * x))))


def sigmoid(x):
    return 0.5 * jnp.tanh(0.5 * x) + 0.5


def softplus(x):
    return jnp.maximum(x, 0.0) + jnp.log1p(jnp.exp(-jnp.abs(x)))


def lane_groups(width):
    return [slice(g * LANES, (g + 1) * LANES) for g in range(width // LANES)]


def put(ref, rows, value):
    for g, lanes in enumerate(lane_groups(value.shape[1])):
        ref[g, rows, :] = value[:, lanes]


def take(ref, rows):
    return jnp.concatenate([ref[g, rows, :] for g in range(ref.shape[0])], axis=1)


def strided_scan(steps, groups, load, store):
    def step(k, carry):
        i = steps(k)
        out = []
        for g in range(groups):
            state, total = carry[g]
            factor, term = load(g, i)
            state = factor * state + term
            total = factor * total
            store(g, i, state, total)
            out.append((state, total))
        return tuple(out)

    return step


TAP, CONV_B, RATE_B, ENTRY_B, DECAY = 0, 4, 5, 6, 7


def gate_values(pre, log_scale, width):
    r = sigmoid(pre[:, :width])
    e = sigmoid(pre[:, width:])
    a = jnp.exp(r * log_scale)
    room = 1.0 - a * a
    m = jnp.sqrt(jnp.maximum(room, MULT_FLOOR))
    return r, e, a, room, m


class Place:
    def __init__(self, outer, inner, shards):
        self.outer, self.inner, self.shards = outer, inner, shards
        self.parts, self.ys, self.count = outer * inner, shards // 2, outer * inner * shards
        self.chips = inner * self.ys
        self.s, self.h = lax.axis_index("seq"), lax.axis_index("shard")
        self.o, self.i = self.s // inner, lax.rem(self.s, inner)
        self.y, self.core = self.h // 2, lax.rem(self.h, 2)
        self.beside = (self.o * inner + 1 - self.i, self.h)
        self.above, self.below = (self.s + inner, self.h), (self.s - inner, self.h)
        self.sibling = (self.s, self.along(0, 1))

    def along(self, dy, other=0):
        y = lax.rem(self.y + dy + self.ys, self.ys)
        return y * 2 + lax.rem(self.core + other, 2)

    def chip(self, q, back=False):
        di, dy = q // self.ys, q - q // self.ys * self.ys
        if back:
            di, dy = self.inner - di, self.ys - dy
        return lax.rem(self.i + di, self.inner), lax.rem(self.y + dy, self.ys)

    def near(self, q, other=0, back=False):
        i, y = self.chip(q, back)
        h = y * 2 + lax.rem(self.core + other, 2)
        return (self.o * self.inner + i, h), i * self.shards + h

    def far_first(self, n):
        sign = 2 * ((2 * self.o) // self.outer) - 1
        return lax.rem(self.o + sign * (n + 1) + 2 * self.outer, self.outer)

    def branches(self, fn):
        for o0 in range(self.outer):
            pl.when(self.o == o0)(functools.partial(fn, o0))


def hello(to):
    barrier = pltpu.get_barrier_semaphore()
    pl.semaphore_signal(barrier, inc=1, device_id=to, device_id_type=MESH)


def welcome(n):
    pl.semaphore_wait(pltpu.get_barrier_semaphore(), n)


def greet(others):
    for to in others:
        hello(to)
    welcome(len(others))


def greet_with_line(at, others):
    up, down = at.o < at.outer - 1, at.o > 0
    for to in others:
        hello(to)
    pl.when(up)(lambda: hello(at.above))
    pl.when(down)(lambda: hello(at.below))
    ends = lax.rem(at.o, at.outer - 1) == 0
    pl.when(ends)(lambda: welcome(len(others) + 1))
    pl.when(jnp.logical_not(ends))(lambda: welcome(len(others) + 2))


class Sent:
    def __init__(self):
        self.copies = []

    def __call__(self, src, dst, sems, at, to):
        copy = remote(src, dst, sems.at[(0,) + at], sems.at[(1,) + at], to)
        copy.start()
        self.copies.append(copy)

    def finish(self):
        for copy in self.copies:
            copy.wait_send()


def received(like, here, sems, at, source):
    remote(like, here, sems.at[(0,) + at], sems.at[(1,) + at], source).wait_recv()


def line_gather(
    at,
    o0,
    x_ref,
    out,
    across,
    up,
    down,
    between=lambda k: None,
    each=lambda row: None,
    side=None,
    slim=0,
):
    send = Sent()
    rows = x_ref.shape[0]
    half = rows // HALVES
    low = pl.ds(rows - slim, slim)

    def slot(row, other=False):
        return out.at[row * at.inner + (1 - at.i if other else at.i)]

    def some(row, part):
        less = slim if slim and row != o0 and part == HALVES - 1 else 0
        return pl.ds(part * half, half - less)

    def pass_on(row, part, sems, to):
        some_rows = pl.ds(part * half, half)
        src = x_ref if row == o0 else slot(row)
        send(src.at[some_rows], slot(row).at[some_rows], sems, (row, part), to)

    def cross(row, part):
        src = x_ref if row == o0 else slot(row)
        send(src.at[some(row, part)], slot(row).at[some(row, part)], across, (row, part), at.beside)

    def crossed(row):
        for part in range(HALVES):
            here = slot(row, True).at[some(row, part)]
            received(here, here, across, (row, part), at.beside)

    def slim_on(row):
        here = slot(row, True).at[low]
        if row <= o0 < at.outer - 1:
            send(here, here, side[0], (row,), at.above)
        if row >= o0 > 0:
            send(here, here, side[1], (row,), at.below)

    def slim_came(row, sems, source):
        here = slot(row, True).at[low]
        received(here, here, sems, (row,), source)

    for k in range(at.outer):
        lower, upper = o0 - k, o0 + k
        for part in range(HALVES):
            here = x_ref.at[pl.ds(part * half, half)]
            if lower >= 0:
                if k > 0:
                    received(here, here, up, (lower, part), at.below)
                if o0 < at.outer - 1:
                    pass_on(lower, part, up, at.above)
                cross(lower, part)
            if upper < at.outer:
                if k > 0:
                    received(here, here, down, (upper, part), at.above)
                if o0 > 0:
                    pass_on(upper, part, down, at.below)
                if k > 0:
                    cross(upper, part)
        if slim and k == 1:
            crossed(o0)
            slim_on(o0)
        if slim and k > 1:
            for row, sems, source in (
                (o0 - k + 1, side[0], at.below),
                (o0 + k - 1, side[1], at.above),
            ):
                if 0 <= row < at.outer:
                    slim_came(row, sems, source)
                    slim_on(row)
        between(k)
    between(at.outer)
    for row in sorted(range(at.outer), key=lambda row: abs(row - o0)):
        if row != o0 or not slim:
            crossed(row)
        if slim and row != o0 and abs(row - o0) == at.outer - 1:
            slim_came(row, side[0] if row < o0 else side[1], at.below if row < o0 else at.above)
        each(row)
    send.finish()


class LineSum:
    def __init__(self, at, p, bufs, sems, side=None):
        self.at, self.p = at, p
        self.x_in, self.up_in, self.down_in, self.sums = bufs
        self.across, self.up, self.down = sems
        self.rows = self.x_in.shape[1]
        self.slim = 0
        if side is not None:
            self.s_up_in, self.s_down_in, self.s_sums, self.s_in = side[:4]
            self.s_up, self.s_down, self.s_across = side[4:]
            self.slim = self.s_in.shape[0]

    def block(self, d, i):
        return self.p.at[d, pl.ds(pl.multiple_of(i * self.rows, self.rows), self.rows)]

    def cross(self, d, part):
        half = self.rows // HALVES
        some = pl.ds(part * half, half - (self.slim if part == HALVES - 1 else 0))
        return remote(
            self.block(d, 1 - self.at.i).at[some],
            self.x_in.at[d].at[some],
            self.across.at[0, d, part],
            self.across.at[1, d, part],
            self.at.beside,
        )

    def start(self, d):
        for part in range(HALVES):
            self.cross(d, part).start()

    def steps(self, o0, last_add, between=lambda n: None):
        at, rows, slim = self.at, self.rows, self.slim
        send = Sent()
        order = sorted(range(at.outer), key=lambda d: (-abs(d - o0), d))
        low, half = rows - slim, rows // HALVES

        def arrivals(d, index, mine, up_in, down_in, up, down):
            terms = []
            if d >= o0 > 0:
                received(mine, mine, up, index, at.below)
                terms.append(up_in.at[d])
            if d <= o0 < at.outer - 1:
                received(mine, mine, down, index, at.above)
                terms.append(down_in.at[d])
            return terms

        def total_of(terms, some):
            total = terms[0][some, :].astype(F32)
            for term in terms[1:]:
                total = total + term[some, :].astype(F32)
            return total

        for n, d in enumerate(order):
            mine = self.block(d, at.i)
            target = self.sums.at[d]
            for part in range(HALVES):
                part_rows = pl.ds(part * half, half)
                self.cross(d, part).wait_recv()
                along = [mine] + arrivals(
                    d,
                    (d, part),
                    mine.at[part_rows],
                    self.up_in,
                    self.down_in,
                    self.up,
                    self.down,
                )
                both = along + [self.x_in.at[d]]

                def add(some, both=both, target=target, d=d):
                    total = total_of(both, some)
                    if d == o0:
                        last_add(some, total)
                    else:
                        target[some, :] = total.astype(BF16)

                def add_low(some, along=along, target=target):
                    target[some, :] = total_of(along, some).astype(BF16)

                add_rows(min((part + 1) * half, low), add, part * half)
                if slim and d != o0 and part == HALVES - 1:
                    add_rows(rows, add_low, low)
                if d > o0:
                    here, there = target.at[part_rows], self.up_in.at[d].at[part_rows]
                    send(here, there, self.up, (d, part), at.above)
                if d < o0:
                    here, there = target.at[part_rows], self.down_in.at[d].at[part_rows]
                    send(here, there, self.down, (d, part), at.below)
            if slim:
                theirs = self.block(d, 1 - at.i).at[pl.ds(low, slim)]
                extra = [theirs] + arrivals(
                    d, (d,), theirs, self.s_up_in, self.s_down_in, self.s_up, self.s_down
                )
                aside = self.s_sums.at[d]

                def add_aside(some, extra=extra, aside=aside):
                    aside[some, :] = total_of(extra, some).astype(BF16)

                add_rows(slim, add_aside)
                if d > o0:
                    send(aside, self.s_up_in.at[d], self.s_up, (d,), at.above)
                if d < o0:
                    send(aside, self.s_down_in.at[d], self.s_down, (d,), at.below)
                if d == o0:
                    send(aside, self.s_in, self.s_across, (), at.beside)
                    received(aside, self.s_in, self.s_across, (), at.beside)
                    for k in range(slim // 16):
                        some, here = pl.ds(low + 16 * k, 16), pl.ds(16 * k, 16)
                        last_add(some, total_of(along, some) + self.s_in[here, :].astype(F32))
            between(n)
        for d in range(at.outer):
            for part in range(HALVES):
                self.cross(d, part).wait_send()
        send.finish()


class LineReduce:
    def __init__(self, at, own, land, up, down):
        self.at, self.own, self.land, self.up, self.down = at, own, land, up, down

    def order(self, o0):
        return sorted(range(self.at.outer), key=lambda d: (-abs(d - o0), d))

    def ascent(self, d):
        at = self.at
        return remote(
            self.own.at[d], self.land.at[d], self.up.at[0, d], self.up.at[1, d], at.above
        )

    def descent(self, o0, d):
        slot = d if d != o0 - 1 else self.at.outer
        return remote(
            self.own.at[d], self.land.at[slot], self.down.at[0, d], self.down.at[1, d], self.at.below
        )

    def early(self, n, d, limit):
        at = self.at
        inside = n < limit
        last = at.outer - 1
        pl.when(jnp.logical_and(at.o == 0, inside))(lambda: self.ascent(d).start())
        far = remote(
            self.own.at[d], self.land.at[d], self.down.at[0, d], self.down.at[1, d], at.below
        )
        pl.when(jnp.logical_and(at.o == last, inside))(lambda: far.start())

    def push(self, o0, d):
        if d > o0:
            self.ascent(d).start()
        if d < o0:
            self.descent(o0, d).start()

    def absorb(self, o0, d):
        terms = []
        if d >= o0 > 0:
            self.ascent(d).wait_recv()
            terms.append(self.land.at[d])
        if d <= o0 < self.at.outer - 1:
            slot = d if d < o0 else self.at.outer
            self.descent(o0 + 1, d).wait_recv()
            terms.append(self.land.at[slot])
        mine = self.own.at[d]

        def add(rows):
            total = mine[rows, :].astype(F32)
            for term in terms:
                total = total + term[rows, :].astype(F32)
            mine[rows, :] = total.astype(BF16)

        if terms:
            add_rows(mine.shape[0], add)

    def step(self, o0, n):
        d = self.order(o0)[n]
        self.absorb(o0, d)
        self.push(o0, d)

    def finish(self, o0):
        for d in range(self.at.outer):
            if d > o0:
                self.ascent(d).wait_send()
            if d < o0:
                self.descent(o0, d).wait_send()


def first_half(hidden):
    return -(-(hidden // 2) // LANES) * LANES


def line_reduce_scratch(outer, rows, cols):
    blocks = [pltpu.VMEM((outer, rows, cols), BF16), pltpu.VMEM((outer + 1, rows, cols), BF16)]
    return blocks, [DMA((2, outer))] * 2


SLIM = 16
HALVES = 2


def slim_scratch(outer, cols):
    blocks = [pltpu.VMEM((outer, SLIM, cols), BF16)] * 3 + [pltpu.VMEM((SLIM, cols), BF16)]
    return blocks, [DMA((2, outer))] * 2 + [DMA((2,))]


def line_sum_scratch(outer, rows, cols):
    return [pltpu.VMEM((outer, rows, cols), BF16)] * 4, [DMA((2, outer, HALVES))] * 3


def row_rms(values):
    return lax.rsqrt(jnp.mean(values * values, axis=-1, keepdims=True) + EPSILON)


def rms_back(values, scale, gain, grad):
    k = grad * gain
    mean = jnp.mean(k * values, axis=-1, keepdims=True)
    return scale * k - scale * scale * scale * values * mean


def run_scan(
    parts, quarters, chunk, proj_ref, par_ref, gates_ref, z_ref, h_ref, v_ref, u_pad, a_s, b_s
):
    length, width = h_ref.shape
    seg = length // SEGMENTS
    chunks = length // chunk

    def place(c):
        q = c // parts
        s = c - q * parts
        return pl.multiple_of((s * quarters + q) * chunk, chunk)

    def time_of(c):
        return pl.multiple_of(c * chunk, chunk)

    log_scale = -DECAY_SCALE * softplus(-par_ref[DECAY : DECAY + 1, :])
    bias = jnp.concatenate(
        [par_ref[RATE_B : RATE_B + 1, :], par_ref[ENTRY_B : ENTRY_B + 1, :]], axis=1
    )
    u_pad[0:8, :] = jnp.zeros((8, width), F32)

    def first(c, carry):
        u = proj_ref[pl.ds(place(c), chunk), width : 2 * width].astype(BF16).astype(F32)
        u_pad[pl.ds(pl.multiple_of(time_of(c) + 8, 8), chunk), :] = u
        wide = u_pad[pl.ds(time_of(c), chunk + 8), :]
        v = par_ref[CONV_B : CONV_B + 1, :] + par_ref[0:1, :] * wide[8:]
        for k in range(1, 4):
            v = v + par_ref[k : k + 1, :] * wide[8 - k : 8 - k + chunk]
        v = v.astype(BF16)
        v_ref[pl.ds(time_of(c), chunk), :] = v
        pre = dot(v, gates_ref[...]) + bias
        r, e, a, room, m = gate_values(pre, log_scale, width)
        put(a_s, pl.ds(time_of(c), chunk), a)
        put(b_s, pl.ds(time_of(c), chunk), m * e * v.astype(F32))
        return carry

    lax.fori_loop(0, chunks, first, 0)

    def load(g, i):
        at = pl.ds(i, SEGMENTS, stride=seg)
        return a_s[g, at, :], b_s[g, at, :]

    def store(g, i, state, total):
        at = pl.ds(i, SEGMENTS, stride=seg)
        b_s[g, at, :] = state
        a_s[g, at, :] = total

    groups = width // LANES
    start = (jnp.zeros((SEGMENTS, LANES), F32), jnp.ones((SEGMENTS, LANES), F32))
    ends = lax.fori_loop(
        0, seg, strided_scan(lambda k: k, groups, load, store), (start,) * groups, unroll=8
    )
    final = jnp.concatenate([e[0] for e in ends], axis=1)
    totals = jnp.concatenate([e[1] for e in ends], axis=1)
    carries = [jnp.zeros((1, width), F32)]
    for j in range(SEGMENTS - 1):
        carries.append(totals[j : j + 1] * carries[j] + final[j : j + 1])
    for j in range(SEGMENTS):
        per = seg // chunk

        def last(k, carry, j=j, per=per):
            c = j * per + k
            rows = pl.ds(time_of(c), chunk)
            h = take(b_s, rows) + take(a_s, rows) * carries[j]
            h_ref[rows, :] = h
            y = gelu_tanh(proj_ref[pl.ds(place(c), chunk), 0:width])
            z_ref[pl.ds(place(c), chunk), :] = (h.astype(BF16).astype(F32) * y).astype(BF16)
            return carry

        lax.fori_loop(0, per, last, 0)


def forward_kernel(
    outer,
    inner,
    shards,
    quarters,
    chunk,
    x_ref,
    gain1_ref,
    gain2_ref,
    taps_ref,
    conv_b_ref,
    rate_b_ref,
    entry_b_ref,
    decay_ref,
    rate_ref,
    entry_ref,
    cot_ref,
    wi_ref,
    wo_ref,
    par_ref,
    mid_ref,
    z_out,
    h_out,
    v_out,
    proj_out,
    gates_out,
    n1_out,
    wi_out,
    wo_out,
    n2_out,
    cot_out,
    own_s,
    n1_s,
    wi_s,
    wo_s,
    gates_s,
    u_pad,
    a_s,
    b_s,
    z_ref,
    h_ref,
    v_ref,
    proj_ref,
    gates_ref,
    p_s,
    cot_s,
    x_in,
    up_in,
    down_in,
    line_out,
    g_across,
    g_up,
    g_down,
    w_far,
    w_near,
    across,
    up,
    down,
    far,
    near,
    c_side,
    c_far,
    c_near,
    local,
    s_up_in,
    s_down_in,
    s_sums,
    s_in,
    s_up,
    s_down,
    s_across,
    g_side_up,
    g_side_down,
):
    at = Place(outer, inner, shards)
    parts, rows = at.parts, x_ref.shape[0]
    steps = list(range(1, at.ys))
    width2 = wi_ref.shape[1]
    width, depth, cols = width2 // 2, wi_ref.shape[0], wo_ref.shape[1]

    def normalize(some):
        x = x_ref[some, :].astype(F32)
        own_s[some, :] = (x * row_rms(x) * gain1_ref[...]).astype(BF16)

    add_rows(rows, normalize)
    greet_with_line(at, [at.sibling] + [at.near(q)[0] for q in range(1, at.chips)])
    weights = ((wi_ref, wi_s), (wo_ref, wo_s))
    keep = [
        pltpu.make_async_copy(own_s, n1_s.at[at.s], local.at[0]),
        pltpu.make_async_copy(wi_ref, wi_s.at[at.h], local.at[1]),
        pltpu.make_async_copy(wo_ref, wo_s.at[at.h], local.at[2]),
    ]
    for copy in keep:
        copy.start()
    send = Sent()

    def send_weights():
        for n, (src, dst) in enumerate(weights):
            for dy in steps:
                send(src, dst.at[at.h], w_far, (n, dy), (at.s, at.along(dy)))
            send(src, dst.at[at.h], w_near, (n, 0), at.sibling)

    send_weights()
    def build_gates():
        channels = decay_ref.shape[0]
        par_ref[...] = jnp.zeros(par_ref.shape, F32)
        par_ref[0:4, :channels] = taps_ref[...].astype(F32)
        for row, src in (
            (CONV_B, conv_b_ref),
            (RATE_B, rate_b_ref),
            (ENTRY_B, entry_b_ref),
            (DECAY, decay_ref),
        ):
            par_ref[row, :channels] = src[...]
        gates_s[...] = jnp.zeros(gates_s.shape, F32)
        block_width, blocks = rate_ref.shape[0], rate_ref.shape[1]
        for gate, src in enumerate((rate_ref, entry_ref)):
            for j in range(blocks):
                top, lane = j * block_width, gate * width + j * block_width
                gates_s[top : top + block_width, lane : lane + block_width] = src[:, j, :].astype(F32)
        gates_ref[...] = gates_s[...].astype(BF16)

    def project(d):
        total = None
        for k in range(shards):
            lanes = slice(k * depth, (k + 1) * depth)
            pair = jnp.concatenate([n1_s[d * inner + i, :, lanes] for i in range(inner)], axis=0)
            term = dot(pair, wi_s[k])
            total = term if total is None else total + term
        proj_ref[d * inner * rows : (d + 1) * inner * rows, :] = total

    def gather(o0):
        forward = Sent()

        def between(k):
            if k == 0:
                build_gates()
            if k != outer - 1:
                return
            for n, (src, dst) in enumerate(weights):
                for dy in steps:
                    source = at.along(-dy)
                    received(src, dst.at[source], w_far, (n, dy), (at.s, source))
                    forward(dst.at[source], dst.at[source], w_near, (n, dy), at.sibling)
            for n, (src, dst) in enumerate(weights):
                for dy in range(at.ys):
                    received(src, dst.at[at.along(-dy, 1)], w_near, (n, dy), at.sibling)
            for copy in keep:
                copy.wait()

        def each(row):
            project(row)

        side = (g_side_up, g_side_down)
        line_gather(at, o0, own_s, n1_s, g_across, g_up, g_down, between, each, side, SLIM)
        forward.finish()

    at.branches(gather)
    send(cot_ref, cot_s, c_side, (), at.beside)
    keep = [
        pltpu.make_async_copy(n1_s, n1_out, local.at[0]),
        pltpu.make_async_copy(wi_s, wi_out, local.at[1]),
        pltpu.make_async_copy(wo_s, wo_out, local.at[2]),
    ]
    for copy in keep:
        copy.start()
    run_scan(
        parts, quarters, chunk, proj_ref, par_ref, gates_ref, z_ref, h_ref, v_ref, u_pad, a_s, b_s
    )
    made = (
        (z_ref, z_out),
        (h_ref, h_out),
        (v_ref, v_out),
        (proj_ref, proj_out),
        (gates_ref, gates_out),
    )
    for n, (src, dst) in enumerate(made):
        keep.append(pltpu.make_async_copy(src, dst, local.at[6 + n]))
        keep[-1].start()
    side = (s_up_in, s_down_in, s_sums, s_in, s_up, s_down, s_across)
    line = LineSum(at, p_s, (x_in, up_in, down_in, line_out), (across, up, down), side)

    def back_project(n, carry):
        d = at.far_first(n)
        some = pl.ds(pl.multiple_of(d * inner * rows, inner * rows), inner * rows)
        for k in range(shards):
            p_s[d, :, k * cols : (k + 1) * cols] = dot(z_ref[some, :], wo_s[k]).astype(BF16)
        line.start(d)
        return carry

    lax.fori_loop(0, outer, back_project, 0)
    received(cot_ref, cot_s, c_side, (), at.beside)

    def slot(side, dy, other=0):
        i = 1 - at.i if side else at.i
        return cot_out.at[i * shards + at.along(dy, other)]

    mine = (cot_ref, cot_s)
    for side in range(2):
        keep.append(pltpu.make_async_copy(mine[side], slot(side, 0), local.at[3 + side]))
        keep[-1].start()
        for dy in steps:
            send(mine[side], slot(side, 0), c_far, (side, dy), (at.s, at.along(dy)))
        send(mine[side], slot(side, 0), c_near, (side, 0), at.sibling)

    def last_add(some, total):
        mid = x_ref[some, :].astype(F32) + total
        mid_ref[some, :] = mid
        own_s[some, :] = (mid * row_rms(mid) * gain2_ref[...]).astype(BF16)

    def branch(o0):
        forward = Sent()

        def between(n):
            if n != outer - 2:
                return
            for side in range(2):
                for dy in steps:
                    here = slot(side, -dy)
                    received(cot_ref, here, c_far, (side, dy), (at.s, at.along(-dy)))
                    forward(here, here, c_near, (side, dy), at.sibling)

        line.steps(o0, last_add, between)
        forward.finish()

    at.branches(branch)
    _, me = at.near(0)
    keep.append(pltpu.make_async_copy(own_s, n2_out.at[me], local.at[5]))
    keep[-1].start()
    quad = inner == 2 and at.ys == 2
    for q in (1, 2) if quad else reversed(range(1, at.chips)):
        send(own_s, n2_out.at[me], far, (q,), at.near(q)[0])
    send(own_s, n2_out.at[me], near, (0,), at.sibling)
    for q in (1, 2) if quad else range(1, at.chips):
        source, there = at.near(q, back=True)
        here = n2_out.at[there]
        received(own_s, here, far, (q,), source)
        if quad:
            half = here.at[pl.ds((2 - q) * (rows // 2), rows // 2)]
            send(half, half, far, (3 if q == 2 else 0,), at.near(3 - q)[0])
        send(here, here, near, (q,), at.sibling)
    if quad:
        here = n2_out.at[at.near(3)[1]]
        for q in (1, 2):
            half = here.at[pl.ds((q - 1) * (rows // 2), rows // 2)]
            received(half, half, far, (3 if q == 1 else 0,), at.near(q)[0])
        send(here, here, near, (3,), at.sibling)
    for q in range(at.chips):
        received(own_s, n2_out.at[at.near(q, 1, True)[1]], near, (q,), at.sibling)
    for side in range(2):
        for dy in range(at.ys):
            received(cot_ref, slot(side, -dy, 1), c_near, (side, dy), at.sibling)
    send.finish()
    for copy in keep:
        copy.wait()


def forward(
    x,
    gain1,
    gain2,
    channel,
    rate,
    entry,
    cot,
    w_in,
    w_out,
    quarters,
    chunk,
    outer,
    inner,
    shards,
    collective,
):
    rows, cols = x.shape
    parts, ys, chips = outer * inner, shards // 2, inner * shards // 2
    length, width = parts * rows, w_in.shape[1] // 2
    bufs, sems = line_sum_scratch(outer, rows, cols)
    side_vmem, side_sems = slim_scratch(outer, cols)
    plane = jax.ShapeDtypeStruct((inner * shards, rows, cols), BF16)
    lanes = pltpu.VMEM((width // LANES, length, LANES), F32)
    made = (
        ((length, width), BF16),
        ((length, width), F32),
        ((length, width), BF16),
        ((length, 2 * width), F32),
        ((width, 2 * width), BF16),
    )
    return pl.pallas_call(
        functools.partial(forward_kernel, outer, inner, shards, quarters, chunk),
        out_shape=(
            jax.ShapeDtypeStruct((8, width), F32),
            jax.ShapeDtypeStruct((rows, cols), F32),
            *[jax.ShapeDtypeStruct(shape, dtype) for shape, dtype in made],
            jax.ShapeDtypeStruct((parts, rows, cols), BF16),
            jax.ShapeDtypeStruct((shards,) + w_in.shape, BF16),
            jax.ShapeDtypeStruct((shards,) + w_out.shape, BF16),
            plane,
            plane,
        ),
        in_specs=[IN_VMEM] * 11 + [IN_HBM] * 2,
        out_specs=[IN_VMEM] * 2 + [IN_HBM] * 10,
        scratch_shapes=[
            pltpu.VMEM((rows, cols), BF16),
            pltpu.VMEM((parts, rows, cols), BF16),
            pltpu.VMEM((shards,) + w_in.shape, BF16),
            pltpu.VMEM((shards,) + w_out.shape, BF16),
            pltpu.VMEM((width, 2 * width), F32),
            pltpu.VMEM((length + 8, width), F32),
            lanes,
            lanes,
            *[pltpu.VMEM(shape, dtype) for shape, dtype in made],
            pltpu.VMEM((outer, inner * rows, cols), BF16),
            pltpu.VMEM((rows, cols), BF16),
        ]
        + bufs
        + [DMA((2, outer, HALVES))] * 3
        + [DMA((2, 2, ys))] * 2
        + sems
        + [DMA((2, chips))] * 2
        + [DMA((2,))]
        + [DMA((2, 2, ys))] * 2
        + [DMA((11,))]
        + side_vmem
        + side_sems
        + [DMA((2, outer))] * 2,
        compiler_params=pltpu.CompilerParams(
            collective_id=collective, has_side_effects=True, vmem_limit_bytes=60 * 2**20
        ),
        cost_estimate=cost(140),
        name="forward",
    )(x, gain1, gain2, *channel, rate, entry, cot, w_in, w_out)


class PlaneSum:
    def __init__(self, at, n, p, near_in, far_in, far_out, near, far):
        self.at, self.n, self.p = at, n, p
        self.near_in, self.far_in, self.far_out = near_in, far_in, far_out
        self.near, self.far = near, far
        self.rows = near_in.shape[2]

    def block(self, q, other):
        i, y = self.at.chip(q)
        core = lax.rem(self.at.core + other, 2)
        rows = pl.ds(pl.multiple_of(core * self.rows, self.rows), self.rows)
        return self.p.at[i * self.at.ys + y, rows]

    def to_sibling(self, q):
        n = self.n
        return remote(
            self.block(q, 1),
            self.near_in.at[n, q],
            self.near.at[0, n, q],
            self.near.at[1, n, q],
            self.at.sibling,
        )

    def onward(self, q, back=False):
        n = self.n
        return remote(
            self.far_out.at[n, q],
            self.far_in.at[n, q],
            self.far.at[0, n, q],
            self.far.at[1, n, q],
            self.at.near(q, 0, back)[0],
        )

    def combine_one(self, k, own=None):
        q = self.at.chips - 1 - k
        self.to_sibling(q).wait_recv()
        mine = self.block(q, 0) if own is None else own.at[q]

        def add(rows):
            total = mine[rows, :].astype(F32) + self.near_in[self.n, q, rows, :].astype(F32)
            self.far_out[self.n, q, rows, :] = total.astype(BF16)

        add_rows(self.rows, add)
        self.onward(q).start()

    def combine(self, own=None):
        def one(k, carry):
            self.combine_one(k, own)
            return carry

        lax.fori_loop(0, self.at.chips - 1, one, 0)
        self.to_sibling(0).wait_recv()

    def total(self, rows, own=None):
        n = self.n
        mine = self.block(0, 0) if own is None else own.at[0]
        value = mine[rows, :].astype(F32) + self.near_in[n, 0, rows, :].astype(F32)
        for q in range(1, self.at.chips):
            value = value + self.far_in[n, q, rows, :].astype(F32)
        return value

    def arrive(self):
        for q in range(1, self.at.chips):
            self.onward(q, True).wait_recv()

    def finish(self):
        for q in range(self.at.chips):
            self.to_sibling(q).wait_send()
        for q in range(1, self.at.chips):
            self.onward(q).wait_send()


def turn_kernel(
    outer,
    inner,
    shards,
    dgm_from,
    dum_from,
    mm_from,
    mid_from,
    cot_from,
    gain_ref,
    wg_ref,
    wu_ref,
    wd_ref,
    n2_ref,
    cots_ref,
    dmid_ref,
    gain_grad_ref,
    dout_ref,
    q_ref,
    down_ref,
    gate_ref,
    rest_ref,
    up_ref,
    mm_ref,
    dgm_ref,
    dum_ref,
    mid_ref,
    cot_ref,
    early_sem,
    p_s,
    q_s,
    dout_s,
    gain_s,
    wg_s,
    wu_s,
    wd_s,
    n2_s,
    cots_s,
    u_s,
    r_s,
    near_in,
    far_in,
    far_out,
    down_own,
    down_land,
    gate_own,
    gate_land,
    near,
    far,
    across,
    up,
    low,
    down_up,
    down_low,
    gate_up,
    gate_low,
    local,
    q_sem,
    u_sem,
    r_sem,
):
    at = Place(outer, inner, shards)
    model, hidden = wg_s.shape
    tile = min(512, model)
    pair = p_s.shape[1]
    span = model // outer
    own = pl.ds(pl.multiple_of(at.i * hidden, hidden), hidden)
    first = load_all([(mm_from, mm_ref)], early_sem)
    load = [
        pltpu.make_async_copy(cots_ref, cots_s, local.at[1]),
        pltpu.make_async_copy(wg_ref.at[:, own], wg_s, local.at[2]),
        pltpu.make_async_copy(wu_ref.at[:, own], wu_s, local.at[3]),
        pltpu.make_async_copy(n2_ref, n2_s, local.at[4]),
        pltpu.make_async_copy(wd_ref.at[own, :], wd_s, local.at[5]),
    ]
    for copy in load[:3]:
        copy.start()
    second = load_all([(dgm_from, dgm_ref), (dum_from, dum_ref)], early_sem.at[pl.ds(1, 2)])
    for copy in load[3:]:
        copy.start()
    third = load_all([(mid_from, mid_ref), (cot_from, cot_ref)], early_sem.at[pl.ds(3, 2)])
    greet_with_line(at, [at.sibling] + [at.near(q)[0] for q in range(1, at.chips)])
    grad = PlaneSum(at, 0, p_s, near_in, far_in, far_out, near, far)
    down = LineReduce(at, down_own, down_land, down_up, down_low)
    gate = LineReduce(at, gate_own, gate_land, gate_up, gate_low)

    def columns(d):
        return pl.ds(pl.multiple_of(d * span, span), span)

    load[0].wait()
    first[0].wait()

    def down_grad(n, carry):
        d = at.far_first(n)
        down_own[d] = dot(cots_s[:, columns(d)], mm_ref[...], ((0,), (0,))).astype(BF16)
        down.early(n, d, outer - 2)
        return carry

    down_grad(0, 0)
    for copy in load[1:3] + second:
        copy.wait()

    def back(k, carry):
        q = at.chips - 1 - k
        i, y = at.chip(q)
        c = i * at.ys + y
        rows = pl.ds(pl.multiple_of(c * pair, pair), pair)
        for lane in range(0, model, tile):
            lanes = slice(lane, lane + tile)
            block = dot(dgm_ref[rows, :], wg_s[lanes, :], ((1,), (1,)))
            block = block + dot(dum_ref[rows, :], wu_s[lanes, :], ((1,), (1,)))
            p_s[c, :, lanes] = block.astype(BF16)
        grad.to_sibling(q).start()
        pl.when(k > 0)(lambda: grad.combine_one(k - 1))
        return carry

    lax.fori_loop(0, at.chips, back, 0)
    grad.to_sibling(0).wait_recv()
    lax.fori_loop(1, outer, down_grad, 0)
    load[3].wait()

    cut = gate_own.shape[2]

    def keep_r(n):
        slot = lax.rem(n, 2)
        there = rest_ref.at[at.far_first(n), :, : hidden - cut]
        return pltpu.make_async_copy(r_s.at[slot], there, r_sem.at[slot])

    def gate_grad(n, carry):
        d = at.far_first(n)
        pl.when(n >= 2)(lambda: keep_r(n - 2).wait())
        block = dot(n2_s[:, columns(d)], dgm_ref[...], ((0,), (0,))).astype(BF16)
        gate_own[d] = block[:, :cut]
        r_s[lax.rem(n, 2)] = block[:, cut:]
        keep_r(n).start()
        return carry

    lax.fori_loop(0, outer, gate_grad, 0)
    for n in range(max(outer - 2, 0), outer):
        keep_r(n).wait()

    def first_down(o0):
        if 0 < o0 < outer - 1:
            down.step(o0, 0)

    at.branches(first_down)
    load[4].wait()

    def keep_q(c):
        slot = lax.rem(c, 2)
        return pltpu.make_async_copy(q_s.at[slot], q_ref.at[c], q_sem.at[slot])

    def ahead(c, carry):
        rows = pl.ds(pl.multiple_of(c * pair, pair), pair)
        pl.when(c >= 2)(lambda: keep_q(c - 2).wait())
        for lane in range(0, model, tile):
            lanes = slice(lane, lane + tile)
            q_s[lax.rem(c, 2), :, lanes] = dot(mm_ref[rows, :], wd_s[:, lanes]).astype(BF16)
        keep_q(c).start()
        return carry

    lax.fori_loop(0, at.chips, ahead, 0)
    for c in range(max(at.chips - 2, 0), at.chips):
        keep_q(c).wait()
    gain_s[...] = jnp.zeros(gain_s.shape, F32)
    for copy in third:
        copy.wait()
    grad.arrive()

    def norm_back(rows):
        dn2 = grad.total(rows)
        mid = mid_ref[rows, :]
        scale = row_rms(mid)
        gain_s[...] += dn2 * mid * scale
        dmid = cot_ref[rows, :].astype(F32) + rms_back(mid, scale, gain_ref[...], dn2)
        dmid_ref[rows, :] = dmid
        dout_s[rows, :] = dmid.astype(BF16)

    add_rows(dout_s.shape[0], norm_back)
    gain_grad_ref[...] = jnp.sum(gain_s[...], axis=0, keepdims=True)
    keep = pltpu.make_async_copy(dout_s, dout_ref.at[at.s], local.at[0])
    keep.start()

    head = u_s.shape[2] - up_ref.shape[2]

    class keep_u:
        def __init__(self, n):
            slot, d = lax.rem(n, 2), at.far_first(n)
            block = u_s.at[slot]
            self.copies = (
                pltpu.make_async_copy(
                    block.at[:, :head], rest_ref.at[d, :, hidden - cut :], u_sem.at[0, slot]
                ),
                pltpu.make_async_copy(block.at[:, head:], up_ref.at[d], u_sem.at[1, slot]),
            )

        def start(self):
            for copy in self.copies:
                copy.start()

        def wait(self):
            for copy in self.copies:
                copy.wait()

    def up_grad(n, carry):
        pl.when(n >= 2)(lambda: keep_u(n - 2).wait())
        u_s[lax.rem(n, 2)] = dot(
            n2_s[:, columns(at.far_first(n))], dum_ref[...], ((0,), (0,))
        ).astype(BF16)
        keep_u(n).start()
        return carry

    def branch(o0):
        ends = o0 in (0, outer - 1)

        def between(k):
            if k == 0:
                if ends:
                    down.push(o0, down.order(o0)[outer - 2])
                    for d in gate.order(o0)[:-1]:
                        gate.push(o0, d)
                else:
                    for n in range(1, outer - 1):
                        down.step(o0, n)
                lax.fori_loop(0, outer, up_grad, 0)
            if k == outer - 1:
                down.absorb(o0, o0)
            if k == outer and not ends:
                for n in range(outer - 1):
                    gate.step(o0, n)

        line_gather(at, o0, dout_s, dout_ref, across, up, low, between)
        gate.absorb(o0, o0)
        down.finish(o0)
        gate.finish(o0)

    at.branches(branch)
    last = [
        pltpu.make_async_copy(down_own.at[at.o], down_ref, local.at[1]),
        pltpu.make_async_copy(gate_own.at[at.o], gate_ref, local.at[2]),
    ]
    for copy in last:
        copy.start()
    for n in range(max(outer - 2, 0), outer):
        keep_u(n).wait()
    grad.finish()
    keep.wait()
    for copy in last:
        copy.wait()


def turn(
    dgm, dum, mm, mid, cot, gain, wg, wu, wd, n2, cots, outer, inner, shards, collective
):
    rows, cols = mid.shape
    tokens, hidden = dgm.shape
    chips, span = inner * shards // 2, cols // outer
    buffers = pltpu.VMEM((1, chips, rows, cols), BF16)
    cut = first_half(hidden)
    down_vmem, reduce_sems = line_reduce_scratch(outer, span, hidden)
    gate_vmem, _ = line_reduce_scratch(outer, span, cut)
    return pl.pallas_call(
        functools.partial(turn_kernel, outer, inner, shards),
        out_shape=(
            jax.ShapeDtypeStruct((rows, cols), F32),
            jax.ShapeDtypeStruct((1, cols), F32),
            jax.ShapeDtypeStruct((outer * inner, rows, cols), BF16),
            jax.ShapeDtypeStruct((chips, 2 * rows, cols), BF16),
            jax.ShapeDtypeStruct((span, hidden), BF16),
            jax.ShapeDtypeStruct((span, cut), BF16),
            jax.ShapeDtypeStruct((outer, span, hidden - cut + LANES), BF16),
            jax.ShapeDtypeStruct((outer, span, hidden - LANES), BF16),
        ),
        in_specs=[IN_HBM] * 5 + [IN_VMEM] + [IN_HBM] * 5,
        out_specs=[IN_VMEM] * 2 + [IN_HBM] * 6,
        scratch_shapes=[
            pltpu.VMEM((tokens, hidden), BF16),
            pltpu.VMEM((tokens, hidden), BF16),
            pltpu.VMEM((tokens, hidden), BF16),
            pltpu.VMEM((rows, cols), F32),
            pltpu.VMEM((rows, cols), BF16),
            DMA((5,)),
            pltpu.VMEM((chips, 2 * rows, cols), BF16),
            pltpu.VMEM((2, 2 * rows, cols), BF16),
            pltpu.VMEM((rows, cols), BF16),
            pltpu.VMEM((16, cols), F32),
            pltpu.VMEM((cols, hidden), BF16),
            pltpu.VMEM((cols, hidden), BF16),
            pltpu.VMEM((hidden, cols), BF16),
            pltpu.VMEM((tokens, cols), BF16),
            pltpu.VMEM((tokens, cols), BF16),
            pltpu.VMEM((2, span, hidden), BF16),
            pltpu.VMEM((2, span, hidden - cut), BF16),
        ]
        + [buffers] * 3
        + down_vmem
        + gate_vmem
        + [DMA((2, 1, chips))] * 2
        + [DMA((2, outer, HALVES))] * 3
        + reduce_sems * 2
        + [DMA((6,)), DMA((2,)), DMA((2, 2)), DMA((2,))],
        compiler_params=pltpu.CompilerParams(
            collective_id=collective, has_side_effects=True, vmem_limit_bytes=60 * 2**20
        ),
        cost_estimate=cost(110),
        name="turn",
    )(dgm, dum, mm, mid, cot, gain, wg, wu, wd, n2, cots)


def scan_backward_kernel(
    outer,
    inner,
    shards,
    quarters,
    chunk,
    blocks,
    block_width,
    dout_ref,
    wo_from,
    proj_from,
    h_from,
    v_from,
    mid_from,
    par_ref,
    gates_ref,
    q_ref,
    rest_ref,
    both_ref,
    blocks_ref,
    totals_ref,
    result_ref,
    rest_out,
    wo_ref,
    proj_ref,
    h_ref,
    v_ref,
    mid_ref,
    early_sem,
    q_s,
    near_in,
    far_in,
    far_out,
    rest_own,
    rest_land,
    near,
    far,
    q_sem,
    r_up,
    r_low,
    r_sem,
    dout_s,
    dz_s,
    sems,
    sums_ref,
    gate_grad_ref,
    a_s,
    g_s,
    t_s,
    h_pad,
    pre_s,
    dpre_s,
    dv_s,
    u_pad,
):
    length, width = h_ref.shape
    seg = length // SEGMENTS
    chunks = length // chunk

    def place(c):
        q = c // parts
        s = c - q * parts
        return pl.multiple_of((s * quarters + q) * chunk, chunk)

    def time_of(c):
        return pl.multiple_of(c * chunk, chunk)

    at = Place(outer, inner, shards)
    parts = at.parts
    rest = LineReduce(at, rest_own, rest_land, r_up, r_low)
    fetch = pltpu.make_async_copy(rest_ref, rest_own, r_sem)
    fetch.start()
    greet_with_line(at, [at.sibling] + [at.near(q)[0] for q in range(1, at.chips)])
    fetch.wait()

    def rest_early(o0):
        if o0 in (0, outer - 1):
            for d in rest.order(o0)[:-1]:
                rest.push(o0, d)

    def rest_step(n, o0):
        if 0 < o0 < outer - 1:
            rest.step(o0, n)

    def rest_last(o0):
        rest.absorb(o0, o0)
        rest.finish(o0)

    at.branches(rest_early)
    value = PlaneSum(at, 0, q_ref, near_in, far_in, far_out, near, far)

    def keep(q):
        return pltpu.make_async_copy(value.block(q, 0), q_s.at[q], q_sem.at[q])

    for q in reversed(range(at.chips)):
        value.to_sibling(q).start()
        keep(q).start()
    early = load_all([(wo_from, wo_ref)], early_sem)
    span = quarters * chunk

    def load(p):
        return pltpu.make_async_copy(
            dout_ref.at[p], dout_s.at[pl.ds(pl.multiple_of(p * span, span), span)], sems.at[p]
        )

    for p in range(parts):
        load(p).start()
    later = load_all(
        [(proj_from, proj_ref), (h_from, h_ref), (v_from, v_ref), (mid_from, mid_ref)],
        early_sem.at[pl.ds(1, 4)],
    )
    early[0].wait()

    def back_project(k, carry):
        load(2 * k).wait()
        load(2 * k + 1).wait()
        some = pl.ds(pl.multiple_of(k * 2 * span, 2 * span), 2 * span)
        depth = wo_ref.shape[2]
        total = dot(dout_s[some, 0:depth], wo_ref[0], ((1,), (1,)))
        for p in range(1, wo_ref.shape[0]):
            lanes = slice(p * depth, (p + 1) * depth)
            total = total + dot(dout_s[some, lanes], wo_ref[p], ((1,), (1,)))
        dz_s[some, :] = total
        return carry

    lax.fori_loop(0, parts // 2, back_project, 0)
    for q in range(at.chips):
        keep(q).wait()
    value.combine(q_s)
    for copy in later:
        copy.wait()
    log_scale = -DECAY_SCALE * softplus(-par_ref[DECAY : DECAY + 1, :])
    bias = jnp.concatenate(
        [par_ref[RATE_B : RATE_B + 1, :], par_ref[ENTRY_B : ENTRY_B + 1, :]], axis=1
    )
    zeros8 = jnp.zeros((8, width), F32)
    put(a_s, pl.ds(length, 8), zeros8)
    h_pad[0:8, :] = zeros8
    u_pad[0:8, :] = zeros8
    dv_s[pl.ds(length, 8), :] = zeros8

    def first(c, carry):
        rows = pl.ds(time_of(c), chunk)
        later = pl.ds(pl.multiple_of(time_of(c) + 8, 8), chunk)
        there = pl.ds(place(c), chunk)
        h = h_ref[rows, :]
        h_pad[later, :] = h
        u_pad[later, :] = proj_ref[there, width : 2 * width].astype(BF16).astype(F32)
        y, slope = gelu_and_slope(proj_ref[there, 0:width])
        dz = dz_s[there, :]
        put(g_s, rows, (dz * y).astype(BF16).astype(F32))
        both_ref[there, 0:width] = (dz * h.astype(BF16).astype(F32) * slope).astype(BF16)
        pre = dot(v_ref[rows, :], gates_ref[...]) + bias
        pre_s[rows, :] = pre
        put(a_s, rows, jnp.exp(sigmoid(pre[:, :width]) * log_scale))
        return carry

    lax.fori_loop(0, chunks, first, 0)

    def load(g, i):
        return (
            a_s[g, pl.ds(i + 1, SEGMENTS, stride=seg), :],
            g_s[g, pl.ds(i, SEGMENTS, stride=seg), :],
        )

    def store(g, i, state, total):
        g_s[g, pl.ds(i, SEGMENTS, stride=seg), :] = state
        t_s[g, pl.ds(i, SEGMENTS, stride=seg), :] = total

    groups = width // LANES
    start = (jnp.zeros((SEGMENTS, LANES), F32), jnp.ones((SEGMENTS, LANES), F32))
    ends = lax.fori_loop(
        0,
        seg,
        strided_scan(lambda k: seg - 1 - k, groups, load, store),
        (start,) * groups,
        unroll=8,
    )
    firsts = jnp.concatenate([e[0] for e in ends], axis=1)
    totals = jnp.concatenate([e[1] for e in ends], axis=1)
    carries = [None] * SEGMENTS
    carries[SEGMENTS - 1] = jnp.zeros((1, width), F32)
    for j in range(SEGMENTS - 2, -1, -1):
        carries[j] = totals[j + 1 : j + 2] * carries[j + 1] + firsts[j + 1 : j + 2]

    def fold(values):
        return jnp.sum(values.reshape(chunk // 8, 8, values.shape[1]), axis=0)

    sums_ref[...] = jnp.zeros(sums_ref.shape, F32)

    for j in range(SEGMENTS):
        per = seg // chunk

        def middle(k, carry, j=j, per=per):
            c = j * per + k
            rows = pl.ds(time_of(c), chunk)
            g = take(g_s, rows) + take(t_s, rows) * carries[j]
            before = h_pad[pl.ds(time_of(c), chunk + 8), :][7 : 7 + chunk]
            v = v_ref[rows, :].astype(F32)
            r, e, a, room, m = gate_values(pre_s[rows, :], log_scale, width)
            gv = g * v
            held = jnp.where(room > MULT_FLOOR, gv * e * a / m, 0.0)
            ta = (g * before - held) * a * r
            drpre = (ta * (log_scale * (1.0 - r))).astype(BF16)
            depre = (gv * m * e * (1.0 - e)).astype(BF16)
            dpre_s[rows, 0:width] = drpre
            dpre_s[rows, width : 2 * width] = depre
            sums_ref[0:8, :] += fold(ta)
            sums_ref[8:16, :] += fold(drpre.astype(F32))
            sums_ref[16:24, :] += fold(depre.astype(F32))
            dv = g * m * e + dot(dpre_s[rows, :], gates_ref[...], ((1,), (1,)))
            dv_s[rows, :] = dv
            sums_ref[24:32, :] += fold(dv)
            wide = u_pad[pl.ds(time_of(c), chunk + 8), :]
            for tap in range(4):
                top = 32 + 8 * tap
                sums_ref[top : top + 8, :] += fold(dv * wide[8 - tap : 8 - tap + chunk])
            return carry

        lax.fori_loop(0, per, middle, 0)
        if j == 2:
            at.branches(functools.partial(rest_step, 0))
        if j == SEGMENTS - 2:
            at.branches(functools.partial(rest_step, 1))
    for n in range(2, outer - 1):
        at.branches(functools.partial(rest_step, n))
    sums_ref[0:8, :] = sums_ref[0:8, :] * (
        DECAY_SCALE * sigmoid(-par_ref[DECAY : DECAY + 1, :])
    )

    def last(c, carry):
        wide = dv_s[pl.ds(time_of(c), chunk + 8), :]
        du = par_ref[0:1, :] * wide[0:chunk]
        for tap in range(1, 4):
            du = du + par_ref[tap : tap + 1, :] * wide[tap : tap + chunk]
        both_ref[pl.ds(place(c), chunk), width : 2 * width] = du.astype(BF16)
        return carry

    lax.fori_loop(0, chunks, last, 0)
    gate_grad_ref[...] = dot(v_ref[...], dpre_s[...], ((0,), (0,)))
    blocks_ref[...] = jnp.zeros(blocks_ref.shape, F32)
    tall = blocks_ref.shape[0] // (2 * blocks)
    for gate in range(2):
        for j in range(blocks):
            top, lanes = (gate * blocks + j) * tall, gate * width + j * block_width
            rows = slice(j * block_width, (j + 1) * block_width)
            blocks_ref[top : top + block_width, :block_width] = gate_grad_ref[
                rows, lanes : lanes + block_width
            ]
    for k in range(8):
        totals_ref[k : k + 1, :] = jnp.sum(sums_ref[8 * k : 8 * k + 8, :], axis=0, keepdims=True)
    value.arrive()

    def output(rows):
        result_ref[rows, :] = (mid_ref[rows, :] + value.total(rows, q_s)).astype(BF16)

    add_rows(span, output)
    value.finish()
    at.branches(rest_last)
    out = pltpu.make_async_copy(rest_own.at[at.o], rest_out, r_sem)
    out.start()
    out.wait()


def scan_backward(
    quarters,
    chunk,
    blocks,
    block_width,
    dout,
    w_out,
    proj,
    h,
    v,
    params,
    gates,
    mid,
    q,
    rest,
    outer,
    inner,
    shards,
    collective,
):
    parts = dout.shape[0]
    rows, cols = mid.shape
    chips = q.shape[0]
    rest_vmem, rest_sems = line_reduce_scratch(*rest.shape)
    buffers = pltpu.VMEM((1, chips, rows, cols), BF16)
    length, width = h.shape
    tall, wide = -(-block_width // 8) * 8, -(-block_width // LANES) * LANES
    return pl.pallas_call(
        functools.partial(
            scan_backward_kernel, outer, inner, shards, quarters, chunk, blocks, block_width
        ),
        out_shape=(
            jax.ShapeDtypeStruct((length, 2 * width), BF16),
            jax.ShapeDtypeStruct((2 * blocks * tall, wide), F32),
            jax.ShapeDtypeStruct((8, width), F32),
            jax.ShapeDtypeStruct((rows, cols), BF16),
            jax.ShapeDtypeStruct(rest.shape[1:], BF16),
        ),
        in_specs=[IN_HBM] * 6 + [IN_VMEM] * 2 + [IN_HBM] * 2,
        out_specs=[IN_VMEM] * 4 + [IN_HBM],
        scratch_shapes=[
            *[pltpu.VMEM(x.shape, x.dtype) for x in (w_out, proj, h, v, mid)],
            DMA((5,)),
            pltpu.VMEM((chips, rows, cols), BF16),
            buffers,
            buffers,
            buffers,
            *rest_vmem,
            DMA((2, 1, chips)),
            DMA((2, 1, chips)),
            DMA((chips,)),
            *rest_sems,
            DMA,
            pltpu.VMEM((length, dout.shape[2]), BF16),
            pltpu.VMEM((length, width), F32),
            DMA((parts,)),
            pltpu.VMEM((64, width), F32),
            pltpu.VMEM((width, 2 * width), F32),
            pltpu.VMEM((width // LANES, length + 8, LANES), F32),
            pltpu.VMEM((width // LANES, length, LANES), F32),
            pltpu.VMEM((width // LANES, length, LANES), F32),
            pltpu.VMEM((length + 8, width), F32),
            pltpu.VMEM((length, 2 * width), F32),
            pltpu.VMEM((length, 2 * width), BF16),
            pltpu.VMEM((length + 8, width), F32),
            pltpu.VMEM((length + 8, width), F32),
        ],
        compiler_params=pltpu.CompilerParams(
            collective_id=collective, has_side_effects=True, vmem_limit_bytes=60 * 2**20
        ),
        cost_estimate=cost(21),
        name="scan_backward",
    )(dout, w_out, proj, h, v, mid, params, gates, q, rest)


def remote(src, dst, send, recv, to):
    return pltpu.make_async_remote_copy(
        src_ref=src, dst_ref=dst, send_sem=send, recv_sem=recv, device_id=to, device_id_type=MESH
    )


def add_rows(rows, fn, start=0):
    def one(k, carry):
        fn(pl.ds(pl.multiple_of(k * 16, 16), 16))
        return carry

    lax.fori_loop(start // 16, rows // 16, one, 0)


def load_all(pairs, sems):
    copies = [
        pltpu.make_async_copy(src, dst, sems.at[k]) for k, (src, dst) in enumerate(pairs)
    ]
    for copy in copies:
        copy.start()
    return copies


class PlaneExchange:
    def __init__(self, at, n, x, out, sems, local):
        self.at, self.n, self.x, self.out, self.sems, self.local = at, n, x, out, sems, local
        _, self.me = at.near(0)
        self.hops = [(q, c) for q in reversed(range(1, at.chips)) for c in range(2)] + [(0, 1)]

    def rows(self, slot):
        piece = self.out.shape[1]
        return self.x.at[pl.ds(pl.multiple_of(slot * piece, piece), piece)]

    def mine(self):
        return pltpu.make_async_copy(self.rows(self.me), self.out.at[self.me], self.local)

    def hop(self, k):
        to, slot = self.at.near(*self.hops[k])
        sems, n = self.sems, self.n
        return remote(
            self.rows(slot), self.out.at[self.me], sems.at[0, n, k], sems.at[1, n, k], to
        )

    def start(self):
        for k in range(len(self.hops)):
            self.hop(k).start()
        self.mine().start()

    def finish(self):
        for k, (q, other) in enumerate(self.hops):
            source, slot = self.at.near(q, other, True)
            received(self.rows(self.me), self.out.at[slot], self.sems, (self.n, k), source)
        for k in range(len(self.hops)):
            self.hop(k).wait_send()
        self.mine().wait()


def closing_kernel(
    outer,
    inner,
    shards,
    both_from,
    wi_from,
    z_from,
    x_from,
    dmid_from,
    gain_ref,
    gain2_ref,
    blocks_ref,
    sums_ref,
    n1_ref,
    dout_ref,
    down_ref,
    gate_ref,
    rest_ref,
    up_ref,
    grad_ref,
    mix_ref,
    blocks_out,
    sums_out,
    gains_out,
    down_out,
    gate_out,
    rest_out,
    up_out,
    both_ref,
    wi_ref,
    z_ref,
    x_ref,
    dmid_ref,
    early_sem,
    p_s,
    up_own,
    up_land,
    up_sum,
    n1_s,
    dout_s,
    g_s,
    gain_s,
    gain_rows,
    gain_slots,
    near_in,
    far_in,
    far_out,
    done,
    block_slots,
    sum_slots,
    x_in,
    up_in,
    down_in,
    line_out,
    across,
    up,
    low,
    near,
    far,
    final,
    s_far,
    s_near,
    swap,
    g_sem,
    stripe,
    u_up,
    u_low,
    local,
):
    at = Place(outer, inner, shards)
    s, h, parts, ys = at.s, at.h, at.parts, at.ys
    steps = list(range(1, ys))
    line = LineSum(at, p_s, (x_in, up_in, down_in, line_out), (across, up, low))
    model = x_ref.shape[1]
    tile = min(512, model)
    piece = done.shape[1]
    span = shards * piece
    width2 = both_ref.shape[1]
    me = s * shards + h
    small = ((blocks_ref, block_slots, blocks_out), (sums_ref, sum_slots, sums_out))
    fetch = pltpu.make_async_copy(up_ref, up_own, local.at[0])
    fetch.start()

    def stripes(k):
        lanes = pl.ds(pl.multiple_of(owner(k) * span, span), span)
        slot = lax.rem(k, 2)
        return (
            pltpu.make_async_copy(n1_ref.at[:, lanes], n1_s.at[slot], stripe.at[0, slot]),
            pltpu.make_async_copy(dout_ref.at[:, lanes], dout_s.at[slot], stripe.at[1, slot]),
        )

    def owner(k):
        return lax.rem(s + k + 1, parts)

    pairs = [(both_from, both_ref), (wi_from, wi_ref)]
    first = load_all(pairs, early_sem)
    for copy in stripes(0):
        copy.start()
    pairs = [(z_from, z_ref), (x_from, x_ref), (dmid_from, dmid_ref)]
    second = load_all(pairs, early_sem.at[pl.ds(2, 3)])

    def anyone(k):
        to = lax.rem(me + k, at.count)
        return (to // shards, lax.rem(to, shards)), to

    def greet_one(k, carry):
        hello(anyone(k)[0])
        return carry

    lax.fori_loop(1, at.count, greet_one, 0)
    welcome(at.count - 1)
    ups = LineReduce(at, up_own, up_land, u_up, u_low)
    fetch.wait()

    ups.early(0, at.far_first(0), min(1, outer - 2))

    for copy in first:
        copy.wait()

    def back(n, carry):
        d = at.far_first(n)
        rows = pl.ds(pl.multiple_of(d * p_s.shape[1], p_s.shape[1]), p_s.shape[1])
        for lane in range(0, model, tile):
            lanes = slice(lane, lane + tile)
            p_s[d, :, lanes] = dot(both_ref[rows, :], wi_ref[lanes, :], ((1,), (1,))).astype(BF16)
        line.start(d)
        return carry

    lax.fori_loop(0, outer, back, 0)
    send = Sent()
    for n, (src, slots, _) in enumerate(small):
        for dy in steps:
            send(src, slots.at[h], s_far, (n, dy), (s, at.along(dy)))
        send(src, slots.at[h], s_near, (n, 0), at.sibling)
        slots[h] = src[...]

    def mix_rows(p, shard):
        return g_s.at[p, pl.ds(pl.multiple_of(shard * piece, piece), piece)]

    def to_sibling(k, dy):
        p = owner(k)
        return remote(
            mix_rows(p, at.along(dy, 1)),
            near_in.at[dy, p],
            near.at[0, dy, k],
            near.at[1, dy, k],
            at.sibling,
        )

    def to_shard(k, dy, source=False):
        p = owner(k)
        return remote(
            far_out.at[dy - 1, p],
            far_in.at[dy - 1, p],
            far.at[0, dy, k],
            far.at[1, dy, k],
            (s, at.along(-dy if source else dy)),
        )

    def to_owner(k, source=False):
        p = lax.rem(s + parts - k - 1, parts) if source else owner(k)
        return remote(
            done.at[owner(k)],
            mix_ref.at[p if source else s],
            final.at[0, k],
            final.at[1, k],
            (p, h),
        )

    for copy in second:
        copy.wait()

    def weight_grads(k, carry):
        p, slot = owner(k), lax.rem(k, 2)
        for copy in stripes(k):
            copy.wait()

        @pl.when(k < parts - 1)
        def _():
            for copy in stripes(k + 1):
                copy.start()

        g_s[p, :, 0:width2] = dot(n1_s[slot], both_ref[...], ((0,), (0,))).astype(BF16)
        g_s[p, :, width2:] = dot(dout_s[slot], z_ref[...], ((0,), (0,))).astype(BF16)
        for dy in steps + [0]:
            to_sibling(k, dy).start()
        return carry

    lax.fori_loop(0, parts, weight_grads, 0)
    exchanges = [
        PlaneExchange(at, 0, down_ref, down_out, swap, local.at[2]),
        PlaneExchange(at, 1, gate_ref, gate_out, swap, local.at[3]),
        PlaneExchange(at, 3, rest_ref, rest_out, swap, local.at[5]),
    ]
    up_exchange = PlaneExchange(at, 2, up_sum, up_out, swap, local.at[1])

    def sibling_sums(k, carry):
        p = owner(k)
        for dy in steps:
            to_sibling(k, dy).wait_recv()
            mine = mix_rows(p, at.along(dy))

            def add(rows, dy=dy, mine=mine):
                total = mine[rows, :].astype(F32) + near_in[dy, p, rows, :].astype(F32)
                far_out[dy - 1, p, rows, :] = total.astype(BF16)

            add_rows(piece, add)
            to_shard(k, dy).start()
        return carry

    lax.fori_loop(0, parts, sibling_sums, 0)
    gain_s[...] = jnp.zeros(gain_s.shape, F32)

    def mix_step(k):
        p = owner(k)
        mine = mix_rows(p, h)
        to_sibling(k, 0).wait_recv()
        for dy in steps:
            to_shard(k, dy, True).wait_recv()

        def add(rows):
            total = mine[rows, :].astype(F32) + near_in[0, p, rows, :].astype(F32)
            for dy in steps:
                total = total + far_in[dy - 1, p, rows, :].astype(F32)
            done[p, rows, :] = total.astype(BF16)

        add_rows(piece, add)
        if k < parts - 1:
            to_owner(k).start()

    def last_add(rows, dn1):
        x = x_ref[rows, :].astype(F32)
        scale = row_rms(x)
        gain_s[...] += dn1 * x * scale
        grad_ref[rows, :] = dmid_ref[rows, :] + rms_back(x, scale, gain_ref[...], dn1)

    def finish_ups(o0):
        ups.absorb(o0, o0)

        def keep_up(rows):
            up_sum[rows, :] = up_own[at.o, rows, :]

        add_rows(up_sum.shape[0], keep_up)
        up_exchange.start()

    def branch(o0):
        ends = o0 in (0, outer - 1)

        sooner = min(1, outer - 2) if ends else 0

        def between(n):
            if n + sooner < outer - 1 and ends:
                ups.push(o0, ups.order(o0)[n + sooner])
            for k in range(n * inner, parts if n == outer - 2 else (n + 1) * inner):
                if n < outer - 1:
                    mix_step(k)
            if n + 1 < outer - 1 and not ends:
                ups.step(o0, n + 1)
            if n == outer - 2:
                for exchange in exchanges:
                    exchange.start()

        if not ends:
            ups.step(o0, 0)
        line.steps(o0, last_add, between)

    at.branches(branch)
    keep = pltpu.make_async_copy(done.at[s], mix_ref.at[s], local.at[4])
    keep.start()
    gain1, gain2 = jnp.sum(gain_s[...], axis=0, keepdims=True), gain2_ref[...]
    spare = gain_rows.shape[2] - 2 * piece
    for k in range(at.count):
        lanes = slice(k * piece, (k + 1) * piece)
        parts_of = [gain1[:, lanes], gain2[:, lanes]]
        if spare:
            parts_of.append(jnp.zeros((1, spare), F32))
        gain_rows[k] = jnp.concatenate(parts_of, axis=1)

    def gain(k):
        to, row = anyone(k)
        return remote(gain_rows.at[row], gain_slots.at[k], g_sem.at[0, k], g_sem.at[1, k], to)

    def gain_start(k, carry):
        gain(k).start()
        return carry

    def gain_arrive(k, total):
        gain(k).wait_recv()
        return total + gain_slots[k]

    def gain_leave(k, carry):
        gain(k).wait_send()
        return carry

    lax.fori_loop(1, at.count, gain_start, 0)
    at.branches(finish_ups)

    for n, (src, slots, out) in enumerate(small):
        for dy in steps:
            here = slots.at[at.along(-dy)]
            received(src, here, s_far, (n, dy), (s, at.along(-dy)))
            send(here, here, s_near, (n, dy), at.sibling)
    for n, (src, slots, out) in enumerate(small):
        for dy in range(ys):
            received(src, slots.at[at.along(-dy, 1)], s_near, (n, dy), at.sibling)

        def add(k, carry, slots=slots, out=out):
            rows = pl.ds(pl.multiple_of(k * 8, 8), 8)
            total = slots[0, rows, :]
            for j in range(1, shards):
                total = total + slots[j, rows, :]
            out[rows, :] = total
            return carry

        lax.fori_loop(0, src.shape[0] // 8, add, 0)
    gains_out[...] = lax.fori_loop(1, at.count, gain_arrive, gain_rows[me])
    for k in range(parts - 1):
        to_owner(k, True).wait_recv()
    for exchange in exchanges + [up_exchange]:
        exchange.finish()
    at.branches(ups.finish)
    for k in range(parts):
        for dy in range(ys):
            to_sibling(k, dy).wait_send()
        for dy in steps:
            to_shard(k, dy).wait_send()
        if k < parts - 1:
            to_owner(k).wait_send()
    lax.fori_loop(1, at.count, gain_leave, 0)
    send.finish()
    keep.wait()


def closing(
    both,
    w_in,
    z,
    x,
    dmid,
    gain,
    gain2,
    small,
    sums,
    n1,
    dout,
    down,
    gate,
    rest,
    ups,
    outer,
    inner,
    shards,
    collective,
):
    rows, cols = x.shape
    parts, ys, count = outer * inner, shards // 2, outer * inner * shards
    piece = cols // count
    width = z.shape[1]
    lanes = -(-2 * piece // LANES) * LANES
    bufs, sems = line_sum_scratch(outer, rows, cols)
    pieces = pltpu.VMEM((max(ys - 1, 1), parts, piece, 3 * width), BF16)
    stripes = pltpu.VMEM((2, parts * rows, cols // parts), BF16)
    span, hidden = ups.shape[1:]

    def swapped(array):
        shape = (inner * shards, span // (inner * shards), array.shape[-1])
        return jax.ShapeDtypeStruct(shape, BF16)

    reduce_vmem, reduce_sems = line_reduce_scratch(outer, span, hidden)
    return pl.pallas_call(
        functools.partial(closing_kernel, outer, inner, shards),
        out_shape=(
            jax.ShapeDtypeStruct((rows, cols), F32),
            jax.ShapeDtypeStruct((parts, piece, 3 * width), BF16),
            jax.ShapeDtypeStruct(small.shape, F32),
            jax.ShapeDtypeStruct(sums.shape, F32),
            jax.ShapeDtypeStruct((1, lanes), F32),
            *[swapped(array) for array in (down, gate, rest, ups)],
        ),
        in_specs=[IN_HBM] * 5 + [IN_VMEM] * 4 + [IN_HBM] * 6,
        out_specs=[IN_VMEM] * 5 + [IN_HBM] * 4,
        scratch_shapes=[
            *[pltpu.VMEM(value.shape, value.dtype) for value in (both, w_in, z, x, dmid)],
            DMA((5,)),
            pltpu.VMEM((outer, inner * rows, cols), BF16),
            *reduce_vmem,
            pltpu.VMEM((span, hidden), BF16),
            stripes,
            stripes,
            pltpu.VMEM((parts, shards * piece, 3 * width), BF16),
            pltpu.VMEM((16, cols), F32),
            pltpu.VMEM((count, 1, lanes), F32),
            pltpu.VMEM((count, 1, lanes), F32),
            pltpu.VMEM((ys, parts, piece, 3 * width), BF16),
            pieces,
            pieces,
            pltpu.VMEM((parts, piece, 3 * width), BF16),
            pltpu.VMEM((shards,) + small.shape, F32),
            pltpu.VMEM((shards,) + sums.shape, F32),
        ]
        + bufs
        + sems
        + [DMA((2, ys, parts))] * 2
        + [DMA((2, parts))]
        + [DMA((2, 2, ys))] * 2
        + [DMA((2, 4, inner * shards)), DMA((2, count)), DMA((2, 2))]
        + reduce_sems
        + [DMA((6,))],
        compiler_params=pltpu.CompilerParams(
            collective_id=collective, has_side_effects=True, vmem_limit_bytes=60 * 2**20
        ),
        cost_estimate=cost(80),
        name="closing",
    )(
        both,
        w_in,
        z,
        x,
        dmid,
        gain,
        gain2,
        small,
        sums,
        n1,
        dout,
        down,
        gate,
        rest,
        ups,
    )


def unpack_kernel(inner, channels, block_width, *refs):
    sources, targets = refs[:10], refs[10:27]
    held, made, in_sem, out_sem = refs[27:36], refs[36:42], refs[42], refs[43]
    gate_ref, rest_ref, up_ref, down_ref, mix_ref, blocks_ref, sums_ref = held[:7]
    fetch = [
        pltpu.make_async_copy(sources[k], held[k], in_sem.at[k]) for k in range(len(held))
    ]
    for copy in fetch:
        copy.start()
    store = []
    gains_ref = sources[9]
    rate, entry, taps, conv_b, rate_b, entry_b, decay, first_gain, second_gain = targets[8:]
    for copy in fetch:
        copy.wait()
    for k in range(2):
        copy = pltpu.make_async_copy(held[7 + k], targets[6 + k], out_sem.at[6 + k])
        copy.start()
        store.append(copy)
    gate, up, down = made[:3]
    slots, piece, hidden = down_ref.shape
    cut = gate_ref.shape[2]
    tail = hidden - cut
    head = hidden - up_ref.shape[2]
    shards = slots // inner
    parts, width = mix_ref.shape[0], mix_ref.shape[2] // 3
    places = [
        ((h * inner + i) * hidden, i * shards + h) for i in range(inner) for h in range(shards)
    ]

    def ship(k):
        copy = pltpu.make_async_copy(made[k], targets[k], out_sem.at[k])
        copy.start()
        store.append(copy)

    for first, slot in places:
        gate[:, first : first + cut] = gate_ref[slot].astype(F32)
        gate[:, first + cut : first + hidden] = rest_ref[slot][:, :tail].astype(F32)
    ship(0)
    for first, slot in places:
        up[:, first : first + head] = rest_ref[slot][:, tail:].astype(F32)
        up[:, first + head : first + hidden] = up_ref[slot].astype(F32)
    ship(1)
    for first, slot in places:
        down[:, first : first + hidden] = down_ref[slot].astype(F32)
    ship(2)
    for k in range(3):
        lanes = slice(k * width, k * width + width)
        made[3 + k][...] = jnp.concatenate(
            [mix_ref[p][:, lanes].astype(F32)[:, :channels] for p in range(parts)], axis=1
        )
        ship(3 + k)
    blocks = rate.shape[1]
    tall = blocks_ref.shape[0] // (2 * blocks)
    for k, dst in enumerate((rate, entry)):
        for j in range(blocks):
            top = (k * blocks + j) * tall
            dst[:, j, :] = blocks_ref[top : top + block_width, :block_width]
    taps[...] = sums_ref[4:8, :channels]
    for row, dst in ((3, conv_b), (1, rate_b), (2, entry_b), (0, decay)):
        dst[...] = sums_ref[row, :channels]
    first_gain[...] = gains_ref[0, :piece]
    second_gain[...] = gains_ref[0, piece : 2 * piece]
    for copy in store:
        copy.wait()


def unpack(
    gate, rest, up, down, mix, small, sums, result, grad, gains, inner, channels, blocks, block_width
):
    slots, piece, hidden = down.shape
    across = jax.ShapeDtypeStruct((piece, slots * hidden), F32)
    wide = jax.ShapeDtypeStruct((piece, mix.shape[0] * channels), F32)
    square = jax.ShapeDtypeStruct((block_width, blocks, block_width), F32)
    vector = jax.ShapeDtypeStruct((channels,), F32)
    taps = jax.ShapeDtypeStruct((4, channels), F32)
    gain = jax.ShapeDtypeStruct((piece,), F32)
    held = (gate, rest, up, down, mix, small, sums, result, grad)
    made = (across,) * 3 + (wide,) * 3
    return pl.pallas_call(
        functools.partial(unpack_kernel, inner, channels, block_width),
        out_shape=made
        + tuple(jax.ShapeDtypeStruct(x.shape, x.dtype) for x in (result, grad))
        + (square,) * 2
        + (taps,)
        + (vector,) * 4
        + (gain,) * 2,
        in_specs=[IN_HBM] * 9 + [IN_VMEM],
        out_specs=[IN_HBM] * 8 + [IN_VMEM] * 9,
        scratch_shapes=[pltpu.VMEM(x.shape, x.dtype) for x in held + made]
        + [DMA((len(held),)), DMA((8,))],
        compiler_params=pltpu.CompilerParams(vmem_limit_bytes=60 * 2**20),
        cost_estimate=cost(5),
        name="unpack",
    )(*held, gains)


def body(
    tokens,
    first_gain,
    branch_weight,
    input_weight,
    conv_weight,
    conv_bias,
    rate_weight,
    rate_bias,
    entry_weight,
    entry_bias,
    decay_param,
    output_weight,
    second_gain,
    hidden_gate,
    hidden_up,
    hidden_down,
    cotangent,
):
    quarters, _, chunk, model = tokens.shape
    rows = quarters * chunk
    parts = lax.axis_size("seq")
    shards = lax.axis_size("shard")
    inner = 2
    outer = parts // inner
    seq_at = lax.axis_index("seq")
    inner_at = lax.rem(seq_at, inner)
    lru = branch_weight.shape[1]
    channels = lru // parts
    width = (channels + LANES) // LANES * LANES
    spare = width - channels
    blocks, block_width = rate_weight.shape[0], rate_weight.shape[1]
    piece = model // (parts * shards)

    def own(weight, axis):
        part = lax.dynamic_slice_in_dim(weight, seq_at * channels, channels, axis)
        pads = [(0, 0), (0, 0)]
        pads[axis] = (0, spare)
        return jnp.pad(part, pads)

    x = tokens.reshape(rows, model)
    cot = cotangent.reshape(rows, model)
    gain1, gain2 = first_gain[None], second_gain[None]
    params, mid, z, h, v, proj, gates, n1, w_in, w_out, n2, cot_all = forward(
        x,
        gain1,
        gain2,
        (conv_weight, conv_bias, rate_bias, entry_bias, decay_param),
        rate_weight.transpose(1, 0, 2),
        entry_weight.transpose(1, 0, 2),
        cot,
        jnp.concatenate([own(branch_weight, 1), own(input_weight, 1)], axis=1),
        own(output_weight, 0),
        quarters,
        chunk,
        outer,
        inner,
        shards,
        0,
    )
    w_in = w_in.reshape(model, 2 * width)
    n2 = n2.reshape(inner * shards * rows, model)
    cot_all = cot_all.reshape(inner * shards * rows, model)
    hidden = hidden_gate.shape[1] // inner
    wg = lax.dynamic_slice_in_dim(hidden_gate, inner_at * hidden, hidden, 1)
    wu = lax.dynamic_slice_in_dim(hidden_up, inner_at * hidden, hidden, 1)
    wd = lax.dynamic_slice_in_dim(hidden_down, inner_at * hidden, hidden, 0)

    gm = dot(n2, wg)
    um = dot(n2, wu)
    act, slope = gelu_and_slope(gm)
    mm = (act * um).astype(BF16)
    dmm = dot(cot_all, wd, ((1,), (1,)))
    dgm = (dmm * um * slope).astype(BF16)
    dum = (dmm * act).astype(BF16)
    dmid, gain2_grad, dout, partial, down_sum, gate_sum, rest_terms, up_terms = turn(
        dgm,
        dum,
        mm,
        mid,
        cot,
        gain2,
        hidden_gate,
        hidden_up,
        hidden_down,
        n2,
        cot_all,
        outer,
        inner,
        shards,
        1,
    )
    both, small, sums, result, rest_sum = scan_backward(
        quarters,
        chunk,
        blocks,
        block_width,
        dout,
        w_out,
        proj,
        h,
        v,
        params,
        gates,
        mid,
        partial,
        rest_terms,
        outer,
        inner,
        shards,
        2,
    )
    tokens_grad, mix, small, sums, gains, down_sum, gate_sum, rest_sum, up_sum = closing(
        both,
        w_in,
        z,
        x,
        dmid,
        gain1,
        gain2_grad,
        small,
        sums,
        n1.reshape(parts * rows, model),
        dout.reshape(parts * rows, model),
        down_sum,
        gate_sum,
        rest_sum,
        up_terms,
        outer,
        inner,
        shards,
        3,
    )
    (
        gate_grad,
        up_grad,
        down_grad,
        branch_grad,
        input_grad,
        output_grad,
        result,
        tokens_grad,
        rate_grad,
        entry_grad,
        tap_grad,
        conv_bias_grad,
        rate_bias_grad,
        entry_bias_grad,
        decay_grad,
        gain1_grad,
        gain2_grad,
    ) = unpack(
        gate_sum,
        rest_sum,
        up_sum,
        down_sum,
        mix,
        small,
        sums,
        result,
        tokens_grad,
        gains,
        inner,
        channels,
        blocks,
        block_width,
    )
    return (
        result.reshape(tokens.shape),
        tokens_grad.reshape(tokens.shape),
        gain1_grad,
        branch_grad,
        input_grad,
        tap_grad,
        conv_bias_grad,
        rate_grad.transpose(1, 0, 2),
        rate_bias_grad,
        entry_grad.transpose(1, 0, 2),
        entry_bias_grad,
        decay_grad,
        output_grad.T,
        gain2_grad,
        gate_grad,
        up_grad,
        down_grad.T,
    )


def solution(mesh):
    placed = (
        P(None, "shard", "seq", None),
        P(),
        P("shard", None),
        P("shard", None),
        P(None, "seq"),
        P("seq"),
        P("seq", None, None),
        P("seq"),
        P("seq", None, None),
        P("seq"),
        P("seq"),
        P(None, "shard"),
        P(),
        P(None, "shard"),
        P(None, "shard"),
        P("shard", None),
        P(None, "shard", "seq", None),
    )
    return jax.shard_map(
        body,
        mesh=mesh,
        in_specs=placed,
        out_specs=(
            P(None, "shard", "seq", None),
            P(None, "shard", "seq", None),
            P(("seq", "shard")),
            P(("seq", "shard"), None),
            P(("seq", "shard"), None),
            P(None, "seq"),
            P("seq"),
            P("seq", None, None),
            P("seq"),
            P("seq", None, None),
            P("seq"),
            P("seq"),
            P(None, ("seq", "shard")),
            P(("seq", "shard")),
            P(("seq", "shard"), None),
            P(("seq", "shard"), None),
            P(None, ("seq", "shard")),
        ),
        check_vma=False,
    )
```

```python
import functools

import jax
import jax.numpy as jnp
from jax import lax
from jax.experimental import pallas as pl
from jax.experimental.pallas import tpu as pltpu
from jax.sharding import PartitionSpec as P

EPSILON = 1e-06
DECAY_SCALE = 8.0
MULT_FLOOR = 0.01
LANES = 128
SEGMENTS = 8
GELU_C = 0.7978845608028654
GELU_A = 0.044715
F32 = jnp.float32
BF16 = jnp.bfloat16


MESH = pl.DeviceIdType.MESH
IN_HBM = pl.BlockSpec(memory_space=pltpu.HBM)
IN_VMEM = pl.BlockSpec(memory_space=pltpu.VMEM)
DMA = pltpu.SemaphoreType.DMA


def cost(us):
    return pl.CostEstimate(flops=0, bytes_accessed=int(us * 3.3e6), transcendentals=0)


def dot(left, right, dims=((1,), (0,))):
    return lax.dot_general(left, right, (dims, ((), ())), preferred_element_type=F32)


def gelu_and_slope(x):
    inner = GELU_C * (x + GELU_A * x * x * x)
    t = jnp.tanh(inner)
    half = 0.5 * (1.0 + t)
    slope = half + 0.5 * x * (1.0 - t * t) * (GELU_C * (1.0 + 3.0 * GELU_A * x * x))
    return x * half, slope


def gelu_tanh(x):
    return x * (0.5 * (1.0 + jnp.tanh(GELU_C * (x + GELU_A * x * x * x))))


def sigmoid(x):
    return 0.5 * jnp.tanh(0.5 * x) + 0.5


def softplus(x):
    return jnp.maximum(x, 0.0) + jnp.log1p(jnp.exp(-jnp.abs(x)))


def lane_groups(width):
    return [slice(g * LANES, (g + 1) * LANES) for g in range(width // LANES)]


def put(ref, rows, value):
    for g, lanes in enumerate(lane_groups(value.shape[1])):
        ref[g, rows, :] = value[:, lanes]


def take(ref, rows):
    return jnp.concatenate([ref[g, rows, :] for g in range(ref.shape[0])], axis=1)


def strided_scan(steps, groups, load, store):
    def step(k, carry):
        i = steps(k)
        out = []
        for g in range(groups):
            state, total = carry[g]
            factor, term = load(g, i)
            state = factor * state + term
            total = factor * total
            store(g, i, state, total)
            out.append((state, total))
        return tuple(out)

    return step


TAP, CONV_B, RATE_B, ENTRY_B, DECAY = 0, 4, 5, 6, 7


def gate_values(pre, log_scale, width):
    r = sigmoid(pre[:, :width])
    e = sigmoid(pre[:, width:])
    a = jnp.exp(r * log_scale)
    room = 1.0 - a * a
    m = jnp.sqrt(jnp.maximum(room, MULT_FLOOR))
    return r, e, a, room, m


class Place:
    def __init__(self, outer, inner, shards):
        self.outer, self.inner, self.shards = outer, inner, shards
        self.parts, self.ys, self.count = outer * inner, shards // 2, outer * inner * shards
        self.chips = inner * self.ys
        self.s, self.h = lax.axis_index("seq"), lax.axis_index("shard")
        self.o, self.i = self.s // inner, lax.rem(self.s, inner)
        self.y, self.core = self.h // 2, lax.rem(self.h, 2)
        self.beside = (self.o * inner + 1 - self.i, self.h)
        self.above, self.below = (self.s + inner, self.h), (self.s - inner, self.h)
        self.sibling = (self.s, self.along(0, 1))

    def along(self, dy, other=0):
        y = lax.rem(self.y + dy + self.ys, self.ys)
        return y * 2 + lax.rem(self.core + other, 2)

    def chip(self, q, back=False):
        di, dy = q // self.ys, q - q // self.ys * self.ys
        if back:
            di, dy = self.inner - di, self.ys - dy
        return lax.rem(self.i + di, self.inner), lax.rem(self.y + dy, self.ys)

    def near(self, q, other=0, back=False):
        i, y = self.chip(q, back)
        h = y * 2 + lax.rem(self.core + other, 2)
        return (self.o * self.inner + i, h), i * self.shards + h

    def far_first(self, n):
        sign = 2 * ((2 * self.o) // self.outer) - 1
        return lax.rem(self.o + sign * (n + 1) + 2 * self.outer, self.outer)

    def branches(self, fn):
        for o0 in range(self.outer):
            pl.when(self.o == o0)(functools.partial(fn, o0))


def hello(to):
    barrier = pltpu.get_barrier_semaphore()
    pl.semaphore_signal(barrier, inc=1, device_id=to, device_id_type=MESH)


def welcome(n):
    pl.semaphore_wait(pltpu.get_barrier_semaphore(), n)


def greet(others):
    for to in others:
        hello(to)
    welcome(len(others))


def greet_with_line(at, others):
    up, down = at.o < at.outer - 1, at.o > 0
    for to in others:
        hello(to)
    pl.when(up)(lambda: hello(at.above))
    pl.when(down)(lambda: hello(at.below))
    ends = lax.rem(at.o, at.outer - 1) == 0
    pl.when(ends)(lambda: welcome(len(others) + 1))
    pl.when(jnp.logical_not(ends))(lambda: welcome(len(others) + 2))


class Sent:
    def __init__(self):
        self.copies = []

    def __call__(self, src, dst, sems, at, to):
        copy = remote(src, dst, sems.at[(0,) + at], sems.at[(1,) + at], to)
        copy.start()
        self.copies.append(copy)

    def finish(self):
        for copy in self.copies:
            copy.wait_send()


def received(like, here, sems, at, source):
    remote(like, here, sems.at[(0,) + at], sems.at[(1,) + at], source).wait_recv()


def line_gather(
    at,
    o0,
    x_ref,
    out,
    across,
    up,
    down,
    between=lambda k: None,
    each=lambda row: None,
    side=None,
    slim=0,
):
    send = Sent()
    rows = x_ref.shape[0]
    half = rows // HALVES
    low = pl.ds(rows - slim, slim)

    def slot(row, other=False):
        return out.at[row * at.inner + (1 - at.i if other else at.i)]

    def some(row, part):
        less = slim if slim and row != o0 and part == HALVES - 1 else 0
        return pl.ds(part * half, half - less)

    def pass_on(row, part, sems, to):
        some_rows = pl.ds(part * half, half)
        src = x_ref if row == o0 else slot(row)
        send(src.at[some_rows], slot(row).at[some_rows], sems, (row, part), to)

    def cross(row, part):
        src = x_ref if row == o0 else slot(row)
        send(src.at[some(row, part)], slot(row).at[some(row, part)], across, (row, part), at.beside)

    def crossed(row):
        for part in range(HALVES):
            here = slot(row, True).at[some(row, part)]
            received(here, here, across, (row, part), at.beside)

    def slim_on(row):
        here = slot(row, True).at[low]
        if row <= o0 < at.outer - 1:
            send(here, here, side[0], (row,), at.above)
        if row >= o0 > 0:
            send(here, here, side[1], (row,), at.below)

    def slim_came(row, sems, source):
        here = slot(row, True).at[low]
        received(here, here, sems, (row,), source)

    for k in range(at.outer):
        lower, upper = o0 - k, o0 + k
        for part in range(HALVES):
            here = x_ref.at[pl.ds(part * half, half)]
            if lower >= 0:
                if k > 0:
                    received(here, here, up, (lower, part), at.below)
                if o0 < at.outer - 1:
                    pass_on(lower, part, up, at.above)
                cross(lower, part)
            if upper < at.outer:
                if k > 0:
                    received(here, here, down, (upper, part), at.above)
                if o0 > 0:
                    pass_on(upper, part, down, at.below)
                if k > 0:
                    cross(upper, part)
        if slim and k == 1:
            crossed(o0)
            slim_on(o0)
        if slim and k > 1:
            for row, sems, source in (
                (o0 - k + 1, side[0], at.below),
                (o0 + k - 1, side[1], at.above),
            ):
                if 0 <= row < at.outer:
                    slim_came(row, sems, source)
                    slim_on(row)
        between(k)
    between(at.outer)
    for row in sorted(range(at.outer), key=lambda row: abs(row - o0)):
        if row != o0 or not slim:
            crossed(row)
        if slim and row != o0 and abs(row - o0) == at.outer - 1:
            slim_came(row, side[0] if row < o0 else side[1], at.below if row < o0 else at.above)
        each(row)
    send.finish()


class LineSum:
    def __init__(self, at, p, bufs, sems, side=None):
        self.at, self.p = at, p
        self.x_in, self.up_in, self.down_in, self.sums = bufs
        self.across, self.up, self.down = sems
        self.rows = self.x_in.shape[1]
        self.slim = 0
        if side is not None:
            self.s_up_in, self.s_down_in, self.s_sums, self.s_in = side[:4]
            self.s_up, self.s_down, self.s_across = side[4:]
            self.slim = self.s_in.shape[0]

    def block(self, d, i):
        return self.p.at[d, pl.ds(pl.multiple_of(i * self.rows, self.rows), self.rows)]

    def cross(self, d, part):
        half = self.rows // HALVES
        some = pl.ds(part * half, half - (self.slim if part == HALVES - 1 else 0))
        return remote(
            self.block(d, 1 - self.at.i).at[some],
            self.x_in.at[d].at[some],
            self.across.at[0, d, part],
            self.across.at[1, d, part],
            self.at.beside,
        )

    def start(self, d):
        for part in range(HALVES):
            self.cross(d, part).start()

    def steps(self, o0, last_add, between=lambda n: None):
        at, rows, slim = self.at, self.rows, self.slim
        send = Sent()
        order = sorted(range(at.outer), key=lambda d: (-abs(d - o0), d))
        low, half = rows - slim, rows // HALVES

        def arrivals(d, index, mine, up_in, down_in, up, down):
            terms = []
            if d >= o0 > 0:
                received(mine, mine, up, index, at.below)
                terms.append(up_in.at[d])
            if d <= o0 < at.outer - 1:
                received(mine, mine, down, index, at.above)
                terms.append(down_in.at[d])
            return terms

        def total_of(terms, some):
            total = terms[0][some, :].astype(F32)
            for term in terms[1:]:
                total = total + term[some, :].astype(F32)
            return total

        for n, d in enumerate(order):
            mine = self.block(d, at.i)
            target = self.sums.at[d]
            for part in range(HALVES):
                part_rows = pl.ds(part * half, half)
                self.cross(d, part).wait_recv()
                along = [mine] + arrivals(
                    d,
                    (d, part),
                    mine.at[part_rows],
                    self.up_in,
                    self.down_in,
                    self.up,
                    self.down,
                )
                both = along + [self.x_in.at[d]]

                def add(some, both=both, target=target, d=d):
                    total = total_of(both, some)
                    if d == o0:
                        last_add(some, total)
                    else:
                        target[some, :] = total.astype(BF16)

                def add_low(some, along=along, target=target):
                    target[some, :] = total_of(along, some).astype(BF16)

                add_rows(min((part + 1) * half, low), add, part * half)
                if slim and d != o0 and part == HALVES - 1:
                    add_rows(rows, add_low, low)
                if d > o0:
                    here, there = target.at[part_rows], self.up_in.at[d].at[part_rows]
                    send(here, there, self.up, (d, part), at.above)
                if d < o0:
                    here, there = target.at[part_rows], self.down_in.at[d].at[part_rows]
                    send(here, there, self.down, (d, part), at.below)
            if slim:
                theirs = self.block(d, 1 - at.i).at[pl.ds(low, slim)]
                extra = [theirs] + arrivals(
                    d, (d,), theirs, self.s_up_in, self.s_down_in, self.s_up, self.s_down
                )
                aside = self.s_sums.at[d]

                def add_aside(some, extra=extra, aside=aside):
                    aside[some, :] = total_of(extra, some).astype(BF16)

                add_rows(slim, add_aside)
                if d > o0:
                    send(aside, self.s_up_in.at[d], self.s_up, (d,), at.above)
                if d < o0:
                    send(aside, self.s_down_in.at[d], self.s_down, (d,), at.below)
                if d == o0:
                    send(aside, self.s_in, self.s_across, (), at.beside)
                    received(aside, self.s_in, self.s_across, (), at.beside)
                    for k in range(slim // 16):
                        some, here = pl.ds(low + 16 * k, 16), pl.ds(16 * k, 16)
                        last_add(some, total_of(along, some) + self.s_in[here, :].astype(F32))
            between(n)
        for d in range(at.outer):
            for part in range(HALVES):
                self.cross(d, part).wait_send()
        send.finish()


class LineReduce:
    def __init__(self, at, own, land, up, down):
        self.at, self.own, self.land, self.up, self.down = at, own, land, up, down

    def order(self, o0):
        return sorted(range(self.at.outer), key=lambda d: (-abs(d - o0), d))

    def ascent(self, d):
        at = self.at
        return remote(
            self.own.at[d], self.land.at[d], self.up.at[0, d], self.up.at[1, d], at.above
        )

    def descent(self, o0, d):
        slot = d if d != o0 - 1 else self.at.outer
        return remote(
            self.own.at[d], self.land.at[slot], self.down.at[0, d], self.down.at[1, d], self.at.below
        )

    def early(self, n, d, limit):
        at = self.at
        inside = n < limit
        last = at.outer - 1
        pl.when(jnp.logical_and(at.o == 0, inside))(lambda: self.ascent(d).start())
        far = remote(
            self.own.at[d], self.land.at[d], self.down.at[0, d], self.down.at[1, d], at.below
        )
        pl.when(jnp.logical_and(at.o == last, inside))(lambda: far.start())

    def push(self, o0, d):
        if d > o0:
            self.ascent(d).start()
        if d < o0:
            self.descent(o0, d).start()

    def absorb(self, o0, d):
        terms = []
        if d >= o0 > 0:
            self.ascent(d).wait_recv()
            terms.append(self.land.at[d])
        if d <= o0 < self.at.outer - 1:
            slot = d if d < o0 else self.at.outer
            self.descent(o0 + 1, d).wait_recv()
            terms.append(self.land.at[slot])
        mine = self.own.at[d]

        def add(rows):
            total = mine[rows, :].astype(F32)
            for term in terms:
                total = total + term[rows, :].astype(F32)
            mine[rows, :] = total.astype(BF16)

        if terms:
            add_rows(mine.shape[0], add)

    def step(self, o0, n):
        d = self.order(o0)[n]
        self.absorb(o0, d)
        self.push(o0, d)

    def finish(self, o0):
        for d in range(self.at.outer):
            if d > o0:
                self.ascent(d).wait_send()
            if d < o0:
                self.descent(o0, d).wait_send()


def first_half(hidden):
    return -(-(hidden // 2) // LANES) * LANES


def line_reduce_scratch(outer, rows, cols):
    blocks = [pltpu.VMEM((outer, rows, cols), BF16), pltpu.VMEM((outer + 1, rows, cols), BF16)]
    return blocks, [DMA((2, outer))] * 2


SLIM = 16
HALVES = 2


def slim_scratch(outer, cols):
    blocks = [pltpu.VMEM((outer, SLIM, cols), BF16)] * 3 + [pltpu.VMEM((SLIM, cols), BF16)]
    return blocks, [DMA((2, outer))] * 2 + [DMA((2,))]


def line_sum_scratch(outer, rows, cols):
    return [pltpu.VMEM((outer, rows, cols), BF16)] * 4, [DMA((2, outer, HALVES))] * 3


def row_rms(values):
    return lax.rsqrt(jnp.mean(values * values, axis=-1, keepdims=True) + EPSILON)


def rms_back(values, scale, gain, grad):
    k = grad * gain
    mean = jnp.mean(k * values, axis=-1, keepdims=True)
    return scale * k - scale * scale * scale * values * mean


def run_scan(
    parts, quarters, chunk, proj_ref, par_ref, gates_ref, z_ref, h_ref, v_ref, u_pad, a_s, b_s
):
    length, width = h_ref.shape
    seg = length // SEGMENTS
    chunks = length // chunk

    def place(c):
        q = c // parts
        s = c - q * parts
        return pl.multiple_of((s * quarters + q) * chunk, chunk)

    def time_of(c):
        return pl.multiple_of(c * chunk, chunk)

    log_scale = -DECAY_SCALE * softplus(-par_ref[DECAY : DECAY + 1, :])
    bias = jnp.concatenate(
        [par_ref[RATE_B : RATE_B + 1, :], par_ref[ENTRY_B : ENTRY_B + 1, :]], axis=1
    )
    u_pad[0:8, :] = jnp.zeros((8, width), F32)

    def first(c, carry):
        u = proj_ref[pl.ds(place(c), chunk), width : 2 * width].astype(BF16).astype(F32)
        u_pad[pl.ds(pl.multiple_of(time_of(c) + 8, 8), chunk), :] = u
        wide = u_pad[pl.ds(time_of(c), chunk + 8), :]
        v = par_ref[CONV_B : CONV_B + 1, :] + par_ref[0:1, :] * wide[8:]
        for k in range(1, 4):
            v = v + par_ref[k : k + 1, :] * wide[8 - k : 8 - k + chunk]
        v = v.astype(BF16)
        v_ref[pl.ds(time_of(c), chunk), :] = v
        pre = dot(v, gates_ref[...]) + bias
        r, e, a, room, m = gate_values(pre, log_scale, width)
        put(a_s, pl.ds(time_of(c), chunk), a)
        put(b_s, pl.ds(time_of(c), chunk), m * e * v.astype(F32))
        return carry

    lax.fori_loop(0, chunks, first, 0)

    def load(g, i):
        at = pl.ds(i, SEGMENTS, stride=seg)
        return a_s[g, at, :], b_s[g, at, :]

    def store(g, i, state, total):
        at = pl.ds(i, SEGMENTS, stride=seg)
        b_s[g, at, :] = state
        a_s[g, at, :] = total

    groups = width // LANES
    start = (jnp.zeros((SEGMENTS, LANES), F32), jnp.ones((SEGMENTS, LANES), F32))
    ends = lax.fori_loop(
        0, seg, strided_scan(lambda k: k, groups, load, store), (start,) * groups, unroll=8
    )
    final = jnp.concatenate([e[0] for e in ends], axis=1)
    totals = jnp.concatenate([e[1] for e in ends], axis=1)
    carries = [jnp.zeros((1, width), F32)]
    for j in range(SEGMENTS - 1):
        carries.append(totals[j : j + 1] * carries[j] + final[j : j + 1])
    for j in range(SEGMENTS):
        per = seg // chunk

        def last(k, carry, j=j, per=per):
            c = j * per + k
            rows = pl.ds(time_of(c), chunk)
            h = take(b_s, rows) + take(a_s, rows) * carries[j]
            h_ref[rows, :] = h
            y = gelu_tanh(proj_ref[pl.ds(place(c), chunk), 0:width])
            z_ref[pl.ds(place(c), chunk), :] = (h.astype(BF16).astype(F32) * y).astype(BF16)
            return carry

        lax.fori_loop(0, per, last, 0)


def forward_kernel(
    outer,
    inner,
    shards,
    quarters,
    chunk,
    x_ref,
    gain1_ref,
    gain2_ref,
    taps_ref,
    conv_b_ref,
    rate_b_ref,
    entry_b_ref,
    decay_ref,
    rate_ref,
    entry_ref,
    cot_ref,
    wi_ref,
    wo_ref,
    par_ref,
    mid_ref,
    z_out,
    h_out,
    v_out,
    proj_out,
    gates_out,
    n1_out,
    wi_out,
    wo_out,
    n2_out,
    cot_out,
    own_s,
    n1_s,
    wi_s,
    wo_s,
    gates_s,
    u_pad,
    a_s,
    b_s,
    z_ref,
    h_ref,
    v_ref,
    proj_ref,
    gates_ref,
    p_s,
    cot_s,
    x_in,
    up_in,
    down_in,
    line_out,
    g_across,
    g_up,
    g_down,
    w_far,
    w_near,
    across,
    up,
    down,
    far,
    near,
    c_side,
    c_far,
    c_near,
    local,
    s_up_in,
    s_down_in,
    s_sums,
    s_in,
    s_up,
    s_down,
    s_across,
    g_side_up,
    g_side_down,
):
    at = Place(outer, inner, shards)
    parts, rows = at.parts, x_ref.shape[0]
    steps = list(range(1, at.ys))
    width2 = wi_ref.shape[1]
    width, depth, cols = width2 // 2, wi_ref.shape[0], wo_ref.shape[1]

    def normalize(some):
        x = x_ref[some, :].astype(F32)
        own_s[some, :] = (x * row_rms(x) * gain1_ref[...]).astype(BF16)

    add_rows(rows, normalize)
    greet_with_line(at, [at.sibling] + [at.near(q)[0] for q in range(1, at.chips)])
    weights = ((wi_ref, wi_s), (wo_ref, wo_s))
    keep = [
        pltpu.make_async_copy(own_s, n1_s.at[at.s], local.at[0]),
        pltpu.make_async_copy(wi_ref, wi_s.at[at.h], local.at[1]),
        pltpu.make_async_copy(wo_ref, wo_s.at[at.h], local.at[2]),
    ]
    for copy in keep:
        copy.start()
    send = Sent()

    def send_weights():
        for n, (src, dst) in enumerate(weights):
            for dy in steps:
                send(src, dst.at[at.h], w_far, (n, dy), (at.s, at.along(dy)))
            send(src, dst.at[at.h], w_near, (n, 0), at.sibling)

    send_weights()
    def build_gates():
        channels = decay_ref.shape[0]
        par_ref[...] = jnp.zeros(par_ref.shape, F32)
        par_ref[0:4, :channels] = taps_ref[...].astype(F32)
        for row, src in (
            (CONV_B, conv_b_ref),
            (RATE_B, rate_b_ref),
            (ENTRY_B, entry_b_ref),
            (DECAY, decay_ref),
        ):
            par_ref[row, :channels] = src[...]
        gates_s[...] = jnp.zeros(gates_s.shape, F32)
        block_width, blocks = rate_ref.shape[0], rate_ref.shape[1]
        for gate, src in enumerate((rate_ref, entry_ref)):
            for j in range(blocks):
                top, lane = j * block_width, gate * width + j * block_width
                gates_s[top : top + block_width, lane : lane + block_width] = src[:, j, :].astype(F32)
        gates_ref[...] = gates_s[...].astype(BF16)

    def project(d):
        total = None
        for k in range(shards):
            lanes = slice(k * depth, (k + 1) * depth)
            pair = jnp.concatenate([n1_s[d * inner + i, :, lanes] for i in range(inner)], axis=0)
            term = dot(pair, wi_s[k])
            total = term if total is None else total + term
        proj_ref[d * inner * rows : (d + 1) * inner * rows, :] = total

    def gather(o0):
        forward = Sent()

        def between(k):
            if k == 0:
                build_gates()
            if k != outer - 1:
                return
            for n, (src, dst) in enumerate(weights):
                for dy in steps:
                    source = at.along(-dy)
                    received(src, dst.at[source], w_far, (n, dy), (at.s, source))
                    forward(dst.at[source], dst.at[source], w_near, (n, dy), at.sibling)
            for n, (src, dst) in enumerate(weights):
                for dy in range(at.ys):
                    received(src, dst.at[at.along(-dy, 1)], w_near, (n, dy), at.sibling)
            for copy in keep:
                copy.wait()

        def each(row):
            project(row)

        side = (g_side_up, g_side_down)
        line_gather(at, o0, own_s, n1_s, g_across, g_up, g_down, between, each, side, SLIM)
        forward.finish()

    at.branches(gather)
    send(cot_ref, cot_s, c_side, (), at.beside)
    keep = [
        pltpu.make_async_copy(n1_s, n1_out, local.at[0]),
        pltpu.make_async_copy(wi_s, wi_out, local.at[1]),
        pltpu.make_async_copy(wo_s, wo_out, local.at[2]),
    ]
    for copy in keep:
        copy.start()
    run_scan(
        parts, quarters, chunk, proj_ref, par_ref, gates_ref, z_ref, h_ref, v_ref, u_pad, a_s, b_s
    )
    made = (
        (z_ref, z_out),
        (h_ref, h_out),
        (v_ref, v_out),
        (proj_ref, proj_out),
        (gates_ref, gates_out),
    )
    for n, (src, dst) in enumerate(made):
        keep.append(pltpu.make_async_copy(src, dst, local.at[6 + n]))
        keep[-1].start()
    side = (s_up_in, s_down_in, s_sums, s_in, s_up, s_down, s_across)
    line = LineSum(at, p_s, (x_in, up_in, down_in, line_out), (across, up, down), side)

    def back_project(n, carry):
        d = at.far_first(n)
        some = pl.ds(pl.multiple_of(d * inner * rows, inner * rows), inner * rows)
        for k in range(shards):
            p_s[d, :, k * cols : (k + 1) * cols] = dot(z_ref[some, :], wo_s[k]).astype(BF16)
        line.start(d)
        return carry

    lax.fori_loop(0, outer, back_project, 0)
    received(cot_ref, cot_s, c_side, (), at.beside)

    def slot(side, dy, other=0):
        i = 1 - at.i if side else at.i
        return cot_out.at[i * shards + at.along(dy, other)]

    mine = (cot_ref, cot_s)
    for side in range(2):
        keep.append(pltpu.make_async_copy(mine[side], slot(side, 0), local.at[3 + side]))
        keep[-1].start()
        for dy in steps:
            send(mine[side], slot(side, 0), c_far, (side, dy), (at.s, at.along(dy)))
        send(mine[side], slot(side, 0), c_near, (side, 0), at.sibling)

    def last_add(some, total):
        mid = x_ref[some, :].astype(F32) + total
        mid_ref[some, :] = mid
        own_s[some, :] = (mid * row_rms(mid) * gain2_ref[...]).astype(BF16)

    def branch(o0):
        forward = Sent()

        def between(n):
            if n != outer - 2:
                return
            for side in range(2):
                for dy in steps:
                    here = slot(side, -dy)
                    received(cot_ref, here, c_far, (side, dy), (at.s, at.along(-dy)))
                    forward(here, here, c_near, (side, dy), at.sibling)

        line.steps(o0, last_add, between)
        forward.finish()

    at.branches(branch)
    _, me = at.near(0)
    keep.append(pltpu.make_async_copy(own_s, n2_out.at[me], local.at[5]))
    keep[-1].start()
    quad = inner == 2 and at.ys == 2
    for q in (1, 2) if quad else reversed(range(1, at.chips)):
        send(own_s, n2_out.at[me], far, (q,), at.near(q)[0])
    send(own_s, n2_out.at[me], near, (0,), at.sibling)
    for q in (1, 2) if quad else range(1, at.chips):
        source, there = at.near(q, back=True)
        here = n2_out.at[there]
        received(own_s, here, far, (q,), source)
        if quad:
            half = here.at[pl.ds((2 - q) * (rows // 2), rows // 2)]
            send(half, half, far, (3 if q == 2 else 0,), at.near(3 - q)[0])
        send(here, here, near, (q,), at.sibling)
    if quad:
        here = n2_out.at[at.near(3)[1]]
        for q in (1, 2):
            half = here.at[pl.ds((q - 1) * (rows // 2), rows // 2)]
            received(half, half, far, (3 if q == 1 else 0,), at.near(q)[0])
        send(here, here, near, (3,), at.sibling)
    for q in range(at.chips):
        received(own_s, n2_out.at[at.near(q, 1, True)[1]], near, (q,), at.sibling)
    for side in range(2):
        for dy in range(at.ys):
            received(cot_ref, slot(side, -dy, 1), c_near, (side, dy), at.sibling)
    send.finish()
    for copy in keep:
        copy.wait()


def forward(
    x,
    gain1,
    gain2,
    channel,
    rate,
    entry,
    cot,
    w_in,
    w_out,
    quarters,
    chunk,
    outer,
    inner,
    shards,
    collective,
):
    rows, cols = x.shape
    parts, ys, chips = outer * inner, shards // 2, inner * shards // 2
    length, width = parts * rows, w_in.shape[1] // 2
    bufs, sems = line_sum_scratch(outer, rows, cols)
    side_vmem, side_sems = slim_scratch(outer, cols)
    plane = jax.ShapeDtypeStruct((inner * shards, rows, cols), BF16)
    lanes = pltpu.VMEM((width // LANES, length, LANES), F32)
    made = (
        ((length, width), BF16),
        ((length, width), F32),
        ((length, width), BF16),
        ((length, 2 * width), F32),
        ((width, 2 * width), BF16),
    )
    return pl.pallas_call(
        functools.partial(forward_kernel, outer, inner, shards, quarters, chunk),
        out_shape=(
            jax.ShapeDtypeStruct((8, width), F32),
            jax.ShapeDtypeStruct((rows, cols), F32),
            *[jax.ShapeDtypeStruct(shape, dtype) for shape, dtype in made],
            jax.ShapeDtypeStruct((parts, rows, cols), BF16),
            jax.ShapeDtypeStruct((shards,) + w_in.shape, BF16),
            jax.ShapeDtypeStruct((shards,) + w_out.shape, BF16),
            plane,
            plane,
        ),
        in_specs=[IN_VMEM] * 11 + [IN_HBM] * 2,
        out_specs=[IN_VMEM] * 2 + [IN_HBM] * 10,
        scratch_shapes=[
            pltpu.VMEM((rows, cols), BF16),
            pltpu.VMEM((parts, rows, cols), BF16),
            pltpu.VMEM((shards,) + w_in.shape, BF16),
            pltpu.VMEM((shards,) + w_out.shape, BF16),
            pltpu.VMEM((width, 2 * width), F32),
            pltpu.VMEM((length + 8, width), F32),
            lanes,
            lanes,
            *[pltpu.VMEM(shape, dtype) for shape, dtype in made],
            pltpu.VMEM((outer, inner * rows, cols), BF16),
            pltpu.VMEM((rows, cols), BF16),
        ]
        + bufs
        + [DMA((2, outer, HALVES))] * 3
        + [DMA((2, 2, ys))] * 2
        + sems
        + [DMA((2, chips))] * 2
        + [DMA((2,))]
        + [DMA((2, 2, ys))] * 2
        + [DMA((11,))]
        + side_vmem
        + side_sems
        + [DMA((2, outer))] * 2,
        compiler_params=pltpu.CompilerParams(
            collective_id=collective, has_side_effects=True, vmem_limit_bytes=60 * 2**20
        ),
        cost_estimate=cost(140),
        name="forward",
    )(x, gain1, gain2, *channel, rate, entry, cot, w_in, w_out)


class PlaneSum:
    def __init__(self, at, n, p, near_in, far_in, far_out, near, far):
        self.at, self.n, self.p = at, n, p
        self.near_in, self.far_in, self.far_out = near_in, far_in, far_out
        self.near, self.far = near, far
        self.rows = near_in.shape[2]

    def block(self, q, other):
        i, y = self.at.chip(q)
        core = lax.rem(self.at.core + other, 2)
        rows = pl.ds(pl.multiple_of(core * self.rows, self.rows), self.rows)
        return self.p.at[i * self.at.ys + y, rows]

    def to_sibling(self, q):
        n = self.n
        return remote(
            self.block(q, 1),
            self.near_in.at[n, q],
            self.near.at[0, n, q],
            self.near.at[1, n, q],
            self.at.sibling,
        )

    def onward(self, q, back=False):
        n = self.n
        return remote(
            self.far_out.at[n, q],
            self.far_in.at[n, q],
            self.far.at[0, n, q],
            self.far.at[1, n, q],
            self.at.near(q, 0, back)[0],
        )

    def combine_one(self, k, own=None):
        q = self.at.chips - 1 - k
        self.to_sibling(q).wait_recv()
        mine = self.block(q, 0) if own is None else own.at[q]

        def add(rows):
            total = mine[rows, :].astype(F32) + self.near_in[self.n, q, rows, :].astype(F32)
            self.far_out[self.n, q, rows, :] = total.astype(BF16)

        add_rows(self.rows, add)
        self.onward(q).start()

    def combine(self, own=None):
        def one(k, carry):
            self.combine_one(k, own)
            return carry

        lax.fori_loop(0, self.at.chips - 1, one, 0)
        self.to_sibling(0).wait_recv()

    def total(self, rows, own=None):
        n = self.n
        mine = self.block(0, 0) if own is None else own.at[0]
        value = mine[rows, :].astype(F32) + self.near_in[n, 0, rows, :].astype(F32)
        for q in range(1, self.at.chips):
            value = value + self.far_in[n, q, rows, :].astype(F32)
        return value

    def arrive(self):
        for q in range(1, self.at.chips):
            self.onward(q, True).wait_recv()

    def finish(self):
        for q in range(self.at.chips):
            self.to_sibling(q).wait_send()
        for q in range(1, self.at.chips):
            self.onward(q).wait_send()


def turn_kernel(
    outer,
    inner,
    shards,
    dgm_from,
    dum_from,
    mm_from,
    mid_from,
    cot_from,
    gain_ref,
    wg_ref,
    wu_ref,
    wd_ref,
    n2_ref,
    cots_ref,
    dmid_ref,
    gain_grad_ref,
    dout_ref,
    q_ref,
    down_ref,
    gate_ref,
    rest_ref,
    up_ref,
    mm_ref,
    dgm_ref,
    dum_ref,
    mid_ref,
    cot_ref,
    early_sem,
    p_s,
    q_s,
    dout_s,
    gain_s,
    wg_s,
    wu_s,
    wd_s,
    n2_s,
    cots_s,
    u_s,
    r_s,
    near_in,
    far_in,
    far_out,
    down_own,
    down_land,
    gate_own,
    gate_land,
    near,
    far,
    across,
    up,
    low,
    down_up,
    down_low,
    gate_up,
    gate_low,
    local,
    q_sem,
    u_sem,
    r_sem,
):
    at = Place(outer, inner, shards)
    model, hidden = wg_s.shape
    tile = min(512, model)
    pair = p_s.shape[1]
    span = model // outer
    own = pl.ds(pl.multiple_of(at.i * hidden, hidden), hidden)
    first = load_all([(mm_from, mm_ref)], early_sem)
    load = [
        pltpu.make_async_copy(cots_ref, cots_s, local.at[1]),
        pltpu.make_async_copy(wg_ref.at[:, own], wg_s, local.at[2]),
        pltpu.make_async_copy(wu_ref.at[:, own], wu_s, local.at[3]),
        pltpu.make_async_copy(n2_ref, n2_s, local.at[4]),
        pltpu.make_async_copy(wd_ref.at[own, :], wd_s, local.at[5]),
    ]
    for copy in load[:3]:
        copy.start()
    second = load_all([(dgm_from, dgm_ref), (dum_from, dum_ref)], early_sem.at[pl.ds(1, 2)])
    for copy in load[3:]:
        copy.start()
    third = load_all([(mid_from, mid_ref), (cot_from, cot_ref)], early_sem.at[pl.ds(3, 2)])
    greet_with_line(at, [at.sibling] + [at.near(q)[0] for q in range(1, at.chips)])
    grad = PlaneSum(at, 0, p_s, near_in, far_in, far_out, near, far)
    down = LineReduce(at, down_own, down_land, down_up, down_low)
    gate = LineReduce(at, gate_own, gate_land, gate_up, gate_low)

    def columns(d):
        return pl.ds(pl.multiple_of(d * span, span), span)

    load[0].wait()
    first[0].wait()

    def down_grad(n, carry):
        d = at.far_first(n)
        down_own[d] = dot(cots_s[:, columns(d)], mm_ref[...], ((0,), (0,))).astype(BF16)
        down.early(n, d, outer - 2)
        return carry

    down_grad(0, 0)
    for copy in load[1:3] + second:
        copy.wait()

    def back(k, carry):
        q = at.chips - 1 - k
        i, y = at.chip(q)
        c = i * at.ys + y
        rows = pl.ds(pl.multiple_of(c * pair, pair), pair)
        for lane in range(0, model, tile):
            lanes = slice(lane, lane + tile)
            block = dot(dgm_ref[rows, :], wg_s[lanes, :], ((1,), (1,)))
            block = block + dot(dum_ref[rows, :], wu_s[lanes, :], ((1,), (1,)))
            p_s[c, :, lanes] = block.astype(BF16)
        grad.to_sibling(q).start()
        pl.when(k > 0)(lambda: grad.combine_one(k - 1))
        return carry

    lax.fori_loop(0, at.chips, back, 0)
    grad.to_sibling(0).wait_recv()
    lax.fori_loop(1, outer, down_grad, 0)
    def first_down(o0):
        if 0 < o0 < outer - 1:
            down.step(o0, 0)

    at.branches(first_down)
    load[3].wait()
    cut = gate_own.shape[2]

    def keep_r(n):
        slot = lax.rem(n, 2)
        there = rest_ref.at[at.far_first(n), :, : hidden - cut]
        return pltpu.make_async_copy(r_s.at[slot], there, r_sem.at[slot])

    def gate_grad(n, carry):
        d = at.far_first(n)
        pl.when(n >= 2)(lambda: keep_r(n - 2).wait())
        block = dot(n2_s[:, columns(d)], dgm_ref[...], ((0,), (0,))).astype(BF16)
        gate_own[d] = block[:, :cut]
        r_s[lax.rem(n, 2)] = block[:, cut:]
        keep_r(n).start()
        return carry

    lax.fori_loop(0, outer, gate_grad, 0)
    for n in range(max(outer - 2, 0), outer):
        keep_r(n).wait()

    load[4].wait()

    def keep_q(c):
        slot = lax.rem(c, 2)
        return pltpu.make_async_copy(q_s.at[slot], q_ref.at[c], q_sem.at[slot])

    def ahead(c, carry):
        rows = pl.ds(pl.multiple_of(c * pair, pair), pair)
        pl.when(c >= 2)(lambda: keep_q(c - 2).wait())
        for lane in range(0, model, tile):
            lanes = slice(lane, lane + tile)
            q_s[lax.rem(c, 2), :, lanes] = dot(mm_ref[rows, :], wd_s[:, lanes]).astype(BF16)
        keep_q(c).start()
        return carry

    gain_s[...] = jnp.zeros(gain_s.shape, F32)
    for copy in third:
        copy.wait()
    grad.arrive()

    def norm_back(rows):
        dn2 = grad.total(rows)
        mid = mid_ref[rows, :]
        scale = row_rms(mid)
        gain_s[...] += dn2 * mid * scale
        dmid = cot_ref[rows, :].astype(F32) + rms_back(mid, scale, gain_ref[...], dn2)
        dmid_ref[rows, :] = dmid
        dout_s[rows, :] = dmid.astype(BF16)

    add_rows(dout_s.shape[0], norm_back)
    gain_grad_ref[...] = jnp.sum(gain_s[...], axis=0, keepdims=True)
    keep = pltpu.make_async_copy(dout_s, dout_ref.at[at.s], local.at[0])
    keep.start()

    head = u_s.shape[2] - up_ref.shape[2]

    class keep_u:
        def __init__(self, n):
            slot, d = lax.rem(n, 2), at.far_first(n)
            block = u_s.at[slot]
            self.copies = (
                pltpu.make_async_copy(
                    block.at[:, :head], rest_ref.at[d, :, hidden - cut :], u_sem.at[0, slot]
                ),
                pltpu.make_async_copy(block.at[:, head:], up_ref.at[d], u_sem.at[1, slot]),
            )

        def start(self):
            for copy in self.copies:
                copy.start()

        def wait(self):
            for copy in self.copies:
                copy.wait()

    def up_grad(n, carry):
        pl.when(n >= 2)(lambda: keep_u(n - 2).wait())
        u_s[lax.rem(n, 2)] = dot(
            n2_s[:, columns(at.far_first(n))], dum_ref[...], ((0,), (0,))
        ).astype(BF16)
        keep_u(n).start()
        return carry

    def branch(o0):
        ends = o0 in (0, outer - 1)

        def between(k):
            if k == 0:
                if ends:
                    down.push(o0, down.order(o0)[outer - 2])
                    for d in gate.order(o0)[:-1]:
                        gate.push(o0, d)
                lax.fori_loop(0, at.chips, ahead, 0)
            if k == 1:
                if not ends:
                    for n in range(1, outer - 1):
                        down.step(o0, n)
                lax.fori_loop(0, outer, up_grad, 0)
            if k == outer - 1:
                down.absorb(o0, o0)
            if k == outer and not ends:
                for n in range(outer - 1):
                    gate.step(o0, n)

        line_gather(at, o0, dout_s, dout_ref, across, up, low, between)
        gate.absorb(o0, o0)
        down.finish(o0)
        gate.finish(o0)

    at.branches(branch)
    last = [
        pltpu.make_async_copy(down_own.at[at.o], down_ref, local.at[1]),
        pltpu.make_async_copy(gate_own.at[at.o], gate_ref, local.at[2]),
    ]
    for copy in last:
        copy.start()
    for n in range(max(outer - 2, 0), outer):
        keep_u(n).wait()
    for c in range(max(at.chips - 2, 0), at.chips):
        keep_q(c).wait()
    grad.finish()
    keep.wait()
    for copy in last:
        copy.wait()


def turn(
    dgm, dum, mm, mid, cot, gain, wg, wu, wd, n2, cots, outer, inner, shards, collective
):
    rows, cols = mid.shape
    tokens, hidden = dgm.shape
    chips, span = inner * shards // 2, cols // outer
    buffers = pltpu.VMEM((1, chips, rows, cols), BF16)
    cut = first_half(hidden)
    down_vmem, reduce_sems = line_reduce_scratch(outer, span, hidden)
    gate_vmem, _ = line_reduce_scratch(outer, span, cut)
    return pl.pallas_call(
        functools.partial(turn_kernel, outer, inner, shards),
        out_shape=(
            jax.ShapeDtypeStruct((rows, cols), F32),
            jax.ShapeDtypeStruct((1, cols), F32),
            jax.ShapeDtypeStruct((outer * inner, rows, cols), BF16),
            jax.ShapeDtypeStruct((chips, 2 * rows, cols), BF16),
            jax.ShapeDtypeStruct((span, hidden), BF16),
            jax.ShapeDtypeStruct((span, cut), BF16),
            jax.ShapeDtypeStruct((outer, span, hidden - cut + LANES), BF16),
            jax.ShapeDtypeStruct((outer, span, hidden - LANES), BF16),
        ),
        in_specs=[IN_HBM] * 5 + [IN_VMEM] + [IN_HBM] * 5,
        out_specs=[IN_VMEM] * 2 + [IN_HBM] * 6,
        scratch_shapes=[
            pltpu.VMEM((tokens, hidden), BF16),
            pltpu.VMEM((tokens, hidden), BF16),
            pltpu.VMEM((tokens, hidden), BF16),
            pltpu.VMEM((rows, cols), F32),
            pltpu.VMEM((rows, cols), BF16),
            DMA((5,)),
            pltpu.VMEM((chips, 2 * rows, cols), BF16),
            pltpu.VMEM((2, 2 * rows, cols), BF16),
            pltpu.VMEM((rows, cols), BF16),
            pltpu.VMEM((16, cols), F32),
            pltpu.VMEM((cols, hidden), BF16),
            pltpu.VMEM((cols, hidden), BF16),
            pltpu.VMEM((hidden, cols), BF16),
            pltpu.VMEM((tokens, cols), BF16),
            pltpu.VMEM((tokens, cols), BF16),
            pltpu.VMEM((2, span, hidden), BF16),
            pltpu.VMEM((2, span, hidden - cut), BF16),
        ]
        + [buffers] * 3
        + down_vmem
        + gate_vmem
        + [DMA((2, 1, chips))] * 2
        + [DMA((2, outer, HALVES))] * 3
        + reduce_sems * 2
        + [DMA((6,)), DMA((2,)), DMA((2, 2)), DMA((2,))],
        compiler_params=pltpu.CompilerParams(
            collective_id=collective, has_side_effects=True, vmem_limit_bytes=60 * 2**20
        ),
        cost_estimate=cost(110),
        name="turn",
    )(dgm, dum, mm, mid, cot, gain, wg, wu, wd, n2, cots)


def scan_backward_kernel(
    outer,
    inner,
    shards,
    quarters,
    chunk,
    blocks,
    block_width,
    dout_ref,
    wo_from,
    proj_from,
    h_from,
    v_from,
    mid_from,
    par_ref,
    gates_ref,
    q_ref,
    rest_ref,
    both_ref,
    blocks_ref,
    totals_ref,
    result_ref,
    rest_out,
    wo_ref,
    proj_ref,
    h_ref,
    v_ref,
    mid_ref,
    early_sem,
    q_s,
    near_in,
    far_in,
    far_out,
    rest_own,
    rest_land,
    near,
    far,
    q_sem,
    r_up,
    r_low,
    r_sem,
    dout_s,
    dz_s,
    sems,
    sums_ref,
    gate_grad_ref,
    a_s,
    g_s,
    t_s,
    h_pad,
    pre_s,
    dpre_s,
    dv_s,
    u_pad,
):
    length, width = h_ref.shape
    seg = length // SEGMENTS
    chunks = length // chunk

    def place(c):
        q = c // parts
        s = c - q * parts
        return pl.multiple_of((s * quarters + q) * chunk, chunk)

    def time_of(c):
        return pl.multiple_of(c * chunk, chunk)

    at = Place(outer, inner, shards)
    parts = at.parts
    rest = LineReduce(at, rest_own, rest_land, r_up, r_low)
    fetch = pltpu.make_async_copy(rest_ref, rest_own, r_sem)
    fetch.start()
    greet_with_line(at, [at.sibling] + [at.near(q)[0] for q in range(1, at.chips)])
    fetch.wait()

    def rest_early(o0):
        if o0 in (0, outer - 1):
            for d in rest.order(o0)[:-1]:
                rest.push(o0, d)

    def rest_step(n, o0):
        if 0 < o0 < outer - 1:
            rest.step(o0, n)

    def rest_last(o0):
        rest.absorb(o0, o0)
        rest.finish(o0)

    at.branches(rest_early)
    value = PlaneSum(at, 0, q_ref, near_in, far_in, far_out, near, far)

    def keep(q):
        return pltpu.make_async_copy(value.block(q, 0), q_s.at[q], q_sem.at[q])

    for q in reversed(range(at.chips)):
        value.to_sibling(q).start()
        keep(q).start()
    early = load_all([(wo_from, wo_ref)], early_sem)
    span = quarters * chunk

    def load(p):
        return pltpu.make_async_copy(
            dout_ref.at[p], dout_s.at[pl.ds(pl.multiple_of(p * span, span), span)], sems.at[p]
        )

    for p in range(parts):
        load(p).start()
    later = load_all(
        [(proj_from, proj_ref), (h_from, h_ref), (v_from, v_ref), (mid_from, mid_ref)],
        early_sem.at[pl.ds(1, 4)],
    )
    early[0].wait()

    def back_project(k, carry):
        load(2 * k).wait()
        load(2 * k + 1).wait()
        some = pl.ds(pl.multiple_of(k * 2 * span, 2 * span), 2 * span)
        depth = wo_ref.shape[2]
        total = dot(dout_s[some, 0:depth], wo_ref[0], ((1,), (1,)))
        for p in range(1, wo_ref.shape[0]):
            lanes = slice(p * depth, (p + 1) * depth)
            total = total + dot(dout_s[some, lanes], wo_ref[p], ((1,), (1,)))
        dz_s[some, :] = total
        return carry

    lax.fori_loop(0, parts // 2, back_project, 0)
    for q in range(at.chips):
        keep(q).wait()
    value.combine(q_s)
    for copy in later:
        copy.wait()
    log_scale = -DECAY_SCALE * softplus(-par_ref[DECAY : DECAY + 1, :])
    bias = jnp.concatenate(
        [par_ref[RATE_B : RATE_B + 1, :], par_ref[ENTRY_B : ENTRY_B + 1, :]], axis=1
    )
    zeros8 = jnp.zeros((8, width), F32)
    put(a_s, pl.ds(length, 8), zeros8)
    h_pad[0:8, :] = zeros8
    u_pad[0:8, :] = zeros8
    dv_s[pl.ds(length, 8), :] = zeros8

    def first(c, carry):
        rows = pl.ds(time_of(c), chunk)
        later = pl.ds(pl.multiple_of(time_of(c) + 8, 8), chunk)
        there = pl.ds(place(c), chunk)
        h = h_ref[rows, :]
        h_pad[later, :] = h
        u_pad[later, :] = proj_ref[there, width : 2 * width].astype(BF16).astype(F32)
        y, slope = gelu_and_slope(proj_ref[there, 0:width])
        dz = dz_s[there, :]
        put(g_s, rows, (dz * y).astype(BF16).astype(F32))
        both_ref[there, 0:width] = (dz * h.astype(BF16).astype(F32) * slope).astype(BF16)
        pre = dot(v_ref[rows, :], gates_ref[...]) + bias
        pre_s[rows, :] = pre
        put(a_s, rows, jnp.exp(sigmoid(pre[:, :width]) * log_scale))
        return carry

    lax.fori_loop(0, chunks, first, 0)

    def load(g, i):
        return (
            a_s[g, pl.ds(i + 1, SEGMENTS, stride=seg), :],
            g_s[g, pl.ds(i, SEGMENTS, stride=seg), :],
        )

    def store(g, i, state, total):
        g_s[g, pl.ds(i, SEGMENTS, stride=seg), :] = state
        t_s[g, pl.ds(i, SEGMENTS, stride=seg), :] = total

    groups = width // LANES
    start = (jnp.zeros((SEGMENTS, LANES), F32), jnp.ones((SEGMENTS, LANES), F32))
    ends = lax.fori_loop(
        0,
        seg,
        strided_scan(lambda k: seg - 1 - k, groups, load, store),
        (start,) * groups,
        unroll=8,
    )
    firsts = jnp.concatenate([e[0] for e in ends], axis=1)
    totals = jnp.concatenate([e[1] for e in ends], axis=1)
    carries = [None] * SEGMENTS
    carries[SEGMENTS - 1] = jnp.zeros((1, width), F32)
    for j in range(SEGMENTS - 2, -1, -1):
        carries[j] = totals[j + 1 : j + 2] * carries[j + 1] + firsts[j + 1 : j + 2]

    def fold(values):
        return jnp.sum(values.reshape(chunk // 8, 8, values.shape[1]), axis=0)

    sums_ref[...] = jnp.zeros(sums_ref.shape, F32)

    for j in range(SEGMENTS):
        per = seg // chunk

        def middle(k, carry, j=j, per=per):
            c = j * per + k
            rows = pl.ds(time_of(c), chunk)
            g = take(g_s, rows) + take(t_s, rows) * carries[j]
            before = h_pad[pl.ds(time_of(c), chunk + 8), :][7 : 7 + chunk]
            v = v_ref[rows, :].astype(F32)
            r, e, a, room, m = gate_values(pre_s[rows, :], log_scale, width)
            gv = g * v
            held = jnp.where(room > MULT_FLOOR, gv * e * a / m, 0.0)
            ta = (g * before - held) * a * r
            drpre = (ta * (log_scale * (1.0 - r))).astype(BF16)
            depre = (gv * m * e * (1.0 - e)).astype(BF16)
            dpre_s[rows, 0:width] = drpre
            dpre_s[rows, width : 2 * width] = depre
            sums_ref[0:8, :] += fold(ta)
            sums_ref[8:16, :] += fold(drpre.astype(F32))
            sums_ref[16:24, :] += fold(depre.astype(F32))
            dv = g * m * e + dot(dpre_s[rows, :], gates_ref[...], ((1,), (1,)))
            dv_s[rows, :] = dv
            sums_ref[24:32, :] += fold(dv)
            wide = u_pad[pl.ds(time_of(c), chunk + 8), :]
            for tap in range(4):
                top = 32 + 8 * tap
                sums_ref[top : top + 8, :] += fold(dv * wide[8 - tap : 8 - tap + chunk])
            return carry

        lax.fori_loop(0, per, middle, 0)
        if j == 2:
            at.branches(functools.partial(rest_step, 0))
        if j == SEGMENTS - 2:
            at.branches(functools.partial(rest_step, 1))
    for n in range(2, outer - 1):
        at.branches(functools.partial(rest_step, n))
    sums_ref[0:8, :] = sums_ref[0:8, :] * (
        DECAY_SCALE * sigmoid(-par_ref[DECAY : DECAY + 1, :])
    )

    def last(c, carry):
        wide = dv_s[pl.ds(time_of(c), chunk + 8), :]
        du = par_ref[0:1, :] * wide[0:chunk]
        for tap in range(1, 4):
            du = du + par_ref[tap : tap + 1, :] * wide[tap : tap + chunk]
        both_ref[pl.ds(place(c), chunk), width : 2 * width] = du.astype(BF16)
        return carry

    lax.fori_loop(0, chunks, last, 0)
    gate_grad_ref[...] = dot(v_ref[...], dpre_s[...], ((0,), (0,)))
    blocks_ref[...] = jnp.zeros(blocks_ref.shape, F32)
    tall = blocks_ref.shape[0] // (2 * blocks)
    for gate in range(2):
        for j in range(blocks):
            top, lanes = (gate * blocks + j) * tall, gate * width + j * block_width
            rows = slice(j * block_width, (j + 1) * block_width)
            blocks_ref[top : top + block_width, :block_width] = gate_grad_ref[
                rows, lanes : lanes + block_width
            ]
    for k in range(8):
        totals_ref[k : k + 1, :] = jnp.sum(sums_ref[8 * k : 8 * k + 8, :], axis=0, keepdims=True)
    value.arrive()

    def output(rows):
        result_ref[rows, :] = (mid_ref[rows, :] + value.total(rows, q_s)).astype(BF16)

    add_rows(span, output)
    value.finish()
    at.branches(rest_last)
    out = pltpu.make_async_copy(rest_own.at[at.o], rest_out, r_sem)
    out.start()
    out.wait()


def scan_backward(
    quarters,
    chunk,
    blocks,
    block_width,
    dout,
    w_out,
    proj,
    h,
    v,
    params,
    gates,
    mid,
    q,
    rest,
    outer,
    inner,
    shards,
    collective,
):
    parts = dout.shape[0]
    rows, cols = mid.shape
    chips = q.shape[0]
    rest_vmem, rest_sems = line_reduce_scratch(*rest.shape)
    buffers = pltpu.VMEM((1, chips, rows, cols), BF16)
    length, width = h.shape
    tall, wide = -(-block_width // 8) * 8, -(-block_width // LANES) * LANES
    return pl.pallas_call(
        functools.partial(
            scan_backward_kernel, outer, inner, shards, quarters, chunk, blocks, block_width
        ),
        out_shape=(
            jax.ShapeDtypeStruct((length, 2 * width), BF16),
            jax.ShapeDtypeStruct((2 * blocks * tall, wide), F32),
            jax.ShapeDtypeStruct((8, width), F32),
            jax.ShapeDtypeStruct((rows, cols), BF16),
            jax.ShapeDtypeStruct(rest.shape[1:], BF16),
        ),
        in_specs=[IN_HBM] * 6 + [IN_VMEM] * 2 + [IN_HBM] * 2,
        out_specs=[IN_VMEM] * 4 + [IN_HBM],
        scratch_shapes=[
            *[pltpu.VMEM(x.shape, x.dtype) for x in (w_out, proj, h, v, mid)],
            DMA((5,)),
            pltpu.VMEM((chips, rows, cols), BF16),
            buffers,
            buffers,
            buffers,
            *rest_vmem,
            DMA((2, 1, chips)),
            DMA((2, 1, chips)),
            DMA((chips,)),
            *rest_sems,
            DMA,
            pltpu.VMEM((length, dout.shape[2]), BF16),
            pltpu.VMEM((length, width), F32),
            DMA((parts,)),
            pltpu.VMEM((64, width), F32),
            pltpu.VMEM((width, 2 * width), F32),
            pltpu.VMEM((width // LANES, length + 8, LANES), F32),
            pltpu.VMEM((width // LANES, length, LANES), F32),
            pltpu.VMEM((width // LANES, length, LANES), F32),
            pltpu.VMEM((length + 8, width), F32),
            pltpu.VMEM((length, 2 * width), F32),
            pltpu.VMEM((length, 2 * width), BF16),
            pltpu.VMEM((length + 8, width), F32),
            pltpu.VMEM((length + 8, width), F32),
        ],
        compiler_params=pltpu.CompilerParams(
            collective_id=collective, has_side_effects=True, vmem_limit_bytes=60 * 2**20
        ),
        cost_estimate=cost(21),
        name="scan_backward",
    )(dout, w_out, proj, h, v, mid, params, gates, q, rest)


def remote(src, dst, send, recv, to):
    return pltpu.make_async_remote_copy(
        src_ref=src, dst_ref=dst, send_sem=send, recv_sem=recv, device_id=to, device_id_type=MESH
    )


def add_rows(rows, fn, start=0):
    def one(k, carry):
        fn(pl.ds(pl.multiple_of(k * 16, 16), 16))
        return carry

    lax.fori_loop(start // 16, rows // 16, one, 0)


def load_all(pairs, sems):
    copies = [
        pltpu.make_async_copy(src, dst, sems.at[k]) for k, (src, dst) in enumerate(pairs)
    ]
    for copy in copies:
        copy.start()
    return copies


class PlaneExchange:
    def __init__(self, at, n, x, out, sems, local):
        self.at, self.n, self.x, self.out, self.sems, self.local = at, n, x, out, sems, local
        _, self.me = at.near(0)
        self.hops = [(q, c) for q in reversed(range(1, at.chips)) for c in range(2)] + [(0, 1)]

    def rows(self, slot):
        piece = self.out.shape[1]
        return self.x.at[pl.ds(pl.multiple_of(slot * piece, piece), piece)]

    def mine(self):
        return pltpu.make_async_copy(self.rows(self.me), self.out.at[self.me], self.local)

    def hop(self, k):
        to, slot = self.at.near(*self.hops[k])
        sems, n = self.sems, self.n
        return remote(
            self.rows(slot), self.out.at[self.me], sems.at[0, n, k], sems.at[1, n, k], to
        )

    def start(self):
        for k in range(len(self.hops)):
            self.hop(k).start()
        self.mine().start()

    def finish(self):
        for k, (q, other) in enumerate(self.hops):
            source, slot = self.at.near(q, other, True)
            received(self.rows(self.me), self.out.at[slot], self.sems, (self.n, k), source)
        for k in range(len(self.hops)):
            self.hop(k).wait_send()
        self.mine().wait()


def closing_kernel(
    outer,
    inner,
    shards,
    both_from,
    wi_from,
    z_from,
    x_from,
    dmid_from,
    gain_ref,
    gain2_ref,
    blocks_ref,
    sums_ref,
    n1_ref,
    dout_ref,
    down_ref,
    gate_ref,
    rest_ref,
    up_ref,
    grad_ref,
    mix_ref,
    blocks_out,
    sums_out,
    gains_out,
    down_out,
    gate_out,
    rest_out,
    up_out,
    both_ref,
    wi_ref,
    z_ref,
    x_ref,
    dmid_ref,
    early_sem,
    p_s,
    up_own,
    up_land,
    up_sum,
    n1_s,
    dout_s,
    g_s,
    gain_s,
    gain_rows,
    gain_slots,
    near_in,
    far_in,
    far_out,
    done,
    block_slots,
    sum_slots,
    x_in,
    up_in,
    down_in,
    line_out,
    across,
    up,
    low,
    near,
    far,
    final,
    s_far,
    s_near,
    swap,
    g_sem,
    stripe,
    u_up,
    u_low,
    local,
):
    at = Place(outer, inner, shards)
    s, h, parts, ys = at.s, at.h, at.parts, at.ys
    steps = list(range(1, ys))
    line = LineSum(at, p_s, (x_in, up_in, down_in, line_out), (across, up, low))
    model = x_ref.shape[1]
    tile = min(512, model)
    piece = done.shape[1]
    span = shards * piece
    width2 = both_ref.shape[1]
    me = s * shards + h
    small = ((blocks_ref, block_slots, blocks_out), (sums_ref, sum_slots, sums_out))
    fetch = pltpu.make_async_copy(up_ref, up_own, local.at[0])
    fetch.start()

    def stripes(k):
        lanes = pl.ds(pl.multiple_of(owner(k) * span, span), span)
        slot = lax.rem(k, 2)
        return (
            pltpu.make_async_copy(n1_ref.at[:, lanes], n1_s.at[slot], stripe.at[0, slot]),
            pltpu.make_async_copy(dout_ref.at[:, lanes], dout_s.at[slot], stripe.at[1, slot]),
        )

    def owner(k):
        return lax.rem(s + k + 1, parts)

    pairs = [(both_from, both_ref), (wi_from, wi_ref)]
    first = load_all(pairs, early_sem)
    for copy in stripes(0):
        copy.start()
    pairs = [(z_from, z_ref), (x_from, x_ref), (dmid_from, dmid_ref)]
    second = load_all(pairs, early_sem.at[pl.ds(2, 3)])

    def anyone(k):
        to = lax.rem(me + k, at.count)
        return (to // shards, lax.rem(to, shards)), to

    def greet_one(k, carry):
        hello(anyone(k)[0])
        return carry

    lax.fori_loop(1, at.count, greet_one, 0)
    welcome(at.count - 1)
    ups = LineReduce(at, up_own, up_land, u_up, u_low)
    fetch.wait()

    ups.early(0, at.far_first(0), min(1, outer - 2))

    for copy in first:
        copy.wait()

    def back(n, carry):
        d = at.far_first(n)
        rows = pl.ds(pl.multiple_of(d * p_s.shape[1], p_s.shape[1]), p_s.shape[1])
        for lane in range(0, model, tile):
            lanes = slice(lane, lane + tile)
            p_s[d, :, lanes] = dot(both_ref[rows, :], wi_ref[lanes, :], ((1,), (1,))).astype(BF16)
        line.start(d)
        return carry

    lax.fori_loop(0, outer, back, 0)
    send = Sent()
    for n, (src, slots, _) in enumerate(small):
        for dy in steps:
            send(src, slots.at[h], s_far, (n, dy), (s, at.along(dy)))
        send(src, slots.at[h], s_near, (n, 0), at.sibling)
        slots[h] = src[...]

    def mix_rows(p, shard):
        return g_s.at[p, pl.ds(pl.multiple_of(shard * piece, piece), piece)]

    def to_sibling(k, dy):
        p = owner(k)
        return remote(
            mix_rows(p, at.along(dy, 1)),
            near_in.at[dy, p],
            near.at[0, dy, k],
            near.at[1, dy, k],
            at.sibling,
        )

    def to_shard(k, dy, source=False):
        p = owner(k)
        return remote(
            far_out.at[dy - 1, p],
            far_in.at[dy - 1, p],
            far.at[0, dy, k],
            far.at[1, dy, k],
            (s, at.along(-dy if source else dy)),
        )

    def to_owner(k, source=False):
        p = lax.rem(s + parts - k - 1, parts) if source else owner(k)
        return remote(
            done.at[owner(k)],
            mix_ref.at[p if source else s],
            final.at[0, k],
            final.at[1, k],
            (p, h),
        )

    for copy in second:
        copy.wait()

    def weight_grads(k, carry):
        p, slot = owner(k), lax.rem(k, 2)
        for copy in stripes(k):
            copy.wait()

        @pl.when(k < parts - 1)
        def _():
            for copy in stripes(k + 1):
                copy.start()

        g_s[p, :, 0:width2] = dot(n1_s[slot], both_ref[...], ((0,), (0,))).astype(BF16)
        g_s[p, :, width2:] = dot(dout_s[slot], z_ref[...], ((0,), (0,))).astype(BF16)
        for dy in steps + [0]:
            to_sibling(k, dy).start()
        return carry

    lax.fori_loop(0, parts, weight_grads, 0)
    exchanges = [
        PlaneExchange(at, 0, down_ref, down_out, swap, local.at[2]),
        PlaneExchange(at, 1, gate_ref, gate_out, swap, local.at[3]),
        PlaneExchange(at, 3, rest_ref, rest_out, swap, local.at[5]),
    ]
    up_exchange = PlaneExchange(at, 2, up_sum, up_out, swap, local.at[1])

    def sibling_sums(k, carry):
        p = owner(k)
        for dy in steps:
            to_sibling(k, dy).wait_recv()
            mine = mix_rows(p, at.along(dy))

            def add(rows, dy=dy, mine=mine):
                total = mine[rows, :].astype(F32) + near_in[dy, p, rows, :].astype(F32)
                far_out[dy - 1, p, rows, :] = total.astype(BF16)

            add_rows(piece, add)
            to_shard(k, dy).start()
        return carry

    lax.fori_loop(0, parts, sibling_sums, 0)
    gain_s[...] = jnp.zeros(gain_s.shape, F32)

    def mix_step(k):
        p = owner(k)
        mine = mix_rows(p, h)
        to_sibling(k, 0).wait_recv()
        for dy in steps:
            to_shard(k, dy, True).wait_recv()

        def add(rows):
            total = mine[rows, :].astype(F32) + near_in[0, p, rows, :].astype(F32)
            for dy in steps:
                total = total + far_in[dy - 1, p, rows, :].astype(F32)
            done[p, rows, :] = total.astype(BF16)

        add_rows(piece, add)
        if k < parts - 1:
            to_owner(k).start()

    def last_add(rows, dn1):
        x = x_ref[rows, :].astype(F32)
        scale = row_rms(x)
        gain_s[...] += dn1 * x * scale
        grad_ref[rows, :] = dmid_ref[rows, :] + rms_back(x, scale, gain_ref[...], dn1)

    def finish_ups(o0):
        ups.absorb(o0, o0)

        def keep_up(rows):
            up_sum[rows, :] = up_own[at.o, rows, :]

        add_rows(up_sum.shape[0], keep_up)
        up_exchange.start()

    def branch(o0):
        ends = o0 in (0, outer - 1)

        sooner = min(1, outer - 2) if ends else 0

        def between(n):
            if n + sooner < outer - 1 and ends:
                ups.push(o0, ups.order(o0)[n + sooner])
            for k in range(n * inner, parts if n == outer - 2 else (n + 1) * inner):
                if n < outer - 1:
                    mix_step(k)
            if n + 1 < outer - 1 and not ends:
                ups.step(o0, n + 1)
            if n == outer - 2:
                for exchange in exchanges:
                    exchange.start()

        if not ends:
            ups.step(o0, 0)
        line.steps(o0, last_add, between)

    at.branches(branch)
    keep = pltpu.make_async_copy(done.at[s], mix_ref.at[s], local.at[4])
    keep.start()
    gain1, gain2 = jnp.sum(gain_s[...], axis=0, keepdims=True), gain2_ref[...]
    spare = gain_rows.shape[2] - 2 * piece
    for k in range(at.count):
        lanes = slice(k * piece, (k + 1) * piece)
        parts_of = [gain1[:, lanes], gain2[:, lanes]]
        if spare:
            parts_of.append(jnp.zeros((1, spare), F32))
        gain_rows[k] = jnp.concatenate(parts_of, axis=1)

    def gain(k):
        to, row = anyone(k)
        return remote(gain_rows.at[row], gain_slots.at[k], g_sem.at[0, k], g_sem.at[1, k], to)

    def gain_start(k, carry):
        gain(k).start()
        return carry

    def gain_arrive(k, total):
        gain(k).wait_recv()
        return total + gain_slots[k]

    def gain_leave(k, carry):
        gain(k).wait_send()
        return carry

    lax.fori_loop(1, at.count, gain_start, 0)
    at.branches(finish_ups)

    for n, (src, slots, out) in enumerate(small):
        for dy in steps:
            here = slots.at[at.along(-dy)]
            received(src, here, s_far, (n, dy), (s, at.along(-dy)))
            send(here, here, s_near, (n, dy), at.sibling)
    for n, (src, slots, out) in enumerate(small):
        for dy in range(ys):
            received(src, slots.at[at.along(-dy, 1)], s_near, (n, dy), at.sibling)

        def add(k, carry, slots=slots, out=out):
            rows = pl.ds(pl.multiple_of(k * 8, 8), 8)
            total = slots[0, rows, :]
            for j in range(1, shards):
                total = total + slots[j, rows, :]
            out[rows, :] = total
            return carry

        lax.fori_loop(0, src.shape[0] // 8, add, 0)
    gains_out[...] = lax.fori_loop(1, at.count, gain_arrive, gain_rows[me])
    for k in range(parts - 1):
        to_owner(k, True).wait_recv()
    for exchange in exchanges + [up_exchange]:
        exchange.finish()
    at.branches(ups.finish)
    for k in range(parts):
        for dy in range(ys):
            to_sibling(k, dy).wait_send()
        for dy in steps:
            to_shard(k, dy).wait_send()
        if k < parts - 1:
            to_owner(k).wait_send()
    lax.fori_loop(1, at.count, gain_leave, 0)
    send.finish()
    keep.wait()


def closing(
    both,
    w_in,
    z,
    x,
    dmid,
    gain,
    gain2,
    small,
    sums,
    n1,
    dout,
    down,
    gate,
    rest,
    ups,
    outer,
    inner,
    shards,
    collective,
):
    rows, cols = x.shape
    parts, ys, count = outer * inner, shards // 2, outer * inner * shards
    piece = cols // count
    width = z.shape[1]
    lanes = -(-2 * piece // LANES) * LANES
    bufs, sems = line_sum_scratch(outer, rows, cols)
    pieces = pltpu.VMEM((max(ys - 1, 1), parts, piece, 3 * width), BF16)
    stripes = pltpu.VMEM((2, parts * rows, cols // parts), BF16)
    span, hidden = ups.shape[1:]

    def swapped(array):
        shape = (inner * shards, span // (inner * shards), array.shape[-1])
        return jax.ShapeDtypeStruct(shape, BF16)

    reduce_vmem, reduce_sems = line_reduce_scratch(outer, span, hidden)
    return pl.pallas_call(
        functools.partial(closing_kernel, outer, inner, shards),
        out_shape=(
            jax.ShapeDtypeStruct((rows, cols), F32),
            jax.ShapeDtypeStruct((parts, piece, 3 * width), BF16),
            jax.ShapeDtypeStruct(small.shape, F32),
            jax.ShapeDtypeStruct(sums.shape, F32),
            jax.ShapeDtypeStruct((1, lanes), F32),
            *[swapped(array) for array in (down, gate, rest, ups)],
        ),
        in_specs=[IN_HBM] * 5 + [IN_VMEM] * 4 + [IN_HBM] * 6,
        out_specs=[IN_VMEM] * 5 + [IN_HBM] * 4,
        scratch_shapes=[
            *[pltpu.VMEM(value.shape, value.dtype) for value in (both, w_in, z, x, dmid)],
            DMA((5,)),
            pltpu.VMEM((outer, inner * rows, cols), BF16),
            *reduce_vmem,
            pltpu.VMEM((span, hidden), BF16),
            stripes,
            stripes,
            pltpu.VMEM((parts, shards * piece, 3 * width), BF16),
            pltpu.VMEM((16, cols), F32),
            pltpu.VMEM((count, 1, lanes), F32),
            pltpu.VMEM((count, 1, lanes), F32),
            pltpu.VMEM((ys, parts, piece, 3 * width), BF16),
            pieces,
            pieces,
            pltpu.VMEM((parts, piece, 3 * width), BF16),
            pltpu.VMEM((shards,) + small.shape, F32),
            pltpu.VMEM((shards,) + sums.shape, F32),
        ]
        + bufs
        + sems
        + [DMA((2, ys, parts))] * 2
        + [DMA((2, parts))]
        + [DMA((2, 2, ys))] * 2
        + [DMA((2, 4, inner * shards)), DMA((2, count)), DMA((2, 2))]
        + reduce_sems
        + [DMA((6,))],
        compiler_params=pltpu.CompilerParams(
            collective_id=collective, has_side_effects=True, vmem_limit_bytes=60 * 2**20
        ),
        cost_estimate=cost(80),
        name="closing",
    )(
        both,
        w_in,
        z,
        x,
        dmid,
        gain,
        gain2,
        small,
        sums,
        n1,
        dout,
        down,
        gate,
        rest,
        ups,
    )


def unpack_kernel(inner, channels, block_width, *refs):
    sources, targets = refs[:10], refs[10:27]
    held, made, in_sem, out_sem = refs[27:36], refs[36:42], refs[42], refs[43]
    gate_ref, rest_ref, up_ref, down_ref, mix_ref, blocks_ref, sums_ref = held[:7]
    fetch = [
        pltpu.make_async_copy(sources[k], held[k], in_sem.at[k]) for k in range(len(held))
    ]
    for copy in fetch[7:] + fetch[:7]:
        copy.start()
    store = []
    gains_ref = sources[9]
    rate, entry, taps, conv_b, rate_b, entry_b, decay, first_gain, second_gain = targets[8:]
    for k in range(2):
        fetch[7 + k].wait()
        copy = pltpu.make_async_copy(held[7 + k], targets[6 + k], out_sem.at[6 + k])
        copy.start()
        store.append(copy)
    fetch[0].wait()
    fetch[1].wait()
    gate, up, down = made[:3]
    slots, piece, hidden = down_ref.shape
    cut = gate_ref.shape[2]
    tail = hidden - cut
    head = hidden - up_ref.shape[2]
    shards = slots // inner
    parts, width = mix_ref.shape[0], mix_ref.shape[2] // 3
    places = [
        ((h * inner + i) * hidden, i * shards + h) for i in range(inner) for h in range(shards)
    ]

    def ship(k):
        copy = pltpu.make_async_copy(made[k], targets[k], out_sem.at[k])
        copy.start()
        store.append(copy)

    for first, slot in places:
        gate[:, first : first + cut] = gate_ref[slot].astype(F32)
        gate[:, first + cut : first + hidden] = rest_ref[slot][:, :tail].astype(F32)
    ship(0)
    fetch[2].wait()
    for first, slot in places:
        up[:, first : first + head] = rest_ref[slot][:, tail:].astype(F32)
        up[:, first + head : first + hidden] = up_ref[slot].astype(F32)
    ship(1)
    fetch[3].wait()
    for first, slot in places:
        down[:, first : first + hidden] = down_ref[slot].astype(F32)
    ship(2)
    fetch[4].wait()
    for k in range(3):
        lanes = slice(k * width, k * width + width)
        made[3 + k][...] = jnp.concatenate(
            [mix_ref[p][:, lanes].astype(F32)[:, :channels] for p in range(parts)], axis=1
        )
        ship(3 + k)
    fetch[5].wait()
    fetch[6].wait()
    blocks = rate.shape[1]
    tall = blocks_ref.shape[0] // (2 * blocks)
    for k, dst in enumerate((rate, entry)):
        for j in range(blocks):
            top = (k * blocks + j) * tall
            dst[:, j, :] = blocks_ref[top : top + block_width, :block_width]
    taps[...] = sums_ref[4:8, :channels]
    for row, dst in ((3, conv_b), (1, rate_b), (2, entry_b), (0, decay)):
        dst[...] = sums_ref[row, :channels]
    first_gain[...] = gains_ref[0, :piece]
    second_gain[...] = gains_ref[0, piece : 2 * piece]
    for copy in store:
        copy.wait()


def unpack(
    gate, rest, up, down, mix, small, sums, result, grad, gains, inner, channels, blocks, block_width
):
    slots, piece, hidden = down.shape
    across = jax.ShapeDtypeStruct((piece, slots * hidden), F32)
    wide = jax.ShapeDtypeStruct((piece, mix.shape[0] * channels), F32)
    square = jax.ShapeDtypeStruct((block_width, blocks, block_width), F32)
    vector = jax.ShapeDtypeStruct((channels,), F32)
    taps = jax.ShapeDtypeStruct((4, channels), F32)
    gain = jax.ShapeDtypeStruct((piece,), F32)
    held = (gate, rest, up, down, mix, small, sums, result, grad)
    made = (across,) * 3 + (wide,) * 3
    return pl.pallas_call(
        functools.partial(unpack_kernel, inner, channels, block_width),
        out_shape=made
        + tuple(jax.ShapeDtypeStruct(x.shape, x.dtype) for x in (result, grad))
        + (square,) * 2
        + (taps,)
        + (vector,) * 4
        + (gain,) * 2,
        in_specs=[IN_HBM] * 9 + [IN_VMEM],
        out_specs=[IN_HBM] * 8 + [IN_VMEM] * 9,
        scratch_shapes=[pltpu.VMEM(x.shape, x.dtype) for x in held + made]
        + [DMA((len(held),)), DMA((8,))],
        compiler_params=pltpu.CompilerParams(vmem_limit_bytes=60 * 2**20),
        cost_estimate=cost(5),
        name="unpack",
    )(*held, gains)


def body(
    tokens,
    first_gain,
    branch_weight,
    input_weight,
    conv_weight,
    conv_bias,
    rate_weight,
    rate_bias,
    entry_weight,
    entry_bias,
    decay_param,
    output_weight,
    second_gain,
    hidden_gate,
    hidden_up,
    hidden_down,
    cotangent,
):
    quarters, _, chunk, model = tokens.shape
    rows = quarters * chunk
    parts = lax.axis_size("seq")
    shards = lax.axis_size("shard")
    inner = 2
    outer = parts // inner
    seq_at = lax.axis_index("seq")
    inner_at = lax.rem(seq_at, inner)
    lru = branch_weight.shape[1]
    channels = lru // parts
    width = (channels + LANES) // LANES * LANES
    spare = width - channels
    blocks, block_width = rate_weight.shape[0], rate_weight.shape[1]
    piece = model // (parts * shards)

    def own(weight, axis):
        part = lax.dynamic_slice_in_dim(weight, seq_at * channels, channels, axis)
        pads = [(0, 0), (0, 0)]
        pads[axis] = (0, spare)
        return jnp.pad(part, pads)

    x = tokens.reshape(rows, model)
    cot = cotangent.reshape(rows, model)
    gain1, gain2 = first_gain[None], second_gain[None]
    params, mid, z, h, v, proj, gates, n1, w_in, w_out, n2, cot_all = forward(
        x,
        gain1,
        gain2,
        (conv_weight, conv_bias, rate_bias, entry_bias, decay_param),
        rate_weight.transpose(1, 0, 2),
        entry_weight.transpose(1, 0, 2),
        cot,
        jnp.concatenate([own(branch_weight, 1), own(input_weight, 1)], axis=1),
        own(output_weight, 0),
        quarters,
        chunk,
        outer,
        inner,
        shards,
        0,
    )
    w_in = w_in.reshape(model, 2 * width)
    n2 = n2.reshape(inner * shards * rows, model)
    cot_all = cot_all.reshape(inner * shards * rows, model)
    hidden = hidden_gate.shape[1] // inner
    wg = lax.dynamic_slice_in_dim(hidden_gate, inner_at * hidden, hidden, 1)
    wu = lax.dynamic_slice_in_dim(hidden_up, inner_at * hidden, hidden, 1)
    wd = lax.dynamic_slice_in_dim(hidden_down, inner_at * hidden, hidden, 0)

    gm = dot(n2, wg)
    um = dot(n2, wu)
    act, slope = gelu_and_slope(gm)
    mm = (act * um).astype(BF16)
    dmm = dot(cot_all, wd, ((1,), (1,)))
    dgm = (dmm * um * slope).astype(BF16)
    dum = (dmm * act).astype(BF16)
    dmid, gain2_grad, dout, partial, down_sum, gate_sum, rest_terms, up_terms = turn(
        dgm,
        dum,
        mm,
        mid,
        cot,
        gain2,
        hidden_gate,
        hidden_up,
        hidden_down,
        n2,
        cot_all,
        outer,
        inner,
        shards,
        1,
    )
    both, small, sums, result, rest_sum = scan_backward(
        quarters,
        chunk,
        blocks,
        block_width,
        dout,
        w_out,
        proj,
        h,
        v,
        params,
        gates,
        mid,
        partial,
        rest_terms,
        outer,
        inner,
        shards,
        2,
    )
    tokens_grad, mix, small, sums, gains, down_sum, gate_sum, rest_sum, up_sum = closing(
        both,
        w_in,
        z,
        x,
        dmid,
        gain1,
        gain2_grad,
        small,
        sums,
        n1.reshape(parts * rows, model),
        dout.reshape(parts * rows, model),
        down_sum,
        gate_sum,
        rest_sum,
        up_terms,
        outer,
        inner,
        shards,
        3,
    )
    (
        gate_grad,
        up_grad,
        down_grad,
        branch_grad,
        input_grad,
        output_grad,
        result,
        tokens_grad,
        rate_grad,
        entry_grad,
        tap_grad,
        conv_bias_grad,
        rate_bias_grad,
        entry_bias_grad,
        decay_grad,
        gain1_grad,
        gain2_grad,
    ) = unpack(
        gate_sum,
        rest_sum,
        up_sum,
        down_sum,
        mix,
        small,
        sums,
        result,
        tokens_grad,
        gains,
        inner,
        channels,
        blocks,
        block_width,
    )
    return (
        result.reshape(tokens.shape),
        tokens_grad.reshape(tokens.shape),
        gain1_grad,
        branch_grad,
        input_grad,
        tap_grad,
        conv_bias_grad,
        rate_grad.transpose(1, 0, 2),
        rate_bias_grad,
        entry_grad.transpose(1, 0, 2),
        entry_bias_grad,
        decay_grad,
        output_grad.T,
        gain2_grad,
        gate_grad,
        up_grad,
        down_grad.T,
    )


def solution(mesh):
    placed = (
        P(None, "shard", "seq", None),
        P(),
        P("shard", None),
        P("shard", None),
        P(None, "seq"),
        P("seq"),
        P("seq", None, None),
        P("seq"),
        P("seq", None, None),
        P("seq"),
        P("seq"),
        P(None, "shard"),
        P(),
        P(None, "shard"),
        P(None, "shard"),
        P("shard", None),
        P(None, "shard", "seq", None),
    )
    return jax.shard_map(
        body,
        mesh=mesh,
        in_specs=placed,
        out_specs=(
            P(None, "shard", "seq", None),
            P(None, "shard", "seq", None),
            P(("seq", "shard")),
            P(("seq", "shard"), None),
            P(("seq", "shard"), None),
            P(None, "seq"),
            P("seq"),
            P("seq", None, None),
            P("seq"),
            P("seq", None, None),
            P("seq"),
            P("seq"),
            P(None, ("seq", "shard")),
            P(("seq", "shard")),
            P(("seq", "shard"), None),
            P(("seq", "shard"), None),
            P(None, ("seq", "shard")),
        ),
        check_vma=False,
    )
```

```python
import functools

import jax
import jax.numpy as jnp
from jax import lax
from jax.experimental import pallas as pl
from jax.experimental.pallas import tpu as pltpu
from jax.sharding import PartitionSpec as P

EPSILON = 1e-06
DECAY_SCALE = 8.0
MULT_FLOOR = 0.01
LANES = 128
SEGMENTS = 8
GELU_C = 0.7978845608028654
GELU_A = 0.044715
F32 = jnp.float32
BF16 = jnp.bfloat16


MESH = pl.DeviceIdType.MESH
IN_HBM = pl.BlockSpec(memory_space=pltpu.HBM)
IN_VMEM = pl.BlockSpec(memory_space=pltpu.VMEM)
DMA = pltpu.SemaphoreType.DMA


def cost(us):
    return pl.CostEstimate(flops=0, bytes_accessed=int(us * 3.3e6), transcendentals=0)


def dot(left, right, dims=((1,), (0,))):
    return lax.dot_general(left, right, (dims, ((), ())), preferred_element_type=F32)


def gelu_and_slope(x):
    inner = GELU_C * (x + GELU_A * x * x * x)
    t = jnp.tanh(inner)
    half = 0.5 * (1.0 + t)
    slope = half + 0.5 * x * (1.0 - t * t) * (GELU_C * (1.0 + 3.0 * GELU_A * x * x))
    return x * half, slope


def gelu_tanh(x):
    return x * (0.5 * (1.0 + jnp.tanh(GELU_C * (x + GELU_A * x * x * x))))


def sigmoid(x):
    return 0.5 * jnp.tanh(0.5 * x) + 0.5


def softplus(x):
    return jnp.maximum(x, 0.0) + jnp.log1p(jnp.exp(-jnp.abs(x)))


def lane_groups(width):
    return [slice(g * LANES, (g + 1) * LANES) for g in range(width // LANES)]


def put(ref, rows, value):
    for g, lanes in enumerate(lane_groups(value.shape[1])):
        ref[g, rows, :] = value[:, lanes]


def take(ref, rows):
    return jnp.concatenate([ref[g, rows, :] for g in range(ref.shape[0])], axis=1)


def strided_scan(steps, groups, load, store):
    def step(k, carry):
        i = steps(k)
        out = []
        for g in range(groups):
            state, total = carry[g]
            factor, term = load(g, i)
            state = factor * state + term
            total = factor * total
            store(g, i, state, total)
            out.append((state, total))
        return tuple(out)

    return step


TAP, CONV_B, RATE_B, ENTRY_B, DECAY = 0, 4, 5, 6, 7


def gate_values(pre, log_scale, width):
    r = sigmoid(pre[:, :width])
    e = sigmoid(pre[:, width:])
    a = jnp.exp(r * log_scale)
    room = 1.0 - a * a
    m = jnp.sqrt(jnp.maximum(room, MULT_FLOOR))
    return r, e, a, room, m


class Place:
    def __init__(self, outer, inner, shards):
        self.outer, self.inner, self.shards = outer, inner, shards
        self.parts, self.ys, self.count = outer * inner, shards // 2, outer * inner * shards
        self.chips = inner * self.ys
        self.s, self.h = lax.axis_index("seq"), lax.axis_index("shard")
        self.o, self.i = self.s // inner, lax.rem(self.s, inner)
        self.y, self.core = self.h // 2, lax.rem(self.h, 2)
        self.beside = (self.o * inner + 1 - self.i, self.h)
        self.above, self.below = (self.s + inner, self.h), (self.s - inner, self.h)
        self.sibling = (self.s, self.along(0, 1))

    def along(self, dy, other=0):
        y = lax.rem(self.y + dy + self.ys, self.ys)
        return y * 2 + lax.rem(self.core + other, 2)

    def chip(self, q, back=False):
        di, dy = q // self.ys, q - q // self.ys * self.ys
        if back:
            di, dy = self.inner - di, self.ys - dy
        return lax.rem(self.i + di, self.inner), lax.rem(self.y + dy, self.ys)

    def near(self, q, other=0, back=False):
        i, y = self.chip(q, back)
        h = y * 2 + lax.rem(self.core + other, 2)
        return (self.o * self.inner + i, h), i * self.shards + h

    def far_first(self, n):
        sign = 2 * ((2 * self.o) // self.outer) - 1
        return lax.rem(self.o + sign * (n + 1) + 2 * self.outer, self.outer)

    def branches(self, fn):
        for o0 in range(self.outer):
            pl.when(self.o == o0)(functools.partial(fn, o0))


def hello(to):
    barrier = pltpu.get_barrier_semaphore()
    pl.semaphore_signal(barrier, inc=1, device_id=to, device_id_type=MESH)


def welcome(n):
    pl.semaphore_wait(pltpu.get_barrier_semaphore(), n)


def greet(others):
    for to in others:
        hello(to)
    welcome(len(others))


def greet_with_line(at, others):
    up, down = at.o < at.outer - 1, at.o > 0
    for to in others:
        hello(to)
    pl.when(up)(lambda: hello(at.above))
    pl.when(down)(lambda: hello(at.below))
    ends = lax.rem(at.o, at.outer - 1) == 0
    pl.when(ends)(lambda: welcome(len(others) + 1))
    pl.when(jnp.logical_not(ends))(lambda: welcome(len(others) + 2))


class Sent:
    def __init__(self):
        self.copies = []

    def __call__(self, src, dst, sems, at, to):
        copy = remote(src, dst, sems.at[(0,) + at], sems.at[(1,) + at], to)
        copy.start()
        self.copies.append(copy)

    def finish(self):
        for copy in self.copies:
            copy.wait_send()


def received(like, here, sems, at, source):
    remote(like, here, sems.at[(0,) + at], sems.at[(1,) + at], source).wait_recv()


def line_gather(
    at,
    o0,
    x_ref,
    out,
    across,
    up,
    down,
    between=lambda k: None,
    each=lambda row: None,
    side=None,
    slim=0,
):
    send = Sent()
    rows = x_ref.shape[0]
    parts = across.shape[2]
    half = rows // parts
    low = pl.ds(rows - slim, slim)

    def slot(row, other=False):
        return out.at[row * at.inner + (1 - at.i if other else at.i)]

    def some(row, part):
        less = slim if slim and row != o0 and part == parts - 1 else 0
        return pl.ds(part * half, half - less)

    def pass_on(row, part, sems, to):
        some_rows = pl.ds(part * half, half)
        src = x_ref if row == o0 else slot(row)
        send(src.at[some_rows], slot(row).at[some_rows], sems, (row, part), to)

    def cross(row, part):
        src = x_ref if row == o0 else slot(row)
        send(src.at[some(row, part)], slot(row).at[some(row, part)], across, (row, part), at.beside)

    def crossed(row):
        for part in range(parts):
            here = slot(row, True).at[some(row, part)]
            received(here, here, across, (row, part), at.beside)

    def slim_on(row):
        here = slot(row, True).at[low]
        if row <= o0 < at.outer - 1:
            send(here, here, side[0], (row,), at.above)
        if row >= o0 > 0:
            send(here, here, side[1], (row,), at.below)

    def slim_came(row, sems, source):
        here = slot(row, True).at[low]
        received(here, here, sems, (row,), source)

    for k in range(at.outer):
        lower, upper = o0 - k, o0 + k
        for part in range(parts):
            here = x_ref.at[pl.ds(part * half, half)]
            if lower >= 0:
                if k > 0:
                    received(here, here, up, (lower, part), at.below)
                if o0 < at.outer - 1:
                    pass_on(lower, part, up, at.above)
                cross(lower, part)
            if upper < at.outer:
                if k > 0:
                    received(here, here, down, (upper, part), at.above)
                if o0 > 0:
                    pass_on(upper, part, down, at.below)
                if k > 0:
                    cross(upper, part)
        if slim and k == 1:
            crossed(o0)
            slim_on(o0)
        if slim and k > 1:
            for row, sems, source in (
                (o0 - k + 1, side[0], at.below),
                (o0 + k - 1, side[1], at.above),
            ):
                if 0 <= row < at.outer:
                    slim_came(row, sems, source)
                    slim_on(row)
        between(k)
    between(at.outer)
    for row in sorted(range(at.outer), key=lambda row: abs(row - o0)):
        if row != o0 or not slim:
            crossed(row)
        if slim and row != o0 and abs(row - o0) == at.outer - 1:
            slim_came(row, side[0] if row < o0 else side[1], at.below if row < o0 else at.above)
        each(row)
    send.finish()


class LineSum:
    def __init__(self, at, p, bufs, sems, side=None):
        self.at, self.p = at, p
        self.x_in, self.up_in, self.down_in, self.sums = bufs
        self.across, self.up, self.down = sems
        self.rows = self.x_in.shape[1]
        self.parts = self.across.shape[2]
        self.slim = 0
        if side is not None:
            self.s_up_in, self.s_down_in, self.s_sums, self.s_in = side[:4]
            self.s_up, self.s_down, self.s_across = side[4:]
            self.slim = self.s_in.shape[0]

    def block(self, d, i):
        return self.p.at[d, pl.ds(pl.multiple_of(i * self.rows, self.rows), self.rows)]

    def cross(self, d, part):
        half = self.rows // self.parts
        some = pl.ds(part * half, half - (self.slim if part == self.parts - 1 else 0))
        return remote(
            self.block(d, 1 - self.at.i).at[some],
            self.x_in.at[d].at[some],
            self.across.at[0, d, part],
            self.across.at[1, d, part],
            self.at.beside,
        )

    def start(self, d):
        for part in range(self.parts):
            self.cross(d, part).start()

    def steps(self, o0, last_add, between=lambda n: None):
        at, rows, slim = self.at, self.rows, self.slim
        send = Sent()
        order = sorted(range(at.outer), key=lambda d: (-abs(d - o0), d))
        low, half = rows - slim, rows // self.parts

        def arrivals(d, index, mine, up_in, down_in, up, down):
            terms = []
            if d >= o0 > 0:
                received(mine, mine, up, index, at.below)
                terms.append(up_in.at[d])
            if d <= o0 < at.outer - 1:
                received(mine, mine, down, index, at.above)
                terms.append(down_in.at[d])
            return terms

        def total_of(terms, some):
            total = terms[0][some, :].astype(F32)
            for term in terms[1:]:
                total = total + term[some, :].astype(F32)
            return total

        for n, d in enumerate(order):
            mine = self.block(d, at.i)
            target = self.sums.at[d]
            for part in range(self.parts):
                part_rows = pl.ds(part * half, half)
                self.cross(d, part).wait_recv()
                along = [mine] + arrivals(
                    d,
                    (d, part),
                    mine.at[part_rows],
                    self.up_in,
                    self.down_in,
                    self.up,
                    self.down,
                )
                both = along + [self.x_in.at[d]]

                def add(some, both=both, target=target, d=d):
                    total = total_of(both, some)
                    if d == o0:
                        last_add(some, total)
                    else:
                        target[some, :] = total.astype(BF16)

                def add_low(some, along=along, target=target):
                    target[some, :] = total_of(along, some).astype(BF16)

                add_rows(min((part + 1) * half, low), add, part * half)
                if slim and d != o0 and part == self.parts - 1:
                    add_rows(rows, add_low, low)
                if d > o0:
                    here, there = target.at[part_rows], self.up_in.at[d].at[part_rows]
                    send(here, there, self.up, (d, part), at.above)
                if d < o0:
                    here, there = target.at[part_rows], self.down_in.at[d].at[part_rows]
                    send(here, there, self.down, (d, part), at.below)
            if slim:
                theirs = self.block(d, 1 - at.i).at[pl.ds(low, slim)]
                extra = [theirs] + arrivals(
                    d, (d,), theirs, self.s_up_in, self.s_down_in, self.s_up, self.s_down
                )
                aside = self.s_sums.at[d]

                def add_aside(some, extra=extra, aside=aside):
                    aside[some, :] = total_of(extra, some).astype(BF16)

                add_rows(slim, add_aside)
                if d > o0:
                    send(aside, self.s_up_in.at[d], self.s_up, (d,), at.above)
                if d < o0:
                    send(aside, self.s_down_in.at[d], self.s_down, (d,), at.below)
                if d == o0:
                    send(aside, self.s_in, self.s_across, (), at.beside)
                    received(aside, self.s_in, self.s_across, (), at.beside)
                    for k in range(slim // 16):
                        some, here = pl.ds(low + 16 * k, 16), pl.ds(16 * k, 16)
                        last_add(some, total_of(along, some) + self.s_in[here, :].astype(F32))
            between(n)
        for d in range(at.outer):
            for part in range(self.parts):
                self.cross(d, part).wait_send()
        send.finish()


class LineReduce:
    def __init__(self, at, own, land, up, down):
        self.at, self.own, self.land, self.up, self.down = at, own, land, up, down

    def order(self, o0):
        return sorted(range(self.at.outer), key=lambda d: (-abs(d - o0), d))

    def ascent(self, d):
        at = self.at
        return remote(
            self.own.at[d], self.land.at[d], self.up.at[0, d], self.up.at[1, d], at.above
        )

    def descent(self, o0, d):
        slot = d if d != o0 - 1 else self.at.outer
        return remote(
            self.own.at[d], self.land.at[slot], self.down.at[0, d], self.down.at[1, d], self.at.below
        )

    def early(self, n, d, limit):
        at = self.at
        inside = n < limit
        last = at.outer - 1
        pl.when(jnp.logical_and(at.o == 0, inside))(lambda: self.ascent(d).start())
        far = remote(
            self.own.at[d], self.land.at[d], self.down.at[0, d], self.down.at[1, d], at.below
        )
        pl.when(jnp.logical_and(at.o == last, inside))(lambda: far.start())

    def push(self, o0, d):
        if d > o0:
            self.ascent(d).start()
        if d < o0:
            self.descent(o0, d).start()

    def absorb(self, o0, d):
        terms = []
        if d >= o0 > 0:
            self.ascent(d).wait_recv()
            terms.append(self.land.at[d])
        if d <= o0 < self.at.outer - 1:
            slot = d if d < o0 else self.at.outer
            self.descent(o0 + 1, d).wait_recv()
            terms.append(self.land.at[slot])
        mine = self.own.at[d]

        def add(rows):
            total = mine[rows, :].astype(F32)
            for term in terms:
                total = total + term[rows, :].astype(F32)
            mine[rows, :] = total.astype(BF16)

        if terms:
            add_rows(mine.shape[0], add)

    def step(self, o0, n):
        d = self.order(o0)[n]
        self.absorb(o0, d)
        self.push(o0, d)

    def finish(self, o0):
        for d in range(self.at.outer):
            if d > o0:
                self.ascent(d).wait_send()
            if d < o0:
                self.descent(o0, d).wait_send()


def first_half(hidden):
    return -(-(hidden // 2) // LANES) * LANES


def line_reduce_scratch(outer, rows, cols):
    blocks = [pltpu.VMEM((outer, rows, cols), BF16), pltpu.VMEM((outer + 1, rows, cols), BF16)]
    return blocks, [DMA((2, outer))] * 2


SLIM = 16
HALVES = 2


def slim_scratch(outer, cols):
    blocks = [pltpu.VMEM((outer, SLIM, cols), BF16)] * 3 + [pltpu.VMEM((SLIM, cols), BF16)]
    return blocks, [DMA((2, outer))] * 2 + [DMA((2,))]


def line_sum_scratch(outer, rows, cols, parts=HALVES):
    return [pltpu.VMEM((outer, rows, cols), BF16)] * 4, [DMA((2, outer, parts))] * 3


def row_rms(values):
    return lax.rsqrt(jnp.mean(values * values, axis=-1, keepdims=True) + EPSILON)


def rms_back(values, scale, gain, grad):
    k = grad * gain
    mean = jnp.mean(k * values, axis=-1, keepdims=True)
    return scale * k - scale * scale * scale * values * mean


def run_scan(
    parts, quarters, chunk, proj_ref, par_ref, gates_ref, z_ref, h_ref, v_ref, u_pad, a_s, b_s
):
    length, width = h_ref.shape
    seg = length // SEGMENTS
    chunks = length // chunk

    def place(c):
        q = c // parts
        s = c - q * parts
        return pl.multiple_of((s * quarters + q) * chunk, chunk)

    def time_of(c):
        return pl.multiple_of(c * chunk, chunk)

    log_scale = -DECAY_SCALE * softplus(-par_ref[DECAY : DECAY + 1, :])
    bias = jnp.concatenate(
        [par_ref[RATE_B : RATE_B + 1, :], par_ref[ENTRY_B : ENTRY_B + 1, :]], axis=1
    )
    u_pad[0:8, :] = jnp.zeros((8, width), F32)

    def first(c, carry):
        u = proj_ref[pl.ds(place(c), chunk), width : 2 * width].astype(BF16).astype(F32)
        u_pad[pl.ds(pl.multiple_of(time_of(c) + 8, 8), chunk), :] = u
        wide = u_pad[pl.ds(time_of(c), chunk + 8), :]
        v = par_ref[CONV_B : CONV_B + 1, :] + par_ref[0:1, :] * wide[8:]
        for k in range(1, 4):
            v = v + par_ref[k : k + 1, :] * wide[8 - k : 8 - k + chunk]
        v = v.astype(BF16)
        v_ref[pl.ds(time_of(c), chunk), :] = v
        pre = dot(v, gates_ref[...]) + bias
        r, e, a, room, m = gate_values(pre, log_scale, width)
        put(a_s, pl.ds(time_of(c), chunk), a)
        put(b_s, pl.ds(time_of(c), chunk), m * e * v.astype(F32))
        return carry

    lax.fori_loop(0, chunks, first, 0)

    def load(g, i):
        at = pl.ds(i, SEGMENTS, stride=seg)
        return a_s[g, at, :], b_s[g, at, :]

    def store(g, i, state, total):
        at = pl.ds(i, SEGMENTS, stride=seg)
        b_s[g, at, :] = state
        a_s[g, at, :] = total

    groups = width // LANES
    start = (jnp.zeros((SEGMENTS, LANES), F32), jnp.ones((SEGMENTS, LANES), F32))
    ends = lax.fori_loop(
        0, seg, strided_scan(lambda k: k, groups, load, store), (start,) * groups, unroll=8
    )
    final = jnp.concatenate([e[0] for e in ends], axis=1)
    totals = jnp.concatenate([e[1] for e in ends], axis=1)
    carries = [jnp.zeros((1, width), F32)]
    for j in range(SEGMENTS - 1):
        carries.append(totals[j : j + 1] * carries[j] + final[j : j + 1])
    for j in range(SEGMENTS):
        per = seg // chunk

        def last(k, carry, j=j, per=per):
            c = j * per + k
            rows = pl.ds(time_of(c), chunk)
            h = take(b_s, rows) + take(a_s, rows) * carries[j]
            h_ref[rows, :] = h
            y = gelu_tanh(proj_ref[pl.ds(place(c), chunk), 0:width])
            z_ref[pl.ds(place(c), chunk), :] = (h.astype(BF16).astype(F32) * y).astype(BF16)
            return carry

        lax.fori_loop(0, per, last, 0)


def forward_kernel(
    outer,
    inner,
    shards,
    quarters,
    chunk,
    x_ref,
    gain1_ref,
    gain2_ref,
    taps_ref,
    conv_b_ref,
    rate_b_ref,
    entry_b_ref,
    decay_ref,
    rate_ref,
    entry_ref,
    cot_ref,
    wi_ref,
    wo_ref,
    par_ref,
    mid_ref,
    z_out,
    h_out,
    v_out,
    proj_out,
    gates_out,
    n1_out,
    wi_out,
    wo_out,
    n2_out,
    cot_out,
    own_s,
    n1_s,
    wi_s,
    wo_s,
    gates_s,
    u_pad,
    a_s,
    b_s,
    z_ref,
    h_ref,
    v_ref,
    proj_ref,
    gates_ref,
    p_s,
    cot_s,
    x_in,
    up_in,
    down_in,
    line_out,
    g_across,
    g_up,
    g_down,
    w_far,
    w_near,
    across,
    up,
    down,
    far,
    near,
    c_side,
    c_far,
    c_near,
    local,
    s_up_in,
    s_down_in,
    s_sums,
    s_in,
    s_up,
    s_down,
    s_across,
    g_side_up,
    g_side_down,
):
    at = Place(outer, inner, shards)
    parts, rows = at.parts, x_ref.shape[0]
    steps = list(range(1, at.ys))
    width2 = wi_ref.shape[1]
    width, depth, cols = width2 // 2, wi_ref.shape[0], wo_ref.shape[1]

    def normalize(some):
        x = x_ref[some, :].astype(F32)
        own_s[some, :] = (x * row_rms(x) * gain1_ref[...]).astype(BF16)

    add_rows(rows, normalize)
    greet_with_line(at, [at.sibling] + [at.near(q)[0] for q in range(1, at.chips)])
    weights = ((wi_ref, wi_s), (wo_ref, wo_s))
    keep = [
        pltpu.make_async_copy(own_s, n1_s.at[at.s], local.at[0]),
        pltpu.make_async_copy(wi_ref, wi_s.at[at.h], local.at[1]),
        pltpu.make_async_copy(wo_ref, wo_s.at[at.h], local.at[2]),
    ]
    for copy in keep:
        copy.start()
    send = Sent()

    def send_weights():
        for n, (src, dst) in enumerate(weights):
            for dy in steps:
                send(src, dst.at[at.h], w_far, (n, dy), (at.s, at.along(dy)))
            send(src, dst.at[at.h], w_near, (n, 0), at.sibling)

    send_weights()
    def build_gates():
        channels = decay_ref.shape[0]
        par_ref[...] = jnp.zeros(par_ref.shape, F32)
        par_ref[0:4, :channels] = taps_ref[...].astype(F32)
        for row, src in (
            (CONV_B, conv_b_ref),
            (RATE_B, rate_b_ref),
            (ENTRY_B, entry_b_ref),
            (DECAY, decay_ref),
        ):
            par_ref[row, :channels] = src[...]
        gates_s[...] = jnp.zeros(gates_s.shape, F32)
        block_width, blocks = rate_ref.shape[0], rate_ref.shape[1]
        for gate, src in enumerate((rate_ref, entry_ref)):
            for j in range(blocks):
                top, lane = j * block_width, gate * width + j * block_width
                gates_s[top : top + block_width, lane : lane + block_width] = src[:, j, :].astype(F32)
        gates_ref[...] = gates_s[...].astype(BF16)

    def project(d):
        total = None
        for k in range(shards):
            lanes = slice(k * depth, (k + 1) * depth)
            pair = jnp.concatenate([n1_s[d * inner + i, :, lanes] for i in range(inner)], axis=0)
            term = dot(pair, wi_s[k])
            total = term if total is None else total + term
        proj_ref[d * inner * rows : (d + 1) * inner * rows, :] = total

    def gather(o0):
        forward = Sent()

        def between(k):
            if k == 0:
                build_gates()
            if k != outer - 1:
                return
            for n, (src, dst) in enumerate(weights):
                for dy in steps:
                    source = at.along(-dy)
                    received(src, dst.at[source], w_far, (n, dy), (at.s, source))
                    forward(dst.at[source], dst.at[source], w_near, (n, dy), at.sibling)
            for n, (src, dst) in enumerate(weights):
                for dy in range(at.ys):
                    received(src, dst.at[at.along(-dy, 1)], w_near, (n, dy), at.sibling)
            for copy in keep:
                copy.wait()

        def each(row):
            project(row)

        side = (g_side_up, g_side_down)
        line_gather(at, o0, own_s, n1_s, g_across, g_up, g_down, between, each, side, SLIM)
        forward.finish()

    at.branches(gather)
    send(cot_ref, cot_s, c_side, (), at.beside)
    keep = [
        pltpu.make_async_copy(n1_s, n1_out, local.at[0]),
        pltpu.make_async_copy(wi_s, wi_out, local.at[1]),
        pltpu.make_async_copy(wo_s, wo_out, local.at[2]),
    ]
    for copy in keep:
        copy.start()
    run_scan(
        parts, quarters, chunk, proj_ref, par_ref, gates_ref, z_ref, h_ref, v_ref, u_pad, a_s, b_s
    )
    made = (
        (z_ref, z_out),
        (h_ref, h_out),
        (v_ref, v_out),
        (proj_ref, proj_out),
        (gates_ref, gates_out),
    )
    for n, (src, dst) in enumerate(made):
        keep.append(pltpu.make_async_copy(src, dst, local.at[6 + n]))
        keep[-1].start()
    side = (s_up_in, s_down_in, s_sums, s_in, s_up, s_down, s_across)
    line = LineSum(at, p_s, (x_in, up_in, down_in, line_out), (across, up, down), side)

    def back_project(n, carry):
        d = at.far_first(n)
        some = pl.ds(pl.multiple_of(d * inner * rows, inner * rows), inner * rows)
        for k in range(shards):
            p_s[d, :, k * cols : (k + 1) * cols] = dot(z_ref[some, :], wo_s[k]).astype(BF16)
        line.start(d)
        return carry

    lax.fori_loop(0, outer, back_project, 0)
    received(cot_ref, cot_s, c_side, (), at.beside)

    def slot(side, dy, other=0):
        i = 1 - at.i if side else at.i
        return cot_out.at[i * shards + at.along(dy, other)]

    mine = (cot_ref, cot_s)
    for side in range(2):
        keep.append(pltpu.make_async_copy(mine[side], slot(side, 0), local.at[3 + side]))
        keep[-1].start()
        for dy in steps:
            send(mine[side], slot(side, 0), c_far, (side, dy), (at.s, at.along(dy)))
        send(mine[side], slot(side, 0), c_near, (side, 0), at.sibling)

    def last_add(some, total):
        mid = x_ref[some, :].astype(F32) + total
        mid_ref[some, :] = mid
        own_s[some, :] = (mid * row_rms(mid) * gain2_ref[...]).astype(BF16)

    def branch(o0):
        forward = Sent()

        def between(n):
            if n != outer - 2:
                return
            for side in range(2):
                for dy in steps:
                    here = slot(side, -dy)
                    received(cot_ref, here, c_far, (side, dy), (at.s, at.along(-dy)))
                    forward(here, here, c_near, (side, dy), at.sibling)

        line.steps(o0, last_add, between)
        forward.finish()

    at.branches(branch)
    _, me = at.near(0)
    keep.append(pltpu.make_async_copy(own_s, n2_out.at[me], local.at[5]))
    keep[-1].start()
    quad = inner == 2 and at.ys == 2
    for q in (1, 2) if quad else reversed(range(1, at.chips)):
        send(own_s, n2_out.at[me], far, (q,), at.near(q)[0])
    send(own_s, n2_out.at[me], near, (0,), at.sibling)
    for q in (1, 2) if quad else range(1, at.chips):
        source, there = at.near(q, back=True)
        here = n2_out.at[there]
        received(own_s, here, far, (q,), source)
        if quad:
            half = here.at[pl.ds((2 - q) * (rows // 2), rows // 2)]
            send(half, half, far, (3 if q == 2 else 0,), at.near(3 - q)[0])
        send(here, here, near, (q,), at.sibling)
    if quad:
        here = n2_out.at[at.near(3)[1]]
        for q in (1, 2):
            half = here.at[pl.ds((q - 1) * (rows // 2), rows // 2)]
            received(half, half, far, (3 if q == 1 else 0,), at.near(q)[0])
        send(here, here, near, (3,), at.sibling)
    for q in range(at.chips):
        received(own_s, n2_out.at[at.near(q, 1, True)[1]], near, (q,), at.sibling)
    for side in range(2):
        for dy in range(at.ys):
            received(cot_ref, slot(side, -dy, 1), c_near, (side, dy), at.sibling)
    send.finish()
    for copy in keep:
        copy.wait()


def forward(
    x,
    gain1,
    gain2,
    channel,
    rate,
    entry,
    cot,
    w_in,
    w_out,
    quarters,
    chunk,
    outer,
    inner,
    shards,
    collective,
):
    rows, cols = x.shape
    parts, ys, chips = outer * inner, shards // 2, inner * shards // 2
    length, width = parts * rows, w_in.shape[1] // 2
    bufs, sems = line_sum_scratch(outer, rows, cols, 2 * HALVES)
    side_vmem, side_sems = slim_scratch(outer, cols)
    plane = jax.ShapeDtypeStruct((inner * shards, rows, cols), BF16)
    lanes = pltpu.VMEM((width // LANES, length, LANES), F32)
    made = (
        ((length, width), BF16),
        ((length, width), F32),
        ((length, width), BF16),
        ((length, 2 * width), F32),
        ((width, 2 * width), BF16),
    )
    return pl.pallas_call(
        functools.partial(forward_kernel, outer, inner, shards, quarters, chunk),
        out_shape=(
            jax.ShapeDtypeStruct((8, width), F32),
            jax.ShapeDtypeStruct((rows, cols), F32),
            *[jax.ShapeDtypeStruct(shape, dtype) for shape, dtype in made],
            jax.ShapeDtypeStruct((parts, rows, cols), BF16),
            jax.ShapeDtypeStruct((shards,) + w_in.shape, BF16),
            jax.ShapeDtypeStruct((shards,) + w_out.shape, BF16),
            plane,
            plane,
        ),
        in_specs=[IN_VMEM] * 11 + [IN_HBM] * 2,
        out_specs=[IN_VMEM] * 2 + [IN_HBM] * 10,
        scratch_shapes=[
            pltpu.VMEM((rows, cols), BF16),
            pltpu.VMEM((parts, rows, cols), BF16),
            pltpu.VMEM((shards,) + w_in.shape, BF16),
            pltpu.VMEM((shards,) + w_out.shape, BF16),
            pltpu.VMEM((width, 2 * width), F32),
            pltpu.VMEM((length + 8, width), F32),
            lanes,
            lanes,
            *[pltpu.VMEM(shape, dtype) for shape, dtype in made],
            pltpu.VMEM((outer, inner * rows, cols), BF16),
            pltpu.VMEM((rows, cols), BF16),
        ]
        + bufs
        + [DMA((2, outer, 2 * HALVES))] * 3
        + [DMA((2, 2, ys))] * 2
        + sems
        + [DMA((2, chips))] * 2
        + [DMA((2,))]
        + [DMA((2, 2, ys))] * 2
        + [DMA((11,))]
        + side_vmem
        + side_sems
        + [DMA((2, outer))] * 2,
        compiler_params=pltpu.CompilerParams(
            collective_id=collective, has_side_effects=True, vmem_limit_bytes=60 * 2**20
        ),
        cost_estimate=cost(140),
        name="forward",
    )(x, gain1, gain2, *channel, rate, entry, cot, w_in, w_out)


class PlaneSum:
    def __init__(self, at, n, p, near_in, far_in, far_out, near, far):
        self.at, self.n, self.p = at, n, p
        self.near_in, self.far_in, self.far_out = near_in, far_in, far_out
        self.near, self.far = near, far
        self.rows = near_in.shape[2]

    def block(self, q, other):
        i, y = self.at.chip(q)
        core = lax.rem(self.at.core + other, 2)
        rows = pl.ds(pl.multiple_of(core * self.rows, self.rows), self.rows)
        return self.p.at[i * self.at.ys + y, rows]

    def to_sibling(self, q):
        n = self.n
        return remote(
            self.block(q, 1),
            self.near_in.at[n, q],
            self.near.at[0, n, q],
            self.near.at[1, n, q],
            self.at.sibling,
        )

    def onward(self, q, back=False):
        n = self.n
        return remote(
            self.far_out.at[n, q],
            self.far_in.at[n, q],
            self.far.at[0, n, q],
            self.far.at[1, n, q],
            self.at.near(q, 0, back)[0],
        )

    def combine_one(self, k, own=None):
        q = self.at.chips - 1 - k
        self.to_sibling(q).wait_recv()
        mine = self.block(q, 0) if own is None else own.at[q]

        def add(rows):
            total = mine[rows, :].astype(F32) + self.near_in[self.n, q, rows, :].astype(F32)
            self.far_out[self.n, q, rows, :] = total.astype(BF16)

        add_rows(self.rows, add)
        self.onward(q).start()

    def combine(self, own=None):
        def one(k, carry):
            self.combine_one(k, own)
            return carry

        lax.fori_loop(0, self.at.chips - 1, one, 0)
        self.to_sibling(0).wait_recv()

    def total(self, rows, own=None):
        n = self.n
        mine = self.block(0, 0) if own is None else own.at[0]
        value = mine[rows, :].astype(F32) + self.near_in[n, 0, rows, :].astype(F32)
        for q in range(1, self.at.chips):
            value = value + self.far_in[n, q, rows, :].astype(F32)
        return value

    def arrive(self):
        for q in range(1, self.at.chips):
            self.onward(q, True).wait_recv()

    def finish(self):
        for q in range(self.at.chips):
            self.to_sibling(q).wait_send()
        for q in range(1, self.at.chips):
            self.onward(q).wait_send()


def turn_kernel(
    outer,
    inner,
    shards,
    dgm_from,
    dum_from,
    mm_from,
    mid_from,
    cot_from,
    gain_ref,
    wg_ref,
    wu_ref,
    wd_ref,
    n2_ref,
    cots_ref,
    dmid_ref,
    gain_grad_ref,
    dout_ref,
    q_ref,
    down_ref,
    gate_ref,
    rest_ref,
    up_ref,
    mm_ref,
    dgm_ref,
    dum_ref,
    mid_ref,
    cot_ref,
    early_sem,
    p_s,
    q_s,
    dout_s,
    gain_s,
    wg_s,
    wu_s,
    wd_s,
    n2_s,
    cots_s,
    u_s,
    r_s,
    near_in,
    far_in,
    far_out,
    down_own,
    down_land,
    gate_own,
    gate_land,
    near,
    far,
    across,
    up,
    low,
    down_up,
    down_low,
    gate_up,
    gate_low,
    local,
    q_sem,
    u_sem,
    r_sem,
):
    at = Place(outer, inner, shards)
    model, hidden = wg_s.shape
    tile = min(512, model)
    pair = p_s.shape[1]
    span = model // outer
    own = pl.ds(pl.multiple_of(at.i * hidden, hidden), hidden)
    first = load_all([(mm_from, mm_ref)], early_sem)
    load = [
        pltpu.make_async_copy(cots_ref, cots_s, local.at[1]),
        pltpu.make_async_copy(wg_ref.at[:, own], wg_s, local.at[2]),
        pltpu.make_async_copy(wu_ref.at[:, own], wu_s, local.at[3]),
        pltpu.make_async_copy(n2_ref, n2_s, local.at[4]),
        pltpu.make_async_copy(wd_ref.at[own, :], wd_s, local.at[5]),
    ]
    for copy in load[:3]:
        copy.start()
    second = load_all([(dgm_from, dgm_ref), (dum_from, dum_ref)], early_sem.at[pl.ds(1, 2)])
    for copy in load[3:]:
        copy.start()
    third = load_all([(mid_from, mid_ref), (cot_from, cot_ref)], early_sem.at[pl.ds(3, 2)])
    greet_with_line(at, [at.sibling] + [at.near(q)[0] for q in range(1, at.chips)])
    grad = PlaneSum(at, 0, p_s, near_in, far_in, far_out, near, far)
    down = LineReduce(at, down_own, down_land, down_up, down_low)
    gate = LineReduce(at, gate_own, gate_land, gate_up, gate_low)

    def columns(d):
        return pl.ds(pl.multiple_of(d * span, span), span)

    load[0].wait()
    first[0].wait()

    def down_grad(n, carry):
        d = at.far_first(n)
        down_own[d] = dot(cots_s[:, columns(d)], mm_ref[...], ((0,), (0,))).astype(BF16)
        down.early(n, d, outer - 2)
        return carry

    down_grad(0, 0)
    for copy in load[1:3] + second:
        copy.wait()

    def back(k, carry):
        q = at.chips - 1 - k
        i, y = at.chip(q)
        c = i * at.ys + y
        rows = pl.ds(pl.multiple_of(c * pair, pair), pair)
        for lane in range(0, model, tile):
            lanes = slice(lane, lane + tile)
            block = dot(dgm_ref[rows, :], wg_s[lanes, :], ((1,), (1,)))
            block = block + dot(dum_ref[rows, :], wu_s[lanes, :], ((1,), (1,)))
            p_s[c, :, lanes] = block.astype(BF16)
        grad.to_sibling(q).start()
        pl.when(k > 0)(lambda: grad.combine_one(k - 1))
        return carry

    lax.fori_loop(0, at.chips, back, 0)
    grad.to_sibling(0).wait_recv()
    lax.fori_loop(1, outer, down_grad, 0)
    def first_down(o0):
        if 0 < o0 < outer - 1:
            down.step(o0, 0)

    at.branches(first_down)
    load[3].wait()
    cut = gate_own.shape[2]

    def keep_r(n):
        slot = lax.rem(n, 2)
        there = rest_ref.at[at.far_first(n), :, : hidden - cut]
        return pltpu.make_async_copy(r_s.at[slot], there, r_sem.at[slot])

    def gate_grad(n, carry):
        d = at.far_first(n)
        pl.when(n >= 2)(lambda: keep_r(n - 2).wait())
        block = dot(n2_s[:, columns(d)], dgm_ref[...], ((0,), (0,))).astype(BF16)
        gate_own[d] = block[:, :cut]
        r_s[lax.rem(n, 2)] = block[:, cut:]
        keep_r(n).start()
        return carry

    lax.fori_loop(0, outer, gate_grad, 0)
    for n in range(max(outer - 2, 0), outer):
        keep_r(n).wait()

    load[4].wait()

    def keep_q(c):
        slot = lax.rem(c, 2)
        return pltpu.make_async_copy(q_s.at[slot], q_ref.at[c], q_sem.at[slot])

    def ahead(c, carry):
        rows = pl.ds(pl.multiple_of(c * pair, pair), pair)
        pl.when(c >= 2)(lambda: keep_q(c - 2).wait())
        for lane in range(0, model, tile):
            lanes = slice(lane, lane + tile)
            q_s[lax.rem(c, 2), :, lanes] = dot(mm_ref[rows, :], wd_s[:, lanes]).astype(BF16)
        keep_q(c).start()
        return carry

    gain_s[...] = jnp.zeros(gain_s.shape, F32)
    for copy in third:
        copy.wait()
    grad.arrive()

    def norm_back(rows):
        dn2 = grad.total(rows)
        mid = mid_ref[rows, :]
        scale = row_rms(mid)
        gain_s[...] += dn2 * mid * scale
        dmid = cot_ref[rows, :].astype(F32) + rms_back(mid, scale, gain_ref[...], dn2)
        dmid_ref[rows, :] = dmid
        dout_s[rows, :] = dmid.astype(BF16)

    add_rows(dout_s.shape[0], norm_back)
    gain_grad_ref[...] = jnp.sum(gain_s[...], axis=0, keepdims=True)
    keep = pltpu.make_async_copy(dout_s, dout_ref.at[at.s], local.at[0])
    keep.start()

    head = u_s.shape[2] - up_ref.shape[2]

    class keep_u:
        def __init__(self, n):
            slot, d = lax.rem(n, 2), at.far_first(n)
            block = u_s.at[slot]
            self.copies = (
                pltpu.make_async_copy(
                    block.at[:, :head], rest_ref.at[d, :, hidden - cut :], u_sem.at[0, slot]
                ),
                pltpu.make_async_copy(block.at[:, head:], up_ref.at[d], u_sem.at[1, slot]),
            )

        def start(self):
            for copy in self.copies:
                copy.start()

        def wait(self):
            for copy in self.copies:
                copy.wait()

    def up_grad(n, carry):
        pl.when(n >= 2)(lambda: keep_u(n - 2).wait())
        u_s[lax.rem(n, 2)] = dot(
            n2_s[:, columns(at.far_first(n))], dum_ref[...], ((0,), (0,))
        ).astype(BF16)
        keep_u(n).start()
        return carry

    def branch(o0):
        ends = o0 in (0, outer - 1)

        def between(k):
            if k == 0:
                if ends:
                    down.push(o0, down.order(o0)[outer - 2])
                    for d in gate.order(o0)[:-1]:
                        gate.push(o0, d)
                lax.fori_loop(0, at.chips, ahead, 0)
            if k == 1:
                if not ends:
                    for n in range(1, outer - 1):
                        down.step(o0, n)
                lax.fori_loop(0, outer, up_grad, 0)
            if k == outer - 1:
                down.absorb(o0, o0)
            if k == outer and not ends:
                for n in range(outer - 1):
                    gate.step(o0, n)

        line_gather(at, o0, dout_s, dout_ref, across, up, low, between)
        gate.absorb(o0, o0)
        down.finish(o0)
        gate.finish(o0)

    at.branches(branch)
    last = [
        pltpu.make_async_copy(down_own.at[at.o], down_ref, local.at[1]),
        pltpu.make_async_copy(gate_own.at[at.o], gate_ref, local.at[2]),
    ]
    for copy in last:
        copy.start()
    for n in range(max(outer - 2, 0), outer):
        keep_u(n).wait()
    for c in range(max(at.chips - 2, 0), at.chips):
        keep_q(c).wait()
    grad.finish()
    keep.wait()
    for copy in last:
        copy.wait()


def turn(
    dgm, dum, mm, mid, cot, gain, wg, wu, wd, n2, cots, outer, inner, shards, collective
):
    rows, cols = mid.shape
    tokens, hidden = dgm.shape
    chips, span = inner * shards // 2, cols // outer
    buffers = pltpu.VMEM((1, chips, rows, cols), BF16)
    cut = first_half(hidden)
    down_vmem, reduce_sems = line_reduce_scratch(outer, span, hidden)
    gate_vmem, _ = line_reduce_scratch(outer, span, cut)
    return pl.pallas_call(
        functools.partial(turn_kernel, outer, inner, shards),
        out_shape=(
            jax.ShapeDtypeStruct((rows, cols), F32),
            jax.ShapeDtypeStruct((1, cols), F32),
            jax.ShapeDtypeStruct((outer * inner, rows, cols), BF16),
            jax.ShapeDtypeStruct((chips, 2 * rows, cols), BF16),
            jax.ShapeDtypeStruct((span, hidden), BF16),
            jax.ShapeDtypeStruct((span, cut), BF16),
            jax.ShapeDtypeStruct((outer, span, hidden - cut + LANES), BF16),
            jax.ShapeDtypeStruct((outer, span, hidden - LANES), BF16),
        ),
        in_specs=[IN_HBM] * 5 + [IN_VMEM] + [IN_HBM] * 5,
        out_specs=[IN_VMEM] * 2 + [IN_HBM] * 6,
        scratch_shapes=[
            pltpu.VMEM((tokens, hidden), BF16),
            pltpu.VMEM((tokens, hidden), BF16),
            pltpu.VMEM((tokens, hidden), BF16),
            pltpu.VMEM((rows, cols), F32),
            pltpu.VMEM((rows, cols), BF16),
            DMA((5,)),
            pltpu.VMEM((chips, 2 * rows, cols), BF16),
            pltpu.VMEM((2, 2 * rows, cols), BF16),
            pltpu.VMEM((rows, cols), BF16),
            pltpu.VMEM((16, cols), F32),
            pltpu.VMEM((cols, hidden), BF16),
            pltpu.VMEM((cols, hidden), BF16),
            pltpu.VMEM((hidden, cols), BF16),
            pltpu.VMEM((tokens, cols), BF16),
            pltpu.VMEM((tokens, cols), BF16),
            pltpu.VMEM((2, span, hidden), BF16),
            pltpu.VMEM((2, span, hidden - cut), BF16),
        ]
        + [buffers] * 3
        + down_vmem
        + gate_vmem
        + [DMA((2, 1, chips))] * 2
        + [DMA((2, outer, HALVES))] * 3
        + reduce_sems * 2
        + [DMA((6,)), DMA((2,)), DMA((2, 2)), DMA((2,))],
        compiler_params=pltpu.CompilerParams(
            collective_id=collective, has_side_effects=True, vmem_limit_bytes=60 * 2**20
        ),
        cost_estimate=cost(110),
        name="turn",
    )(dgm, dum, mm, mid, cot, gain, wg, wu, wd, n2, cots)


def scan_backward_kernel(
    outer,
    inner,
    shards,
    quarters,
    chunk,
    blocks,
    block_width,
    dout_ref,
    wo_from,
    proj_from,
    h_from,
    v_from,
    mid_from,
    par_ref,
    gates_ref,
    q_ref,
    rest_ref,
    both_ref,
    blocks_ref,
    totals_ref,
    result_ref,
    rest_out,
    wo_ref,
    proj_ref,
    h_ref,
    v_ref,
    mid_ref,
    early_sem,
    q_s,
    near_in,
    far_in,
    far_out,
    rest_own,
    rest_land,
    near,
    far,
    q_sem,
    r_up,
    r_low,
    r_sem,
    dout_s,
    dz_s,
    sems,
    sums_ref,
    gate_grad_ref,
    a_s,
    g_s,
    t_s,
    h_pad,
    pre_s,
    dpre_s,
    dv_s,
    u_pad,
):
    length, width = h_ref.shape
    seg = length // SEGMENTS
    chunks = length // chunk

    def place(c):
        q = c // parts
        s = c - q * parts
        return pl.multiple_of((s * quarters + q) * chunk, chunk)

    def time_of(c):
        return pl.multiple_of(c * chunk, chunk)

    at = Place(outer, inner, shards)
    parts = at.parts
    rest = LineReduce(at, rest_own, rest_land, r_up, r_low)
    fetch = pltpu.make_async_copy(rest_ref, rest_own, r_sem)
    fetch.start()
    greet_with_line(at, [at.sibling] + [at.near(q)[0] for q in range(1, at.chips)])
    fetch.wait()

    def rest_early(o0):
        if o0 in (0, outer - 1):
            for d in rest.order(o0)[:-1]:
                rest.push(o0, d)

    def rest_step(n, o0):
        if 0 < o0 < outer - 1:
            rest.step(o0, n)

    def rest_last(o0):
        rest.absorb(o0, o0)
        rest.finish(o0)

    at.branches(rest_early)
    value = PlaneSum(at, 0, q_ref, near_in, far_in, far_out, near, far)

    def keep(q):
        return pltpu.make_async_copy(value.block(q, 0), q_s.at[q], q_sem.at[q])

    for q in reversed(range(at.chips)):
        value.to_sibling(q).start()
        keep(q).start()
    early = load_all([(wo_from, wo_ref)], early_sem)
    span = quarters * chunk

    def load(p):
        return pltpu.make_async_copy(
            dout_ref.at[p], dout_s.at[pl.ds(pl.multiple_of(p * span, span), span)], sems.at[p]
        )

    for p in range(parts):
        load(p).start()
    later = load_all(
        [(proj_from, proj_ref), (h_from, h_ref), (v_from, v_ref), (mid_from, mid_ref)],
        early_sem.at[pl.ds(1, 4)],
    )
    early[0].wait()

    def back_project(k, carry):
        load(2 * k).wait()
        load(2 * k + 1).wait()
        some = pl.ds(pl.multiple_of(k * 2 * span, 2 * span), 2 * span)
        depth = wo_ref.shape[2]
        total = dot(dout_s[some, 0:depth], wo_ref[0], ((1,), (1,)))
        for p in range(1, wo_ref.shape[0]):
            lanes = slice(p * depth, (p + 1) * depth)
            total = total + dot(dout_s[some, lanes], wo_ref[p], ((1,), (1,)))
        dz_s[some, :] = total
        return carry

    lax.fori_loop(0, parts // 2, back_project, 0)
    for q in range(at.chips):
        keep(q).wait()
    value.combine(q_s)
    for copy in later:
        copy.wait()
    log_scale = -DECAY_SCALE * softplus(-par_ref[DECAY : DECAY + 1, :])
    bias = jnp.concatenate(
        [par_ref[RATE_B : RATE_B + 1, :], par_ref[ENTRY_B : ENTRY_B + 1, :]], axis=1
    )
    zeros8 = jnp.zeros((8, width), F32)
    put(a_s, pl.ds(length, 8), zeros8)
    h_pad[0:8, :] = zeros8
    u_pad[0:8, :] = zeros8
    dv_s[pl.ds(length, 8), :] = zeros8

    def first(c, carry):
        rows = pl.ds(time_of(c), chunk)
        later = pl.ds(pl.multiple_of(time_of(c) + 8, 8), chunk)
        there = pl.ds(place(c), chunk)
        h = h_ref[rows, :]
        h_pad[later, :] = h
        u_pad[later, :] = proj_ref[there, width : 2 * width].astype(BF16).astype(F32)
        y, slope = gelu_and_slope(proj_ref[there, 0:width])
        dz = dz_s[there, :]
        put(g_s, rows, (dz * y).astype(BF16).astype(F32))
        both_ref[there, 0:width] = (dz * h.astype(BF16).astype(F32) * slope).astype(BF16)
        pre = dot(v_ref[rows, :], gates_ref[...]) + bias
        pre_s[rows, :] = pre
        put(a_s, rows, jnp.exp(sigmoid(pre[:, :width]) * log_scale))
        return carry

    lax.fori_loop(0, chunks, first, 0)

    def load(g, i):
        return (
            a_s[g, pl.ds(i + 1, SEGMENTS, stride=seg), :],
            g_s[g, pl.ds(i, SEGMENTS, stride=seg), :],
        )

    def store(g, i, state, total):
        g_s[g, pl.ds(i, SEGMENTS, stride=seg), :] = state
        t_s[g, pl.ds(i, SEGMENTS, stride=seg), :] = total

    groups = width // LANES
    start = (jnp.zeros((SEGMENTS, LANES), F32), jnp.ones((SEGMENTS, LANES), F32))
    ends = lax.fori_loop(
        0,
        seg,
        strided_scan(lambda k: seg - 1 - k, groups, load, store),
        (start,) * groups,
        unroll=8,
    )
    firsts = jnp.concatenate([e[0] for e in ends], axis=1)
    totals = jnp.concatenate([e[1] for e in ends], axis=1)
    carries = [None] * SEGMENTS
    carries[SEGMENTS - 1] = jnp.zeros((1, width), F32)
    for j in range(SEGMENTS - 2, -1, -1):
        carries[j] = totals[j + 1 : j + 2] * carries[j + 1] + firsts[j + 1 : j + 2]

    def fold(values):
        return jnp.sum(values.reshape(chunk // 8, 8, values.shape[1]), axis=0)

    sums_ref[...] = jnp.zeros(sums_ref.shape, F32)

    for j in range(SEGMENTS):
        per = seg // chunk

        def middle(k, carry, j=j, per=per):
            c = j * per + k
            rows = pl.ds(time_of(c), chunk)
            g = take(g_s, rows) + take(t_s, rows) * carries[j]
            before = h_pad[pl.ds(time_of(c), chunk + 8), :][7 : 7 + chunk]
            v = v_ref[rows, :].astype(F32)
            r, e, a, room, m = gate_values(pre_s[rows, :], log_scale, width)
            gv = g * v
            held = jnp.where(room > MULT_FLOOR, gv * e * a / m, 0.0)
            ta = (g * before - held) * a * r
            drpre = (ta * (log_scale * (1.0 - r))).astype(BF16)
            depre = (gv * m * e * (1.0 - e)).astype(BF16)
            dpre_s[rows, 0:width] = drpre
            dpre_s[rows, width : 2 * width] = depre
            sums_ref[0:8, :] += fold(ta)
            sums_ref[8:16, :] += fold(drpre.astype(F32))
            sums_ref[16:24, :] += fold(depre.astype(F32))
            dv = g * m * e + dot(dpre_s[rows, :], gates_ref[...], ((1,), (1,)))
            dv_s[rows, :] = dv
            sums_ref[24:32, :] += fold(dv)
            wide = u_pad[pl.ds(time_of(c), chunk + 8), :]
            for tap in range(4):
                top = 32 + 8 * tap
                sums_ref[top : top + 8, :] += fold(dv * wide[8 - tap : 8 - tap + chunk])
            return carry

        lax.fori_loop(0, per, middle, 0)
        if j == 2:
            at.branches(functools.partial(rest_step, 0))
        if j == SEGMENTS - 2:
            at.branches(functools.partial(rest_step, 1))
    for n in range(2, outer - 1):
        at.branches(functools.partial(rest_step, n))
    sums_ref[0:8, :] = sums_ref[0:8, :] * (
        DECAY_SCALE * sigmoid(-par_ref[DECAY : DECAY + 1, :])
    )

    def last(c, carry):
        wide = dv_s[pl.ds(time_of(c), chunk + 8), :]
        du = par_ref[0:1, :] * wide[0:chunk]
        for tap in range(1, 4):
            du = du + par_ref[tap : tap + 1, :] * wide[tap : tap + chunk]
        both_ref[pl.ds(place(c), chunk), width : 2 * width] = du.astype(BF16)
        return carry

    lax.fori_loop(0, chunks, last, 0)
    gate_grad_ref[...] = dot(v_ref[...], dpre_s[...], ((0,), (0,)))
    blocks_ref[...] = jnp.zeros(blocks_ref.shape, F32)
    tall = blocks_ref.shape[0] // (2 * blocks)
    for gate in range(2):
        for j in range(blocks):
            top, lanes = (gate * blocks + j) * tall, gate * width + j * block_width
            rows = slice(j * block_width, (j + 1) * block_width)
            blocks_ref[top : top + block_width, :block_width] = gate_grad_ref[
                rows, lanes : lanes + block_width
            ]
    for k in range(8):
        totals_ref[k : k + 1, :] = jnp.sum(sums_ref[8 * k : 8 * k + 8, :], axis=0, keepdims=True)
    value.arrive()

    def output(rows):
        result_ref[rows, :] = (mid_ref[rows, :] + value.total(rows, q_s)).astype(BF16)

    add_rows(span, output)
    value.finish()
    at.branches(rest_last)
    out = pltpu.make_async_copy(rest_own.at[at.o], rest_out, r_sem)
    out.start()
    out.wait()


def scan_backward(
    quarters,
    chunk,
    blocks,
    block_width,
    dout,
    w_out,
    proj,
    h,
    v,
    params,
    gates,
    mid,
    q,
    rest,
    outer,
    inner,
    shards,
    collective,
):
    parts = dout.shape[0]
    rows, cols = mid.shape
    chips = q.shape[0]
    rest_vmem, rest_sems = line_reduce_scratch(*rest.shape)
    buffers = pltpu.VMEM((1, chips, rows, cols), BF16)
    length, width = h.shape
    tall, wide = -(-block_width // 8) * 8, -(-block_width // LANES) * LANES
    return pl.pallas_call(
        functools.partial(
            scan_backward_kernel, outer, inner, shards, quarters, chunk, blocks, block_width
        ),
        out_shape=(
            jax.ShapeDtypeStruct((length, 2 * width), BF16),
            jax.ShapeDtypeStruct((2 * blocks * tall, wide), F32),
            jax.ShapeDtypeStruct((8, width), F32),
            jax.ShapeDtypeStruct((rows, cols), BF16),
            jax.ShapeDtypeStruct(rest.shape[1:], BF16),
        ),
        in_specs=[IN_HBM] * 6 + [IN_VMEM] * 2 + [IN_HBM] * 2,
        out_specs=[IN_VMEM] * 4 + [IN_HBM],
        scratch_shapes=[
            *[pltpu.VMEM(x.shape, x.dtype) for x in (w_out, proj, h, v, mid)],
            DMA((5,)),
            pltpu.VMEM((chips, rows, cols), BF16),
            buffers,
            buffers,
            buffers,
            *rest_vmem,
            DMA((2, 1, chips)),
            DMA((2, 1, chips)),
            DMA((chips,)),
            *rest_sems,
            DMA,
            pltpu.VMEM((length, dout.shape[2]), BF16),
            pltpu.VMEM((length, width), F32),
            DMA((parts,)),
            pltpu.VMEM((64, width), F32),
            pltpu.VMEM((width, 2 * width), F32),
            pltpu.VMEM((width // LANES, length + 8, LANES), F32),
            pltpu.VMEM((width // LANES, length, LANES), F32),
            pltpu.VMEM((width // LANES, length, LANES), F32),
            pltpu.VMEM((length + 8, width), F32),
            pltpu.VMEM((length, 2 * width), F32),
            pltpu.VMEM((length, 2 * width), BF16),
            pltpu.VMEM((length + 8, width), F32),
            pltpu.VMEM((length + 8, width), F32),
        ],
        compiler_params=pltpu.CompilerParams(
            collective_id=collective, has_side_effects=True, vmem_limit_bytes=60 * 2**20
        ),
        cost_estimate=cost(21),
        name="scan_backward",
    )(dout, w_out, proj, h, v, mid, params, gates, q, rest)


def remote(src, dst, send, recv, to):
    return pltpu.make_async_remote_copy(
        src_ref=src, dst_ref=dst, send_sem=send, recv_sem=recv, device_id=to, device_id_type=MESH
    )


def add_rows(rows, fn, start=0):
    def one(k, carry):
        fn(pl.ds(pl.multiple_of(k * 16, 16), 16))
        return carry

    lax.fori_loop(start // 16, rows // 16, one, 0)


def load_all(pairs, sems):
    copies = [
        pltpu.make_async_copy(src, dst, sems.at[k]) for k, (src, dst) in enumerate(pairs)
    ]
    for copy in copies:
        copy.start()
    return copies


class PlaneExchange:
    def __init__(self, at, n, x, out, sems, local):
        self.at, self.n, self.x, self.out, self.sems, self.local = at, n, x, out, sems, local
        _, self.me = at.near(0)
        self.hops = [(q, c) for q in reversed(range(1, at.chips)) for c in range(2)] + [(0, 1)]

    def rows(self, slot):
        piece = self.out.shape[1]
        return self.x.at[pl.ds(pl.multiple_of(slot * piece, piece), piece)]

    def mine(self):
        return pltpu.make_async_copy(self.rows(self.me), self.out.at[self.me], self.local)

    def hop(self, k):
        to, slot = self.at.near(*self.hops[k])
        sems, n = self.sems, self.n
        return remote(
            self.rows(slot), self.out.at[self.me], sems.at[0, n, k], sems.at[1, n, k], to
        )

    def start(self):
        for k in range(len(self.hops)):
            self.hop(k).start()
        self.mine().start()

    def finish(self):
        for k, (q, other) in enumerate(self.hops):
            source, slot = self.at.near(q, other, True)
            received(self.rows(self.me), self.out.at[slot], self.sems, (self.n, k), source)
        for k in range(len(self.hops)):
            self.hop(k).wait_send()
        self.mine().wait()


def closing_kernel(
    outer,
    inner,
    shards,
    both_from,
    wi_from,
    z_from,
    x_from,
    dmid_from,
    gain_ref,
    gain2_ref,
    blocks_ref,
    sums_ref,
    n1_ref,
    dout_ref,
    down_ref,
    gate_ref,
    rest_ref,
    up_ref,
    grad_ref,
    mix_ref,
    blocks_out,
    sums_out,
    gains_out,
    down_out,
    gate_out,
    rest_out,
    up_out,
    both_ref,
    wi_ref,
    z_ref,
    x_ref,
    dmid_ref,
    early_sem,
    p_s,
    up_own,
    up_land,
    up_sum,
    n1_s,
    dout_s,
    g_s,
    gain_s,
    gain_rows,
    gain_slots,
    near_in,
    far_in,
    far_out,
    done,
    block_slots,
    sum_slots,
    x_in,
    up_in,
    down_in,
    line_out,
    across,
    up,
    low,
    near,
    far,
    final,
    s_far,
    s_near,
    swap,
    g_sem,
    stripe,
    u_up,
    u_low,
    local,
):
    at = Place(outer, inner, shards)
    s, h, parts, ys = at.s, at.h, at.parts, at.ys
    steps = list(range(1, ys))
    line = LineSum(at, p_s, (x_in, up_in, down_in, line_out), (across, up, low))
    model = x_ref.shape[1]
    tile = min(512, model)
    piece = done.shape[1]
    span = shards * piece
    width2 = both_ref.shape[1]
    me = s * shards + h
    small = ((blocks_ref, block_slots, blocks_out), (sums_ref, sum_slots, sums_out))
    fetch = pltpu.make_async_copy(up_ref, up_own, local.at[0])
    fetch.start()

    def stripes(k):
        lanes = pl.ds(pl.multiple_of(owner(k) * span, span), span)
        slot = lax.rem(k, 2)
        return (
            pltpu.make_async_copy(n1_ref.at[:, lanes], n1_s.at[slot], stripe.at[0, slot]),
            pltpu.make_async_copy(dout_ref.at[:, lanes], dout_s.at[slot], stripe.at[1, slot]),
        )

    def owner(k):
        return lax.rem(s + k + 1, parts)

    pairs = [(both_from, both_ref), (wi_from, wi_ref)]
    first = load_all(pairs, early_sem)
    for copy in stripes(0):
        copy.start()
    pairs = [(z_from, z_ref), (x_from, x_ref), (dmid_from, dmid_ref)]
    second = load_all(pairs, early_sem.at[pl.ds(2, 3)])

    def anyone(k):
        to = lax.rem(me + k, at.count)
        return (to // shards, lax.rem(to, shards)), to

    def greet_one(k, carry):
        hello(anyone(k)[0])
        return carry

    lax.fori_loop(1, at.count, greet_one, 0)
    welcome(at.count - 1)
    ups = LineReduce(at, up_own, up_land, u_up, u_low)
    fetch.wait()

    ups.early(0, at.far_first(0), min(1, outer - 2))

    for copy in first:
        copy.wait()

    def back(n, carry):
        d = at.far_first(n)
        rows = pl.ds(pl.multiple_of(d * p_s.shape[1], p_s.shape[1]), p_s.shape[1])
        for lane in range(0, model, tile):
            lanes = slice(lane, lane + tile)
            p_s[d, :, lanes] = dot(both_ref[rows, :], wi_ref[lanes, :], ((1,), (1,))).astype(BF16)
        line.start(d)
        return carry

    lax.fori_loop(0, outer, back, 0)
    send = Sent()
    for n, (src, slots, _) in enumerate(small):
        for dy in steps:
            send(src, slots.at[h], s_far, (n, dy), (s, at.along(dy)))
        send(src, slots.at[h], s_near, (n, 0), at.sibling)
        slots[h] = src[...]

    def mix_rows(p, shard):
        return g_s.at[p, pl.ds(pl.multiple_of(shard * piece, piece), piece)]

    def to_sibling(k, dy):
        p = owner(k)
        return remote(
            mix_rows(p, at.along(dy, 1)),
            near_in.at[dy, p],
            near.at[0, dy, k],
            near.at[1, dy, k],
            at.sibling,
        )

    def to_shard(k, dy, source=False):
        p = owner(k)
        return remote(
            far_out.at[dy - 1, p],
            far_in.at[dy - 1, p],
            far.at[0, dy, k],
            far.at[1, dy, k],
            (s, at.along(-dy if source else dy)),
        )

    def to_owner(k, source=False):
        p = lax.rem(s + parts - k - 1, parts) if source else owner(k)
        return remote(
            done.at[owner(k)],
            mix_ref.at[p if source else s],
            final.at[0, k],
            final.at[1, k],
            (p, h),
        )

    for copy in second:
        copy.wait()

    def weight_grads(k, carry):
        p, slot = owner(k), lax.rem(k, 2)
        for copy in stripes(k):
            copy.wait()

        @pl.when(k < parts - 1)
        def _():
            for copy in stripes(k + 1):
                copy.start()

        g_s[p, :, 0:width2] = dot(n1_s[slot], both_ref[...], ((0,), (0,))).astype(BF16)
        g_s[p, :, width2:] = dot(dout_s[slot], z_ref[...], ((0,), (0,))).astype(BF16)
        for dy in steps + [0]:
            to_sibling(k, dy).start()
        return carry

    lax.fori_loop(0, parts, weight_grads, 0)
    exchanges = [
        PlaneExchange(at, 0, down_ref, down_out, swap, local.at[2]),
        PlaneExchange(at, 1, gate_ref, gate_out, swap, local.at[3]),
        PlaneExchange(at, 3, rest_ref, rest_out, swap, local.at[5]),
    ]
    up_exchange = PlaneExchange(at, 2, up_sum, up_out, swap, local.at[1])

    def sibling_sums(k, carry):
        p = owner(k)
        for dy in steps:
            to_sibling(k, dy).wait_recv()
            mine = mix_rows(p, at.along(dy))

            def add(rows, dy=dy, mine=mine):
                total = mine[rows, :].astype(F32) + near_in[dy, p, rows, :].astype(F32)
                far_out[dy - 1, p, rows, :] = total.astype(BF16)

            add_rows(piece, add)
            to_shard(k, dy).start()
        return carry

    lax.fori_loop(0, parts, sibling_sums, 0)
    gain_s[...] = jnp.zeros(gain_s.shape, F32)

    def mix_step(k):
        p = owner(k)
        mine = mix_rows(p, h)
        to_sibling(k, 0).wait_recv()
        for dy in steps:
            to_shard(k, dy, True).wait_recv()

        def add(rows):
            total = mine[rows, :].astype(F32) + near_in[0, p, rows, :].astype(F32)
            for dy in steps:
                total = total + far_in[dy - 1, p, rows, :].astype(F32)
            done[p, rows, :] = total.astype(BF16)

        add_rows(piece, add)
        if k < parts - 1:
            to_owner(k).start()

    def last_add(rows, dn1):
        x = x_ref[rows, :].astype(F32)
        scale = row_rms(x)
        gain_s[...] += dn1 * x * scale
        grad_ref[rows, :] = dmid_ref[rows, :] + rms_back(x, scale, gain_ref[...], dn1)

    def finish_ups(o0):
        ups.absorb(o0, o0)

        def keep_up(rows):
            up_sum[rows, :] = up_own[at.o, rows, :]

        add_rows(up_sum.shape[0], keep_up)
        up_exchange.start()

    def branch(o0):
        ends = o0 in (0, outer - 1)

        sooner = min(1, outer - 2) if ends else 0

        def between(n):
            if n + sooner < outer - 1 and ends:
                ups.push(o0, ups.order(o0)[n + sooner])
            for k in range(n * inner, parts if n == outer - 2 else (n + 1) * inner):
                if n < outer - 1:
                    mix_step(k)
            if n + 1 < outer - 1 and not ends:
                ups.step(o0, n + 1)
            if n == outer - 2:
                for exchange in exchanges:
                    exchange.start()
                finish_ups(o0)

        if not ends:
            ups.step(o0, 0)
        line.steps(o0, last_add, between)

    at.branches(branch)
    keep = pltpu.make_async_copy(done.at[s], mix_ref.at[s], local.at[4])
    keep.start()
    gain1, gain2 = jnp.sum(gain_s[...], axis=0, keepdims=True), gain2_ref[...]
    spare = gain_rows.shape[2] - 2 * piece
    for k in range(at.count):
        lanes = slice(k * piece, (k + 1) * piece)
        parts_of = [gain1[:, lanes], gain2[:, lanes]]
        if spare:
            parts_of.append(jnp.zeros((1, spare), F32))
        gain_rows[k] = jnp.concatenate(parts_of, axis=1)

    def gain(k):
        to, row = anyone(k)
        return remote(gain_rows.at[row], gain_slots.at[k], g_sem.at[0, k], g_sem.at[1, k], to)

    def gain_start(k, carry):
        gain(k).start()
        return carry

    def gain_arrive(k, total):
        gain(k).wait_recv()
        return total + gain_slots[k]

    def gain_leave(k, carry):
        gain(k).wait_send()
        return carry

    lax.fori_loop(1, at.count, gain_start, 0)

    for n, (src, slots, out) in enumerate(small):
        for dy in steps:
            here = slots.at[at.along(-dy)]
            received(src, here, s_far, (n, dy), (s, at.along(-dy)))
            send(here, here, s_near, (n, dy), at.sibling)
    for n, (src, slots, out) in enumerate(small):
        for dy in range(ys):
            received(src, slots.at[at.along(-dy, 1)], s_near, (n, dy), at.sibling)

        def add(k, carry, slots=slots, out=out):
            rows = pl.ds(pl.multiple_of(k * 8, 8), 8)
            total = slots[0, rows, :]
            for j in range(1, shards):
                total = total + slots[j, rows, :]
            out[rows, :] = total
            return carry

        lax.fori_loop(0, src.shape[0] // 8, add, 0)
    gains_out[...] = lax.fori_loop(1, at.count, gain_arrive, gain_rows[me])
    for k in range(parts - 1):
        to_owner(k, True).wait_recv()
    for exchange in exchanges + [up_exchange]:
        exchange.finish()
    at.branches(ups.finish)
    for k in range(parts):
        for dy in range(ys):
            to_sibling(k, dy).wait_send()
        for dy in steps:
            to_shard(k, dy).wait_send()
        if k < parts - 1:
            to_owner(k).wait_send()
    lax.fori_loop(1, at.count, gain_leave, 0)
    send.finish()
    keep.wait()


def closing(
    both,
    w_in,
    z,
    x,
    dmid,
    gain,
    gain2,
    small,
    sums,
    n1,
    dout,
    down,
    gate,
    rest,
    ups,
    outer,
    inner,
    shards,
    collective,
):
    rows, cols = x.shape
    parts, ys, count = outer * inner, shards // 2, outer * inner * shards
    piece = cols // count
    width = z.shape[1]
    lanes = -(-2 * piece // LANES) * LANES
    bufs, sems = line_sum_scratch(outer, rows, cols)
    pieces = pltpu.VMEM((max(ys - 1, 1), parts, piece, 3 * width), BF16)
    stripes = pltpu.VMEM((2, parts * rows, cols // parts), BF16)
    span, hidden = ups.shape[1:]

    def swapped(array):
        shape = (inner * shards, span // (inner * shards), array.shape[-1])
        return jax.ShapeDtypeStruct(shape, BF16)

    reduce_vmem, reduce_sems = line_reduce_scratch(outer, span, hidden)
    return pl.pallas_call(
        functools.partial(closing_kernel, outer, inner, shards),
        out_shape=(
            jax.ShapeDtypeStruct((rows, cols), F32),
            jax.ShapeDtypeStruct((parts, piece, 3 * width), BF16),
            jax.ShapeDtypeStruct(small.shape, F32),
            jax.ShapeDtypeStruct(sums.shape, F32),
            jax.ShapeDtypeStruct((1, lanes), F32),
            *[swapped(array) for array in (down, gate, rest, ups)],
        ),
        in_specs=[IN_HBM] * 5 + [IN_VMEM] * 4 + [IN_HBM] * 6,
        out_specs=[IN_VMEM] * 5 + [IN_HBM] * 4,
        scratch_shapes=[
            *[pltpu.VMEM(value.shape, value.dtype) for value in (both, w_in, z, x, dmid)],
            DMA((5,)),
            pltpu.VMEM((outer, inner * rows, cols), BF16),
            *reduce_vmem,
            pltpu.VMEM((span, hidden), BF16),
            stripes,
            stripes,
            pltpu.VMEM((parts, shards * piece, 3 * width), BF16),
            pltpu.VMEM((16, cols), F32),
            pltpu.VMEM((count, 1, lanes), F32),
            pltpu.VMEM((count, 1, lanes), F32),
            pltpu.VMEM((ys, parts, piece, 3 * width), BF16),
            pieces,
            pieces,
            pltpu.VMEM((parts, piece, 3 * width), BF16),
            pltpu.VMEM((shards,) + small.shape, F32),
            pltpu.VMEM((shards,) + sums.shape, F32),
        ]
        + bufs
        + sems
        + [DMA((2, ys, parts))] * 2
        + [DMA((2, parts))]
        + [DMA((2, 2, ys))] * 2
        + [DMA((2, 4, inner * shards)), DMA((2, count)), DMA((2, 2))]
        + reduce_sems
        + [DMA((6,))],
        compiler_params=pltpu.CompilerParams(
            collective_id=collective, has_side_effects=True, vmem_limit_bytes=60 * 2**20
        ),
        cost_estimate=cost(80),
        name="closing",
    )(
        both,
        w_in,
        z,
        x,
        dmid,
        gain,
        gain2,
        small,
        sums,
        n1,
        dout,
        down,
        gate,
        rest,
        ups,
    )


def unpack_kernel(inner, channels, block_width, *refs):
    sources, targets = refs[:10], refs[10:27]
    held, made, in_sem, out_sem = refs[27:36], refs[36:42], refs[42], refs[43]
    gate_ref, rest_ref, up_ref, down_ref, mix_ref, blocks_ref, sums_ref = held[:7]
    fetch = [
        pltpu.make_async_copy(sources[k], held[k], in_sem.at[k]) for k in range(len(held))
    ]
    for copy in fetch[7:] + fetch[:7]:
        copy.start()
    store = []
    gains_ref = sources[9]
    rate, entry, taps, conv_b, rate_b, entry_b, decay, first_gain, second_gain = targets[8:]
    for k in range(2):
        fetch[7 + k].wait()
        copy = pltpu.make_async_copy(held[7 + k], targets[6 + k], out_sem.at[6 + k])
        copy.start()
        store.append(copy)
    fetch[0].wait()
    fetch[1].wait()
    gate, up, down = made[:3]
    slots, piece, hidden = down_ref.shape
    cut = gate_ref.shape[2]
    tail = hidden - cut
    head = hidden - up_ref.shape[2]
    shards = slots // inner
    parts, width = mix_ref.shape[0], mix_ref.shape[2] // 3
    places = [
        ((h * inner + i) * hidden, i * shards + h) for i in range(inner) for h in range(shards)
    ]

    def ship(k):
        copy = pltpu.make_async_copy(made[k], targets[k], out_sem.at[k])
        copy.start()
        store.append(copy)

    for first, slot in places:
        gate[:, first : first + cut] = gate_ref[slot].astype(F32)
        gate[:, first + cut : first + hidden] = rest_ref[slot][:, :tail].astype(F32)
    ship(0)
    fetch[2].wait()
    for first, slot in places:
        up[:, first : first + head] = rest_ref[slot][:, tail:].astype(F32)
        up[:, first + head : first + hidden] = up_ref[slot].astype(F32)
    ship(1)
    fetch[3].wait()
    for first, slot in places:
        down[:, first : first + hidden] = down_ref[slot].astype(F32)
    ship(2)
    fetch[4].wait()
    for k in range(3):
        lanes = slice(k * width, k * width + width)
        made[3 + k][...] = jnp.concatenate(
            [mix_ref[p][:, lanes].astype(F32)[:, :channels] for p in range(parts)], axis=1
        )
        ship(3 + k)
    fetch[5].wait()
    fetch[6].wait()
    blocks = rate.shape[1]
    tall = blocks_ref.shape[0] // (2 * blocks)
    for k, dst in enumerate((rate, entry)):
        for j in range(blocks):
            top = (k * blocks + j) * tall
            dst[:, j, :] = blocks_ref[top : top + block_width, :block_width]
    taps[...] = sums_ref[4:8, :channels]
    for row, dst in ((3, conv_b), (1, rate_b), (2, entry_b), (0, decay)):
        dst[...] = sums_ref[row, :channels]
    first_gain[...] = gains_ref[0, :piece]
    second_gain[...] = gains_ref[0, piece : 2 * piece]
    for copy in store:
        copy.wait()


def unpack(
    gate, rest, up, down, mix, small, sums, result, grad, gains, inner, channels, blocks, block_width
):
    slots, piece, hidden = down.shape
    across = jax.ShapeDtypeStruct((piece, slots * hidden), F32)
    wide = jax.ShapeDtypeStruct((piece, mix.shape[0] * channels), F32)
    square = jax.ShapeDtypeStruct((block_width, blocks, block_width), F32)
    vector = jax.ShapeDtypeStruct((channels,), F32)
    taps = jax.ShapeDtypeStruct((4, channels), F32)
    gain = jax.ShapeDtypeStruct((piece,), F32)
    held = (gate, rest, up, down, mix, small, sums, result, grad)
    made = (across,) * 3 + (wide,) * 3
    return pl.pallas_call(
        functools.partial(unpack_kernel, inner, channels, block_width),
        out_shape=made
        + tuple(jax.ShapeDtypeStruct(x.shape, x.dtype) for x in (result, grad))
        + (square,) * 2
        + (taps,)
        + (vector,) * 4
        + (gain,) * 2,
        in_specs=[IN_HBM] * 9 + [IN_VMEM],
        out_specs=[IN_HBM] * 8 + [IN_VMEM] * 9,
        scratch_shapes=[pltpu.VMEM(x.shape, x.dtype) for x in held + made]
        + [DMA((len(held),)), DMA((8,))],
        compiler_params=pltpu.CompilerParams(vmem_limit_bytes=60 * 2**20),
        cost_estimate=cost(5),
        name="unpack",
    )(*held, gains)


def body(
    tokens,
    first_gain,
    branch_weight,
    input_weight,
    conv_weight,
    conv_bias,
    rate_weight,
    rate_bias,
    entry_weight,
    entry_bias,
    decay_param,
    output_weight,
    second_gain,
    hidden_gate,
    hidden_up,
    hidden_down,
    cotangent,
):
    quarters, _, chunk, model = tokens.shape
    rows = quarters * chunk
    parts = lax.axis_size("seq")
    shards = lax.axis_size("shard")
    inner = 2
    outer = parts // inner
    seq_at = lax.axis_index("seq")
    inner_at = lax.rem(seq_at, inner)
    lru = branch_weight.shape[1]
    channels = lru // parts
    width = (channels + LANES) // LANES * LANES
    spare = width - channels
    blocks, block_width = rate_weight.shape[0], rate_weight.shape[1]
    piece = model // (parts * shards)

    def own(weight, axis):
        part = lax.dynamic_slice_in_dim(weight, seq_at * channels, channels, axis)
        pads = [(0, 0), (0, 0)]
        pads[axis] = (0, spare)
        return jnp.pad(part, pads)

    x = tokens.reshape(rows, model)
    cot = cotangent.reshape(rows, model)
    gain1, gain2 = first_gain[None], second_gain[None]
    params, mid, z, h, v, proj, gates, n1, w_in, w_out, n2, cot_all = forward(
        x,
        gain1,
        gain2,
        (conv_weight, conv_bias, rate_bias, entry_bias, decay_param),
        rate_weight.transpose(1, 0, 2),
        entry_weight.transpose(1, 0, 2),
        cot,
        jnp.concatenate([own(branch_weight, 1), own(input_weight, 1)], axis=1),
        own(output_weight, 0),
        quarters,
        chunk,
        outer,
        inner,
        shards,
        0,
    )
    w_in = w_in.reshape(model, 2 * width)
    n2 = n2.reshape(inner * shards * rows, model)
    cot_all = cot_all.reshape(inner * shards * rows, model)
    hidden = hidden_gate.shape[1] // inner
    wg = lax.dynamic_slice_in_dim(hidden_gate, inner_at * hidden, hidden, 1)
    wu = lax.dynamic_slice_in_dim(hidden_up, inner_at * hidden, hidden, 1)
    wd = lax.dynamic_slice_in_dim(hidden_down, inner_at * hidden, hidden, 0)

    gm = dot(n2, wg)
    um = dot(n2, wu)
    act, slope = gelu_and_slope(gm)
    mm = (act * um).astype(BF16)
    dmm = dot(cot_all, wd, ((1,), (1,)))
    dgm = (dmm * um * slope).astype(BF16)
    dum = (dmm * act).astype(BF16)
    dmid, gain2_grad, dout, partial, down_sum, gate_sum, rest_terms, up_terms = turn(
        dgm,
        dum,
        mm,
        mid,
        cot,
        gain2,
        hidden_gate,
        hidden_up,
        hidden_down,
        n2,
        cot_all,
        outer,
        inner,
        shards,
        1,
    )
    both, small, sums, result, rest_sum = scan_backward(
        quarters,
        chunk,
        blocks,
        block_width,
        dout,
        w_out,
        proj,
        h,
        v,
        params,
        gates,
        mid,
        partial,
        rest_terms,
        outer,
        inner,
        shards,
        2,
    )
    tokens_grad, mix, small, sums, gains, down_sum, gate_sum, rest_sum, up_sum = closing(
        both,
        w_in,
        z,
        x,
        dmid,
        gain1,
        gain2_grad,
        small,
        sums,
        n1.reshape(parts * rows, model),
        dout.reshape(parts * rows, model),
        down_sum,
        gate_sum,
        rest_sum,
        up_terms,
        outer,
        inner,
        shards,
        3,
    )
    (
        gate_grad,
        up_grad,
        down_grad,
        branch_grad,
        input_grad,
        output_grad,
        result,
        tokens_grad,
        rate_grad,
        entry_grad,
        tap_grad,
        conv_bias_grad,
        rate_bias_grad,
        entry_bias_grad,
        decay_grad,
        gain1_grad,
        gain2_grad,
    ) = unpack(
        gate_sum,
        rest_sum,
        up_sum,
        down_sum,
        mix,
        small,
        sums,
        result,
        tokens_grad,
        gains,
        inner,
        channels,
        blocks,
        block_width,
    )
    return (
        result.reshape(tokens.shape),
        tokens_grad.reshape(tokens.shape),
        gain1_grad,
        branch_grad,
        input_grad,
        tap_grad,
        conv_bias_grad,
        rate_grad.transpose(1, 0, 2),
        rate_bias_grad,
        entry_grad.transpose(1, 0, 2),
        entry_bias_grad,
        decay_grad,
        output_grad.T,
        gain2_grad,
        gate_grad,
        up_grad,
        down_grad.T,
    )


def solution(mesh):
    placed = (
        P(None, "shard", "seq", None),
        P(),
        P("shard", None),
        P("shard", None),
        P(None, "seq"),
        P("seq"),
        P("seq", None, None),
        P("seq"),
        P("seq", None, None),
        P("seq"),
        P("seq"),
        P(None, "shard"),
        P(),
        P(None, "shard"),
        P(None, "shard"),
        P("shard", None),
        P(None, "shard", "seq", None),
    )
    return jax.shard_map(
        body,
        mesh=mesh,
        in_specs=placed,
        out_specs=(
            P(None, "shard", "seq", None),
            P(None, "shard", "seq", None),
            P(("seq", "shard")),
            P(("seq", "shard"), None),
            P(("seq", "shard"), None),
            P(None, "seq"),
            P("seq"),
            P("seq", None, None),
            P("seq"),
            P("seq", None, None),
            P("seq"),
            P("seq"),
            P(None, ("seq", "shard")),
            P(("seq", "shard")),
            P(("seq", "shard"), None),
            P(("seq", "shard"), None),
            P(None, ("seq", "shard")),
        ),
        check_vma=False,
    )
```
